512 devices in a mesh: gx: 16 (over z), gy: 8 (over x_hi, y), gz: 4 (over x_lo, core).
Axes of the slice: x: 4 (x_hi: 2, x_lo: 2; x = x_hi * 2 + x_lo), y: 4, z: 16, core: 2. Of those that a mesh axis runs over, the one named last changes fastest.
Arguments:
- stress_trial: float32 [6, 12582912], P(None, ('gx', 'gy', 'gz')), may hold values from -6 to 6
- mean_stress: float32 [12582912], P(('gx', 'gy', 'gz')), may hold values from 0.3 to 2
- consolidation: float32 [12582912], P(('gx', 'gy', 'gz')), may hold values from 2.5 to 4
- point_velocity: float32 [3, 12582912], P(None, ('gx', 'gy', 'gz')), may hold values from -6 to 6
- point_weight: float32 [12582912], P(('gx', 'gy', 'gz')), may hold values from 0.5 to 1
- point_cell: int32 [12582912], P(('gx', 'gy', 'gz')), may hold values from 0 to 16383
- yield_flag: int32 [12582912], P(('gx', 'gy', 'gz')), may hold values 0 or 1
- point_count: int32 [16, 8, 4], P('gx', 'gy', 'gz'), may hold values from 12288 to 24576, as said below
- porosity: float32 [64, 128, 1024], P('gz', 'gx', 'gy'), may hold values from 0.2 to 0.5
- permeability: float32 [64, 128, 1024], P('gz', 'gx', 'gy'), may hold values from 1 to 10
Outputs:
- velocity: float32 [3, 64, 128, 1024], P(None, 'gz', 'gx', 'gy')
- pressure: float32 [64, 128, 1024], P('gz', 'gx', 'gy')
The draws below stay inside these ranges and needn't reach their ends.
Inputs may be any that keep to these rules, and one draw needn't show every extreme that they name: `point_cell`: a cell index within the brick, levels slowest, then rows, then columns. `point_count`: slots below the count hold live points, the rest are empty; some brick is full.
All inputs are finite; a program needn't handle non-finite values. No bound on the sum of `yield_flag` on one device may be relied on, other than what follows from the above.
Results may differ from the reference program's by a relative error of at most 0.0003.
Values sent between devices are 32-bit elements; how exact they have to be, the bound alone decides.
A program may use at most 128 MiB of HBM per device.

```python
import math
import jax
import jax.numpy as jnp

CX = 8
CY = 128
CZ = 16
NP_DEV = 24576
NX = 128
NY = 1024
NZ = 64
NP = 12582912
N_GX = 16
N_GY = 8
N_GZ = 4


def draw_point_count(key, part):
    bricks = N_GX * N_GY * N_GZ
    key_counts = jax.random.fold_in(key, 11)
    key_full = jax.random.fold_in(key, 23)
    counts = jax.random.randint(key_counts, (bricks,), NP_DEV // 2, NP_DEV + 1)
    chosen = jax.random.randint(key_full, (), 0, bricks)
    counts = jnp.where(jnp.arange(bricks) == chosen, NP_DEV, counts)
    return counts.reshape(N_GX, N_GY, N_GZ).astype(jnp.int32)


def place_ends(values, stream_key, low, top_value):
    longest = values.shape.index(max(values.shape))
    spots = []
    for shift in (0, 1):
        where = [jax.random.randint(jax.random.fold_in(stream_key, axis), (), 0, length) for axis, length in enumerate(values.shape)]
        where[longest] = (where[longest] + shift) % values.shape[longest]
        spots.append(tuple(where))
    return values.at[spots[0]].set(low).at[spots[1]].set(top_value)


def steps_of(own_key, extent, split, smallest, largest):
    gain, own = 1.0, jax.random.fold_in(own_key, 6)
    for position, parts in split:
        draws = jnp.exp(jax.random.uniform(jax.random.fold_in(own, position), (parts,), jnp.float32, smallest / len(split), largest / len(split)))
        gain = gain * jnp.repeat(draws, extent[position] // parts).reshape([-1 if axis == position else 1 for axis in range(len(extent))])
    return gain


def noise(stream_key, dims, scale, reach, split=(), kind=jnp.bfloat16):
    values = jax.random.normal(stream_key, dims, jnp.float32) * scale
    if len(split) > 0:
        values = steps_of(stream_key, dims, split, -0.22, 0.18) * values
    return jnp.clip(values, min=-reach, max=reach).astype(kind)


def setup_inputs(seed: int = 0) -> dict:
    key_list = jax.random.split(jax.random.key(seed), 11)
    return {
        "stress_trial": noise(key_list[0], (6, NP), 1.0, 6.0, ((1, 512),), jnp.float32),
        "mean_stress": jnp.clip(jnp.exp(math.log(2.0) - 1.89712 * jax.random.uniform(key_list[1], (NP,), jnp.float32) ** steps_of(key_list[1], (NP,), ((0, 512),), -0.2, 0.2)), 0.3, 2.0),
        "consolidation": jnp.clip(2.5 + 1.5 * jax.random.uniform(key_list[2], (NP,), jnp.float32) ** steps_of(key_list[2], (NP,), ((0, 512),), -0.2, 0.2), 2.5, 4.0),
        "point_velocity": noise(key_list[3], (3, NP), 1.0, 6.0, ((1, 512),), jnp.float32),
        "point_weight": jnp.clip(0.5 + 0.5 * jax.random.uniform(key_list[4], (NP,), jnp.float32) ** steps_of(key_list[4], (NP,), ((0, 512),), -0.2, 0.2), 0.5, 1.0),
        "point_cell": place_ends(jax.random.randint(key_list[5], (NP,), 0, CZ * CX * CY), jax.random.fold_in(key_list[5], 1), 0, (CZ * CX * CY) - 1).astype(jnp.int32),
        "yield_flag": place_ends((jax.random.randint(key_list[6], (NP,), 0, 2) < 1).astype(jnp.int32), jax.random.fold_in(key_list[6], 1), 0, 1),
        "point_count": draw_point_count(jax.random.fold_in(key_list[10], 71), 0),
        "porosity": jnp.clip(0.2 + 0.3 * jax.random.uniform(key_list[8], (NZ, NX, NY), jnp.float32) ** steps_of(key_list[8], (NZ, NX, NY), ((0, 4), (1, 16), (2, 8)), -0.2, 0.2), 0.2, 0.5),
        "permeability": jnp.clip(jnp.exp(math.log(10.0) - 2.3025851 * jax.random.uniform(key_list[9], (NZ, NX, NY), jnp.float32) ** steps_of(key_list[9], (NZ, NX, NY), ((0, 4), (1, 16), (2, 8)), -0.2, 0.2)), 1.0, 10.0),
    }


time_step = 0.25
storage_rate = 0.002
source_rate = 0.003
critical_slope = 1.2
mass_floor = 0.5
shear_floor = 1.0

def along_x(padded):
    return (padded[..., 1:-1, 2:, 1:-1] - padded[..., 1:-1, :-2, 1:-1]) * 0.5

def along_y(padded):
    return (padded[..., 1:-1, 1:-1, 2:] - padded[..., 1:-1, 1:-1, :-2]) * 0.5

def along_z(padded):
    return (padded[..., 2:, 1:-1, 1:-1] - padded[..., :-2, 1:-1, 1:-1]) * 0.5

def harmonic(former, latter):
    return 2.0 * former * latter / (former + latter)

def returned_stress(stress_trial, mean_stress, consolidation, yield_flag):
    sq_normal = stress_trial[0] * stress_trial[0] + stress_trial[1] * stress_trial[1] + stress_trial[2] * stress_trial[2]
    sq_shear = stress_trial[3] * stress_trial[3] + stress_trial[4] * stress_trial[4] + stress_trial[5] * stress_trial[5]
    shear_size = jnp.sqrt(1.5 * (sq_normal + 2.0 * sq_shear))
    yield_size = critical_slope * jnp.sqrt(mean_stress * (consolidation - mean_stress))
    factor = jnp.where(yield_flag == 1, yield_size / jnp.maximum(shear_size, shear_floor), 1.0)
    isotropic = jnp.array([1.0, 1.0, 1.0, 0.0, 0.0, 0.0], dtype=jnp.float32)[:, None]
    return stress_trial * factor - isotropic * mean_stress

def point_sums(stress, point_velocity, weight, cell_index, segments):
    stacked = jnp.concatenate([stress * weight, point_velocity * weight, weight[None]], axis=0)
    return jax.vmap(lambda component: jax.ops.segment_sum(component, cell_index, num_segments=segments))(stacked)

def brick_velocity(cell_sums, padded):
    floored = jnp.maximum(cell_sums[9], mass_floor)
    force_x = along_x(padded[0]) + along_y(padded[3]) + along_z(padded[5])
    force_y = along_x(padded[3]) + along_y(padded[1]) + along_z(padded[4])
    force_z = along_x(padded[5]) + along_y(padded[4]) + along_z(padded[2])
    return jnp.stack([(cell_sums[6] + time_step * force_x) / floored, (cell_sums[7] + time_step * force_y) / floored, (cell_sums[8] + time_step * force_z) / floored])

def divergence(padded_velocity):
    return along_x(padded_velocity[0]) + along_y(padded_velocity[1]) + along_z(padded_velocity[2])

def band_terms(porosity, permeability, level_below, level_above, at_top, dilation):
    up_face = harmonic(permeability, level_above)
    down_face = harmonic(level_below, permeability)
    top_face = jnp.where(at_top, permeability, up_face)
    lower_band = -time_step * down_face
    upper_band = -time_step * up_face
    main_band = storage_rate * porosity + time_step * (down_face + top_face)
    right_side = -source_rate * (1.0 - porosity) * dilation
    return (lower_band, main_band, upper_band, right_side)

def earlier(values, stride, filler):
    head = jnp.full((stride,) + values.shape[1:], filler, values.dtype)
    return jnp.concatenate([head, values[:-stride]], axis=0)

def later(values, stride, filler):
    tail = jnp.full((stride,) + values.shape[1:], filler, values.dtype)
    return jnp.concatenate([values[stride:], tail], axis=0)

def cyclic_solve(lower_band, main_band, upper_band, right_side):
    length = main_band.shape[0]
    for bit in range((length - 1).bit_length()):
        stride = 1 << bit
        back_weight = -lower_band / earlier(main_band, stride, 1.0)
        ahead_weight = -upper_band / later(main_band, stride, 1.0)
        new_lower = back_weight * earlier(lower_band, stride, 0.0)
        new_upper = ahead_weight * later(upper_band, stride, 0.0)
        new_main = main_band + back_weight * earlier(upper_band, stride, 0.0) + ahead_weight * later(lower_band, stride, 0.0)
        new_right = right_side + back_weight * earlier(right_side, stride, 0.0) + ahead_weight * later(right_side, stride, 0.0)
        lower_band, main_band, upper_band, right_side = (new_lower, new_main, new_upper, new_right)
    return right_side / main_band

def reference(stress_trial, mean_stress, consolidation, point_velocity, point_weight, point_cell, yield_flag, point_count, porosity, permeability):
    point_total = mean_stress.shape[0]
    slot_index = jnp.arange(point_total, dtype=jnp.int32)
    device = slot_index // NP_DEV
    is_live = slot_index % NP_DEV < point_count.reshape(-1)[device]
    row_index = device // (N_GY * N_GZ)
    column_index = device // N_GZ % N_GY
    layer_index = device % N_GZ
    local_z = point_cell // (CX * CY)
    local_x = point_cell // CY % CX
    local_y = point_cell % CY
    cell_index = ((layer_index * CZ + local_z) * NX + row_index * CX + local_x) * NY + column_index * CY + local_y
    weight = jnp.where(is_live, point_weight, 0.0)
    stress = returned_stress(stress_trial, mean_stress, consolidation, yield_flag)
    cell_sums = point_sums(stress, point_velocity, weight, cell_index, NZ * NX * NY).reshape(10, NZ, NX, NY)
    padded = jnp.pad(cell_sums[:6], ((0, 0), (1, 1), (1, 1), (1, 1)))
    velocity = brick_velocity(cell_sums, padded)
    dilation = divergence(jnp.pad(velocity, ((0, 0), (1, 1), (1, 1), (1, 1))))
    zero_level = jnp.zeros((1, NX, NY), permeability.dtype)
    level_above = jnp.concatenate([permeability[1:], zero_level], axis=0)
    level_below = jnp.concatenate([zero_level, permeability[:-1]], axis=0)
    at_top = (jnp.arange(NZ, dtype=jnp.int32) == NZ - 1)[:, None, None]
    band_set = band_terms(porosity, permeability, level_below, level_above, at_top, dilation)
    solved = cyclic_solve(band_set[0].reshape(NZ, NX * NY), band_set[1].reshape(NZ, NX * NY), band_set[2].reshape(NZ, NX * NY), band_set[3].reshape(NZ, NX * NY))
    pressure = solved.reshape(NZ, NX, NY)
    padded_pressure = jnp.pad(pressure, 1)
    gradient = jnp.stack([along_x(padded_pressure), along_y(padded_pressure), along_z(padded_pressure)])
    return (velocity - time_step * gradient, pressure)
```

```python
import jax
import jax.numpy as jnp
from jax import lax
from jax.sharding import PartitionSpec as P

time_step = 0.25
storage_rate = 0.002
source_rate = 0.003
critical_slope = 1.2
mass_floor = 0.5
shear_floor = 1.0

from jax.experimental import pallas as pl
from jax.experimental.pallas import tpu as pltpu

CHUNK = 1024
M_ROWS = 32
N_COLS = 512


def _split3(v):
    hi = v.astype(jnp.bfloat16)
    rest = v - hi.astype(jnp.float32)
    mid = rest.astype(jnp.bfloat16)
    lo = (rest - mid.astype(jnp.float32)).astype(jnp.bfloat16)
    return [hi, mid, lo]


def sums_kernel(count_ref, st_ref, ms_ref, cons_ref, vel_ref, w_ref, cell_ref, yf_ref, out_ref, acc_ref):
    count = count_ref[0, 0]
    acc_ref[...] = jnp.zeros_like(acc_ref)
    chunks = st_ref.shape[1] // CHUNK

    def body(k, carry):
        start = pl.multiple_of(k * CHUNK, CHUNK)
        span = pl.ds(start, CHUNK)
        st = [st_ref[pl.ds(i, 1), span] for i in range(6)]
        ms = ms_ref[:, span]
        cons = cons_ref[:, span]
        yf = yf_ref[:, span]
        slot = start + lax.broadcasted_iota(jnp.int32, (1, CHUNK), 1)
        weight = jnp.where(slot < count, w_ref[:, span], 0.0)
        sq_normal = st[0] * st[0] + st[1] * st[1] + st[2] * st[2]
        sq_shear = st[3] * st[3] + st[4] * st[4] + st[5] * st[5]
        shear_size = jnp.sqrt(1.5 * (sq_normal + 2.0 * sq_shear))
        yield_size = critical_slope * jnp.sqrt(ms * (cons - ms))
        factor = jnp.where(yf == 1, yield_size / jnp.maximum(shear_size, shear_floor), 1.0)
        stress = [st[i] * factor - ms if i < 3 else st[i] * factor for i in range(6)]
        values = [s * weight for s in stress]
        values += [vel_ref[pl.ds(i, 1), span] * weight for i in range(3)]
        values.append(weight)
        cell = cell_ref[:, span]
        m_key = (cell >> 12) * 8 + ((cell >> 7) & 7)
        n_key = ((cell >> 10) & 3) * 128 + (cell & 127)
        m_mask = lax.broadcasted_iota(jnp.int32, (M_ROWS, CHUNK), 0) == m_key
        zero = jnp.zeros((M_ROWS, CHUNK), jnp.bfloat16)
        pieces = []
        for v in values:
            for part in _split3(v):
                pieces.append(jnp.where(m_mask, jnp.broadcast_to(part, (M_ROWS, CHUNK)), zero))
        lhs = jnp.concatenate(pieces, axis=0)
        one_hot = jnp.where(
            lax.broadcasted_iota(jnp.int32, (N_COLS, CHUNK), 0) == n_key, 1.0, 0.0
        ).astype(jnp.bfloat16)
        acc_ref[...] += lax.dot_general(
            lhs, one_hot, (((1,), (1,)), ((), ())), preferred_element_type=jnp.float32
        )
        return carry

    lax.fori_loop(0, chunks, body, 0)
    for comp in range(10):
        for level in range(16):
            rows = pl.ds((comp * 3) * M_ROWS + (level >> 2) * 8, 8)
            lanes = pl.ds((level & 3) * 128, 128)
            total = acc_ref[rows, lanes]
            for s in (1, 2):
                total = total + acc_ref[pl.ds((comp * 3 + s) * M_ROWS + (level >> 2) * 8, 8), lanes]
            out_ref[comp, level] = total


def cell_sums_of(stress_trial, mean_stress, consolidation, point_velocity, point_weight, point_cell, yield_flag, point_count, levels, extent, breadth):
    n = mean_stress.shape[0]
    row = lambda a: a.reshape(1, n)
    vmem = pl.BlockSpec(memory_space=pltpu.VMEM)
    return pl.pallas_call(
        sums_kernel,
        out_shape=jax.ShapeDtypeStruct((10, levels, extent, breadth), jnp.float32),
        in_specs=[pl.BlockSpec(memory_space=pltpu.SMEM)] + [vmem] * 7,
        out_specs=vmem,
        scratch_shapes=[pltpu.VMEM((30 * M_ROWS, N_COLS), jnp.float32)],
        cost_estimate=pl.CostEstimate(
            flops=2 * 30 * M_ROWS * N_COLS * n, bytes_accessed=13 * 4 * n + 10 * 4 * levels * extent * breadth,
            transcendentals=3 * n,
        ),
    )(
        point_count.reshape(1, 1), stress_trial, row(mean_stress), row(consolidation), point_velocity,
        row(point_weight), row(point_cell), row(yield_flag),
    )


def padded_2(cells, sides, width):
    for axis, dim in sides:
        count = lax.axis_size(axis)
        ends = count - 1
        head = lax.slice_in_dim(cells, 0, width, axis=dim)
        tail = lax.slice_in_dim(cells, cells.shape[dim] - width, cells.shape[dim], axis=dim)
        cells = jnp.concatenate(
            [
                lax.ppermute(tail, axis, [(i, (i + 1) % count) for i in range(ends)]),
                cells,
                lax.ppermute(head, axis, [((i + 1) % count, i) for i in range(ends)]),
            ],
            axis=dim,
        )
    return cells


def along_x(padded):
    return (padded[..., 1:-1, 2:, 1:-1] - padded[..., 1:-1, :-2, 1:-1]) * 0.5


def along_y(padded):
    return (padded[..., 1:-1, 1:-1, 2:] - padded[..., 1:-1, 1:-1, :-2]) * 0.5


def along_z(padded):
    return (padded[..., 2:, 1:-1, 1:-1] - padded[..., :-2, 1:-1, 1:-1]) * 0.5


def harmonic(former, latter):
    return 2.0 * former * latter / (former + latter)


def returned_stress(stress_trial, mean_stress, consolidation, yield_flag):
    sq_normal = (
        stress_trial[0] * stress_trial[0]
        + stress_trial[1] * stress_trial[1]
        + stress_trial[2] * stress_trial[2]
    )
    sq_shear = (
        stress_trial[3] * stress_trial[3]
        + stress_trial[4] * stress_trial[4]
        + stress_trial[5] * stress_trial[5]
    )
    shear_size = jnp.sqrt(1.5 * (sq_normal + 2.0 * sq_shear))
    yield_size = critical_slope * jnp.sqrt(mean_stress * (consolidation - mean_stress))
    factor = jnp.where(yield_flag == 1, yield_size / jnp.maximum(shear_size, shear_floor), 1.0)
    isotropic = jnp.array([1.0, 1.0, 1.0, 0.0, 0.0, 0.0], dtype=jnp.float32)[:, None]
    return stress_trial * factor - isotropic * mean_stress


def point_sums(stress, point_velocity, weight, cell_index, segments):
    stacked = jnp.concatenate([stress * weight, point_velocity * weight, weight[None]], axis=0)
    return jax.vmap(
        lambda component: jax.ops.segment_sum(component, cell_index, num_segments=segments)
    )(stacked)


def brick_velocity(cell_sums, padded):
    floored = jnp.maximum(cell_sums[9], mass_floor)
    force_x = along_x(padded[0]) + along_y(padded[3]) + along_z(padded[5])
    force_y = along_x(padded[3]) + along_y(padded[1]) + along_z(padded[4])
    force_z = along_x(padded[5]) + along_y(padded[4]) + along_z(padded[2])
    return jnp.stack(
        [
            (cell_sums[6] + time_step * force_x) / floored,
            (cell_sums[7] + time_step * force_y) / floored,
            (cell_sums[8] + time_step * force_z) / floored,
        ]
    )


def divergence(padded_velocity):
    return along_x(padded_velocity[0]) + along_y(padded_velocity[1]) + along_z(padded_velocity[2])


def band_terms(porosity, permeability, level_below, level_above, at_top, dilation):
    up_face = harmonic(permeability, level_above)
    down_face = harmonic(level_below, permeability)
    top_face = jnp.where(at_top, permeability, up_face)
    lower_band = -time_step * down_face
    upper_band = -time_step * up_face
    main_band = storage_rate * porosity + time_step * (down_face + top_face)
    right_side = -source_rate * (1.0 - porosity) * dilation
    return (lower_band, main_band, upper_band, right_side)


def earlier(values, stride, filler):
    head = jnp.full((stride,) + values.shape[1:], filler, values.dtype)
    return jnp.concatenate([head, values[:-stride]], axis=0)


def later(values, stride, filler):
    tail = jnp.full((stride,) + values.shape[1:], filler, values.dtype)
    return jnp.concatenate([values[stride:], tail], axis=0)


def cyclic_solve(lower_band, main_band, upper_band, right_side):
    length = main_band.shape[0]
    for bit in range((length - 1).bit_length()):
        stride = 1 << bit
        back_weight = -lower_band / earlier(main_band, stride, 1.0)
        ahead_weight = -upper_band / later(main_band, stride, 1.0)
        new_lower = back_weight * earlier(lower_band, stride, 0.0)
        new_upper = ahead_weight * later(upper_band, stride, 0.0)
        new_main = (
            main_band
            + back_weight * earlier(upper_band, stride, 0.0)
            + ahead_weight * later(lower_band, stride, 0.0)
        )
        new_right = (
            right_side
            + back_weight * earlier(right_side, stride, 0.0)
            + ahead_weight * later(right_side, stride, 0.0)
        )
        lower_band, main_band, upper_band, right_side = (new_lower, new_main, new_upper, new_right)
    return right_side / main_band


def brick_bands(porosity, permeability, padded, dilation, levels, layer_count):
    level_index = lax.axis_index("gz") * levels + jnp.arange(levels, dtype=jnp.int32)
    at_top = (level_index == levels * layer_count - 1)[:, None, None]
    return band_terms(
        porosity,
        permeability,
        padded[6, :-2, 1:-1, 1:-1],
        padded[6, 2:, 1:-1, 1:-1],
        at_top,
        dilation,
    )


def shards(
    stress_trial,
    mean_stress,
    consolidation,
    point_velocity,
    point_weight,
    point_cell,
    yield_flag,
    point_count,
    porosity,
    permeability,
):
    levels, extent, breadth = porosity.shape
    cell_sums = cell_sums_of(
        stress_trial, mean_stress, consolidation, point_velocity, point_weight, point_cell,
        yield_flag, point_count, levels, extent, breadth,
    )
    outgoing = jnp.concatenate([cell_sums[:6], permeability[None]], axis=0)
    padded = padded_2(outgoing, (("gx", 2), ("gy", 3), ("gz", 1)), 1)
    velocity = brick_velocity(cell_sums, padded)
    padded_velocity = padded_2(velocity, (("gx", 2), ("gy", 3), ("gz", 1)), 1)
    dilation = divergence(padded_velocity)
    layer_count = lax.axis_size("gz")
    band_set = brick_bands(porosity, permeability, padded, dilation, levels, layer_count)
    columns = lax.all_to_all(jnp.stack(band_set), "gz", split_axis=3, concat_axis=1, tiled=True)
    height = columns.shape[1]
    flattened = columns.reshape(4, height, -1)
    solved = cyclic_solve(flattened[0], flattened[1], flattened[2], flattened[3])
    pressure = lax.all_to_all(
        solved.reshape(height, extent, -1), "gz", split_axis=0, concat_axis=2, tiled=True
    )
    padded_pressure = padded_2(pressure, (("gx", 1), ("gy", 2), ("gz", 0)), 1)
    gradient = jnp.stack(
        [along_x(padded_pressure), along_y(padded_pressure), along_z(padded_pressure)]
    )
    return (velocity - time_step * gradient, pressure)


def solution(mesh):
    placed = (
        P(None, ("gx", "gy", "gz")),
        P(("gx", "gy", "gz")),
        P(("gx", "gy", "gz")),
        P(None, ("gx", "gy", "gz")),
        P(("gx", "gy", "gz")),
        P(("gx", "gy", "gz")),
        P(("gx", "gy", "gz")),
        P("gx", "gy", "gz"),
        P("gz", "gx", "gy"),
        P("gz", "gx", "gy"),
    )
    return jax.shard_map(
        shards,
        mesh=mesh,
        in_specs=placed,
        out_specs=(P(None, "gz", "gx", "gy"), P("gz", "gx", "gy")),
        check_vma=False,
    )
```

```python
import jax
import jax.numpy as jnp
from jax import lax
from jax.sharding import PartitionSpec as P

time_step = 0.25
storage_rate = 0.002
source_rate = 0.003
critical_slope = 1.2
mass_floor = 0.5
shear_floor = 1.0

from jax.experimental import pallas as pl
from jax.experimental.pallas import tpu as pltpu

CHUNK = 1024
M_ROWS = 32
N_COLS = 512


def _split3(v):
    hi = v.astype(jnp.bfloat16)
    rest = v - hi.astype(jnp.float32)
    mid = rest.astype(jnp.bfloat16)
    lo = (rest - mid.astype(jnp.float32)).astype(jnp.bfloat16)
    return [hi, mid, lo]


def sums_kernel(count_ref, st_ref, ms_ref, cons_ref, vel_ref, w_ref, cell_ref, yf_ref, out_ref, acc_ref):
    count = count_ref[0, 0]
    acc_ref[...] = jnp.zeros_like(acc_ref)
    chunks = st_ref.shape[1] // CHUNK

    def body(k, carry):
        start = pl.multiple_of(k * CHUNK, CHUNK)
        span = pl.ds(start, CHUNK)
        st = [st_ref[pl.ds(i, 1), span] for i in range(6)]
        ms = ms_ref[:, span]
        cons = cons_ref[:, span]
        yf = yf_ref[:, span]
        slot = start + lax.broadcasted_iota(jnp.int32, (1, CHUNK), 1)
        weight = jnp.where(slot < count, w_ref[:, span], 0.0)
        sq_normal = st[0] * st[0] + st[1] * st[1] + st[2] * st[2]
        sq_shear = st[3] * st[3] + st[4] * st[4] + st[5] * st[5]
        shear_size = jnp.sqrt(1.5 * (sq_normal + 2.0 * sq_shear))
        yield_size = critical_slope * jnp.sqrt(ms * (cons - ms))
        factor = jnp.where(yf == 1, yield_size / jnp.maximum(shear_size, shear_floor), 1.0)
        stress = [st[i] * factor - ms if i < 3 else st[i] * factor for i in range(6)]
        values = [s * weight for s in stress]
        values += [vel_ref[pl.ds(i, 1), span] * weight for i in range(3)]
        values.append(weight)
        cell = cell_ref[:, span]
        m_key = (cell >> 12) * 8 + ((cell >> 7) & 7)
        n_key = ((cell >> 10) & 3) * 128 + (cell & 127)
        m_mask = lax.broadcasted_iota(jnp.int32, (M_ROWS, CHUNK), 0) == m_key
        zero = jnp.zeros((M_ROWS, CHUNK), jnp.bfloat16)
        pieces = []
        for v in values:
            for part in _split3(v):
                pieces.append(jnp.where(m_mask, jnp.broadcast_to(part, (M_ROWS, CHUNK)), zero))
        lhs = jnp.concatenate(pieces, axis=0)
        one_hot = jnp.where(
            lax.broadcasted_iota(jnp.int32, (N_COLS, CHUNK), 0) == n_key, 1.0, 0.0
        ).astype(jnp.bfloat16)
        acc_ref[...] += lax.dot_general(
            lhs, one_hot, (((1,), (1,)), ((), ())), preferred_element_type=jnp.float32
        )
        return carry

    lax.fori_loop(0, chunks, body, 0)
    for comp in range(10):
        for level in range(16):
            rows = pl.ds((comp * 3) * M_ROWS + (level >> 2) * 8, 8)
            lanes = pl.ds((level & 3) * 128, 128)
            total = acc_ref[rows, lanes]
            for s in (1, 2):
                total = total + acc_ref[pl.ds((comp * 3 + s) * M_ROWS + (level >> 2) * 8, 8), lanes]
            out_ref[comp, level] = total


def cell_sums_of(stress_trial, mean_stress, consolidation, point_velocity, point_weight, point_cell, yield_flag, point_count, levels, extent, breadth):
    n = mean_stress.shape[0]
    row = lambda a: a.reshape(1, n)
    vmem = pl.BlockSpec(memory_space=pltpu.VMEM)
    return pl.pallas_call(
        sums_kernel,
        out_shape=jax.ShapeDtypeStruct((10, levels, extent, breadth), jnp.float32),
        in_specs=[pl.BlockSpec(memory_space=pltpu.SMEM)] + [vmem] * 7,
        out_specs=vmem,
        scratch_shapes=[pltpu.VMEM((30 * M_ROWS, N_COLS), jnp.float32)],
        cost_estimate=pl.CostEstimate(
            flops=2 * 30 * M_ROWS * N_COLS * n, bytes_accessed=13 * 4 * n + 10 * 4 * levels * extent * breadth,
            transcendentals=3 * n,
        ),
    )(
        point_count.reshape(1, 1), stress_trial, row(mean_stress), row(consolidation), point_velocity,
        row(point_weight), row(point_cell), row(yield_flag),
    )


def padded_2(cells, sides, width):
    for axis, dim in sides:
        count = lax.axis_size(axis)
        ends = count - 1
        head = lax.slice_in_dim(cells, 0, width, axis=dim)
        tail = lax.slice_in_dim(cells, cells.shape[dim] - width, cells.shape[dim], axis=dim)
        cells = jnp.concatenate(
            [
                lax.ppermute(tail, axis, [(i, (i + 1) % count) for i in range(ends)]),
                cells,
                lax.ppermute(head, axis, [((i + 1) % count, i) for i in range(ends)]),
            ],
            axis=dim,
        )
    return cells


def along_x(padded):
    return (padded[..., 1:-1, 2:, 1:-1] - padded[..., 1:-1, :-2, 1:-1]) * 0.5


def along_y(padded):
    return (padded[..., 1:-1, 1:-1, 2:] - padded[..., 1:-1, 1:-1, :-2]) * 0.5


def along_z(padded):
    return (padded[..., 2:, 1:-1, 1:-1] - padded[..., :-2, 1:-1, 1:-1]) * 0.5


def harmonic(former, latter):
    return 2.0 * former * latter / (former + latter)


def returned_stress(stress_trial, mean_stress, consolidation, yield_flag):
    sq_normal = (
        stress_trial[0] * stress_trial[0]
        + stress_trial[1] * stress_trial[1]
        + stress_trial[2] * stress_trial[2]
    )
    sq_shear = (
        stress_trial[3] * stress_trial[3]
        + stress_trial[4] * stress_trial[4]
        + stress_trial[5] * stress_trial[5]
    )
    shear_size = jnp.sqrt(1.5 * (sq_normal + 2.0 * sq_shear))
    yield_size = critical_slope * jnp.sqrt(mean_stress * (consolidation - mean_stress))
    factor = jnp.where(yield_flag == 1, yield_size / jnp.maximum(shear_size, shear_floor), 1.0)
    isotropic = jnp.array([1.0, 1.0, 1.0, 0.0, 0.0, 0.0], dtype=jnp.float32)[:, None]
    return stress_trial * factor - isotropic * mean_stress


def point_sums(stress, point_velocity, weight, cell_index, segments):
    stacked = jnp.concatenate([stress * weight, point_velocity * weight, weight[None]], axis=0)
    return jax.vmap(
        lambda component: jax.ops.segment_sum(component, cell_index, num_segments=segments)
    )(stacked)


def brick_velocity(cell_sums, padded):
    floored = jnp.maximum(cell_sums[9], mass_floor)
    force_x = along_x(padded[0]) + along_y(padded[3]) + along_z(padded[5])
    force_y = along_x(padded[3]) + along_y(padded[1]) + along_z(padded[4])
    force_z = along_x(padded[5]) + along_y(padded[4]) + along_z(padded[2])
    return jnp.stack(
        [
            (cell_sums[6] + time_step * force_x) / floored,
            (cell_sums[7] + time_step * force_y) / floored,
            (cell_sums[8] + time_step * force_z) / floored,
        ]
    )


def divergence(padded_velocity):
    return along_x(padded_velocity[0]) + along_y(padded_velocity[1]) + along_z(padded_velocity[2])


def band_terms(porosity, permeability, level_below, level_above, at_top, dilation):
    up_face = harmonic(permeability, level_above)
    down_face = harmonic(level_below, permeability)
    top_face = jnp.where(at_top, permeability, up_face)
    lower_band = -time_step * down_face
    upper_band = -time_step * up_face
    main_band = storage_rate * porosity + time_step * (down_face + top_face)
    right_side = -source_rate * (1.0 - porosity) * dilation
    return (lower_band, main_band, upper_band, right_side)


def earlier(values, stride, filler):
    head = jnp.full((stride,) + values.shape[1:], filler, values.dtype)
    return jnp.concatenate([head, values[:-stride]], axis=0)


def later(values, stride, filler):
    tail = jnp.full((stride,) + values.shape[1:], filler, values.dtype)
    return jnp.concatenate([values[stride:], tail], axis=0)


def cyclic_solve(lower_band, main_band, upper_band, right_side):
    length = main_band.shape[0]
    for bit in range((length - 1).bit_length()):
        stride = 1 << bit
        back_weight = -lower_band / earlier(main_band, stride, 1.0)
        ahead_weight = -upper_band / later(main_band, stride, 1.0)
        new_lower = back_weight * earlier(lower_band, stride, 0.0)
        new_upper = ahead_weight * later(upper_band, stride, 0.0)
        new_main = (
            main_band
            + back_weight * earlier(upper_band, stride, 0.0)
            + ahead_weight * later(lower_band, stride, 0.0)
        )
        new_right = (
            right_side
            + back_weight * earlier(right_side, stride, 0.0)
            + ahead_weight * later(right_side, stride, 0.0)
        )
        lower_band, main_band, upper_band, right_side = (new_lower, new_main, new_upper, new_right)
    return right_side / main_band


def face_from(part, axis, from_lower):
    count = lax.axis_size(axis)
    if from_lower:
        pairs = [(i, i + 1) for i in range(count - 1)]
    else:
        pairs = [(i + 1, i) for i in range(count - 1)]
    return lax.ppermute(part, axis, pairs)


def faces_of(cells, sides):
    got = {}
    for axis, dim in sides:
        size = cells.shape[dim]
        got[dim] = (
            face_from(lax.slice_in_dim(cells, size - 1, size, axis=dim), axis, True),
            face_from(lax.slice_in_dim(cells, 0, 1, axis=dim), axis, False),
        )
    return got


def along(cells, faces, dim):
    size = cells.shape[dim]
    lower, upper = faces[dim]
    ahead = jnp.concatenate([lax.slice_in_dim(cells, 1, size, axis=dim), upper], axis=dim)
    behind = jnp.concatenate([lower, lax.slice_in_dim(cells, 0, size - 1, axis=dim)], axis=dim)
    return (ahead - behind) * 0.5


def shards(
    stress_trial,
    mean_stress,
    consolidation,
    point_velocity,
    point_weight,
    point_cell,
    yield_flag,
    point_count,
    porosity,
    permeability,
):
    levels, extent, breadth = porosity.shape
    all_porosity = lax.all_gather(porosity, "gz", axis=0, tiled=True)
    all_permeability = lax.all_gather(permeability, "gz", axis=0, tiled=True)
    height = all_porosity.shape[0]
    cell_sums = cell_sums_of(
        stress_trial, mean_stress, consolidation, point_velocity, point_weight, point_cell,
        yield_flag, point_count, levels, extent, breadth,
    )
    sides = (("gx", 2), ("gy", 3), ("gz", 1))
    stress_sums = cell_sums[:6]
    sf = faces_of(stress_sums, sides)
    d_x = lambda c: along(stress_sums[c:c + 1], {2: (sf[2][0][c:c + 1], sf[2][1][c:c + 1])}, 2)[0]
    d_y = lambda c: along(stress_sums[c:c + 1], {3: (sf[3][0][c:c + 1], sf[3][1][c:c + 1])}, 3)[0]
    d_z = lambda c: along(stress_sums[c:c + 1], {1: (sf[1][0][c:c + 1], sf[1][1][c:c + 1])}, 1)[0]
    floored = jnp.maximum(cell_sums[9], mass_floor)
    force_x = d_x(0) + d_y(3) + d_z(5)
    force_y = d_x(3) + d_y(1) + d_z(4)
    force_z = d_x(5) + d_y(4) + d_z(2)
    velocity = jnp.stack(
        [
            (cell_sums[6] + time_step * force_x) / floored,
            (cell_sums[7] + time_step * force_y) / floored,
            (cell_sums[8] + time_step * force_z) / floored,
        ]
    )
    vf = faces_of(velocity, sides)
    dilation = (
        along(velocity[0:1], {2: (vf[2][0][0:1], vf[2][1][0:1])}, 2)[0]
        + along(velocity[1:2], {3: (vf[3][0][1:2], vf[3][1][1:2])}, 3)[0]
        + along(velocity[2:3], {1: (vf[1][0][2:3], vf[1][1][2:3])}, 1)[0]
    )
    right_side = -source_rate * (1.0 - porosity) * dilation
    all_right = lax.all_gather(right_side, "gz", axis=0, tiled=True)
    zero_level = jnp.zeros((1, extent, breadth), jnp.float32)
    level_above = jnp.concatenate([all_permeability[1:], zero_level], axis=0)
    level_below = jnp.concatenate([zero_level, all_permeability[:-1]], axis=0)
    at_top = (jnp.arange(height, dtype=jnp.int32) == height - 1)[:, None, None]
    up_face = harmonic(all_permeability, level_above)
    down_face = harmonic(level_below, all_permeability)
    top_face = jnp.where(at_top, all_permeability, up_face)
    lower_band = -time_step * down_face
    upper_band = -time_step * up_face
    main_band = storage_rate * all_porosity + time_step * (down_face + top_face)
    column = height, extent * breadth
    solved = cyclic_solve(
        lower_band.reshape(column), main_band.reshape(column), upper_band.reshape(column),
        all_right.reshape(column),
    ).reshape(height, extent, breadth)
    first = lax.axis_index("gz") * levels
    around = lax.dynamic_slice_in_dim(
        jnp.concatenate([zero_level, solved, zero_level], axis=0), first, levels + 2, axis=0
    )
    pressure = around[1:-1]
    pf = faces_of(pressure, (("gx", 1), ("gy", 2)))
    gradient = jnp.stack(
        [
            along(pressure, pf, 1),
            along(pressure, pf, 2),
            (around[2:] - around[:-2]) * 0.5,
        ]
    )
    return (velocity - time_step * gradient, pressure)


def solution(mesh):
    placed = (
        P(None, ("gx", "gy", "gz")),
        P(("gx", "gy", "gz")),
        P(("gx", "gy", "gz")),
        P(None, ("gx", "gy", "gz")),
        P(("gx", "gy", "gz")),
        P(("gx", "gy", "gz")),
        P(("gx", "gy", "gz")),
        P("gx", "gy", "gz"),
        P("gz", "gx", "gy"),
        P("gz", "gx", "gy"),
    )
    return jax.shard_map(
        shards,
        mesh=mesh,
        in_specs=placed,
        out_specs=(P(None, "gz", "gx", "gy"), P("gz", "gx", "gy")),
        check_vma=False,
    )
```

```python
import functools

import jax
import jax.numpy as jnp
from jax import lax
from jax.sharding import PartitionSpec as P

time_step = 0.25
storage_rate = 0.002
source_rate = 0.003
critical_slope = 1.2
mass_floor = 0.5
shear_floor = 1.0

from jax.experimental import pallas as pl
from jax.experimental.pallas import tpu as pltpu

CHUNK = 1024
M_ROWS = 32
N_COLS = 512


def _split3(v):
    hi = v.astype(jnp.bfloat16)
    rest = v - hi.astype(jnp.float32)
    mid = rest.astype(jnp.bfloat16)
    lo = (rest - mid.astype(jnp.float32)).astype(jnp.bfloat16)
    return [hi, mid, lo]


def sums_kernel(count_ref, st_ref, ms_ref, cons_ref, vel_ref, w_ref, cell_ref, yf_ref, out_ref, acc_ref):
    count = count_ref[0, 0]
    acc_ref[...] = jnp.zeros_like(acc_ref)
    chunks = st_ref.shape[1] // CHUNK

    def body(k, carry):
        start = pl.multiple_of(k * CHUNK, CHUNK)
        span = pl.ds(start, CHUNK)
        st = [st_ref[pl.ds(i, 1), span] for i in range(6)]
        ms = ms_ref[:, span]
        cons = cons_ref[:, span]
        yf = yf_ref[:, span]
        slot = start + lax.broadcasted_iota(jnp.int32, (1, CHUNK), 1)
        weight = jnp.where(slot < count, w_ref[:, span], 0.0)
        sq_normal = st[0] * st[0] + st[1] * st[1] + st[2] * st[2]
        sq_shear = st[3] * st[3] + st[4] * st[4] + st[5] * st[5]
        shear_size = jnp.sqrt(1.5 * (sq_normal + 2.0 * sq_shear))
        yield_size = critical_slope * jnp.sqrt(ms * (cons - ms))
        factor = jnp.where(yf == 1, yield_size / jnp.maximum(shear_size, shear_floor), 1.0)
        stress = [st[i] * factor - ms if i < 3 else st[i] * factor for i in range(6)]
        values = [s * weight for s in stress]
        values += [vel_ref[pl.ds(i, 1), span] * weight for i in range(3)]
        values.append(weight)
        cell = cell_ref[:, span]
        m_key = (cell >> 12) * 8 + ((cell >> 7) & 7)
        n_key = ((cell >> 10) & 3) * 128 + (cell & 127)
        m_mask = lax.broadcasted_iota(jnp.int32, (M_ROWS, CHUNK), 0) == m_key
        zero = jnp.zeros((M_ROWS, CHUNK), jnp.bfloat16)
        pieces = []
        for v in values:
            for part in _split3(v):
                pieces.append(jnp.where(m_mask, jnp.broadcast_to(part, (M_ROWS, CHUNK)), zero))
        lhs = jnp.concatenate(pieces, axis=0)
        one_hot = jnp.where(
            lax.broadcasted_iota(jnp.int32, (N_COLS, CHUNK), 0) == n_key, 1.0, 0.0
        ).astype(jnp.bfloat16)
        acc_ref[...] += lax.dot_general(
            lhs, one_hot, (((1,), (1,)), ((), ())), preferred_element_type=jnp.float32
        )
        return carry

    lax.fori_loop(0, chunks, body, 0)
    for comp in range(10):
        for level in range(16):
            rows = pl.ds((comp * 3) * M_ROWS + (level >> 2) * 8, 8)
            lanes = pl.ds((level & 3) * 128, 128)
            total = acc_ref[rows, lanes]
            for s in (1, 2):
                total = total + acc_ref[pl.ds((comp * 3 + s) * M_ROWS + (level >> 2) * 8, 8), lanes]
            out_ref[comp, level] = total


def cell_sums_of(stress_trial, mean_stress, consolidation, point_velocity, point_weight, point_cell, yield_flag, point_count, levels, extent, breadth):
    n = mean_stress.shape[0]
    row = lambda a: a.reshape(1, n)
    vmem = pl.BlockSpec(memory_space=pltpu.VMEM)
    return pl.pallas_call(
        sums_kernel,
        out_shape=jax.ShapeDtypeStruct((10, levels, extent, breadth), jnp.float32),
        in_specs=[pl.BlockSpec(memory_space=pltpu.SMEM)] + [vmem] * 7,
        out_specs=vmem,
        scratch_shapes=[pltpu.VMEM((30 * M_ROWS, N_COLS), jnp.float32)],
        cost_estimate=pl.CostEstimate(
            flops=2 * 30 * M_ROWS * N_COLS * n, bytes_accessed=13 * 4 * n + 10 * 4 * levels * extent * breadth,
            transcendentals=3 * n,
        ),
    )(
        point_count.reshape(1, 1), stress_trial, row(mean_stress), row(consolidation), point_velocity,
        row(point_weight), row(point_cell), row(yield_flag),
    )


def padded_2(cells, sides, width):
    for axis, dim in sides:
        count = lax.axis_size(axis)
        ends = count - 1
        head = lax.slice_in_dim(cells, 0, width, axis=dim)
        tail = lax.slice_in_dim(cells, cells.shape[dim] - width, cells.shape[dim], axis=dim)
        cells = jnp.concatenate(
            [
                lax.ppermute(tail, axis, [(i, (i + 1) % count) for i in range(ends)]),
                cells,
                lax.ppermute(head, axis, [((i + 1) % count, i) for i in range(ends)]),
            ],
            axis=dim,
        )
    return cells


def along_x(padded):
    return (padded[..., 1:-1, 2:, 1:-1] - padded[..., 1:-1, :-2, 1:-1]) * 0.5


def along_y(padded):
    return (padded[..., 1:-1, 1:-1, 2:] - padded[..., 1:-1, 1:-1, :-2]) * 0.5


def along_z(padded):
    return (padded[..., 2:, 1:-1, 1:-1] - padded[..., :-2, 1:-1, 1:-1]) * 0.5


def harmonic(former, latter):
    return 2.0 * former * latter / (former + latter)


def returned_stress(stress_trial, mean_stress, consolidation, yield_flag):
    sq_normal = (
        stress_trial[0] * stress_trial[0]
        + stress_trial[1] * stress_trial[1]
        + stress_trial[2] * stress_trial[2]
    )
    sq_shear = (
        stress_trial[3] * stress_trial[3]
        + stress_trial[4] * stress_trial[4]
        + stress_trial[5] * stress_trial[5]
    )
    shear_size = jnp.sqrt(1.5 * (sq_normal + 2.0 * sq_shear))
    yield_size = critical_slope * jnp.sqrt(mean_stress * (consolidation - mean_stress))
    factor = jnp.where(yield_flag == 1, yield_size / jnp.maximum(shear_size, shear_floor), 1.0)
    isotropic = jnp.array([1.0, 1.0, 1.0, 0.0, 0.0, 0.0], dtype=jnp.float32)[:, None]
    return stress_trial * factor - isotropic * mean_stress


def point_sums(stress, point_velocity, weight, cell_index, segments):
    stacked = jnp.concatenate([stress * weight, point_velocity * weight, weight[None]], axis=0)
    return jax.vmap(
        lambda component: jax.ops.segment_sum(component, cell_index, num_segments=segments)
    )(stacked)


def brick_velocity(cell_sums, padded):
    floored = jnp.maximum(cell_sums[9], mass_floor)
    force_x = along_x(padded[0]) + along_y(padded[3]) + along_z(padded[5])
    force_y = along_x(padded[3]) + along_y(padded[1]) + along_z(padded[4])
    force_z = along_x(padded[5]) + along_y(padded[4]) + along_z(padded[2])
    return jnp.stack(
        [
            (cell_sums[6] + time_step * force_x) / floored,
            (cell_sums[7] + time_step * force_y) / floored,
            (cell_sums[8] + time_step * force_z) / floored,
        ]
    )


def divergence(padded_velocity):
    return along_x(padded_velocity[0]) + along_y(padded_velocity[1]) + along_z(padded_velocity[2])


def band_terms(porosity, permeability, level_below, level_above, at_top, dilation):
    up_face = harmonic(permeability, level_above)
    down_face = harmonic(level_below, permeability)
    top_face = jnp.where(at_top, permeability, up_face)
    lower_band = -time_step * down_face
    upper_band = -time_step * up_face
    main_band = storage_rate * porosity + time_step * (down_face + top_face)
    right_side = -source_rate * (1.0 - porosity) * dilation
    return (lower_band, main_band, upper_band, right_side)


def earlier(values, stride, filler):
    head = jnp.full((stride,) + values.shape[1:], filler, values.dtype)
    return jnp.concatenate([head, values[:-stride]], axis=0)


def later(values, stride, filler):
    tail = jnp.full((stride,) + values.shape[1:], filler, values.dtype)
    return jnp.concatenate([values[stride:], tail], axis=0)


def cyclic_solve(lower_band, main_band, upper_band, right_side):
    length = main_band.shape[0]
    for bit in range((length - 1).bit_length()):
        stride = 1 << bit
        back_weight = -lower_band / earlier(main_band, stride, 1.0)
        ahead_weight = -upper_band / later(main_band, stride, 1.0)
        new_lower = back_weight * earlier(lower_band, stride, 0.0)
        new_upper = ahead_weight * later(upper_band, stride, 0.0)
        new_main = (
            main_band
            + back_weight * earlier(upper_band, stride, 0.0)
            + ahead_weight * later(lower_band, stride, 0.0)
        )
        new_right = (
            right_side
            + back_weight * earlier(right_side, stride, 0.0)
            + ahead_weight * later(right_side, stride, 0.0)
        )
        lower_band, main_band, upper_band, right_side = (new_lower, new_main, new_upper, new_right)
    return right_side / main_band


MESH_AXES = ("gx", "gy", "gz")


def halo_kernel(sides, sizes, *refs):
    count = len(sides)
    sends = refs[:2 * count]
    recvs = refs[2 * count:4 * count]
    send_sem, recv_sem = refs[4 * count:]
    me = {a: lax.axis_index(a) for a in MESH_AXES}

    def peer(axis, delta):
        return tuple(me[a] + delta if a == axis else me[a] for a in MESH_AXES)

    links = []
    for i, axis in enumerate(sides):
        links.append((axis, -1, me[axis] > 0, 2 * i, 2 * i + 1))
        links.append((axis, 1, me[axis] < sizes[i] - 1, 2 * i + 1, 2 * i))
    barrier = pltpu.get_barrier_semaphore()
    for axis, delta, present, _, _ in links:
        @pl.when(present)
        def _():
            pl.semaphore_signal(barrier, 1, device_id=peer(axis, delta), device_id_type=pl.DeviceIdType.MESH)
    peers = sum(present.astype(jnp.int32) for _, _, present, _, _ in links)
    pl.semaphore_wait(barrier, peers)
    copies = []
    for axis, delta, present, src, dst in links:
        copy = pltpu.make_async_remote_copy(
            src_ref=sends[src], dst_ref=recvs[dst], send_sem=send_sem.at[src], recv_sem=recv_sem.at[dst],
            device_id=peer(axis, delta), device_id_type=pl.DeviceIdType.MESH,
        )
        copies.append((present, copy))

        @pl.when(present)
        def _():
            copy.start()
    for axis, delta, present, src, dst in links:
        incoming = pltpu.make_async_remote_copy(
            src_ref=sends[dst], dst_ref=recvs[src], send_sem=send_sem.at[dst], recv_sem=recv_sem.at[src],
            device_id=peer(axis, delta), device_id_type=pl.DeviceIdType.MESH,
        )

        @pl.when(present)
        def _():
            incoming.wait_recv()

        @pl.when(jnp.logical_not(present))
        def _():
            recvs[src][...] = jnp.zeros(recvs[src].shape, recvs[src].dtype)
    for present, copy in copies:
        @pl.when(present)
        def _():
            copy.wait_send()


def exchange(cells, sides, collective):
    sends = []
    for axis, dim in sides:
        size = cells.shape[dim]
        sends.append(lax.index_in_dim(cells, 0, axis=dim, keepdims=False))
        sends.append(lax.index_in_dim(cells, size - 1, axis=dim, keepdims=False))
    axes = tuple(axis for axis, _ in sides)
    sizes = tuple(lax.axis_size(axis) for axis in axes)
    vmem = pl.BlockSpec(memory_space=pltpu.VMEM)
    recvs = pl.pallas_call(
        functools.partial(halo_kernel, axes, sizes),
        out_shape=[jax.ShapeDtypeStruct(s.shape, s.dtype) for s in sends],
        in_specs=[vmem] * len(sends),
        out_specs=[vmem] * len(sends),
        scratch_shapes=[pltpu.SemaphoreType.DMA((len(sends),)), pltpu.SemaphoreType.DMA((len(sends),))],
        compiler_params=pltpu.CompilerParams(collective_id=collective, has_side_effects=True),
    )(*sends)
    return {
        dim: (jnp.expand_dims(recvs[2 * i], dim), jnp.expand_dims(recvs[2 * i + 1], dim))
        for i, (axis, dim) in enumerate(sides)
    }


def face_from(part, axis, from_lower):
    count = lax.axis_size(axis)
    if from_lower:
        pairs = [(i, i + 1) for i in range(count - 1)]
    else:
        pairs = [(i + 1, i) for i in range(count - 1)]
    return lax.ppermute(part, axis, pairs)


def faces_of(cells, sides):
    got = {}
    for axis, dim in sides:
        size = cells.shape[dim]
        got[dim] = (
            face_from(lax.slice_in_dim(cells, size - 1, size, axis=dim), axis, True),
            face_from(lax.slice_in_dim(cells, 0, 1, axis=dim), axis, False),
        )
    return got


def along(cells, faces, dim):
    size = cells.shape[dim]
    lower, upper = faces[dim]
    ahead = jnp.concatenate([lax.slice_in_dim(cells, 1, size, axis=dim), upper], axis=dim)
    behind = jnp.concatenate([lower, lax.slice_in_dim(cells, 0, size - 1, axis=dim)], axis=dim)
    return (ahead - behind) * 0.5


def shards(
    stress_trial,
    mean_stress,
    consolidation,
    point_velocity,
    point_weight,
    point_cell,
    yield_flag,
    point_count,
    porosity,
    permeability,
):
    levels, extent, breadth = porosity.shape
    all_porosity = lax.all_gather(porosity, "gz", axis=0, tiled=True)
    all_permeability = lax.all_gather(permeability, "gz", axis=0, tiled=True)
    height = all_porosity.shape[0]
    cell_sums = cell_sums_of(
        stress_trial, mean_stress, consolidation, point_velocity, point_weight, point_cell,
        yield_flag, point_count, levels, extent, breadth,
    )
    sides = (("gx", 2), ("gy", 3), ("gz", 1))
    stress_sums = cell_sums[:6]
    sf = exchange(stress_sums, sides, 0)
    d_x = lambda c: along(stress_sums[c:c + 1], {2: (sf[2][0][c:c + 1], sf[2][1][c:c + 1])}, 2)[0]
    d_y = lambda c: along(stress_sums[c:c + 1], {3: (sf[3][0][c:c + 1], sf[3][1][c:c + 1])}, 3)[0]
    d_z = lambda c: along(stress_sums[c:c + 1], {1: (sf[1][0][c:c + 1], sf[1][1][c:c + 1])}, 1)[0]
    floored = jnp.maximum(cell_sums[9], mass_floor)
    force_x = d_x(0) + d_y(3) + d_z(5)
    force_y = d_x(3) + d_y(1) + d_z(4)
    force_z = d_x(5) + d_y(4) + d_z(2)
    velocity = jnp.stack(
        [
            (cell_sums[6] + time_step * force_x) / floored,
            (cell_sums[7] + time_step * force_y) / floored,
            (cell_sums[8] + time_step * force_z) / floored,
        ]
    )
    vf = exchange(velocity, sides, 1)
    dilation = (
        along(velocity[0:1], {2: (vf[2][0][0:1], vf[2][1][0:1])}, 2)[0]
        + along(velocity[1:2], {3: (vf[3][0][1:2], vf[3][1][1:2])}, 3)[0]
        + along(velocity[2:3], {1: (vf[1][0][2:3], vf[1][1][2:3])}, 1)[0]
    )
    right_side = -source_rate * (1.0 - porosity) * dilation
    all_right = lax.all_gather(right_side, "gz", axis=0, tiled=True)
    zero_level = jnp.zeros((1, extent, breadth), jnp.float32)
    level_above = jnp.concatenate([all_permeability[1:], zero_level], axis=0)
    level_below = jnp.concatenate([zero_level, all_permeability[:-1]], axis=0)
    at_top = (jnp.arange(height, dtype=jnp.int32) == height - 1)[:, None, None]
    up_face = harmonic(all_permeability, level_above)
    down_face = harmonic(level_below, all_permeability)
    top_face = jnp.where(at_top, all_permeability, up_face)
    lower_band = -time_step * down_face
    upper_band = -time_step * up_face
    main_band = storage_rate * all_porosity + time_step * (down_face + top_face)
    column = height, extent * breadth
    solved = cyclic_solve(
        lower_band.reshape(column), main_band.reshape(column), upper_band.reshape(column),
        all_right.reshape(column),
    ).reshape(height, extent, breadth)
    first = lax.axis_index("gz") * levels
    around = lax.dynamic_slice_in_dim(
        jnp.concatenate([zero_level, solved, zero_level], axis=0), first, levels + 2, axis=0
    )
    pressure = around[1:-1]
    pf = exchange(pressure, (("gx", 1), ("gy", 2)), 2)
    gradient = jnp.stack(
        [
            along(pressure, pf, 1),
            along(pressure, pf, 2),
            (around[2:] - around[:-2]) * 0.5,
        ]
    )
    return (velocity - time_step * gradient, pressure)


def solution(mesh):
    placed = (
        P(None, ("gx", "gy", "gz")),
        P(("gx", "gy", "gz")),
        P(("gx", "gy", "gz")),
        P(None, ("gx", "gy", "gz")),
        P(("gx", "gy", "gz")),
        P(("gx", "gy", "gz")),
        P(("gx", "gy", "gz")),
        P("gx", "gy", "gz"),
        P("gz", "gx", "gy"),
        P("gz", "gx", "gy"),
    )
    return jax.shard_map(
        shards,
        mesh=mesh,
        in_specs=placed,
        out_specs=(P(None, "gz", "gx", "gy"), P("gz", "gx", "gy")),
        check_vma=False,
    )
```

```python
import functools

import jax
import jax.numpy as jnp
from jax import lax
from jax.sharding import PartitionSpec as P

time_step = 0.25
storage_rate = 0.002
source_rate = 0.003
critical_slope = 1.2
mass_floor = 0.5
shear_floor = 1.0

from jax.experimental import pallas as pl
from jax.experimental.pallas import tpu as pltpu

CHUNK = 1024
M_ROWS = 32
N_COLS = 512


SPLITS = 2


def _split(v):
    hi = v.astype(jnp.bfloat16)
    lo = (v - hi.astype(jnp.float32)).astype(jnp.bfloat16)
    return [hi, lo]


def sums_kernel(count_ref, st_ref, ms_ref, cons_ref, vel_ref, w_ref, cell_ref, yf_ref, out_ref, acc_ref):
    count = count_ref[0, 0]
    acc_ref[...] = jnp.zeros_like(acc_ref)
    chunks = st_ref.shape[1] // CHUNK

    def body(k, carry):
        start = pl.multiple_of(k * CHUNK, CHUNK)
        span = pl.ds(start, CHUNK)
        st = [st_ref[pl.ds(i, 1), span] for i in range(6)]
        ms = ms_ref[:, span]
        cons = cons_ref[:, span]
        yf = yf_ref[:, span]
        slot = start + lax.broadcasted_iota(jnp.int32, (1, CHUNK), 1)
        weight = jnp.where(slot < count, w_ref[:, span], 0.0)
        sq_normal = st[0] * st[0] + st[1] * st[1] + st[2] * st[2]
        sq_shear = st[3] * st[3] + st[4] * st[4] + st[5] * st[5]
        shear_size = jnp.sqrt(1.5 * (sq_normal + 2.0 * sq_shear))
        yield_size = critical_slope * jnp.sqrt(ms * (cons - ms))
        factor = jnp.where(yf == 1, yield_size / jnp.maximum(shear_size, shear_floor), 1.0)
        stress = [st[i] * factor - ms if i < 3 else st[i] * factor for i in range(6)]
        values = [s * weight for s in stress]
        values += [vel_ref[pl.ds(i, 1), span] * weight for i in range(3)]
        values.append(weight)
        cell = cell_ref[:, span]
        m_key = (cell >> 12) * 8 + ((cell >> 7) & 7)
        n_key = ((cell >> 10) & 3) * 128 + (cell & 127)
        m_mask = lax.broadcasted_iota(jnp.int32, (M_ROWS, CHUNK), 0) == m_key
        zero = jnp.zeros((M_ROWS, CHUNK), jnp.bfloat16)
        pieces = []
        for v in values:
            for part in _split(v):
                pieces.append(jnp.where(m_mask, jnp.broadcast_to(part, (M_ROWS, CHUNK)), zero))
        lhs = jnp.concatenate(pieces, axis=0)
        one_hot = jnp.where(
            lax.broadcasted_iota(jnp.int32, (N_COLS, CHUNK), 0) == n_key, 1.0, 0.0
        ).astype(jnp.bfloat16)
        acc_ref[...] += lax.dot_general(
            lhs, one_hot, (((1,), (1,)), ((), ())), preferred_element_type=jnp.float32
        )
        return carry

    lax.fori_loop(0, chunks, body, 0)
    for comp in range(10):
        for level in range(16):
            rows = pl.ds((comp * SPLITS) * M_ROWS + (level >> 2) * 8, 8)
            lanes = pl.ds((level & 3) * 128, 128)
            total = acc_ref[rows, lanes]
            for s in range(1, SPLITS):
                total = total + acc_ref[pl.ds((comp * SPLITS + s) * M_ROWS + (level >> 2) * 8, 8), lanes]
            out_ref[comp, level] = total


def cell_sums_of(stress_trial, mean_stress, consolidation, point_velocity, point_weight, point_cell, yield_flag, point_count, levels, extent, breadth):
    n = mean_stress.shape[0]
    row = lambda a: a.reshape(1, n)
    vmem = pl.BlockSpec(memory_space=pltpu.VMEM)
    return pl.pallas_call(
        sums_kernel,
        out_shape=jax.ShapeDtypeStruct((10, levels, extent, breadth), jnp.float32),
        in_specs=[pl.BlockSpec(memory_space=pltpu.SMEM)] + [vmem] * 7,
        out_specs=vmem,
        scratch_shapes=[pltpu.VMEM((10 * SPLITS * M_ROWS, N_COLS), jnp.float32)],
        cost_estimate=pl.CostEstimate(
            flops=2 * 10 * SPLITS * M_ROWS * N_COLS * n, bytes_accessed=13 * 4 * n + 10 * 4 * levels * extent * breadth,
            transcendentals=3 * n,
        ),
    )(
        point_count.reshape(1, 1), stress_trial, row(mean_stress), row(consolidation), point_velocity,
        row(point_weight), row(point_cell), row(yield_flag),
    )


def padded_2(cells, sides, width):
    for axis, dim in sides:
        count = lax.axis_size(axis)
        ends = count - 1
        head = lax.slice_in_dim(cells, 0, width, axis=dim)
        tail = lax.slice_in_dim(cells, cells.shape[dim] - width, cells.shape[dim], axis=dim)
        cells = jnp.concatenate(
            [
                lax.ppermute(tail, axis, [(i, (i + 1) % count) for i in range(ends)]),
                cells,
                lax.ppermute(head, axis, [((i + 1) % count, i) for i in range(ends)]),
            ],
            axis=dim,
        )
    return cells


def along_x(padded):
    return (padded[..., 1:-1, 2:, 1:-1] - padded[..., 1:-1, :-2, 1:-1]) * 0.5


def along_y(padded):
    return (padded[..., 1:-1, 1:-1, 2:] - padded[..., 1:-1, 1:-1, :-2]) * 0.5


def along_z(padded):
    return (padded[..., 2:, 1:-1, 1:-1] - padded[..., :-2, 1:-1, 1:-1]) * 0.5


def harmonic(former, latter):
    return 2.0 * former * latter / (former + latter)


def returned_stress(stress_trial, mean_stress, consolidation, yield_flag):
    sq_normal = (
        stress_trial[0] * stress_trial[0]
        + stress_trial[1] * stress_trial[1]
        + stress_trial[2] * stress_trial[2]
    )
    sq_shear = (
        stress_trial[3] * stress_trial[3]
        + stress_trial[4] * stress_trial[4]
        + stress_trial[5] * stress_trial[5]
    )
    shear_size = jnp.sqrt(1.5 * (sq_normal + 2.0 * sq_shear))
    yield_size = critical_slope * jnp.sqrt(mean_stress * (consolidation - mean_stress))
    factor = jnp.where(yield_flag == 1, yield_size / jnp.maximum(shear_size, shear_floor), 1.0)
    isotropic = jnp.array([1.0, 1.0, 1.0, 0.0, 0.0, 0.0], dtype=jnp.float32)[:, None]
    return stress_trial * factor - isotropic * mean_stress


def point_sums(stress, point_velocity, weight, cell_index, segments):
    stacked = jnp.concatenate([stress * weight, point_velocity * weight, weight[None]], axis=0)
    return jax.vmap(
        lambda component: jax.ops.segment_sum(component, cell_index, num_segments=segments)
    )(stacked)


def brick_velocity(cell_sums, padded):
    floored = jnp.maximum(cell_sums[9], mass_floor)
    force_x = along_x(padded[0]) + along_y(padded[3]) + along_z(padded[5])
    force_y = along_x(padded[3]) + along_y(padded[1]) + along_z(padded[4])
    force_z = along_x(padded[5]) + along_y(padded[4]) + along_z(padded[2])
    return jnp.stack(
        [
            (cell_sums[6] + time_step * force_x) / floored,
            (cell_sums[7] + time_step * force_y) / floored,
            (cell_sums[8] + time_step * force_z) / floored,
        ]
    )


def divergence(padded_velocity):
    return along_x(padded_velocity[0]) + along_y(padded_velocity[1]) + along_z(padded_velocity[2])


def band_terms(porosity, permeability, level_below, level_above, at_top, dilation):
    up_face = harmonic(permeability, level_above)
    down_face = harmonic(level_below, permeability)
    top_face = jnp.where(at_top, permeability, up_face)
    lower_band = -time_step * down_face
    upper_band = -time_step * up_face
    main_band = storage_rate * porosity + time_step * (down_face + top_face)
    right_side = -source_rate * (1.0 - porosity) * dilation
    return (lower_band, main_band, upper_band, right_side)


def earlier(values, stride, filler):
    head = jnp.full((stride,) + values.shape[1:], filler, values.dtype)
    return jnp.concatenate([head, values[:-stride]], axis=0)


def later(values, stride, filler):
    tail = jnp.full((stride,) + values.shape[1:], filler, values.dtype)
    return jnp.concatenate([values[stride:], tail], axis=0)


def cyclic_solve(lower_band, main_band, upper_band, right_side):
    length = main_band.shape[0]
    for bit in range((length - 1).bit_length()):
        stride = 1 << bit
        back_weight = -lower_band / earlier(main_band, stride, 1.0)
        ahead_weight = -upper_band / later(main_band, stride, 1.0)
        new_lower = back_weight * earlier(lower_band, stride, 0.0)
        new_upper = ahead_weight * later(upper_band, stride, 0.0)
        new_main = (
            main_band
            + back_weight * earlier(upper_band, stride, 0.0)
            + ahead_weight * later(lower_band, stride, 0.0)
        )
        new_right = (
            right_side
            + back_weight * earlier(right_side, stride, 0.0)
            + ahead_weight * later(right_side, stride, 0.0)
        )
        lower_band, main_band, upper_band, right_side = (new_lower, new_main, new_upper, new_right)
    return right_side / main_band


MESH_AXES = ("gx", "gy", "gz")


def halo_kernel(sides, sizes, *refs):
    count = len(sides)
    sends = refs[:2 * count]
    recvs = refs[2 * count:4 * count]
    send_sem, recv_sem = refs[4 * count:]
    me = {a: lax.axis_index(a) for a in MESH_AXES}

    def peer(axis, delta):
        return tuple(me[a] + delta if a == axis else me[a] for a in MESH_AXES)

    links = []
    for i, axis in enumerate(sides):
        links.append((axis, -1, me[axis] > 0, 2 * i, 2 * i + 1))
        links.append((axis, 1, me[axis] < sizes[i] - 1, 2 * i + 1, 2 * i))
    barrier = pltpu.get_barrier_semaphore()
    for axis, delta, present, _, _ in links:
        @pl.when(present)
        def _():
            pl.semaphore_signal(barrier, 1, device_id=peer(axis, delta), device_id_type=pl.DeviceIdType.MESH)
    peers = sum(present.astype(jnp.int32) for _, _, present, _, _ in links)
    pl.semaphore_wait(barrier, peers)
    copies = []
    for axis, delta, present, src, dst in links:
        copy = pltpu.make_async_remote_copy(
            src_ref=sends[src], dst_ref=recvs[dst], send_sem=send_sem.at[src], recv_sem=recv_sem.at[dst],
            device_id=peer(axis, delta), device_id_type=pl.DeviceIdType.MESH,
        )
        copies.append((present, copy))

        @pl.when(present)
        def _():
            copy.start()
    for axis, delta, present, src, dst in links:
        incoming = pltpu.make_async_remote_copy(
            src_ref=sends[dst], dst_ref=recvs[src], send_sem=send_sem.at[dst], recv_sem=recv_sem.at[src],
            device_id=peer(axis, delta), device_id_type=pl.DeviceIdType.MESH,
        )

        @pl.when(present)
        def _():
            incoming.wait_recv()

        @pl.when(jnp.logical_not(present))
        def _():
            recvs[src][...] = jnp.zeros(recvs[src].shape, recvs[src].dtype)
    for present, copy in copies:
        @pl.when(present)
        def _():
            copy.wait_send()


def exchange(cells, sides, collective):
    sends = []
    for axis, dim in sides:
        size = cells.shape[dim]
        sends.append(lax.index_in_dim(cells, 0, axis=dim, keepdims=False))
        sends.append(lax.index_in_dim(cells, size - 1, axis=dim, keepdims=False))
    axes = tuple(axis for axis, _ in sides)
    sizes = tuple(lax.axis_size(axis) for axis in axes)
    vmem = pl.BlockSpec(memory_space=pltpu.VMEM)
    recvs = pl.pallas_call(
        functools.partial(halo_kernel, axes, sizes),
        out_shape=[jax.ShapeDtypeStruct(s.shape, s.dtype) for s in sends],
        in_specs=[vmem] * len(sends),
        out_specs=[vmem] * len(sends),
        scratch_shapes=[pltpu.SemaphoreType.DMA((len(sends),)), pltpu.SemaphoreType.DMA((len(sends),))],
        compiler_params=pltpu.CompilerParams(collective_id=collective, has_side_effects=True),
    )(*sends)
    return {
        dim: (jnp.expand_dims(recvs[2 * i], dim), jnp.expand_dims(recvs[2 * i + 1], dim))
        for i, (axis, dim) in enumerate(sides)
    }


def face_from(part, axis, from_lower):
    count = lax.axis_size(axis)
    if from_lower:
        pairs = [(i, i + 1) for i in range(count - 1)]
    else:
        pairs = [(i + 1, i) for i in range(count - 1)]
    return lax.ppermute(part, axis, pairs)


def faces_of(cells, sides):
    got = {}
    for axis, dim in sides:
        size = cells.shape[dim]
        got[dim] = (
            face_from(lax.slice_in_dim(cells, size - 1, size, axis=dim), axis, True),
            face_from(lax.slice_in_dim(cells, 0, 1, axis=dim), axis, False),
        )
    return got


def along(cells, faces, dim):
    size = cells.shape[dim]
    lower, upper = faces[dim]
    ahead = jnp.concatenate([lax.slice_in_dim(cells, 1, size, axis=dim), upper], axis=dim)
    behind = jnp.concatenate([lower, lax.slice_in_dim(cells, 0, size - 1, axis=dim)], axis=dim)
    return (ahead - behind) * 0.5


def shards(
    stress_trial,
    mean_stress,
    consolidation,
    point_velocity,
    point_weight,
    point_cell,
    yield_flag,
    point_count,
    porosity,
    permeability,
):
    levels, extent, breadth = porosity.shape
    all_porosity = lax.all_gather(porosity, "gz", axis=0, tiled=True)
    all_permeability = lax.all_gather(permeability, "gz", axis=0, tiled=True)
    height = all_porosity.shape[0]
    cell_sums = cell_sums_of(
        stress_trial, mean_stress, consolidation, point_velocity, point_weight, point_cell,
        yield_flag, point_count, levels, extent, breadth,
    )
    sides = (("gx", 2), ("gy", 3), ("gz", 1))
    stress_sums = cell_sums[:6]
    sf = exchange(stress_sums, sides, 0)
    d_x = lambda c: along(stress_sums[c:c + 1], {2: (sf[2][0][c:c + 1], sf[2][1][c:c + 1])}, 2)[0]
    d_y = lambda c: along(stress_sums[c:c + 1], {3: (sf[3][0][c:c + 1], sf[3][1][c:c + 1])}, 3)[0]
    d_z = lambda c: along(stress_sums[c:c + 1], {1: (sf[1][0][c:c + 1], sf[1][1][c:c + 1])}, 1)[0]
    floored = jnp.maximum(cell_sums[9], mass_floor)
    force_x = d_x(0) + d_y(3) + d_z(5)
    force_y = d_x(3) + d_y(1) + d_z(4)
    force_z = d_x(5) + d_y(4) + d_z(2)
    velocity = jnp.stack(
        [
            (cell_sums[6] + time_step * force_x) / floored,
            (cell_sums[7] + time_step * force_y) / floored,
            (cell_sums[8] + time_step * force_z) / floored,
        ]
    )
    vf = exchange(velocity, sides, 1)
    dilation = (
        along(velocity[0:1], {2: (vf[2][0][0:1], vf[2][1][0:1])}, 2)[0]
        + along(velocity[1:2], {3: (vf[3][0][1:2], vf[3][1][1:2])}, 3)[0]
        + along(velocity[2:3], {1: (vf[1][0][2:3], vf[1][1][2:3])}, 1)[0]
    )
    right_side = -source_rate * (1.0 - porosity) * dilation
    all_right = lax.all_gather(right_side, "gz", axis=0, tiled=True)
    zero_level = jnp.zeros((1, extent, breadth), jnp.float32)
    level_above = jnp.concatenate([all_permeability[1:], zero_level], axis=0)
    level_below = jnp.concatenate([zero_level, all_permeability[:-1]], axis=0)
    at_top = (jnp.arange(height, dtype=jnp.int32) == height - 1)[:, None, None]
    up_face = harmonic(all_permeability, level_above)
    down_face = harmonic(level_below, all_permeability)
    top_face = jnp.where(at_top, all_permeability, up_face)
    lower_band = -time_step * down_face
    upper_band = -time_step * up_face
    main_band = storage_rate * all_porosity + time_step * (down_face + top_face)
    column = height, extent * breadth
    solved = cyclic_solve(
        lower_band.reshape(column), main_band.reshape(column), upper_band.reshape(column),
        all_right.reshape(column),
    ).reshape(height, extent, breadth)
    first = lax.axis_index("gz") * levels
    around = lax.dynamic_slice_in_dim(
        jnp.concatenate([zero_level, solved, zero_level], axis=0), first, levels + 2, axis=0
    )
    pressure = around[1:-1]
    pf = exchange(pressure, (("gx", 1), ("gy", 2)), 2)
    gradient = jnp.stack(
        [
            along(pressure, pf, 1),
            along(pressure, pf, 2),
            (around[2:] - around[:-2]) * 0.5,
        ]
    )
    return (velocity - time_step * gradient, pressure)


def solution(mesh):
    placed = (
        P(None, ("gx", "gy", "gz")),
        P(("gx", "gy", "gz")),
        P(("gx", "gy", "gz")),
        P(None, ("gx", "gy", "gz")),
        P(("gx", "gy", "gz")),
        P(("gx", "gy", "gz")),
        P(("gx", "gy", "gz")),
        P("gx", "gy", "gz"),
        P("gz", "gx", "gy"),
        P("gz", "gx", "gy"),
    )
    return jax.shard_map(
        shards,
        mesh=mesh,
        in_specs=placed,
        out_specs=(P(None, "gz", "gx", "gy"), P("gz", "gx", "gy")),
        check_vma=False,
    )
```

```python
import functools

import jax
import jax.numpy as jnp
from jax import lax
from jax.sharding import PartitionSpec as P

time_step = 0.25
storage_rate = 0.002
source_rate = 0.003
critical_slope = 1.2
mass_floor = 0.5
shear_floor = 1.0

from jax.experimental import pallas as pl
from jax.experimental.pallas import tpu as pltpu

CHUNK = 1024
M_ROWS = 32
N_COLS = 512


SPLITS = 2


def _split(v):
    hi = v.astype(jnp.bfloat16)
    lo = (v - hi.astype(jnp.float32)).astype(jnp.bfloat16)
    return [hi, lo]


def sums_kernel(count_ref, st_ref, ms_ref, cons_ref, vel_ref, w_ref, cell_ref, yf_ref, out_ref, acc_ref):
    count = count_ref[0, 0]
    acc_ref[...] = jnp.zeros_like(acc_ref)
    chunks = st_ref.shape[1] // CHUNK

    def body(k, carry):
        start = pl.multiple_of(k * CHUNK, CHUNK)
        span = pl.ds(start, CHUNK)
        st = [st_ref[pl.ds(i, 1), span] for i in range(6)]
        ms = ms_ref[:, span]
        cons = cons_ref[:, span]
        yf = yf_ref[:, span]
        slot = start + lax.broadcasted_iota(jnp.int32, (1, CHUNK), 1)
        weight = jnp.where(slot < count, w_ref[:, span], 0.0)
        sq_normal = st[0] * st[0] + st[1] * st[1] + st[2] * st[2]
        sq_shear = st[3] * st[3] + st[4] * st[4] + st[5] * st[5]
        shear_size = jnp.sqrt(1.5 * (sq_normal + 2.0 * sq_shear))
        yield_size = critical_slope * jnp.sqrt(ms * (cons - ms))
        factor = jnp.where(yf == 1, yield_size / jnp.maximum(shear_size, shear_floor), 1.0)
        stress = [st[i] * factor - ms if i < 3 else st[i] * factor for i in range(6)]
        values = [s * weight for s in stress]
        values += [vel_ref[pl.ds(i, 1), span] * weight for i in range(3)]
        values.append(weight)
        cell = cell_ref[:, span]
        m_key = (cell >> 12) * 8 + ((cell >> 7) & 7)
        n_key = ((cell >> 10) & 3) * 128 + (cell & 127)
        m_mask = lax.broadcasted_iota(jnp.int32, (M_ROWS, CHUNK), 0) == m_key
        zero = jnp.zeros((M_ROWS, CHUNK), jnp.bfloat16)
        pieces = []
        for v in values:
            for part in _split(v):
                pieces.append(jnp.where(m_mask, jnp.broadcast_to(part, (M_ROWS, CHUNK)), zero))
        lhs = jnp.concatenate(pieces, axis=0)
        one_hot = jnp.where(
            lax.broadcasted_iota(jnp.int32, (N_COLS, CHUNK), 0) == n_key, 1.0, 0.0
        ).astype(jnp.bfloat16)
        acc_ref[...] += lax.dot_general(
            lhs, one_hot, (((1,), (1,)), ((), ())), preferred_element_type=jnp.float32
        )
        return carry

    lax.fori_loop(0, chunks, body, 0)
    for comp in range(10):
        for level in range(16):
            rows = pl.ds((comp * SPLITS) * M_ROWS + (level >> 2) * 8, 8)
            lanes = pl.ds((level & 3) * 128, 128)
            total = acc_ref[rows, lanes]
            for s in range(1, SPLITS):
                total = total + acc_ref[pl.ds((comp * SPLITS + s) * M_ROWS + (level >> 2) * 8, 8), lanes]
            out_ref[comp, level] = total


def cell_sums_of(stress_trial, mean_stress, consolidation, point_velocity, point_weight, point_cell, yield_flag, point_count, levels, extent, breadth):
    n = mean_stress.shape[0]
    row = lambda a: a.reshape(1, n)
    vmem = pl.BlockSpec(memory_space=pltpu.VMEM)
    return pl.pallas_call(
        sums_kernel,
        out_shape=jax.ShapeDtypeStruct((10, levels, extent, breadth), jnp.float32),
        in_specs=[pl.BlockSpec(memory_space=pltpu.SMEM)] + [vmem] * 7,
        out_specs=vmem,
        scratch_shapes=[pltpu.VMEM((10 * SPLITS * M_ROWS, N_COLS), jnp.float32)],
        cost_estimate=pl.CostEstimate(
            flops=2 * 10 * SPLITS * M_ROWS * N_COLS * n, bytes_accessed=13 * 4 * n + 10 * 4 * levels * extent * breadth,
            transcendentals=3 * n,
        ),
    )(
        point_count.reshape(1, 1), stress_trial, row(mean_stress), row(consolidation), point_velocity,
        row(point_weight), row(point_cell), row(yield_flag),
    )


def padded_2(cells, sides, width):
    for axis, dim in sides:
        count = lax.axis_size(axis)
        ends = count - 1
        head = lax.slice_in_dim(cells, 0, width, axis=dim)
        tail = lax.slice_in_dim(cells, cells.shape[dim] - width, cells.shape[dim], axis=dim)
        cells = jnp.concatenate(
            [
                lax.ppermute(tail, axis, [(i, (i + 1) % count) for i in range(ends)]),
                cells,
                lax.ppermute(head, axis, [((i + 1) % count, i) for i in range(ends)]),
            ],
            axis=dim,
        )
    return cells


def along_x(padded):
    return (padded[..., 1:-1, 2:, 1:-1] - padded[..., 1:-1, :-2, 1:-1]) * 0.5


def along_y(padded):
    return (padded[..., 1:-1, 1:-1, 2:] - padded[..., 1:-1, 1:-1, :-2]) * 0.5


def along_z(padded):
    return (padded[..., 2:, 1:-1, 1:-1] - padded[..., :-2, 1:-1, 1:-1]) * 0.5


def harmonic(former, latter):
    return 2.0 * former * latter / (former + latter)


def returned_stress(stress_trial, mean_stress, consolidation, yield_flag):
    sq_normal = (
        stress_trial[0] * stress_trial[0]
        + stress_trial[1] * stress_trial[1]
        + stress_trial[2] * stress_trial[2]
    )
    sq_shear = (
        stress_trial[3] * stress_trial[3]
        + stress_trial[4] * stress_trial[4]
        + stress_trial[5] * stress_trial[5]
    )
    shear_size = jnp.sqrt(1.5 * (sq_normal + 2.0 * sq_shear))
    yield_size = critical_slope * jnp.sqrt(mean_stress * (consolidation - mean_stress))
    factor = jnp.where(yield_flag == 1, yield_size / jnp.maximum(shear_size, shear_floor), 1.0)
    isotropic = jnp.array([1.0, 1.0, 1.0, 0.0, 0.0, 0.0], dtype=jnp.float32)[:, None]
    return stress_trial * factor - isotropic * mean_stress


def point_sums(stress, point_velocity, weight, cell_index, segments):
    stacked = jnp.concatenate([stress * weight, point_velocity * weight, weight[None]], axis=0)
    return jax.vmap(
        lambda component: jax.ops.segment_sum(component, cell_index, num_segments=segments)
    )(stacked)


def brick_velocity(cell_sums, padded):
    floored = jnp.maximum(cell_sums[9], mass_floor)
    force_x = along_x(padded[0]) + along_y(padded[3]) + along_z(padded[5])
    force_y = along_x(padded[3]) + along_y(padded[1]) + along_z(padded[4])
    force_z = along_x(padded[5]) + along_y(padded[4]) + along_z(padded[2])
    return jnp.stack(
        [
            (cell_sums[6] + time_step * force_x) / floored,
            (cell_sums[7] + time_step * force_y) / floored,
            (cell_sums[8] + time_step * force_z) / floored,
        ]
    )


def divergence(padded_velocity):
    return along_x(padded_velocity[0]) + along_y(padded_velocity[1]) + along_z(padded_velocity[2])


def band_terms(porosity, permeability, level_below, level_above, at_top, dilation):
    up_face = harmonic(permeability, level_above)
    down_face = harmonic(level_below, permeability)
    top_face = jnp.where(at_top, permeability, up_face)
    lower_band = -time_step * down_face
    upper_band = -time_step * up_face
    main_band = storage_rate * porosity + time_step * (down_face + top_face)
    right_side = -source_rate * (1.0 - porosity) * dilation
    return (lower_band, main_band, upper_band, right_side)


def earlier(values, stride, filler):
    head = jnp.full((stride,) + values.shape[1:], filler, values.dtype)
    return jnp.concatenate([head, values[:-stride]], axis=0)


def later(values, stride, filler):
    tail = jnp.full((stride,) + values.shape[1:], filler, values.dtype)
    return jnp.concatenate([values[stride:], tail], axis=0)


def cyclic_solve(lower_band, main_band, upper_band, right_side):
    length = main_band.shape[0]
    for bit in range((length - 1).bit_length()):
        stride = 1 << bit
        back_weight = -lower_band / earlier(main_band, stride, 1.0)
        ahead_weight = -upper_band / later(main_band, stride, 1.0)
        new_lower = back_weight * earlier(lower_band, stride, 0.0)
        new_upper = ahead_weight * later(upper_band, stride, 0.0)
        new_main = (
            main_band
            + back_weight * earlier(upper_band, stride, 0.0)
            + ahead_weight * later(lower_band, stride, 0.0)
        )
        new_right = (
            right_side
            + back_weight * earlier(right_side, stride, 0.0)
            + ahead_weight * later(right_side, stride, 0.0)
        )
        lower_band, main_band, upper_band, right_side = (new_lower, new_main, new_upper, new_right)
    return right_side / main_band


MESH_AXES = ("gx", "gy", "gz")


def halo_kernel(sides, sizes, gathered, group, *refs):
    count = len(sides)
    sends = refs[:2 * count]
    gins = refs[2 * count:2 * count + gathered]
    recvs = refs[2 * count + gathered:4 * count + gathered]
    gouts = refs[4 * count + gathered:4 * count + 2 * gathered]
    send_sem, recv_sem, gsend_sem, grecv_sem = refs[4 * count + 2 * gathered:]
    me = {a: lax.axis_index(a) for a in MESH_AXES}

    def peer(axis, delta):
        return tuple(me[a] + delta if a == axis else me[a] for a in MESH_AXES)

    def across(level):
        return tuple(level if a == "gz" else me[a] for a in MESH_AXES)

    links = []
    for i, axis in enumerate(sides):
        links.append((axis, -1, me[axis] > 0, 2 * i, 2 * i + 1))
        links.append((axis, 1, me[axis] < sizes[i] - 1, 2 * i + 1, 2 * i))
    barrier = pltpu.get_barrier_semaphore()
    peers = 0
    for axis, delta, present, _, _ in links:
        if gathered and axis == "gz":
            continue
        peers = peers + present.astype(jnp.int32)

        @pl.when(present)
        def _():
            pl.semaphore_signal(barrier, 1, device_id=peer(axis, delta), device_id_type=pl.DeviceIdType.MESH)
    if gathered:
        for d in range(1, group):
            pl.semaphore_signal(
                barrier, 1, device_id=across(lax.rem(me["gz"] + d, group)), device_id_type=pl.DeviceIdType.MESH
            )
        peers = peers + (group - 1)
    pl.semaphore_wait(barrier, peers)
    copies = []
    for axis, delta, present, src, dst in links:
        copy = pltpu.make_async_remote_copy(
            src_ref=sends[src], dst_ref=recvs[dst], send_sem=send_sem.at[src], recv_sem=recv_sem.at[dst],
            device_id=peer(axis, delta), device_id_type=pl.DeviceIdType.MESH,
        )
        copies.append((present, copy))

        @pl.when(present)
        def _():
            copy.start()
    gcopies = []
    for j in range(gathered):
        for d in range(1, group):
            slot = j * (group - 1) + d - 1
            copy = pltpu.make_async_remote_copy(
                src_ref=gins[j], dst_ref=gouts[j].at[me["gz"]], send_sem=gsend_sem.at[slot],
                recv_sem=grecv_sem.at[slot], device_id=across(lax.rem(me["gz"] + d, group)),
                device_id_type=pl.DeviceIdType.MESH,
            )
            copy.start()
            gcopies.append(copy)
    for j in range(gathered):
        gouts[j][me["gz"]] = gins[j][...]
    for axis, delta, present, src, dst in links:
        incoming = pltpu.make_async_remote_copy(
            src_ref=sends[dst], dst_ref=recvs[src], send_sem=send_sem.at[dst], recv_sem=recv_sem.at[src],
            device_id=peer(axis, delta), device_id_type=pl.DeviceIdType.MESH,
        )

        @pl.when(present)
        def _():
            incoming.wait_recv()

        @pl.when(jnp.logical_not(present))
        def _():
            recvs[src][...] = jnp.zeros(recvs[src].shape, recvs[src].dtype)
    for j in range(gathered):
        for d in range(1, group):
            slot = j * (group - 1) + d - 1
            origin = lax.rem(me["gz"] + group - d, group)
            incoming = pltpu.make_async_remote_copy(
                src_ref=gins[j], dst_ref=gouts[j].at[origin], send_sem=gsend_sem.at[slot],
                recv_sem=grecv_sem.at[slot], device_id=across(origin), device_id_type=pl.DeviceIdType.MESH,
            )
            incoming.wait_recv()
    for present, copy in copies:
        @pl.when(present)
        def _():
            copy.wait_send()
    for copy in gcopies:
        copy.wait_send()


def exchange(cells, sides, collective, gathers=()):
    sends = []
    for axis, dim in sides:
        size = cells.shape[dim]
        sends.append(lax.index_in_dim(cells, 0, axis=dim, keepdims=False))
        sends.append(lax.index_in_dim(cells, size - 1, axis=dim, keepdims=False))
    axes = tuple(axis for axis, _ in sides)
    sizes = tuple(lax.axis_size(axis) for axis in axes)
    group = lax.axis_size("gz")
    vmem = pl.BlockSpec(memory_space=pltpu.VMEM)
    slots = max(1, len(gathers) * (group - 1))
    outs = pl.pallas_call(
        functools.partial(halo_kernel, axes, sizes, len(gathers), group),
        out_shape=[jax.ShapeDtypeStruct(s.shape, s.dtype) for s in sends]
        + [jax.ShapeDtypeStruct((group,) + g.shape, g.dtype) for g in gathers],
        in_specs=[vmem] * (len(sends) + len(gathers)),
        out_specs=[vmem] * (len(sends) + len(gathers)),
        scratch_shapes=[
            pltpu.SemaphoreType.DMA((max(1, len(sends)),)), pltpu.SemaphoreType.DMA((max(1, len(sends)),)),
            pltpu.SemaphoreType.DMA((slots,)), pltpu.SemaphoreType.DMA((slots,)),
        ],
        compiler_params=pltpu.CompilerParams(collective_id=collective, has_side_effects=True),
    )(*sends, *gathers)
    recvs = outs[:len(sends)]
    faces = {
        dim: (jnp.expand_dims(recvs[2 * i], dim), jnp.expand_dims(recvs[2 * i + 1], dim))
        for i, (axis, dim) in enumerate(sides)
    }
    stacked = [g.reshape((group * g.shape[1],) + g.shape[2:]) for g in outs[len(sends):]]
    return faces, stacked


def face_from(part, axis, from_lower):
    count = lax.axis_size(axis)
    if from_lower:
        pairs = [(i, i + 1) for i in range(count - 1)]
    else:
        pairs = [(i + 1, i) for i in range(count - 1)]
    return lax.ppermute(part, axis, pairs)


def faces_of(cells, sides):
    got = {}
    for axis, dim in sides:
        size = cells.shape[dim]
        got[dim] = (
            face_from(lax.slice_in_dim(cells, size - 1, size, axis=dim), axis, True),
            face_from(lax.slice_in_dim(cells, 0, 1, axis=dim), axis, False),
        )
    return got


def along(cells, faces, dim):
    size = cells.shape[dim]
    lower, upper = faces[dim]
    ahead = jnp.concatenate([lax.slice_in_dim(cells, 1, size, axis=dim), upper], axis=dim)
    behind = jnp.concatenate([lower, lax.slice_in_dim(cells, 0, size - 1, axis=dim)], axis=dim)
    return (ahead - behind) * 0.5


def shards(
    stress_trial,
    mean_stress,
    consolidation,
    point_velocity,
    point_weight,
    point_cell,
    yield_flag,
    point_count,
    porosity,
    permeability,
):
    levels, extent, breadth = porosity.shape
    cell_sums = cell_sums_of(
        stress_trial, mean_stress, consolidation, point_velocity, point_weight, point_cell,
        yield_flag, point_count, levels, extent, breadth,
    )
    sides = (("gx", 2), ("gy", 3), ("gz", 1))
    stress_sums = cell_sums[:6]
    sf, (all_porosity, all_permeability) = exchange(stress_sums, sides, 0, (porosity, permeability))
    height = all_porosity.shape[0]
    d_x = lambda c: along(stress_sums[c:c + 1], {2: (sf[2][0][c:c + 1], sf[2][1][c:c + 1])}, 2)[0]
    d_y = lambda c: along(stress_sums[c:c + 1], {3: (sf[3][0][c:c + 1], sf[3][1][c:c + 1])}, 3)[0]
    d_z = lambda c: along(stress_sums[c:c + 1], {1: (sf[1][0][c:c + 1], sf[1][1][c:c + 1])}, 1)[0]
    floored = jnp.maximum(cell_sums[9], mass_floor)
    force_x = d_x(0) + d_y(3) + d_z(5)
    force_y = d_x(3) + d_y(1) + d_z(4)
    force_z = d_x(5) + d_y(4) + d_z(2)
    velocity = jnp.stack(
        [
            (cell_sums[6] + time_step * force_x) / floored,
            (cell_sums[7] + time_step * force_y) / floored,
            (cell_sums[8] + time_step * force_z) / floored,
        ]
    )
    vf, _ = exchange(velocity, sides, 1)
    dilation = (
        along(velocity[0:1], {2: (vf[2][0][0:1], vf[2][1][0:1])}, 2)[0]
        + along(velocity[1:2], {3: (vf[3][0][1:2], vf[3][1][1:2])}, 3)[0]
        + along(velocity[2:3], {1: (vf[1][0][2:3], vf[1][1][2:3])}, 1)[0]
    )
    right_side = -source_rate * (1.0 - porosity) * dilation
    _, (all_right,) = exchange(right_side, (), 3, (right_side,))
    zero_level = jnp.zeros((1, extent, breadth), jnp.float32)
    level_above = jnp.concatenate([all_permeability[1:], zero_level], axis=0)
    level_below = jnp.concatenate([zero_level, all_permeability[:-1]], axis=0)
    at_top = (jnp.arange(height, dtype=jnp.int32) == height - 1)[:, None, None]
    up_face = harmonic(all_permeability, level_above)
    down_face = harmonic(level_below, all_permeability)
    top_face = jnp.where(at_top, all_permeability, up_face)
    lower_band = -time_step * down_face
    upper_band = -time_step * up_face
    main_band = storage_rate * all_porosity + time_step * (down_face + top_face)
    column = height, extent * breadth
    solved = cyclic_solve(
        lower_band.reshape(column), main_band.reshape(column), upper_band.reshape(column),
        all_right.reshape(column),
    ).reshape(height, extent, breadth)
    first = lax.axis_index("gz") * levels
    around = lax.dynamic_slice_in_dim(
        jnp.concatenate([zero_level, solved, zero_level], axis=0), first, levels + 2, axis=0
    )
    pressure = around[1:-1]
    pf, _ = exchange(pressure, (("gx", 1), ("gy", 2)), 2)
    gradient = jnp.stack(
        [
            along(pressure, pf, 1),
            along(pressure, pf, 2),
            (around[2:] - around[:-2]) * 0.5,
        ]
    )
    return (velocity - time_step * gradient, pressure)


def solution(mesh):
    placed = (
        P(None, ("gx", "gy", "gz")),
        P(("gx", "gy", "gz")),
        P(("gx", "gy", "gz")),
        P(None, ("gx", "gy", "gz")),
        P(("gx", "gy", "gz")),
        P(("gx", "gy", "gz")),
        P(("gx", "gy", "gz")),
        P("gx", "gy", "gz"),
        P("gz", "gx", "gy"),
        P("gz", "gx", "gy"),
    )
    return jax.shard_map(
        shards,
        mesh=mesh,
        in_specs=placed,
        out_specs=(P(None, "gz", "gx", "gy"), P("gz", "gx", "gy")),
        check_vma=False,
    )
```

```python
import functools

import jax
import jax.numpy as jnp
from jax import lax
from jax.sharding import PartitionSpec as P

time_step = 0.25
storage_rate = 0.002
source_rate = 0.003
critical_slope = 1.2
mass_floor = 0.5
shear_floor = 1.0

from jax.experimental import pallas as pl
from jax.experimental.pallas import tpu as pltpu

CHUNK = 1024
M_ROWS = 32
N_COLS = 512


SPLITS = 2


def _split(v):
    hi = v.astype(jnp.bfloat16)
    lo = (v - hi.astype(jnp.float32)).astype(jnp.bfloat16)
    return [hi, lo]


def sums_kernel(count_ref, st_ref, ms_ref, cons_ref, vel_ref, w_ref, cell_ref, yf_ref, out_ref, acc_ref):
    count = count_ref[0, 0]
    acc_ref[...] = jnp.zeros_like(acc_ref)
    chunks = st_ref.shape[1] // CHUNK

    def body(k, carry):
        start = pl.multiple_of(k * CHUNK, CHUNK)
        span = pl.ds(start, CHUNK)
        st = [st_ref[pl.ds(i, 1), span] for i in range(6)]
        ms = ms_ref[:, span]
        cons = cons_ref[:, span]
        yf = yf_ref[:, span]
        slot = start + lax.broadcasted_iota(jnp.int32, (1, CHUNK), 1)
        weight = jnp.where(slot < count, w_ref[:, span], 0.0)
        sq_normal = st[0] * st[0] + st[1] * st[1] + st[2] * st[2]
        sq_shear = st[3] * st[3] + st[4] * st[4] + st[5] * st[5]
        shear_size = jnp.sqrt(1.5 * (sq_normal + 2.0 * sq_shear))
        yield_size = critical_slope * jnp.sqrt(ms * (cons - ms))
        factor = jnp.where(yf == 1, yield_size / jnp.maximum(shear_size, shear_floor), 1.0)
        stress = [st[i] * factor - ms if i < 3 else st[i] * factor for i in range(6)]
        values = [s * weight for s in stress]
        values += [vel_ref[pl.ds(i, 1), span] * weight for i in range(3)]
        values.append(weight)
        cell = cell_ref[:, span]
        m_key = (cell >> 12) * 8 + ((cell >> 7) & 7)
        n_key = ((cell >> 10) & 3) * 128 + (cell & 127)
        m_mask = lax.broadcasted_iota(jnp.int32, (M_ROWS, CHUNK), 0) == m_key
        zero = jnp.zeros((M_ROWS, CHUNK), jnp.bfloat16)
        pieces = []
        for v in values:
            for part in _split(v):
                pieces.append(jnp.where(m_mask, jnp.broadcast_to(part, (M_ROWS, CHUNK)), zero))
        lhs = jnp.concatenate(pieces, axis=0)
        one_hot = jnp.where(
            lax.broadcasted_iota(jnp.int32, (N_COLS, CHUNK), 0) == n_key, 1.0, 0.0
        ).astype(jnp.bfloat16)
        acc_ref[...] += lax.dot_general(
            lhs, one_hot, (((1,), (1,)), ((), ())), preferred_element_type=jnp.float32
        )
        return carry

    lax.fori_loop(0, chunks, body, 0)
    for comp in range(10):
        for level in range(16):
            rows = pl.ds((comp * SPLITS) * M_ROWS + (level >> 2) * 8, 8)
            lanes = pl.ds((level & 3) * 128, 128)
            total = acc_ref[rows, lanes]
            for s in range(1, SPLITS):
                total = total + acc_ref[pl.ds((comp * SPLITS + s) * M_ROWS + (level >> 2) * 8, 8), lanes]
            out_ref[comp, level] = total


def cell_sums_of(stress_trial, mean_stress, consolidation, point_velocity, point_weight, point_cell, yield_flag, point_count, levels, extent, breadth):
    n = mean_stress.shape[0]
    row = lambda a: a.reshape(1, n)
    vmem = pl.BlockSpec(memory_space=pltpu.VMEM)
    return pl.pallas_call(
        sums_kernel,
        out_shape=jax.ShapeDtypeStruct((10, levels, extent, breadth), jnp.float32),
        in_specs=[pl.BlockSpec(memory_space=pltpu.SMEM)] + [vmem] * 7,
        out_specs=vmem,
        scratch_shapes=[pltpu.VMEM((10 * SPLITS * M_ROWS, N_COLS), jnp.float32)],
        cost_estimate=pl.CostEstimate(
            flops=2 * 10 * SPLITS * M_ROWS * N_COLS * n, bytes_accessed=13 * 4 * n + 10 * 4 * levels * extent * breadth,
            transcendentals=3 * n,
        ),
    )(
        point_count.reshape(1, 1), stress_trial, row(mean_stress), row(consolidation), point_velocity,
        row(point_weight), row(point_cell), row(yield_flag),
    )


def padded_2(cells, sides, width):
    for axis, dim in sides:
        count = lax.axis_size(axis)
        ends = count - 1
        head = lax.slice_in_dim(cells, 0, width, axis=dim)
        tail = lax.slice_in_dim(cells, cells.shape[dim] - width, cells.shape[dim], axis=dim)
        cells = jnp.concatenate(
            [
                lax.ppermute(tail, axis, [(i, (i + 1) % count) for i in range(ends)]),
                cells,
                lax.ppermute(head, axis, [((i + 1) % count, i) for i in range(ends)]),
            ],
            axis=dim,
        )
    return cells


def along_x(padded):
    return (padded[..., 1:-1, 2:, 1:-1] - padded[..., 1:-1, :-2, 1:-1]) * 0.5


def along_y(padded):
    return (padded[..., 1:-1, 1:-1, 2:] - padded[..., 1:-1, 1:-1, :-2]) * 0.5


def along_z(padded):
    return (padded[..., 2:, 1:-1, 1:-1] - padded[..., :-2, 1:-1, 1:-1]) * 0.5


def harmonic(former, latter):
    return 2.0 * former * latter / (former + latter)


def returned_stress(stress_trial, mean_stress, consolidation, yield_flag):
    sq_normal = (
        stress_trial[0] * stress_trial[0]
        + stress_trial[1] * stress_trial[1]
        + stress_trial[2] * stress_trial[2]
    )
    sq_shear = (
        stress_trial[3] * stress_trial[3]
        + stress_trial[4] * stress_trial[4]
        + stress_trial[5] * stress_trial[5]
    )
    shear_size = jnp.sqrt(1.5 * (sq_normal + 2.0 * sq_shear))
    yield_size = critical_slope * jnp.sqrt(mean_stress * (consolidation - mean_stress))
    factor = jnp.where(yield_flag == 1, yield_size / jnp.maximum(shear_size, shear_floor), 1.0)
    isotropic = jnp.array([1.0, 1.0, 1.0, 0.0, 0.0, 0.0], dtype=jnp.float32)[:, None]
    return stress_trial * factor - isotropic * mean_stress


def point_sums(stress, point_velocity, weight, cell_index, segments):
    stacked = jnp.concatenate([stress * weight, point_velocity * weight, weight[None]], axis=0)
    return jax.vmap(
        lambda component: jax.ops.segment_sum(component, cell_index, num_segments=segments)
    )(stacked)


def brick_velocity(cell_sums, padded):
    floored = jnp.maximum(cell_sums[9], mass_floor)
    force_x = along_x(padded[0]) + along_y(padded[3]) + along_z(padded[5])
    force_y = along_x(padded[3]) + along_y(padded[1]) + along_z(padded[4])
    force_z = along_x(padded[5]) + along_y(padded[4]) + along_z(padded[2])
    return jnp.stack(
        [
            (cell_sums[6] + time_step * force_x) / floored,
            (cell_sums[7] + time_step * force_y) / floored,
            (cell_sums[8] + time_step * force_z) / floored,
        ]
    )


def divergence(padded_velocity):
    return along_x(padded_velocity[0]) + along_y(padded_velocity[1]) + along_z(padded_velocity[2])


def band_terms(porosity, permeability, level_below, level_above, at_top, dilation):
    up_face = harmonic(permeability, level_above)
    down_face = harmonic(level_below, permeability)
    top_face = jnp.where(at_top, permeability, up_face)
    lower_band = -time_step * down_face
    upper_band = -time_step * up_face
    main_band = storage_rate * porosity + time_step * (down_face + top_face)
    right_side = -source_rate * (1.0 - porosity) * dilation
    return (lower_band, main_band, upper_band, right_side)


def earlier(values, stride, filler):
    head = jnp.full((stride,) + values.shape[1:], filler, values.dtype)
    return jnp.concatenate([head, values[:-stride]], axis=0)


def later(values, stride, filler):
    tail = jnp.full((stride,) + values.shape[1:], filler, values.dtype)
    return jnp.concatenate([values[stride:], tail], axis=0)


def cyclic_solve(lower_band, main_band, upper_band, right_side):
    length = main_band.shape[0]
    for bit in range((length - 1).bit_length()):
        stride = 1 << bit
        back_weight = -lower_band / earlier(main_band, stride, 1.0)
        ahead_weight = -upper_band / later(main_band, stride, 1.0)
        new_lower = back_weight * earlier(lower_band, stride, 0.0)
        new_upper = ahead_weight * later(upper_band, stride, 0.0)
        new_main = (
            main_band
            + back_weight * earlier(upper_band, stride, 0.0)
            + ahead_weight * later(lower_band, stride, 0.0)
        )
        new_right = (
            right_side
            + back_weight * earlier(right_side, stride, 0.0)
            + ahead_weight * later(right_side, stride, 0.0)
        )
        lower_band, main_band, upper_band, right_side = (new_lower, new_main, new_upper, new_right)
    return right_side / main_band


MESH_AXES = ("gx", "gy", "gz")


def halo_kernel(sides, sizes, gathered, group, *refs):
    count = len(sides)
    sends = refs[:2 * count]
    gins = refs[2 * count:2 * count + gathered]
    recvs = refs[2 * count + gathered:4 * count + gathered]
    gouts = refs[4 * count + gathered:4 * count + 2 * gathered]
    send_sem, recv_sem, gsend_sem, grecv_sem = refs[4 * count + 2 * gathered:]
    me = {a: lax.axis_index(a) for a in MESH_AXES}

    def peer(axis, delta):
        return tuple(me[a] + delta if a == axis else me[a] for a in MESH_AXES)

    def across(level):
        return tuple(level if a == "gz" else me[a] for a in MESH_AXES)

    links = []
    for i, axis in enumerate(sides):
        links.append((axis, -1, me[axis] > 0, 2 * i, 2 * i + 1))
        links.append((axis, 1, me[axis] < sizes[i] - 1, 2 * i + 1, 2 * i))
    barrier = pltpu.get_barrier_semaphore()
    peers = 0
    for axis, delta, present, _, _ in links:
        if gathered and axis == "gz":
            continue
        peers = peers + present.astype(jnp.int32)

        @pl.when(present)
        def _():
            pl.semaphore_signal(barrier, 1, device_id=peer(axis, delta), device_id_type=pl.DeviceIdType.MESH)
    if gathered:
        for d in range(1, group):
            pl.semaphore_signal(
                barrier, 1, device_id=across(lax.rem(me["gz"] + d, group)), device_id_type=pl.DeviceIdType.MESH
            )
        peers = peers + (group - 1)
    pl.semaphore_wait(barrier, peers)
    copies = []
    for axis, delta, present, src, dst in links:
        copy = pltpu.make_async_remote_copy(
            src_ref=sends[src], dst_ref=recvs[dst], send_sem=send_sem.at[src], recv_sem=recv_sem.at[dst],
            device_id=peer(axis, delta), device_id_type=pl.DeviceIdType.MESH,
        )
        copies.append((present, copy))

        @pl.when(present)
        def _():
            copy.start()
    gcopies = []
    for j in range(gathered):
        for d in range(1, group):
            slot = j * (group - 1) + d - 1
            copy = pltpu.make_async_remote_copy(
                src_ref=gins[j], dst_ref=gouts[j].at[me["gz"]], send_sem=gsend_sem.at[slot],
                recv_sem=grecv_sem.at[slot], device_id=across(lax.rem(me["gz"] + d, group)),
                device_id_type=pl.DeviceIdType.MESH,
            )
            copy.start()
            gcopies.append(copy)
    for j in range(gathered):
        gouts[j][me["gz"]] = gins[j][...]
    for axis, delta, present, src, dst in links:
        incoming = pltpu.make_async_remote_copy(
            src_ref=sends[dst], dst_ref=recvs[src], send_sem=send_sem.at[dst], recv_sem=recv_sem.at[src],
            device_id=peer(axis, delta), device_id_type=pl.DeviceIdType.MESH,
        )

        @pl.when(present)
        def _():
            incoming.wait_recv()

        @pl.when(jnp.logical_not(present))
        def _():
            recvs[src][...] = jnp.zeros(recvs[src].shape, recvs[src].dtype)
    for j in range(gathered):
        for d in range(1, group):
            slot = j * (group - 1) + d - 1
            origin = lax.rem(me["gz"] + group - d, group)
            incoming = pltpu.make_async_remote_copy(
                src_ref=gins[j], dst_ref=gouts[j].at[origin], send_sem=gsend_sem.at[slot],
                recv_sem=grecv_sem.at[slot], device_id=across(origin), device_id_type=pl.DeviceIdType.MESH,
            )
            incoming.wait_recv()
    for present, copy in copies:
        @pl.when(present)
        def _():
            copy.wait_send()
    for copy in gcopies:
        copy.wait_send()


def exchange(cells, sides, collective, gathers=()):
    sends = []
    for axis, dim in sides:
        size = cells.shape[dim]
        sends.append(lax.index_in_dim(cells, 0, axis=dim, keepdims=False))
        sends.append(lax.index_in_dim(cells, size - 1, axis=dim, keepdims=False))
    axes = tuple(axis for axis, _ in sides)
    sizes = tuple(lax.axis_size(axis) for axis in axes)
    group = lax.axis_size("gz")
    vmem = pl.BlockSpec(memory_space=pltpu.VMEM)
    slots = max(1, len(gathers) * (group - 1))
    outs = pl.pallas_call(
        functools.partial(halo_kernel, axes, sizes, len(gathers), group),
        out_shape=[jax.ShapeDtypeStruct(s.shape, s.dtype) for s in sends]
        + [jax.ShapeDtypeStruct((group,) + g.shape, g.dtype) for g in gathers],
        in_specs=[vmem] * (len(sends) + len(gathers)),
        out_specs=[vmem] * (len(sends) + len(gathers)),
        scratch_shapes=[
            pltpu.SemaphoreType.DMA((max(1, len(sends)),)), pltpu.SemaphoreType.DMA((max(1, len(sends)),)),
            pltpu.SemaphoreType.DMA((slots,)), pltpu.SemaphoreType.DMA((slots,)),
        ],
        compiler_params=pltpu.CompilerParams(collective_id=collective, has_side_effects=True),
    )(*sends, *gathers)
    recvs = outs[:len(sends)]
    faces = {
        dim: (jnp.expand_dims(recvs[2 * i], dim), jnp.expand_dims(recvs[2 * i + 1], dim))
        for i, (axis, dim) in enumerate(sides)
    }
    stacked = [g.reshape((group * g.shape[1],) + g.shape[2:]) for g in outs[len(sends):]]
    return faces, stacked


def column_kernel(sizes, group, v_ref, xlo_s, xhi_s, ylo_s, yhi_s, v_out, xlo_o, xhi_o, ylo_o, yhi_o, send_sem, recv_sem):
    i, j, k = (lax.axis_index(a) for a in MESH_AXES)
    nx, ny = sizes
    mesh_id = pl.DeviceIdType.MESH
    sides = (
        (i > 0, (-1, 0), xlo_s, xhi_o, xlo_o, 1),
        (i < nx - 1, (1, 0), xhi_s, xlo_o, xhi_o, 2),
        (j > 0, (0, -1), ylo_s, yhi_o, ylo_o, 3),
        (j < ny - 1, (0, 1), yhi_s, ylo_o, yhi_o, 4),
    )
    barrier = pltpu.get_barrier_semaphore()
    for d in range(1, group):
        pl.semaphore_signal(barrier, 1, device_id=(i, j, lax.rem(k + d, group)), device_id_type=mesh_id)
    peers = group - 1
    for present, (di, dj), _, _, _, _ in sides:
        peers = peers + group * present.astype(jnp.int32)
        for kk in range(group):
            @pl.when(present)
            def _():
                pl.semaphore_signal(barrier, 1, device_id=(i + di, j + dj, kk), device_id_type=mesh_id)
    pl.semaphore_wait(barrier, peers)
    block_copies = []
    for d in range(1, group):
        copy = pltpu.make_async_remote_copy(
            src_ref=v_ref, dst_ref=v_out.at[:, k], send_sem=send_sem.at[d], recv_sem=recv_sem.at[d],
            device_id=(i, j, lax.rem(k + d, group)), device_id_type=mesh_id,
        )
        copy.start()
        block_copies.append(copy)
    face_copies = []
    for present, (di, dj), face, far_out, _, base in sides:
        for kk in range(group):
            copy = pltpu.make_async_remote_copy(
                src_ref=face, dst_ref=far_out.at[:, k], send_sem=send_sem.at[base * group + kk],
                recv_sem=recv_sem.at[base * group + k], device_id=(i + di, j + dj, kk), device_id_type=mesh_id,
            )
            face_copies.append((present, copy))

            @pl.when(present)
            def _():
                copy.start()
    v_out[:, k] = v_ref[...]
    for d in range(1, group):
        origin = lax.rem(k + group - d, group)
        incoming = pltpu.make_async_remote_copy(
            src_ref=v_ref, dst_ref=v_out.at[:, origin], send_sem=send_sem.at[d], recv_sem=recv_sem.at[d],
            device_id=(i, j, origin), device_id_type=mesh_id,
        )
        incoming.wait_recv()
    for index, (present, (di, dj), face, _, near_out, base) in enumerate(sides):
        partner = sides[index ^ 1]
        for kk in range(group):
            incoming = pltpu.make_async_remote_copy(
                src_ref=partner[2], dst_ref=near_out.at[:, kk], send_sem=send_sem.at[partner[5] * group + kk],
                recv_sem=recv_sem.at[partner[5] * group + kk], device_id=(i + di, j + dj, kk),
                device_id_type=mesh_id,
            )

            @pl.when(present)
            def _():
                incoming.wait_recv()

        @pl.when(jnp.logical_not(present))
        def _():
            near_out[...] = jnp.zeros(near_out.shape, near_out.dtype)
    for copy in block_copies:
        copy.wait_send()
    for present, copy in face_copies:
        @pl.when(present)
        def _():
            copy.wait_send()


def column_exchange(cells, collective):
    chans, levels, extent, breadth = cells.shape
    group = lax.axis_size("gz")
    sizes = (lax.axis_size("gx"), lax.axis_size("gy"))
    sends = [
        cells[:, :, 0, :], cells[:, :, extent - 1, :], cells[:, :, :, 0], cells[:, :, :, breadth - 1],
    ]
    vmem = pl.BlockSpec(memory_space=pltpu.VMEM)
    shapes = [(chans, group, levels, extent, breadth)] + [(chans, group) + s.shape[1:] for s in sends]
    outs = pl.pallas_call(
        functools.partial(column_kernel, sizes, group),
        out_shape=[jax.ShapeDtypeStruct(s, cells.dtype) for s in shapes],
        in_specs=[vmem] * 5,
        out_specs=[vmem] * 5,
        scratch_shapes=[pltpu.SemaphoreType.DMA((5 * group,)), pltpu.SemaphoreType.DMA((5 * group,))],
        compiler_params=pltpu.CompilerParams(collective_id=collective, has_side_effects=True),
    )(cells, *sends)
    height = group * levels
    whole = outs[0].reshape(chans, height, extent, breadth)
    xlo, xhi, ylo, yhi = (o.reshape((chans, height) + o.shape[3:]) for o in outs[1:])
    faces = {
        2: (jnp.expand_dims(xlo, 2), jnp.expand_dims(xhi, 2)),
        3: (jnp.expand_dims(ylo, 3), jnp.expand_dims(yhi, 3)),
    }
    return whole, faces


def face_from(part, axis, from_lower):
    count = lax.axis_size(axis)
    if from_lower:
        pairs = [(i, i + 1) for i in range(count - 1)]
    else:
        pairs = [(i + 1, i) for i in range(count - 1)]
    return lax.ppermute(part, axis, pairs)


def faces_of(cells, sides):
    got = {}
    for axis, dim in sides:
        size = cells.shape[dim]
        got[dim] = (
            face_from(lax.slice_in_dim(cells, size - 1, size, axis=dim), axis, True),
            face_from(lax.slice_in_dim(cells, 0, 1, axis=dim), axis, False),
        )
    return got


def along(cells, faces, dim):
    size = cells.shape[dim]
    lower, upper = faces[dim]
    ahead = jnp.concatenate([lax.slice_in_dim(cells, 1, size, axis=dim), upper], axis=dim)
    behind = jnp.concatenate([lower, lax.slice_in_dim(cells, 0, size - 1, axis=dim)], axis=dim)
    return (ahead - behind) * 0.5


def shards(
    stress_trial,
    mean_stress,
    consolidation,
    point_velocity,
    point_weight,
    point_cell,
    yield_flag,
    point_count,
    porosity,
    permeability,
):
    levels, extent, breadth = porosity.shape
    cell_sums = cell_sums_of(
        stress_trial, mean_stress, consolidation, point_velocity, point_weight, point_cell,
        yield_flag, point_count, levels, extent, breadth,
    )
    sides = (("gx", 2), ("gy", 3), ("gz", 1))
    stress_sums = cell_sums[:6]
    sf, (all_porosity, all_permeability) = exchange(stress_sums, sides, 0, (porosity, permeability))
    height = all_porosity.shape[0]
    d_x = lambda c: along(stress_sums[c:c + 1], {2: (sf[2][0][c:c + 1], sf[2][1][c:c + 1])}, 2)[0]
    d_y = lambda c: along(stress_sums[c:c + 1], {3: (sf[3][0][c:c + 1], sf[3][1][c:c + 1])}, 3)[0]
    d_z = lambda c: along(stress_sums[c:c + 1], {1: (sf[1][0][c:c + 1], sf[1][1][c:c + 1])}, 1)[0]
    floored = jnp.maximum(cell_sums[9], mass_floor)
    force_x = d_x(0) + d_y(3) + d_z(5)
    force_y = d_x(3) + d_y(1) + d_z(4)
    force_z = d_x(5) + d_y(4) + d_z(2)
    velocity = jnp.stack(
        [
            (cell_sums[6] + time_step * force_x) / floored,
            (cell_sums[7] + time_step * force_y) / floored,
            (cell_sums[8] + time_step * force_z) / floored,
        ]
    )
    column_velocity, vf = column_exchange(velocity, 1)
    lid = jnp.zeros((1,) + column_velocity.shape[2:], jnp.float32)
    dilation = (
        along(column_velocity[0:1], {2: (vf[2][0][0:1], vf[2][1][0:1])}, 2)[0]
        + along(column_velocity[1:2], {3: (vf[3][0][1:2], vf[3][1][1:2])}, 3)[0]
        + along(column_velocity[2], {0: (lid, lid)}, 0)
    )
    all_right = -source_rate * (1.0 - all_porosity) * dilation
    zero_level = jnp.zeros((1, extent, breadth), jnp.float32)
    level_above = jnp.concatenate([all_permeability[1:], zero_level], axis=0)
    level_below = jnp.concatenate([zero_level, all_permeability[:-1]], axis=0)
    at_top = (jnp.arange(height, dtype=jnp.int32) == height - 1)[:, None, None]
    up_face = harmonic(all_permeability, level_above)
    down_face = harmonic(level_below, all_permeability)
    top_face = jnp.where(at_top, all_permeability, up_face)
    lower_band = -time_step * down_face
    upper_band = -time_step * up_face
    main_band = storage_rate * all_porosity + time_step * (down_face + top_face)
    column = height, extent * breadth
    solved = cyclic_solve(
        lower_band.reshape(column), main_band.reshape(column), upper_band.reshape(column),
        all_right.reshape(column),
    ).reshape(height, extent, breadth)
    first = lax.axis_index("gz") * levels
    around = lax.dynamic_slice_in_dim(
        jnp.concatenate([zero_level, solved, zero_level], axis=0), first, levels + 2, axis=0
    )
    pressure = around[1:-1]
    pf, _ = exchange(pressure, (("gx", 1), ("gy", 2)), 2)
    gradient = jnp.stack(
        [
            along(pressure, pf, 1),
            along(pressure, pf, 2),
            (around[2:] - around[:-2]) * 0.5,
        ]
    )
    return (velocity - time_step * gradient, pressure)


def solution(mesh):
    placed = (
        P(None, ("gx", "gy", "gz")),
        P(("gx", "gy", "gz")),
        P(("gx", "gy", "gz")),
        P(None, ("gx", "gy", "gz")),
        P(("gx", "gy", "gz")),
        P(("gx", "gy", "gz")),
        P(("gx", "gy", "gz")),
        P("gx", "gy", "gz"),
        P("gz", "gx", "gy"),
        P("gz", "gx", "gy"),
    )
    return jax.shard_map(
        shards,
        mesh=mesh,
        in_specs=placed,
        out_specs=(P(None, "gz", "gx", "gy"), P("gz", "gx", "gy")),
        check_vma=False,
    )
```

```python
import functools

import jax
import jax.numpy as jnp
from jax import lax
from jax.sharding import PartitionSpec as P

time_step = 0.25
storage_rate = 0.002
source_rate = 0.003
critical_slope = 1.2
mass_floor = 0.5
shear_floor = 1.0

from jax.experimental import pallas as pl
from jax.experimental.pallas import tpu as pltpu

CHUNK = 1024
M_ROWS = 32
N_COLS = 512


SPLITS = 2


def _split(v):
    hi = v.astype(jnp.bfloat16)
    lo = (v - hi.astype(jnp.float32)).astype(jnp.bfloat16)
    return [hi, lo]


def sums_kernel(count_ref, st_ref, ms_ref, cons_ref, vel_ref, w_ref, cell_ref, yf_ref, out_ref, xlo_ref, xhi_ref, ylo_ref, yhi_ref, zlo_ref, zhi_ref, acc_ref):
    count = count_ref[0, 0]
    acc_ref[...] = jnp.zeros_like(acc_ref)
    chunks = st_ref.shape[1] // CHUNK

    def body(k, carry):
        start = pl.multiple_of(k * CHUNK, CHUNK)
        span = pl.ds(start, CHUNK)
        st = [st_ref[pl.ds(i, 1), span] for i in range(6)]
        ms = ms_ref[:, span]
        cons = cons_ref[:, span]
        yf = yf_ref[:, span]
        slot = start + lax.broadcasted_iota(jnp.int32, (1, CHUNK), 1)
        weight = jnp.where(slot < count, w_ref[:, span], 0.0)
        sq_normal = st[0] * st[0] + st[1] * st[1] + st[2] * st[2]
        sq_shear = st[3] * st[3] + st[4] * st[4] + st[5] * st[5]
        shear_size = jnp.sqrt(1.5 * (sq_normal + 2.0 * sq_shear))
        yield_size = critical_slope * jnp.sqrt(ms * (cons - ms))
        factor = jnp.where(yf == 1, yield_size / jnp.maximum(shear_size, shear_floor), 1.0)
        stress = [st[i] * factor - ms if i < 3 else st[i] * factor for i in range(6)]
        values = [s * weight for s in stress]
        values += [vel_ref[pl.ds(i, 1), span] * weight for i in range(3)]
        values.append(weight)
        cell = cell_ref[:, span]
        m_key = (cell >> 12) * 8 + ((cell >> 7) & 7)
        n_key = ((cell >> 10) & 3) * 128 + (cell & 127)
        m_mask = lax.broadcasted_iota(jnp.int32, (M_ROWS, CHUNK), 0) == m_key
        zero = jnp.zeros((M_ROWS, CHUNK), jnp.bfloat16)
        pieces = []
        for v in values:
            for part in _split(v):
                pieces.append(jnp.where(m_mask, jnp.broadcast_to(part, (M_ROWS, CHUNK)), zero))
        lhs = jnp.concatenate(pieces, axis=0)
        one_hot = jnp.where(
            lax.broadcasted_iota(jnp.int32, (N_COLS, CHUNK), 0) == n_key, 1.0, 0.0
        ).astype(jnp.bfloat16)
        acc_ref[...] += lax.dot_general(
            lhs, one_hot, (((1,), (1,)), ((), ())), preferred_element_type=jnp.float32
        )
        return carry

    lax.fori_loop(0, chunks, body, 0)
    for comp in range(10):
        for level in range(16):
            rows = pl.ds((comp * SPLITS) * M_ROWS + (level >> 2) * 8, 8)
            lanes = pl.ds((level & 3) * 128, 128)
            total = acc_ref[rows, lanes]
            for s in range(1, SPLITS):
                total = total + acc_ref[pl.ds((comp * SPLITS + s) * M_ROWS + (level >> 2) * 8, 8), lanes]
            out_ref[comp, level] = total
            if comp < 6:
                xlo_ref[comp, pl.ds(level, 1), :] = total[0:1, :]
                xhi_ref[comp, pl.ds(level, 1), :] = total[7:8, :]
                turned = total.T
                ylo_ref[comp, pl.ds(level, 1), :] = turned[0:1, :]
                yhi_ref[comp, pl.ds(level, 1), :] = turned[127:128, :]
                if level == 0:
                    zlo_ref[comp] = total
                if level == 15:
                    zhi_ref[comp] = total


def cell_sums_of(stress_trial, mean_stress, consolidation, point_velocity, point_weight, point_cell, yield_flag, point_count, levels, extent, breadth):
    n = mean_stress.shape[0]
    row = lambda a: a.reshape(1, n)
    vmem = pl.BlockSpec(memory_space=pltpu.VMEM)
    return pl.pallas_call(
        sums_kernel,
        out_shape=[
            jax.ShapeDtypeStruct(s, jnp.float32)
            for s in [(10, levels, extent, breadth)] + [(6, levels, breadth)] * 2 + [(6, levels, extent)] * 2
            + [(6, extent, breadth)] * 2
        ],
        in_specs=[pl.BlockSpec(memory_space=pltpu.SMEM)] + [vmem] * 7,
        out_specs=[vmem] * 7,
        scratch_shapes=[pltpu.VMEM((10 * SPLITS * M_ROWS, N_COLS), jnp.float32)],
        cost_estimate=pl.CostEstimate(
            flops=2 * 10 * SPLITS * M_ROWS * N_COLS * n, bytes_accessed=13 * 4 * n + 10 * 4 * levels * extent * breadth,
            transcendentals=3 * n,
        ),
    )(
        point_count.reshape(1, 1), stress_trial, row(mean_stress), row(consolidation), point_velocity,
        row(point_weight), row(point_cell), row(yield_flag),
    )


def padded_2(cells, sides, width):
    for axis, dim in sides:
        count = lax.axis_size(axis)
        ends = count - 1
        head = lax.slice_in_dim(cells, 0, width, axis=dim)
        tail = lax.slice_in_dim(cells, cells.shape[dim] - width, cells.shape[dim], axis=dim)
        cells = jnp.concatenate(
            [
                lax.ppermute(tail, axis, [(i, (i + 1) % count) for i in range(ends)]),
                cells,
                lax.ppermute(head, axis, [((i + 1) % count, i) for i in range(ends)]),
            ],
            axis=dim,
        )
    return cells


def along_x(padded):
    return (padded[..., 1:-1, 2:, 1:-1] - padded[..., 1:-1, :-2, 1:-1]) * 0.5


def along_y(padded):
    return (padded[..., 1:-1, 1:-1, 2:] - padded[..., 1:-1, 1:-1, :-2]) * 0.5


def along_z(padded):
    return (padded[..., 2:, 1:-1, 1:-1] - padded[..., :-2, 1:-1, 1:-1]) * 0.5


def harmonic(former, latter):
    return 2.0 * former * latter / (former + latter)


def returned_stress(stress_trial, mean_stress, consolidation, yield_flag):
    sq_normal = (
        stress_trial[0] * stress_trial[0]
        + stress_trial[1] * stress_trial[1]
        + stress_trial[2] * stress_trial[2]
    )
    sq_shear = (
        stress_trial[3] * stress_trial[3]
        + stress_trial[4] * stress_trial[4]
        + stress_trial[5] * stress_trial[5]
    )
    shear_size = jnp.sqrt(1.5 * (sq_normal + 2.0 * sq_shear))
    yield_size = critical_slope * jnp.sqrt(mean_stress * (consolidation - mean_stress))
    factor = jnp.where(yield_flag == 1, yield_size / jnp.maximum(shear_size, shear_floor), 1.0)
    isotropic = jnp.array([1.0, 1.0, 1.0, 0.0, 0.0, 0.0], dtype=jnp.float32)[:, None]
    return stress_trial * factor - isotropic * mean_stress


def point_sums(stress, point_velocity, weight, cell_index, segments):
    stacked = jnp.concatenate([stress * weight, point_velocity * weight, weight[None]], axis=0)
    return jax.vmap(
        lambda component: jax.ops.segment_sum(component, cell_index, num_segments=segments)
    )(stacked)


def brick_velocity(cell_sums, padded):
    floored = jnp.maximum(cell_sums[9], mass_floor)
    force_x = along_x(padded[0]) + along_y(padded[3]) + along_z(padded[5])
    force_y = along_x(padded[3]) + along_y(padded[1]) + along_z(padded[4])
    force_z = along_x(padded[5]) + along_y(padded[4]) + along_z(padded[2])
    return jnp.stack(
        [
            (cell_sums[6] + time_step * force_x) / floored,
            (cell_sums[7] + time_step * force_y) / floored,
            (cell_sums[8] + time_step * force_z) / floored,
        ]
    )


def divergence(padded_velocity):
    return along_x(padded_velocity[0]) + along_y(padded_velocity[1]) + along_z(padded_velocity[2])


def band_terms(porosity, permeability, level_below, level_above, at_top, dilation):
    up_face = harmonic(permeability, level_above)
    down_face = harmonic(level_below, permeability)
    top_face = jnp.where(at_top, permeability, up_face)
    lower_band = -time_step * down_face
    upper_band = -time_step * up_face
    main_band = storage_rate * porosity + time_step * (down_face + top_face)
    right_side = -source_rate * (1.0 - porosity) * dilation
    return (lower_band, main_band, upper_band, right_side)


def earlier(values, stride, filler):
    head = jnp.full((stride,) + values.shape[1:], filler, values.dtype)
    return jnp.concatenate([head, values[:-stride]], axis=0)


def later(values, stride, filler):
    tail = jnp.full((stride,) + values.shape[1:], filler, values.dtype)
    return jnp.concatenate([values[stride:], tail], axis=0)


def cyclic_solve(lower_band, main_band, upper_band, right_side):
    length = main_band.shape[0]
    for bit in range((length - 1).bit_length()):
        stride = 1 << bit
        back_weight = -lower_band / earlier(main_band, stride, 1.0)
        ahead_weight = -upper_band / later(main_band, stride, 1.0)
        new_lower = back_weight * earlier(lower_band, stride, 0.0)
        new_upper = ahead_weight * later(upper_band, stride, 0.0)
        new_main = (
            main_band
            + back_weight * earlier(upper_band, stride, 0.0)
            + ahead_weight * later(lower_band, stride, 0.0)
        )
        new_right = (
            right_side
            + back_weight * earlier(right_side, stride, 0.0)
            + ahead_weight * later(right_side, stride, 0.0)
        )
        lower_band, main_band, upper_band, right_side = (new_lower, new_main, new_upper, new_right)
    return right_side / main_band


MESH_AXES = ("gx", "gy", "gz")


def halo_kernel(sides, sizes, gathered, group, *refs):
    count = len(sides)
    sends = refs[:2 * count]
    gins = refs[2 * count:2 * count + gathered]
    recvs = refs[2 * count + gathered:4 * count + gathered]
    gouts = refs[4 * count + gathered:4 * count + 2 * gathered]
    send_sem, recv_sem, gsend_sem, grecv_sem = refs[4 * count + 2 * gathered:]
    me = {a: lax.axis_index(a) for a in MESH_AXES}

    def peer(axis, delta):
        return tuple(me[a] + delta if a == axis else me[a] for a in MESH_AXES)

    def across(level):
        return tuple(level if a == "gz" else me[a] for a in MESH_AXES)

    links = []
    for i, axis in enumerate(sides):
        links.append((axis, -1, me[axis] > 0, 2 * i, 2 * i + 1))
        links.append((axis, 1, me[axis] < sizes[i] - 1, 2 * i + 1, 2 * i))
    barrier = pltpu.get_barrier_semaphore()
    peers = 0
    for axis, delta, present, _, _ in links:
        if gathered and axis == "gz":
            continue
        peers = peers + present.astype(jnp.int32)

        @pl.when(present)
        def _():
            pl.semaphore_signal(barrier, 1, device_id=peer(axis, delta), device_id_type=pl.DeviceIdType.MESH)
    if gathered:
        for d in range(1, group):
            pl.semaphore_signal(
                barrier, 1, device_id=across(lax.rem(me["gz"] + d, group)), device_id_type=pl.DeviceIdType.MESH
            )
        peers = peers + (group - 1)
    pl.semaphore_wait(barrier, peers)
    copies = []
    for axis, delta, present, src, dst in links:
        copy = pltpu.make_async_remote_copy(
            src_ref=sends[src], dst_ref=recvs[dst], send_sem=send_sem.at[src], recv_sem=recv_sem.at[dst],
            device_id=peer(axis, delta), device_id_type=pl.DeviceIdType.MESH,
        )
        copies.append((present, copy))

        @pl.when(present)
        def _():
            copy.start()
    gcopies = []
    for j in range(gathered):
        for d in range(1, group):
            slot = j * (group - 1) + d - 1
            copy = pltpu.make_async_remote_copy(
                src_ref=gins[j], dst_ref=gouts[j].at[me["gz"]], send_sem=gsend_sem.at[slot],
                recv_sem=grecv_sem.at[slot], device_id=across(lax.rem(me["gz"] + d, group)),
                device_id_type=pl.DeviceIdType.MESH,
            )
            copy.start()
            gcopies.append(copy)
    for j in range(gathered):
        gouts[j][me["gz"]] = gins[j][...]
    for axis, delta, present, src, dst in links:
        incoming = pltpu.make_async_remote_copy(
            src_ref=sends[dst], dst_ref=recvs[src], send_sem=send_sem.at[dst], recv_sem=recv_sem.at[src],
            device_id=peer(axis, delta), device_id_type=pl.DeviceIdType.MESH,
        )

        @pl.when(present)
        def _():
            incoming.wait_recv()

        @pl.when(jnp.logical_not(present))
        def _():
            recvs[src][...] = jnp.zeros(recvs[src].shape, recvs[src].dtype)
    for j in range(gathered):
        for d in range(1, group):
            slot = j * (group - 1) + d - 1
            origin = lax.rem(me["gz"] + group - d, group)
            incoming = pltpu.make_async_remote_copy(
                src_ref=gins[j], dst_ref=gouts[j].at[origin], send_sem=gsend_sem.at[slot],
                recv_sem=grecv_sem.at[slot], device_id=across(origin), device_id_type=pl.DeviceIdType.MESH,
            )
            incoming.wait_recv()
    for present, copy in copies:
        @pl.when(present)
        def _():
            copy.wait_send()
    for copy in gcopies:
        copy.wait_send()


def exchange(cells, sides, collective, gathers=(), given=None):
    sends = []
    for axis, dim in sides:
        size = cells.shape[dim]
        sends.append(lax.index_in_dim(cells, 0, axis=dim, keepdims=False))
        sends.append(lax.index_in_dim(cells, size - 1, axis=dim, keepdims=False))
    if given is not None:
        sends = list(given)
    axes = tuple(axis for axis, _ in sides)
    sizes = tuple(lax.axis_size(axis) for axis in axes)
    group = lax.axis_size("gz")
    vmem = pl.BlockSpec(memory_space=pltpu.VMEM)
    slots = max(1, len(gathers) * (group - 1))
    outs = pl.pallas_call(
        functools.partial(halo_kernel, axes, sizes, len(gathers), group),
        out_shape=[jax.ShapeDtypeStruct(s.shape, s.dtype) for s in sends]
        + [jax.ShapeDtypeStruct((group,) + g.shape, g.dtype) for g in gathers],
        in_specs=[vmem] * (len(sends) + len(gathers)),
        out_specs=[vmem] * (len(sends) + len(gathers)),
        scratch_shapes=[
            pltpu.SemaphoreType.DMA((max(1, len(sends)),)), pltpu.SemaphoreType.DMA((max(1, len(sends)),)),
            pltpu.SemaphoreType.DMA((slots,)), pltpu.SemaphoreType.DMA((slots,)),
        ],
        compiler_params=pltpu.CompilerParams(collective_id=collective, has_side_effects=True),
    )(*sends, *gathers)
    recvs = outs[:len(sends)]
    faces = {
        dim: (jnp.expand_dims(recvs[2 * i], dim), jnp.expand_dims(recvs[2 * i + 1], dim))
        for i, (axis, dim) in enumerate(sides)
    }
    stacked = [g.reshape((group * g.shape[1],) + g.shape[2:]) for g in outs[len(sends):]]
    return faces, stacked


def face_from(part, axis, from_lower):
    count = lax.axis_size(axis)
    if from_lower:
        pairs = [(i, i + 1) for i in range(count - 1)]
    else:
        pairs = [(i + 1, i) for i in range(count - 1)]
    return lax.ppermute(part, axis, pairs)


def faces_of(cells, sides):
    got = {}
    for axis, dim in sides:
        size = cells.shape[dim]
        got[dim] = (
            face_from(lax.slice_in_dim(cells, size - 1, size, axis=dim), axis, True),
            face_from(lax.slice_in_dim(cells, 0, 1, axis=dim), axis, False),
        )
    return got


def along(cells, faces, dim):
    size = cells.shape[dim]
    lower, upper = faces[dim]
    ahead = jnp.concatenate([lax.slice_in_dim(cells, 1, size, axis=dim), upper], axis=dim)
    behind = jnp.concatenate([lower, lax.slice_in_dim(cells, 0, size - 1, axis=dim)], axis=dim)
    return (ahead - behind) * 0.5


def shards(
    stress_trial,
    mean_stress,
    consolidation,
    point_velocity,
    point_weight,
    point_cell,
    yield_flag,
    point_count,
    porosity,
    permeability,
):
    levels, extent, breadth = porosity.shape
    cell_sums, *stress_faces = cell_sums_of(
        stress_trial, mean_stress, consolidation, point_velocity, point_weight, point_cell,
        yield_flag, point_count, levels, extent, breadth,
    )
    sides = (("gx", 2), ("gy", 3), ("gz", 1))
    stress_sums = cell_sums[:6]
    sf, (all_porosity, all_permeability) = exchange(
        stress_sums, sides, 0, (porosity, permeability), given=stress_faces
    )
    height = all_porosity.shape[0]
    d_x = lambda c: along(stress_sums[c:c + 1], {2: (sf[2][0][c:c + 1], sf[2][1][c:c + 1])}, 2)[0]
    d_y = lambda c: along(stress_sums[c:c + 1], {3: (sf[3][0][c:c + 1], sf[3][1][c:c + 1])}, 3)[0]
    d_z = lambda c: along(stress_sums[c:c + 1], {1: (sf[1][0][c:c + 1], sf[1][1][c:c + 1])}, 1)[0]
    floored = jnp.maximum(cell_sums[9], mass_floor)
    force_x = d_x(0) + d_y(3) + d_z(5)
    force_y = d_x(3) + d_y(1) + d_z(4)
    force_z = d_x(5) + d_y(4) + d_z(2)
    velocity = jnp.stack(
        [
            (cell_sums[6] + time_step * force_x) / floored,
            (cell_sums[7] + time_step * force_y) / floored,
            (cell_sums[8] + time_step * force_z) / floored,
        ]
    )
    vf, _ = exchange(velocity, sides, 1)
    dilation = (
        along(velocity[0:1], {2: (vf[2][0][0:1], vf[2][1][0:1])}, 2)[0]
        + along(velocity[1:2], {3: (vf[3][0][1:2], vf[3][1][1:2])}, 3)[0]
        + along(velocity[2:3], {1: (vf[1][0][2:3], vf[1][1][2:3])}, 1)[0]
    )
    right_side = -source_rate * (1.0 - porosity) * dilation
    _, (all_right,) = exchange(right_side, (), 3, (right_side,))
    zero_level = jnp.zeros((1, extent, breadth), jnp.float32)
    level_above = jnp.concatenate([all_permeability[1:], zero_level], axis=0)
    level_below = jnp.concatenate([zero_level, all_permeability[:-1]], axis=0)
    at_top = (jnp.arange(height, dtype=jnp.int32) == height - 1)[:, None, None]
    up_face = harmonic(all_permeability, level_above)
    down_face = harmonic(level_below, all_permeability)
    top_face = jnp.where(at_top, all_permeability, up_face)
    lower_band = -time_step * down_face
    upper_band = -time_step * up_face
    main_band = storage_rate * all_porosity + time_step * (down_face + top_face)
    column = height, extent * breadth
    solved = cyclic_solve(
        lower_band.reshape(column), main_band.reshape(column), upper_band.reshape(column),
        all_right.reshape(column),
    ).reshape(height, extent, breadth)
    first = lax.axis_index("gz") * levels
    around = lax.dynamic_slice_in_dim(
        jnp.concatenate([zero_level, solved, zero_level], axis=0), first, levels + 2, axis=0
    )
    pressure = around[1:-1]
    pf, _ = exchange(pressure, (("gx", 1), ("gy", 2)), 2)
    gradient = jnp.stack(
        [
            along(pressure, pf, 1),
            along(pressure, pf, 2),
            (around[2:] - around[:-2]) * 0.5,
        ]
    )
    return (velocity - time_step * gradient, pressure)


def solution(mesh):
    placed = (
        P(None, ("gx", "gy", "gz")),
        P(("gx", "gy", "gz")),
        P(("gx", "gy", "gz")),
        P(None, ("gx", "gy", "gz")),
        P(("gx", "gy", "gz")),
        P(("gx", "gy", "gz")),
        P(("gx", "gy", "gz")),
        P("gx", "gy", "gz"),
        P("gz", "gx", "gy"),
        P("gz", "gx", "gy"),
    )
    return jax.shard_map(
        shards,
        mesh=mesh,
        in_specs=placed,
        out_specs=(P(None, "gz", "gx", "gy"), P("gz", "gx", "gy")),
        check_vma=False,
    )
```

```python
import functools

import jax
import jax.numpy as jnp
from jax import lax
from jax.sharding import PartitionSpec as P

time_step = 0.25
storage_rate = 0.002
source_rate = 0.003
critical_slope = 1.2
mass_floor = 0.5
shear_floor = 1.0

from jax.experimental import pallas as pl
from jax.experimental.pallas import tpu as pltpu

CHUNK = 1024
M_ROWS = 32
N_COLS = 512


SPLITS = 2


def _split(v):
    hi = v.astype(jnp.bfloat16)
    lo = (v - hi.astype(jnp.float32)).astype(jnp.bfloat16)
    return [hi, lo]


def sums_kernel(count_ref, st_ref, ms_ref, cons_ref, vel_ref, w_ref, cell_ref, yf_ref, out_ref, xlo_ref, xhi_ref, ylo_ref, yhi_ref, zlo_ref, zhi_ref, acc_ref):
    count = count_ref[0, 0]
    acc_ref[...] = jnp.zeros_like(acc_ref)
    chunks = st_ref.shape[1] // CHUNK

    def body(k, carry):
        start = pl.multiple_of(k * CHUNK, CHUNK)
        span = pl.ds(start, CHUNK)
        st = [st_ref[pl.ds(i, 1), span] for i in range(6)]
        ms = ms_ref[:, span]
        cons = cons_ref[:, span]
        yf = yf_ref[:, span]
        slot = start + lax.broadcasted_iota(jnp.int32, (1, CHUNK), 1)
        weight = jnp.where(slot < count, w_ref[:, span], 0.0)
        sq_normal = st[0] * st[0] + st[1] * st[1] + st[2] * st[2]
        sq_shear = st[3] * st[3] + st[4] * st[4] + st[5] * st[5]
        shear_size = jnp.sqrt(1.5 * (sq_normal + 2.0 * sq_shear))
        yield_size = critical_slope * jnp.sqrt(ms * (cons - ms))
        factor = jnp.where(yf == 1, yield_size / jnp.maximum(shear_size, shear_floor), 1.0)
        stress = [st[i] * factor - ms if i < 3 else st[i] * factor for i in range(6)]
        values = [s * weight for s in stress]
        values += [vel_ref[pl.ds(i, 1), span] * weight for i in range(3)]
        values.append(weight)
        cell = cell_ref[:, span]
        m_key = (cell >> 12) * 8 + ((cell >> 7) & 7)
        n_key = ((cell >> 10) & 3) * 128 + (cell & 127)
        m_mask = lax.broadcasted_iota(jnp.int32, (M_ROWS, CHUNK), 0) == m_key
        zero = jnp.zeros((M_ROWS, CHUNK), jnp.bfloat16)
        pieces = []
        for v in values:
            for part in _split(v):
                pieces.append(jnp.where(m_mask, jnp.broadcast_to(part, (M_ROWS, CHUNK)), zero))
        lhs = jnp.concatenate(pieces, axis=0)
        one_hot = jnp.where(
            lax.broadcasted_iota(jnp.int32, (N_COLS, CHUNK), 0) == n_key, 1.0, 0.0
        ).astype(jnp.bfloat16)
        acc_ref[...] += lax.dot_general(
            lhs, one_hot, (((1,), (1,)), ((), ())), preferred_element_type=jnp.float32
        )
        return carry

    lax.fori_loop(0, chunks, body, 0)
    for comp in range(10):
        for level in range(16):
            rows = pl.ds((comp * SPLITS) * M_ROWS + (level >> 2) * 8, 8)
            lanes = pl.ds((level & 3) * 128, 128)
            total = acc_ref[rows, lanes]
            for s in range(1, SPLITS):
                total = total + acc_ref[pl.ds((comp * SPLITS + s) * M_ROWS + (level >> 2) * 8, 8), lanes]
            out_ref[comp, level] = total
            if comp < 6:
                xlo_ref[comp, pl.ds(level, 1), :] = total[0:1, :]
                xhi_ref[comp, pl.ds(level, 1), :] = total[7:8, :]
                turned = total.T
                ylo_ref[comp, pl.ds(level, 1), :] = turned[0:1, :]
                yhi_ref[comp, pl.ds(level, 1), :] = turned[127:128, :]
                if level == 0:
                    zlo_ref[comp] = total
                if level == 15:
                    zhi_ref[comp] = total


def cell_sums_of(stress_trial, mean_stress, consolidation, point_velocity, point_weight, point_cell, yield_flag, point_count, levels, extent, breadth):
    n = mean_stress.shape[0]
    row = lambda a: a.reshape(1, n)
    vmem = pl.BlockSpec(memory_space=pltpu.VMEM)
    return pl.pallas_call(
        sums_kernel,
        out_shape=[
            jax.ShapeDtypeStruct(s, jnp.float32)
            for s in [(10, levels, extent, breadth)] + [(6, levels, breadth)] * 2 + [(6, levels, extent)] * 2
            + [(6, extent, breadth)] * 2
        ],
        in_specs=[pl.BlockSpec(memory_space=pltpu.SMEM)] + [vmem] * 7,
        out_specs=[vmem] * 7,
        scratch_shapes=[pltpu.VMEM((10 * SPLITS * M_ROWS, N_COLS), jnp.float32)],
        cost_estimate=pl.CostEstimate(
            flops=2 * 10 * SPLITS * M_ROWS * N_COLS * n, bytes_accessed=13 * 4 * n + 10 * 4 * levels * extent * breadth,
            transcendentals=3 * n,
        ),
    )(
        point_count.reshape(1, 1), stress_trial, row(mean_stress), row(consolidation), point_velocity,
        row(point_weight), row(point_cell), row(yield_flag),
    )


def padded_2(cells, sides, width):
    for axis, dim in sides:
        count = lax.axis_size(axis)
        ends = count - 1
        head = lax.slice_in_dim(cells, 0, width, axis=dim)
        tail = lax.slice_in_dim(cells, cells.shape[dim] - width, cells.shape[dim], axis=dim)
        cells = jnp.concatenate(
            [
                lax.ppermute(tail, axis, [(i, (i + 1) % count) for i in range(ends)]),
                cells,
                lax.ppermute(head, axis, [((i + 1) % count, i) for i in range(ends)]),
            ],
            axis=dim,
        )
    return cells


def along_x(padded):
    return (padded[..., 1:-1, 2:, 1:-1] - padded[..., 1:-1, :-2, 1:-1]) * 0.5


def along_y(padded):
    return (padded[..., 1:-1, 1:-1, 2:] - padded[..., 1:-1, 1:-1, :-2]) * 0.5


def along_z(padded):
    return (padded[..., 2:, 1:-1, 1:-1] - padded[..., :-2, 1:-1, 1:-1]) * 0.5


def harmonic(former, latter):
    return 2.0 * former * latter / (former + latter)


def returned_stress(stress_trial, mean_stress, consolidation, yield_flag):
    sq_normal = (
        stress_trial[0] * stress_trial[0]
        + stress_trial[1] * stress_trial[1]
        + stress_trial[2] * stress_trial[2]
    )
    sq_shear = (
        stress_trial[3] * stress_trial[3]
        + stress_trial[4] * stress_trial[4]
        + stress_trial[5] * stress_trial[5]
    )
    shear_size = jnp.sqrt(1.5 * (sq_normal + 2.0 * sq_shear))
    yield_size = critical_slope * jnp.sqrt(mean_stress * (consolidation - mean_stress))
    factor = jnp.where(yield_flag == 1, yield_size / jnp.maximum(shear_size, shear_floor), 1.0)
    isotropic = jnp.array([1.0, 1.0, 1.0, 0.0, 0.0, 0.0], dtype=jnp.float32)[:, None]
    return stress_trial * factor - isotropic * mean_stress


def point_sums(stress, point_velocity, weight, cell_index, segments):
    stacked = jnp.concatenate([stress * weight, point_velocity * weight, weight[None]], axis=0)
    return jax.vmap(
        lambda component: jax.ops.segment_sum(component, cell_index, num_segments=segments)
    )(stacked)


def brick_velocity(cell_sums, padded):
    floored = jnp.maximum(cell_sums[9], mass_floor)
    force_x = along_x(padded[0]) + along_y(padded[3]) + along_z(padded[5])
    force_y = along_x(padded[3]) + along_y(padded[1]) + along_z(padded[4])
    force_z = along_x(padded[5]) + along_y(padded[4]) + along_z(padded[2])
    return jnp.stack(
        [
            (cell_sums[6] + time_step * force_x) / floored,
            (cell_sums[7] + time_step * force_y) / floored,
            (cell_sums[8] + time_step * force_z) / floored,
        ]
    )


def divergence(padded_velocity):
    return along_x(padded_velocity[0]) + along_y(padded_velocity[1]) + along_z(padded_velocity[2])


def band_terms(porosity, permeability, level_below, level_above, at_top, dilation):
    up_face = harmonic(permeability, level_above)
    down_face = harmonic(level_below, permeability)
    top_face = jnp.where(at_top, permeability, up_face)
    lower_band = -time_step * down_face
    upper_band = -time_step * up_face
    main_band = storage_rate * porosity + time_step * (down_face + top_face)
    right_side = -source_rate * (1.0 - porosity) * dilation
    return (lower_band, main_band, upper_band, right_side)


def earlier(values, stride, filler):
    head = jnp.full((stride,) + values.shape[1:], filler, values.dtype)
    return jnp.concatenate([head, values[:-stride]], axis=0)


def later(values, stride, filler):
    tail = jnp.full((stride,) + values.shape[1:], filler, values.dtype)
    return jnp.concatenate([values[stride:], tail], axis=0)


def cyclic_solve(lower_band, main_band, upper_band, right_side):
    length = main_band.shape[0]
    for bit in range((length - 1).bit_length()):
        stride = 1 << bit
        back_weight = -lower_band / earlier(main_band, stride, 1.0)
        ahead_weight = -upper_band / later(main_band, stride, 1.0)
        new_lower = back_weight * earlier(lower_band, stride, 0.0)
        new_upper = ahead_weight * later(upper_band, stride, 0.0)
        new_main = (
            main_band
            + back_weight * earlier(upper_band, stride, 0.0)
            + ahead_weight * later(lower_band, stride, 0.0)
        )
        new_right = (
            right_side
            + back_weight * earlier(right_side, stride, 0.0)
            + ahead_weight * later(right_side, stride, 0.0)
        )
        lower_band, main_band, upper_band, right_side = (new_lower, new_main, new_upper, new_right)
    return right_side / main_band


MESH_AXES = ("gx", "gy", "gz")


def halo_kernel(sides, sizes, gathered, group, *refs):
    count = len(sides)
    sends = refs[:2 * count]
    gins = refs[2 * count:2 * count + gathered]
    recvs = refs[2 * count + gathered:4 * count + gathered]
    gouts = refs[4 * count + gathered:4 * count + 2 * gathered]
    send_sem, recv_sem, gsend_sem, grecv_sem = refs[4 * count + 2 * gathered:]
    me = {a: lax.axis_index(a) for a in MESH_AXES}

    def peer(axis, delta):
        return tuple(me[a] + delta if a == axis else me[a] for a in MESH_AXES)

    def across(level):
        return tuple(level if a == "gz" else me[a] for a in MESH_AXES)

    links = []
    for i, axis in enumerate(sides):
        links.append((axis, -1, me[axis] > 0, 2 * i, 2 * i + 1))
        links.append((axis, 1, me[axis] < sizes[i] - 1, 2 * i + 1, 2 * i))
    barrier = pltpu.get_barrier_semaphore()
    peers = 0
    for axis, delta, present, _, _ in links:
        if gathered and axis == "gz":
            continue
        peers = peers + present.astype(jnp.int32)

        @pl.when(present)
        def _():
            pl.semaphore_signal(barrier, 1, device_id=peer(axis, delta), device_id_type=pl.DeviceIdType.MESH)
    if gathered:
        for d in range(1, group):
            pl.semaphore_signal(
                barrier, 1, device_id=across(lax.rem(me["gz"] + d, group)), device_id_type=pl.DeviceIdType.MESH
            )
        peers = peers + (group - 1)
    pl.semaphore_wait(barrier, peers)
    copies = []
    for axis, delta, present, src, dst in links:
        copy = pltpu.make_async_remote_copy(
            src_ref=sends[src], dst_ref=recvs[dst], send_sem=send_sem.at[src], recv_sem=recv_sem.at[dst],
            device_id=peer(axis, delta), device_id_type=pl.DeviceIdType.MESH,
        )
        copies.append((present, copy))

        @pl.when(present)
        def _():
            copy.start()
    gcopies = []
    for j in range(gathered):
        for d in range(1, group):
            slot = j * (group - 1) + d - 1
            copy = pltpu.make_async_remote_copy(
                src_ref=gins[j], dst_ref=gouts[j].at[me["gz"]], send_sem=gsend_sem.at[slot],
                recv_sem=grecv_sem.at[slot], device_id=across(lax.rem(me["gz"] + d, group)),
                device_id_type=pl.DeviceIdType.MESH,
            )
            copy.start()
            gcopies.append(copy)
    for j in range(gathered):
        gouts[j][me["gz"]] = gins[j][...]
    for axis, delta, present, src, dst in links:
        incoming = pltpu.make_async_remote_copy(
            src_ref=sends[dst], dst_ref=recvs[src], send_sem=send_sem.at[dst], recv_sem=recv_sem.at[src],
            device_id=peer(axis, delta), device_id_type=pl.DeviceIdType.MESH,
        )

        @pl.when(present)
        def _():
            incoming.wait_recv()

        @pl.when(jnp.logical_not(present))
        def _():
            recvs[src][...] = jnp.zeros(recvs[src].shape, recvs[src].dtype)
    for j in range(gathered):
        for d in range(1, group):
            slot = j * (group - 1) + d - 1
            origin = lax.rem(me["gz"] + group - d, group)
            incoming = pltpu.make_async_remote_copy(
                src_ref=gins[j], dst_ref=gouts[j].at[origin], send_sem=gsend_sem.at[slot],
                recv_sem=grecv_sem.at[slot], device_id=across(origin), device_id_type=pl.DeviceIdType.MESH,
            )
            incoming.wait_recv()
    for present, copy in copies:
        @pl.when(present)
        def _():
            copy.wait_send()
    for copy in gcopies:
        copy.wait_send()


def exchange(cells, sides, collective, gathers=(), given=None):
    sends = []
    for axis, dim in sides:
        size = cells.shape[dim]
        sends.append(lax.index_in_dim(cells, 0, axis=dim, keepdims=False))
        sends.append(lax.index_in_dim(cells, size - 1, axis=dim, keepdims=False))
    if given is not None:
        sends = list(given)
    axes = tuple(axis for axis, _ in sides)
    sizes = tuple(lax.axis_size(axis) for axis in axes)
    group = lax.axis_size("gz")
    vmem = pl.BlockSpec(memory_space=pltpu.VMEM)
    slots = max(1, len(gathers) * (group - 1))
    outs = pl.pallas_call(
        functools.partial(halo_kernel, axes, sizes, len(gathers), group),
        out_shape=[jax.ShapeDtypeStruct(s.shape, s.dtype) for s in sends]
        + [jax.ShapeDtypeStruct((group,) + g.shape, g.dtype) for g in gathers],
        in_specs=[vmem] * (len(sends) + len(gathers)),
        out_specs=[vmem] * (len(sends) + len(gathers)),
        scratch_shapes=[
            pltpu.SemaphoreType.DMA((max(1, len(sends)),)), pltpu.SemaphoreType.DMA((max(1, len(sends)),)),
            pltpu.SemaphoreType.DMA((slots,)), pltpu.SemaphoreType.DMA((slots,)),
        ],
        compiler_params=pltpu.CompilerParams(collective_id=collective, has_side_effects=True),
    )(*sends, *gathers)
    recvs = outs[:len(sends)]
    faces = {
        dim: (jnp.expand_dims(recvs[2 * i], dim), jnp.expand_dims(recvs[2 * i + 1], dim))
        for i, (axis, dim) in enumerate(sides)
    }
    stacked = [g.reshape((group * g.shape[1],) + g.shape[2:]) for g in outs[len(sends):]]
    return faces, stacked


def faces_kernel(with_z, cells_ref, *out_refs):
    chans, levels, extent, breadth = cells_ref.shape
    xlo, xhi, ylo, yhi = out_refs[:4]
    for c in range(chans):
        for level in range(levels):
            tile = cells_ref[c, level]
            xlo[c, pl.ds(level, 1), :] = tile[0:1, :]
            xhi[c, pl.ds(level, 1), :] = tile[extent - 1:extent, :]
            turned = tile.T
            ylo[c, pl.ds(level, 1), :] = turned[0:1, :]
            yhi[c, pl.ds(level, 1), :] = turned[breadth - 1:breadth, :]
        if with_z:
            out_refs[4][c] = cells_ref[c, 0]
            out_refs[5][c] = cells_ref[c, levels - 1]


def faces_by_kernel(cells, with_z):
    chans, levels, extent, breadth = cells.shape
    shapes = [(chans, levels, breadth)] * 2 + [(chans, levels, extent)] * 2
    if with_z:
        shapes += [(chans, extent, breadth)] * 2
    vmem = pl.BlockSpec(memory_space=pltpu.VMEM)
    return pl.pallas_call(
        functools.partial(faces_kernel, with_z),
        out_shape=[jax.ShapeDtypeStruct(s, cells.dtype) for s in shapes],
        in_specs=[vmem],
        out_specs=[vmem] * len(shapes),
    )(cells)


def face_from(part, axis, from_lower):
    count = lax.axis_size(axis)
    if from_lower:
        pairs = [(i, i + 1) for i in range(count - 1)]
    else:
        pairs = [(i + 1, i) for i in range(count - 1)]
    return lax.ppermute(part, axis, pairs)


def faces_of(cells, sides):
    got = {}
    for axis, dim in sides:
        size = cells.shape[dim]
        got[dim] = (
            face_from(lax.slice_in_dim(cells, size - 1, size, axis=dim), axis, True),
            face_from(lax.slice_in_dim(cells, 0, 1, axis=dim), axis, False),
        )
    return got


def along(cells, faces, dim):
    size = cells.shape[dim]
    lower, upper = faces[dim]
    ahead = jnp.concatenate([lax.slice_in_dim(cells, 1, size, axis=dim), upper], axis=dim)
    behind = jnp.concatenate([lower, lax.slice_in_dim(cells, 0, size - 1, axis=dim)], axis=dim)
    return (ahead - behind) * 0.5


def shards(
    stress_trial,
    mean_stress,
    consolidation,
    point_velocity,
    point_weight,
    point_cell,
    yield_flag,
    point_count,
    porosity,
    permeability,
):
    levels, extent, breadth = porosity.shape
    cell_sums, *stress_faces = cell_sums_of(
        stress_trial, mean_stress, consolidation, point_velocity, point_weight, point_cell,
        yield_flag, point_count, levels, extent, breadth,
    )
    sides = (("gx", 2), ("gy", 3), ("gz", 1))
    stress_sums = cell_sums[:6]
    sf, (all_porosity, all_permeability) = exchange(
        stress_sums, sides, 0, (porosity, permeability), given=stress_faces
    )
    height = all_porosity.shape[0]
    d_x = lambda c: along(stress_sums[c:c + 1], {2: (sf[2][0][c:c + 1], sf[2][1][c:c + 1])}, 2)[0]
    d_y = lambda c: along(stress_sums[c:c + 1], {3: (sf[3][0][c:c + 1], sf[3][1][c:c + 1])}, 3)[0]
    d_z = lambda c: along(stress_sums[c:c + 1], {1: (sf[1][0][c:c + 1], sf[1][1][c:c + 1])}, 1)[0]
    floored = jnp.maximum(cell_sums[9], mass_floor)
    force_x = d_x(0) + d_y(3) + d_z(5)
    force_y = d_x(3) + d_y(1) + d_z(4)
    force_z = d_x(5) + d_y(4) + d_z(2)
    velocity = jnp.stack(
        [
            (cell_sums[6] + time_step * force_x) / floored,
            (cell_sums[7] + time_step * force_y) / floored,
            (cell_sums[8] + time_step * force_z) / floored,
        ]
    )
    vf, _ = exchange(velocity, sides, 1, given=faces_by_kernel(velocity, True))
    dilation = (
        along(velocity[0:1], {2: (vf[2][0][0:1], vf[2][1][0:1])}, 2)[0]
        + along(velocity[1:2], {3: (vf[3][0][1:2], vf[3][1][1:2])}, 3)[0]
        + along(velocity[2:3], {1: (vf[1][0][2:3], vf[1][1][2:3])}, 1)[0]
    )
    right_side = -source_rate * (1.0 - porosity) * dilation
    _, (all_right,) = exchange(right_side, (), 3, (right_side,))
    zero_level = jnp.zeros((1, extent, breadth), jnp.float32)
    level_above = jnp.concatenate([all_permeability[1:], zero_level], axis=0)
    level_below = jnp.concatenate([zero_level, all_permeability[:-1]], axis=0)
    at_top = (jnp.arange(height, dtype=jnp.int32) == height - 1)[:, None, None]
    up_face = harmonic(all_permeability, level_above)
    down_face = harmonic(level_below, all_permeability)
    top_face = jnp.where(at_top, all_permeability, up_face)
    lower_band = -time_step * down_face
    upper_band = -time_step * up_face
    main_band = storage_rate * all_porosity + time_step * (down_face + top_face)
    column = height, extent * breadth
    solved = cyclic_solve(
        lower_band.reshape(column), main_band.reshape(column), upper_band.reshape(column),
        all_right.reshape(column),
    ).reshape(height, extent, breadth)
    first = lax.axis_index("gz") * levels
    around = lax.dynamic_slice_in_dim(
        jnp.concatenate([zero_level, solved, zero_level], axis=0), first, levels + 2, axis=0
    )
    pressure = around[1:-1]
    pressure_faces = [f[0] for f in faces_by_kernel(pressure[None], False)]
    pf, _ = exchange(pressure, (("gx", 1), ("gy", 2)), 2, given=pressure_faces)
    gradient = jnp.stack(
        [
            along(pressure, pf, 1),
            along(pressure, pf, 2),
            (around[2:] - around[:-2]) * 0.5,
        ]
    )
    return (velocity - time_step * gradient, pressure)


def solution(mesh):
    placed = (
        P(None, ("gx", "gy", "gz")),
        P(("gx", "gy", "gz")),
        P(("gx", "gy", "gz")),
        P(None, ("gx", "gy", "gz")),
        P(("gx", "gy", "gz")),
        P(("gx", "gy", "gz")),
        P(("gx", "gy", "gz")),
        P("gx", "gy", "gz"),
        P("gz", "gx", "gy"),
        P("gz", "gx", "gy"),
    )
    return jax.shard_map(
        shards,
        mesh=mesh,
        in_specs=placed,
        out_specs=(P(None, "gz", "gx", "gy"), P("gz", "gx", "gy")),
        check_vma=False,
    )
```

```python
import functools

import jax
import jax.numpy as jnp
from jax import lax
from jax.sharding import PartitionSpec as P

time_step = 0.25
storage_rate = 0.002
source_rate = 0.003
critical_slope = 1.2
mass_floor = 0.5
shear_floor = 1.0

from jax.experimental import pallas as pl
from jax.experimental.pallas import tpu as pltpu

CHUNK = 1024
M_ROWS = 32
N_COLS = 512


SPLITS = 2
X_PARTS = (0, 3, 5)
Y_PARTS = (3, 1, 4)
Z_PARTS = (5, 4, 2)


def _split(v):
    hi = v.astype(jnp.bfloat16)
    lo = (v - hi.astype(jnp.float32)).astype(jnp.bfloat16)
    return [hi, lo]


def sums_kernel(count_ref, st_ref, ms_ref, cons_ref, vel_ref, w_ref, cell_ref, yf_ref, out_ref, xlo_ref, xhi_ref, ylo_ref, yhi_ref, zlo_ref, zhi_ref, acc_ref):
    count = count_ref[0, 0]
    acc_ref[...] = jnp.zeros_like(acc_ref)
    chunks = st_ref.shape[1] // CHUNK

    def body(k, carry):
        start = pl.multiple_of(k * CHUNK, CHUNK)
        span = pl.ds(start, CHUNK)
        st = [st_ref[pl.ds(i, 1), span] for i in range(6)]
        ms = ms_ref[:, span]
        cons = cons_ref[:, span]
        yf = yf_ref[:, span]
        slot = start + lax.broadcasted_iota(jnp.int32, (1, CHUNK), 1)
        weight = jnp.where(slot < count, w_ref[:, span], 0.0)
        sq_normal = st[0] * st[0] + st[1] * st[1] + st[2] * st[2]
        sq_shear = st[3] * st[3] + st[4] * st[4] + st[5] * st[5]
        shear_size = jnp.sqrt(1.5 * (sq_normal + 2.0 * sq_shear))
        yield_size = critical_slope * jnp.sqrt(ms * (cons - ms))
        factor = jnp.where(yf == 1, yield_size / jnp.maximum(shear_size, shear_floor), 1.0)
        stress = [st[i] * factor - ms if i < 3 else st[i] * factor for i in range(6)]
        values = [s * weight for s in stress]
        values += [vel_ref[pl.ds(i, 1), span] * weight for i in range(3)]
        values.append(weight)
        cell = cell_ref[:, span]
        m_key = (cell >> 12) * 8 + ((cell >> 7) & 7)
        n_key = ((cell >> 10) & 3) * 128 + (cell & 127)
        m_mask = lax.broadcasted_iota(jnp.int32, (M_ROWS, CHUNK), 0) == m_key
        zero = jnp.zeros((M_ROWS, CHUNK), jnp.bfloat16)
        pieces = []
        for v in values:
            for part in _split(v):
                pieces.append(jnp.where(m_mask, jnp.broadcast_to(part, (M_ROWS, CHUNK)), zero))
        lhs = jnp.concatenate(pieces, axis=0)
        one_hot = jnp.where(
            lax.broadcasted_iota(jnp.int32, (N_COLS, CHUNK), 0) == n_key, 1.0, 0.0
        ).astype(jnp.bfloat16)
        acc_ref[...] += lax.dot_general(
            lhs, one_hot, (((1,), (1,)), ((), ())), preferred_element_type=jnp.float32
        )
        return carry

    lax.fori_loop(0, chunks, body, 0)
    for comp in range(10):
        for level in range(16):
            rows = pl.ds((comp * SPLITS) * M_ROWS + (level >> 2) * 8, 8)
            lanes = pl.ds((level & 3) * 128, 128)
            total = acc_ref[rows, lanes]
            for s in range(1, SPLITS):
                total = total + acc_ref[pl.ds((comp * SPLITS + s) * M_ROWS + (level >> 2) * 8, 8), lanes]
            out_ref[comp, level] = total
            if comp in X_PARTS:
                slot = X_PARTS.index(comp)
                xlo_ref[slot, pl.ds(level, 1), :] = total[0:1, :]
                xhi_ref[slot, pl.ds(level, 1), :] = total[7:8, :]
            if comp in Y_PARTS:
                slot = Y_PARTS.index(comp)
                turned = total.T
                ylo_ref[slot, pl.ds(level, 1), :] = turned[0:1, :]
                yhi_ref[slot, pl.ds(level, 1), :] = turned[127:128, :]
            if comp in Z_PARTS:
                slot = Z_PARTS.index(comp)
                if level == 0:
                    zlo_ref[slot] = total
                if level == 15:
                    zhi_ref[slot] = total


def cell_sums_of(stress_trial, mean_stress, consolidation, point_velocity, point_weight, point_cell, yield_flag, point_count, levels, extent, breadth):
    n = mean_stress.shape[0]
    row = lambda a: a.reshape(1, n)
    vmem = pl.BlockSpec(memory_space=pltpu.VMEM)
    return pl.pallas_call(
        sums_kernel,
        out_shape=[
            jax.ShapeDtypeStruct(s, jnp.float32)
            for s in [(10, levels, extent, breadth)] + [(3, levels, breadth)] * 2 + [(3, levels, extent)] * 2
            + [(3, extent, breadth)] * 2
        ],
        in_specs=[pl.BlockSpec(memory_space=pltpu.SMEM)] + [vmem] * 7,
        out_specs=[vmem] * 7,
        scratch_shapes=[pltpu.VMEM((10 * SPLITS * M_ROWS, N_COLS), jnp.float32)],
        cost_estimate=pl.CostEstimate(
            flops=2 * 10 * SPLITS * M_ROWS * N_COLS * n, bytes_accessed=13 * 4 * n + 10 * 4 * levels * extent * breadth,
            transcendentals=3 * n,
        ),
    )(
        point_count.reshape(1, 1), stress_trial, row(mean_stress), row(consolidation), point_velocity,
        row(point_weight), row(point_cell), row(yield_flag),
    )


def padded_2(cells, sides, width):
    for axis, dim in sides:
        count = lax.axis_size(axis)
        ends = count - 1
        head = lax.slice_in_dim(cells, 0, width, axis=dim)
        tail = lax.slice_in_dim(cells, cells.shape[dim] - width, cells.shape[dim], axis=dim)
        cells = jnp.concatenate(
            [
                lax.ppermute(tail, axis, [(i, (i + 1) % count) for i in range(ends)]),
                cells,
                lax.ppermute(head, axis, [((i + 1) % count, i) for i in range(ends)]),
            ],
            axis=dim,
        )
    return cells


def along_x(padded):
    return (padded[..., 1:-1, 2:, 1:-1] - padded[..., 1:-1, :-2, 1:-1]) * 0.5


def along_y(padded):
    return (padded[..., 1:-1, 1:-1, 2:] - padded[..., 1:-1, 1:-1, :-2]) * 0.5


def along_z(padded):
    return (padded[..., 2:, 1:-1, 1:-1] - padded[..., :-2, 1:-1, 1:-1]) * 0.5


def harmonic(former, latter):
    return 2.0 * former * latter / (former + latter)


def returned_stress(stress_trial, mean_stress, consolidation, yield_flag):
    sq_normal = (
        stress_trial[0] * stress_trial[0]
        + stress_trial[1] * stress_trial[1]
        + stress_trial[2] * stress_trial[2]
    )
    sq_shear = (
        stress_trial[3] * stress_trial[3]
        + stress_trial[4] * stress_trial[4]
        + stress_trial[5] * stress_trial[5]
    )
    shear_size = jnp.sqrt(1.5 * (sq_normal + 2.0 * sq_shear))
    yield_size = critical_slope * jnp.sqrt(mean_stress * (consolidation - mean_stress))
    factor = jnp.where(yield_flag == 1, yield_size / jnp.maximum(shear_size, shear_floor), 1.0)
    isotropic = jnp.array([1.0, 1.0, 1.0, 0.0, 0.0, 0.0], dtype=jnp.float32)[:, None]
    return stress_trial * factor - isotropic * mean_stress


def point_sums(stress, point_velocity, weight, cell_index, segments):
    stacked = jnp.concatenate([stress * weight, point_velocity * weight, weight[None]], axis=0)
    return jax.vmap(
        lambda component: jax.ops.segment_sum(component, cell_index, num_segments=segments)
    )(stacked)


def brick_velocity(cell_sums, padded):
    floored = jnp.maximum(cell_sums[9], mass_floor)
    force_x = along_x(padded[0]) + along_y(padded[3]) + along_z(padded[5])
    force_y = along_x(padded[3]) + along_y(padded[1]) + along_z(padded[4])
    force_z = along_x(padded[5]) + along_y(padded[4]) + along_z(padded[2])
    return jnp.stack(
        [
            (cell_sums[6] + time_step * force_x) / floored,
            (cell_sums[7] + time_step * force_y) / floored,
            (cell_sums[8] + time_step * force_z) / floored,
        ]
    )


def divergence(padded_velocity):
    return along_x(padded_velocity[0]) + along_y(padded_velocity[1]) + along_z(padded_velocity[2])


def band_terms(porosity, permeability, level_below, level_above, at_top, dilation):
    up_face = harmonic(permeability, level_above)
    down_face = harmonic(level_below, permeability)
    top_face = jnp.where(at_top, permeability, up_face)
    lower_band = -time_step * down_face
    upper_band = -time_step * up_face
    main_band = storage_rate * porosity + time_step * (down_face + top_face)
    right_side = -source_rate * (1.0 - porosity) * dilation
    return (lower_band, main_band, upper_band, right_side)


def earlier(values, stride, filler):
    head = jnp.full((stride,) + values.shape[1:], filler, values.dtype)
    return jnp.concatenate([head, values[:-stride]], axis=0)


def later(values, stride, filler):
    tail = jnp.full((stride,) + values.shape[1:], filler, values.dtype)
    return jnp.concatenate([values[stride:], tail], axis=0)


def cyclic_solve(lower_band, main_band, upper_band, right_side):
    length = main_band.shape[0]
    for bit in range((length - 1).bit_length()):
        stride = 1 << bit
        back_weight = -lower_band / earlier(main_band, stride, 1.0)
        ahead_weight = -upper_band / later(main_band, stride, 1.0)
        new_lower = back_weight * earlier(lower_band, stride, 0.0)
        new_upper = ahead_weight * later(upper_band, stride, 0.0)
        new_main = (
            main_band
            + back_weight * earlier(upper_band, stride, 0.0)
            + ahead_weight * later(lower_band, stride, 0.0)
        )
        new_right = (
            right_side
            + back_weight * earlier(right_side, stride, 0.0)
            + ahead_weight * later(right_side, stride, 0.0)
        )
        lower_band, main_band, upper_band, right_side = (new_lower, new_main, new_upper, new_right)
    return right_side / main_band


MESH_AXES = ("gx", "gy", "gz")


def halo_kernel(sides, sizes, gathered, group, *refs):
    count = len(sides)
    sends = refs[:2 * count]
    gins = refs[2 * count:2 * count + gathered]
    recvs = refs[2 * count + gathered:4 * count + gathered]
    gouts = refs[4 * count + gathered:4 * count + 2 * gathered]
    send_sem, recv_sem, gsend_sem, grecv_sem = refs[4 * count + 2 * gathered:]
    me = {a: lax.axis_index(a) for a in MESH_AXES}

    def peer(axis, delta):
        return tuple(me[a] + delta if a == axis else me[a] for a in MESH_AXES)

    def across(level):
        return tuple(level if a == "gz" else me[a] for a in MESH_AXES)

    links = []
    for i, axis in enumerate(sides):
        links.append((axis, -1, me[axis] > 0, 2 * i, 2 * i + 1))
        links.append((axis, 1, me[axis] < sizes[i] - 1, 2 * i + 1, 2 * i))
    barrier = pltpu.get_barrier_semaphore()
    peers = 0
    for axis, delta, present, _, _ in links:
        if gathered and axis == "gz":
            continue
        peers = peers + present.astype(jnp.int32)

        @pl.when(present)
        def _():
            pl.semaphore_signal(barrier, 1, device_id=peer(axis, delta), device_id_type=pl.DeviceIdType.MESH)
    if gathered:
        for d in range(1, group):
            pl.semaphore_signal(
                barrier, 1, device_id=across(lax.rem(me["gz"] + d, group)), device_id_type=pl.DeviceIdType.MESH
            )
        peers = peers + (group - 1)
    pl.semaphore_wait(barrier, peers)
    copies = []
    for axis, delta, present, src, dst in links:
        copy = pltpu.make_async_remote_copy(
            src_ref=sends[src], dst_ref=recvs[dst], send_sem=send_sem.at[src], recv_sem=recv_sem.at[dst],
            device_id=peer(axis, delta), device_id_type=pl.DeviceIdType.MESH,
        )
        copies.append((present, copy))

        @pl.when(present)
        def _():
            copy.start()
    gcopies = []
    for j in range(gathered):
        for d in range(1, group):
            slot = j * (group - 1) + d - 1
            copy = pltpu.make_async_remote_copy(
                src_ref=gins[j], dst_ref=gouts[j].at[me["gz"]], send_sem=gsend_sem.at[slot],
                recv_sem=grecv_sem.at[slot], device_id=across(lax.rem(me["gz"] + d, group)),
                device_id_type=pl.DeviceIdType.MESH,
            )
            copy.start()
            gcopies.append(copy)
    for j in range(gathered):
        gouts[j][me["gz"]] = gins[j][...]
    for axis, delta, present, src, dst in links:
        incoming = pltpu.make_async_remote_copy(
            src_ref=sends[dst], dst_ref=recvs[src], send_sem=send_sem.at[dst], recv_sem=recv_sem.at[src],
            device_id=peer(axis, delta), device_id_type=pl.DeviceIdType.MESH,
        )

        @pl.when(present)
        def _():
            incoming.wait_recv()

        @pl.when(jnp.logical_not(present))
        def _():
            recvs[src][...] = jnp.zeros(recvs[src].shape, recvs[src].dtype)
    for j in range(gathered):
        for d in range(1, group):
            slot = j * (group - 1) + d - 1
            origin = lax.rem(me["gz"] + group - d, group)
            incoming = pltpu.make_async_remote_copy(
                src_ref=gins[j], dst_ref=gouts[j].at[origin], send_sem=gsend_sem.at[slot],
                recv_sem=grecv_sem.at[slot], device_id=across(origin), device_id_type=pl.DeviceIdType.MESH,
            )
            incoming.wait_recv()
    for present, copy in copies:
        @pl.when(present)
        def _():
            copy.wait_send()
    for copy in gcopies:
        copy.wait_send()


def exchange(cells, sides, collective, gathers=(), given=None):
    sends = []
    for axis, dim in sides:
        size = cells.shape[dim]
        sends.append(lax.index_in_dim(cells, 0, axis=dim, keepdims=False))
        sends.append(lax.index_in_dim(cells, size - 1, axis=dim, keepdims=False))
    if given is not None:
        sends = list(given)
    axes = tuple(axis for axis, _ in sides)
    sizes = tuple(lax.axis_size(axis) for axis in axes)
    group = lax.axis_size("gz")
    vmem = pl.BlockSpec(memory_space=pltpu.VMEM)
    slots = max(1, len(gathers) * (group - 1))
    outs = pl.pallas_call(
        functools.partial(halo_kernel, axes, sizes, len(gathers), group),
        out_shape=[jax.ShapeDtypeStruct(s.shape, s.dtype) for s in sends]
        + [jax.ShapeDtypeStruct((group,) + g.shape, g.dtype) for g in gathers],
        in_specs=[vmem] * (len(sends) + len(gathers)),
        out_specs=[vmem] * (len(sends) + len(gathers)),
        scratch_shapes=[
            pltpu.SemaphoreType.DMA((max(1, len(sends)),)), pltpu.SemaphoreType.DMA((max(1, len(sends)),)),
            pltpu.SemaphoreType.DMA((slots,)), pltpu.SemaphoreType.DMA((slots,)),
        ],
        compiler_params=pltpu.CompilerParams(collective_id=collective, has_side_effects=True),
    )(*sends, *gathers)
    recvs = outs[:len(sends)]
    faces = {
        dim: (jnp.expand_dims(recvs[2 * i], dim), jnp.expand_dims(recvs[2 * i + 1], dim))
        for i, (axis, dim) in enumerate(sides)
    }
    stacked = [g.reshape((group * g.shape[1],) + g.shape[2:]) for g in outs[len(sends):]]
    return faces, stacked


def faces_kernel(parts, cells_ref, *out_refs):
    chans, levels, extent, breadth = cells_ref.shape
    xlo, xhi, ylo, yhi = out_refs[:4]
    for slot, c in enumerate(parts[0]):
        for level in range(levels):
            tile = cells_ref[c, level]
            xlo[slot, pl.ds(level, 1), :] = tile[0:1, :]
            xhi[slot, pl.ds(level, 1), :] = tile[extent - 1:extent, :]
    for slot, c in enumerate(parts[1]):
        for level in range(levels):
            turned = cells_ref[c, level].T
            ylo[slot, pl.ds(level, 1), :] = turned[0:1, :]
            yhi[slot, pl.ds(level, 1), :] = turned[breadth - 1:breadth, :]
    if len(parts) > 2:
        for slot, c in enumerate(parts[2]):
            out_refs[4][slot] = cells_ref[c, 0]
            out_refs[5][slot] = cells_ref[c, levels - 1]


def faces_by_kernel(cells, parts):
    chans, levels, extent, breadth = cells.shape
    shapes = [(len(parts[0]), levels, breadth)] * 2 + [(len(parts[1]), levels, extent)] * 2
    if len(parts) > 2:
        shapes += [(len(parts[2]), extent, breadth)] * 2
    vmem = pl.BlockSpec(memory_space=pltpu.VMEM)
    return pl.pallas_call(
        functools.partial(faces_kernel, parts),
        out_shape=[jax.ShapeDtypeStruct(s, cells.dtype) for s in shapes],
        in_specs=[vmem],
        out_specs=[vmem] * len(shapes),
    )(cells)


def face_from(part, axis, from_lower):
    count = lax.axis_size(axis)
    if from_lower:
        pairs = [(i, i + 1) for i in range(count - 1)]
    else:
        pairs = [(i + 1, i) for i in range(count - 1)]
    return lax.ppermute(part, axis, pairs)


def faces_of(cells, sides):
    got = {}
    for axis, dim in sides:
        size = cells.shape[dim]
        got[dim] = (
            face_from(lax.slice_in_dim(cells, size - 1, size, axis=dim), axis, True),
            face_from(lax.slice_in_dim(cells, 0, 1, axis=dim), axis, False),
        )
    return got


def along(cells, faces, dim):
    size = cells.shape[dim]
    lower, upper = faces[dim]
    ahead = jnp.concatenate([lax.slice_in_dim(cells, 1, size, axis=dim), upper], axis=dim)
    behind = jnp.concatenate([lower, lax.slice_in_dim(cells, 0, size - 1, axis=dim)], axis=dim)
    return (ahead - behind) * 0.5


def shards(
    stress_trial,
    mean_stress,
    consolidation,
    point_velocity,
    point_weight,
    point_cell,
    yield_flag,
    point_count,
    porosity,
    permeability,
):
    levels, extent, breadth = porosity.shape
    cell_sums, *stress_faces = cell_sums_of(
        stress_trial, mean_stress, consolidation, point_velocity, point_weight, point_cell,
        yield_flag, point_count, levels, extent, breadth,
    )
    sides = (("gx", 2), ("gy", 3), ("gz", 1))
    stress_sums = cell_sums[:6]
    sf, (all_porosity, all_permeability) = exchange(
        stress_sums, sides, 0, (porosity, permeability), given=stress_faces
    )
    height = all_porosity.shape[0]
    def part(dim, parts, c):
        s = parts.index(c)
        return {dim: (sf[dim][0][s:s + 1], sf[dim][1][s:s + 1])}

    d_x = lambda c: along(stress_sums[c:c + 1], part(2, X_PARTS, c), 2)[0]
    d_y = lambda c: along(stress_sums[c:c + 1], part(3, Y_PARTS, c), 3)[0]
    d_z = lambda c: along(stress_sums[c:c + 1], part(1, Z_PARTS, c), 1)[0]
    floored = jnp.maximum(cell_sums[9], mass_floor)
    force_x = d_x(0) + d_y(3) + d_z(5)
    force_y = d_x(3) + d_y(1) + d_z(4)
    force_z = d_x(5) + d_y(4) + d_z(2)
    velocity = jnp.stack(
        [
            (cell_sums[6] + time_step * force_x) / floored,
            (cell_sums[7] + time_step * force_y) / floored,
            (cell_sums[8] + time_step * force_z) / floored,
        ]
    )
    vf, _ = exchange(velocity, sides, 1, given=faces_by_kernel(velocity, ((0,), (1,), (2,))))
    dilation = (
        along(velocity[0:1], {2: vf[2]}, 2)[0]
        + along(velocity[1:2], {3: vf[3]}, 3)[0]
        + along(velocity[2:3], {1: vf[1]}, 1)[0]
    )
    right_side = -source_rate * (1.0 - porosity) * dilation
    _, (all_right,) = exchange(right_side, (), 3, (right_side,))
    zero_level = jnp.zeros((1, extent, breadth), jnp.float32)
    level_above = jnp.concatenate([all_permeability[1:], zero_level], axis=0)
    level_below = jnp.concatenate([zero_level, all_permeability[:-1]], axis=0)
    at_top = (jnp.arange(height, dtype=jnp.int32) == height - 1)[:, None, None]
    up_face = harmonic(all_permeability, level_above)
    down_face = harmonic(level_below, all_permeability)
    top_face = jnp.where(at_top, all_permeability, up_face)
    lower_band = -time_step * down_face
    upper_band = -time_step * up_face
    main_band = storage_rate * all_porosity + time_step * (down_face + top_face)
    column = height, extent * breadth
    solved = cyclic_solve(
        lower_band.reshape(column), main_band.reshape(column), upper_band.reshape(column),
        all_right.reshape(column),
    ).reshape(height, extent, breadth)
    first = lax.axis_index("gz") * levels
    around = lax.dynamic_slice_in_dim(
        jnp.concatenate([zero_level, solved, zero_level], axis=0), first, levels + 2, axis=0
    )
    pressure = around[1:-1]
    pressure_faces = [f[0] for f in faces_by_kernel(pressure[None], ((0,), (0,)))]
    pf, _ = exchange(pressure, (("gx", 1), ("gy", 2)), 2, given=pressure_faces)
    gradient = jnp.stack(
        [
            along(pressure, pf, 1),
            along(pressure, pf, 2),
            (around[2:] - around[:-2]) * 0.5,
        ]
    )
    return (velocity - time_step * gradient, pressure)


def solution(mesh):
    placed = (
        P(None, ("gx", "gy", "gz")),
        P(("gx", "gy", "gz")),
        P(("gx", "gy", "gz")),
        P(None, ("gx", "gy", "gz")),
        P(("gx", "gy", "gz")),
        P(("gx", "gy", "gz")),
        P(("gx", "gy", "gz")),
        P("gx", "gy", "gz"),
        P("gz", "gx", "gy"),
        P("gz", "gx", "gy"),
    )
    return jax.shard_map(
        shards,
        mesh=mesh,
        in_specs=placed,
        out_specs=(P(None, "gz", "gx", "gy"), P("gz", "gx", "gy")),
        check_vma=False,
    )
```

```python
import functools

import jax
import jax.numpy as jnp
from jax import lax
from jax.sharding import PartitionSpec as P

time_step = 0.25
storage_rate = 0.002
source_rate = 0.003
critical_slope = 1.2
mass_floor = 0.5
shear_floor = 1.0

from jax.experimental import pallas as pl
from jax.experimental.pallas import tpu as pltpu

CHUNK = 1024
M_ROWS = 32
N_COLS = 512


SPLITS = 2
X_PARTS = (0, 3, 5)
Y_PARTS = (3, 1, 4)
Z_PARTS = (5, 4, 2)


def _split(v):
    hi = v.astype(jnp.bfloat16)
    lo = (v - hi.astype(jnp.float32)).astype(jnp.bfloat16)
    return [hi, lo]


def sums_kernel(count_ref, st_ref, ms_ref, cons_ref, vel_ref, w_ref, cell_ref, yf_ref, out_ref, xlo_ref, xhi_ref, ylo_ref, yhi_ref, zlo_ref, zhi_ref, acc_ref):
    count = count_ref[0, 0]
    acc_ref[...] = jnp.zeros_like(acc_ref)
    chunks = st_ref.shape[1] // CHUNK

    def body(k, carry):
        start = pl.multiple_of(k * CHUNK, CHUNK)
        span = pl.ds(start, CHUNK)
        st = [st_ref[pl.ds(i, 1), span] for i in range(6)]
        ms = ms_ref[:, span]
        cons = cons_ref[:, span]
        yf = yf_ref[:, span]
        slot = start + lax.broadcasted_iota(jnp.int32, (1, CHUNK), 1)
        weight = jnp.where(slot < count, w_ref[:, span], 0.0)
        sq_normal = st[0] * st[0] + st[1] * st[1] + st[2] * st[2]
        sq_shear = st[3] * st[3] + st[4] * st[4] + st[5] * st[5]
        shear_size = jnp.sqrt(1.5 * (sq_normal + 2.0 * sq_shear))
        yield_size = critical_slope * jnp.sqrt(ms * (cons - ms))
        factor = jnp.where(yf == 1, yield_size / jnp.maximum(shear_size, shear_floor), 1.0)
        stress = [st[i] * factor - ms if i < 3 else st[i] * factor for i in range(6)]
        values = [s * weight for s in stress]
        values += [vel_ref[pl.ds(i, 1), span] * weight for i in range(3)]
        values.append(weight)
        cell = cell_ref[:, span]
        m_key = (cell >> 12) * 8 + ((cell >> 7) & 7)
        n_key = ((cell >> 10) & 3) * 128 + (cell & 127)
        m_mask = lax.broadcasted_iota(jnp.int32, (M_ROWS, CHUNK), 0) == m_key
        zero = jnp.zeros((M_ROWS, CHUNK), jnp.bfloat16)
        pieces = []
        for v in values:
            for part in _split(v):
                pieces.append(jnp.where(m_mask, jnp.broadcast_to(part, (M_ROWS, CHUNK)), zero))
        lhs = jnp.concatenate(pieces, axis=0)
        one_hot = jnp.where(
            lax.broadcasted_iota(jnp.int32, (N_COLS, CHUNK), 0) == n_key, 1.0, 0.0
        ).astype(jnp.bfloat16)
        acc_ref[...] += lax.dot_general(
            lhs, one_hot, (((1,), (1,)), ((), ())), preferred_element_type=jnp.float32
        )
        return carry

    lax.fori_loop(0, chunks, body, 0)
    for comp in range(10):
        for level in range(16):
            rows = pl.ds((comp * SPLITS) * M_ROWS + (level >> 2) * 8, 8)
            lanes = pl.ds((level & 3) * 128, 128)
            total = acc_ref[rows, lanes]
            for s in range(1, SPLITS):
                total = total + acc_ref[pl.ds((comp * SPLITS + s) * M_ROWS + (level >> 2) * 8, 8), lanes]
            out_ref[comp, level] = total
            if comp in X_PARTS:
                slot = X_PARTS.index(comp)
                xlo_ref[slot, pl.ds(level, 1), :] = total[0:1, :]
                xhi_ref[slot, pl.ds(level, 1), :] = total[7:8, :]
            if comp in Y_PARTS:
                slot = Y_PARTS.index(comp)
                turned = total.T
                ylo_ref[slot, pl.ds(level, 1), :] = turned[0:1, :]
                yhi_ref[slot, pl.ds(level, 1), :] = turned[127:128, :]
            if comp in Z_PARTS:
                slot = Z_PARTS.index(comp)
                if level == 0:
                    zlo_ref[slot] = total
                if level == 15:
                    zhi_ref[slot] = total


def cell_sums_of(stress_trial, mean_stress, consolidation, point_velocity, point_weight, point_cell, yield_flag, point_count, levels, extent, breadth):
    n = mean_stress.shape[0]
    row = lambda a: a.reshape(1, n)
    vmem = pl.BlockSpec(memory_space=pltpu.VMEM)
    return pl.pallas_call(
        sums_kernel,
        out_shape=[
            jax.ShapeDtypeStruct(s, jnp.float32)
            for s in [(10, levels, extent, breadth)] + [(3, levels, breadth)] * 2 + [(3, levels, extent)] * 2
            + [(3, extent, breadth)] * 2
        ],
        in_specs=[pl.BlockSpec(memory_space=pltpu.SMEM)] + [vmem] * 7,
        out_specs=[vmem] * 7,
        scratch_shapes=[pltpu.VMEM((10 * SPLITS * M_ROWS, N_COLS), jnp.float32)],
        cost_estimate=pl.CostEstimate(
            flops=2 * 10 * SPLITS * M_ROWS * N_COLS * n, bytes_accessed=13 * 4 * n + 10 * 4 * levels * extent * breadth,
            transcendentals=3 * n,
        ),
    )(
        point_count.reshape(1, 1), stress_trial, row(mean_stress), row(consolidation), point_velocity,
        row(point_weight), row(point_cell), row(yield_flag),
    )


def padded_2(cells, sides, width):
    for axis, dim in sides:
        count = lax.axis_size(axis)
        ends = count - 1
        head = lax.slice_in_dim(cells, 0, width, axis=dim)
        tail = lax.slice_in_dim(cells, cells.shape[dim] - width, cells.shape[dim], axis=dim)
        cells = jnp.concatenate(
            [
                lax.ppermute(tail, axis, [(i, (i + 1) % count) for i in range(ends)]),
                cells,
                lax.ppermute(head, axis, [((i + 1) % count, i) for i in range(ends)]),
            ],
            axis=dim,
        )
    return cells


def along_x(padded):
    return (padded[..., 1:-1, 2:, 1:-1] - padded[..., 1:-1, :-2, 1:-1]) * 0.5


def along_y(padded):
    return (padded[..., 1:-1, 1:-1, 2:] - padded[..., 1:-1, 1:-1, :-2]) * 0.5


def along_z(padded):
    return (padded[..., 2:, 1:-1, 1:-1] - padded[..., :-2, 1:-1, 1:-1]) * 0.5


def harmonic(former, latter):
    return 2.0 * former * latter / (former + latter)


def returned_stress(stress_trial, mean_stress, consolidation, yield_flag):
    sq_normal = (
        stress_trial[0] * stress_trial[0]
        + stress_trial[1] * stress_trial[1]
        + stress_trial[2] * stress_trial[2]
    )
    sq_shear = (
        stress_trial[3] * stress_trial[3]
        + stress_trial[4] * stress_trial[4]
        + stress_trial[5] * stress_trial[5]
    )
    shear_size = jnp.sqrt(1.5 * (sq_normal + 2.0 * sq_shear))
    yield_size = critical_slope * jnp.sqrt(mean_stress * (consolidation - mean_stress))
    factor = jnp.where(yield_flag == 1, yield_size / jnp.maximum(shear_size, shear_floor), 1.0)
    isotropic = jnp.array([1.0, 1.0, 1.0, 0.0, 0.0, 0.0], dtype=jnp.float32)[:, None]
    return stress_trial * factor - isotropic * mean_stress


def point_sums(stress, point_velocity, weight, cell_index, segments):
    stacked = jnp.concatenate([stress * weight, point_velocity * weight, weight[None]], axis=0)
    return jax.vmap(
        lambda component: jax.ops.segment_sum(component, cell_index, num_segments=segments)
    )(stacked)


def brick_velocity(cell_sums, padded):
    floored = jnp.maximum(cell_sums[9], mass_floor)
    force_x = along_x(padded[0]) + along_y(padded[3]) + along_z(padded[5])
    force_y = along_x(padded[3]) + along_y(padded[1]) + along_z(padded[4])
    force_z = along_x(padded[5]) + along_y(padded[4]) + along_z(padded[2])
    return jnp.stack(
        [
            (cell_sums[6] + time_step * force_x) / floored,
            (cell_sums[7] + time_step * force_y) / floored,
            (cell_sums[8] + time_step * force_z) / floored,
        ]
    )


def divergence(padded_velocity):
    return along_x(padded_velocity[0]) + along_y(padded_velocity[1]) + along_z(padded_velocity[2])


def band_terms(porosity, permeability, level_below, level_above, at_top, dilation):
    up_face = harmonic(permeability, level_above)
    down_face = harmonic(level_below, permeability)
    top_face = jnp.where(at_top, permeability, up_face)
    lower_band = -time_step * down_face
    upper_band = -time_step * up_face
    main_band = storage_rate * porosity + time_step * (down_face + top_face)
    right_side = -source_rate * (1.0 - porosity) * dilation
    return (lower_band, main_band, upper_band, right_side)


def earlier(values, stride, filler):
    head = jnp.full((stride,) + values.shape[1:], filler, values.dtype)
    return jnp.concatenate([head, values[:-stride]], axis=0)


def later(values, stride, filler):
    tail = jnp.full((stride,) + values.shape[1:], filler, values.dtype)
    return jnp.concatenate([values[stride:], tail], axis=0)


def cyclic_solve(lower_band, main_band, upper_band, right_side):
    length = main_band.shape[0]
    for bit in range((length - 1).bit_length()):
        stride = 1 << bit
        back_weight = -lower_band / earlier(main_band, stride, 1.0)
        ahead_weight = -upper_band / later(main_band, stride, 1.0)
        new_lower = back_weight * earlier(lower_band, stride, 0.0)
        new_upper = ahead_weight * later(upper_band, stride, 0.0)
        new_main = (
            main_band
            + back_weight * earlier(upper_band, stride, 0.0)
            + ahead_weight * later(lower_band, stride, 0.0)
        )
        new_right = (
            right_side
            + back_weight * earlier(right_side, stride, 0.0)
            + ahead_weight * later(right_side, stride, 0.0)
        )
        lower_band, main_band, upper_band, right_side = (new_lower, new_main, new_upper, new_right)
    return right_side / main_band


MESH_AXES = ("gx", "gy", "gz")


def halo_kernel(sides, sizes, gathered, group, *refs):
    count = len(sides)
    sends = refs[:2 * count]
    gins = refs[2 * count:2 * count + gathered]
    recvs = refs[2 * count + gathered:4 * count + gathered]
    gouts = refs[4 * count + gathered:4 * count + 2 * gathered]
    send_sem, recv_sem, gsend_sem, grecv_sem = refs[4 * count + 2 * gathered:]
    me = {a: lax.axis_index(a) for a in MESH_AXES}

    def peer(axis, delta):
        return tuple(me[a] + delta if a == axis else me[a] for a in MESH_AXES)

    def across(level):
        return tuple(level if a == "gz" else me[a] for a in MESH_AXES)

    links = []
    for i, axis in enumerate(sides):
        links.append((axis, -1, me[axis] > 0, 2 * i, 2 * i + 1))
        links.append((axis, 1, me[axis] < sizes[i] - 1, 2 * i + 1, 2 * i))
    barrier = pltpu.get_barrier_semaphore()
    peers = 0
    for axis, delta, present, _, _ in links:
        if gathered and axis == "gz":
            continue
        peers = peers + present.astype(jnp.int32)

        @pl.when(present)
        def _():
            pl.semaphore_signal(barrier, 1, device_id=peer(axis, delta), device_id_type=pl.DeviceIdType.MESH)
    if gathered:
        for d in range(1, group):
            pl.semaphore_signal(
                barrier, 1, device_id=across(lax.rem(me["gz"] + d, group)), device_id_type=pl.DeviceIdType.MESH
            )
        peers = peers + (group - 1)
    pl.semaphore_wait(barrier, peers)
    copies = []
    for axis, delta, present, src, dst in links:
        copy = pltpu.make_async_remote_copy(
            src_ref=sends[src], dst_ref=recvs[dst], send_sem=send_sem.at[src], recv_sem=recv_sem.at[dst],
            device_id=peer(axis, delta), device_id_type=pl.DeviceIdType.MESH,
        )
        copies.append((present, copy))

        @pl.when(present)
        def _():
            copy.start()
    gcopies = []
    for j in range(gathered):
        for d in range(1, group):
            slot = j * (group - 1) + d - 1
            copy = pltpu.make_async_remote_copy(
                src_ref=gins[j], dst_ref=gouts[j].at[me["gz"]], send_sem=gsend_sem.at[slot],
                recv_sem=grecv_sem.at[slot], device_id=across(lax.rem(me["gz"] + d, group)),
                device_id_type=pl.DeviceIdType.MESH,
            )
            copy.start()
            gcopies.append(copy)
    for j in range(gathered):
        gouts[j][me["gz"]] = gins[j][...]
    for axis, delta, present, src, dst in links:
        incoming = pltpu.make_async_remote_copy(
            src_ref=sends[dst], dst_ref=recvs[src], send_sem=send_sem.at[dst], recv_sem=recv_sem.at[src],
            device_id=peer(axis, delta), device_id_type=pl.DeviceIdType.MESH,
        )

        @pl.when(present)
        def _():
            incoming.wait_recv()

        @pl.when(jnp.logical_not(present))
        def _():
            recvs[src][...] = jnp.zeros(recvs[src].shape, recvs[src].dtype)
    for j in range(gathered):
        for d in range(1, group):
            slot = j * (group - 1) + d - 1
            origin = lax.rem(me["gz"] + group - d, group)
            incoming = pltpu.make_async_remote_copy(
                src_ref=gins[j], dst_ref=gouts[j].at[origin], send_sem=gsend_sem.at[slot],
                recv_sem=grecv_sem.at[slot], device_id=across(origin), device_id_type=pl.DeviceIdType.MESH,
            )
            incoming.wait_recv()
    for present, copy in copies:
        @pl.when(present)
        def _():
            copy.wait_send()
    for copy in gcopies:
        copy.wait_send()


def exchange(cells, sides, collective, gathers=(), given=None):
    sends = []
    for axis, dim in sides:
        size = cells.shape[dim]
        sends.append(lax.index_in_dim(cells, 0, axis=dim, keepdims=False))
        sends.append(lax.index_in_dim(cells, size - 1, axis=dim, keepdims=False))
    if given is not None:
        sends = list(given)
    axes = tuple(axis for axis, _ in sides)
    sizes = tuple(lax.axis_size(axis) for axis in axes)
    group = lax.axis_size("gz")
    vmem = pl.BlockSpec(memory_space=pltpu.VMEM)
    slots = max(1, len(gathers) * (group - 1))
    outs = pl.pallas_call(
        functools.partial(halo_kernel, axes, sizes, len(gathers), group),
        out_shape=[jax.ShapeDtypeStruct(s.shape, s.dtype) for s in sends]
        + [jax.ShapeDtypeStruct((group,) + g.shape, g.dtype) for g in gathers],
        in_specs=[vmem] * (len(sends) + len(gathers)),
        out_specs=[vmem] * (len(sends) + len(gathers)),
        scratch_shapes=[
            pltpu.SemaphoreType.DMA((max(1, len(sends)),)), pltpu.SemaphoreType.DMA((max(1, len(sends)),)),
            pltpu.SemaphoreType.DMA((slots,)), pltpu.SemaphoreType.DMA((slots,)),
        ],
        compiler_params=pltpu.CompilerParams(collective_id=collective, has_side_effects=True),
    )(*sends, *gathers)
    recvs = outs[:len(sends)]
    faces = {
        dim: (jnp.expand_dims(recvs[2 * i], dim), jnp.expand_dims(recvs[2 * i + 1], dim))
        for i, (axis, dim) in enumerate(sides)
    }
    stacked = [g.reshape((group * g.shape[1],) + g.shape[2:]) for g in outs[len(sends):]]
    return faces, stacked


def faces_kernel(parts, cells_ref, *out_refs):
    chans, levels, extent, breadth = cells_ref.shape
    xlo, xhi, ylo, yhi = out_refs[:4]
    for slot, c in enumerate(parts[0]):
        for level in range(levels):
            tile = cells_ref[c, level]
            xlo[slot, pl.ds(level, 1), :] = tile[0:1, :]
            xhi[slot, pl.ds(level, 1), :] = tile[extent - 1:extent, :]
    for slot, c in enumerate(parts[1]):
        for level in range(levels):
            turned = cells_ref[c, level].T
            ylo[slot, pl.ds(level, 1), :] = turned[0:1, :]
            yhi[slot, pl.ds(level, 1), :] = turned[breadth - 1:breadth, :]
    if len(parts) > 2:
        for slot, c in enumerate(parts[2]):
            out_refs[4][slot] = cells_ref[c, 0]
            out_refs[5][slot] = cells_ref[c, levels - 1]


def faces_by_kernel(cells, parts):
    chans, levels, extent, breadth = cells.shape
    shapes = [(len(parts[0]), levels, breadth)] * 2 + [(len(parts[1]), levels, extent)] * 2
    if len(parts) > 2:
        shapes += [(len(parts[2]), extent, breadth)] * 2
    vmem = pl.BlockSpec(memory_space=pltpu.VMEM)
    return pl.pallas_call(
        functools.partial(faces_kernel, parts),
        out_shape=[jax.ShapeDtypeStruct(s, cells.dtype) for s in shapes],
        in_specs=[vmem],
        out_specs=[vmem] * len(shapes),
    )(cells)


def solve_kernel(poro_ref, perm_ref, right_ref, out_ref):
    perm = perm_ref[...]
    lid = jnp.zeros((1,) + perm.shape[1:], jnp.float32)
    level_above = jnp.concatenate([perm[1:], lid], axis=0)
    level_below = jnp.concatenate([lid, perm[:-1]], axis=0)
    up_face = harmonic(perm, level_above)
    down_face = harmonic(level_below, perm)
    top_face = jnp.concatenate([up_face[:-1], perm[-1:]], axis=0)
    lower_band = -time_step * down_face
    upper_band = -time_step * up_face
    main_band = storage_rate * poro_ref[...] + time_step * (down_face + top_face)
    out_ref[...] = cyclic_solve(lower_band, main_band, upper_band, right_ref[...])


def column_solve(porosity, permeability, right_side):
    vmem = pl.BlockSpec(memory_space=pltpu.VMEM)
    return pl.pallas_call(
        solve_kernel,
        out_shape=jax.ShapeDtypeStruct(right_side.shape, jnp.float32),
        in_specs=[vmem] * 3,
        out_specs=vmem,
    )(porosity, permeability, right_side)


def face_from(part, axis, from_lower):
    count = lax.axis_size(axis)
    if from_lower:
        pairs = [(i, i + 1) for i in range(count - 1)]
    else:
        pairs = [(i + 1, i) for i in range(count - 1)]
    return lax.ppermute(part, axis, pairs)


def faces_of(cells, sides):
    got = {}
    for axis, dim in sides:
        size = cells.shape[dim]
        got[dim] = (
            face_from(lax.slice_in_dim(cells, size - 1, size, axis=dim), axis, True),
            face_from(lax.slice_in_dim(cells, 0, 1, axis=dim), axis, False),
        )
    return got


def along(cells, faces, dim):
    size = cells.shape[dim]
    lower, upper = faces[dim]
    ahead = jnp.concatenate([lax.slice_in_dim(cells, 1, size, axis=dim), upper], axis=dim)
    behind = jnp.concatenate([lower, lax.slice_in_dim(cells, 0, size - 1, axis=dim)], axis=dim)
    return (ahead - behind) * 0.5


def shards(
    stress_trial,
    mean_stress,
    consolidation,
    point_velocity,
    point_weight,
    point_cell,
    yield_flag,
    point_count,
    porosity,
    permeability,
):
    levels, extent, breadth = porosity.shape
    cell_sums, *stress_faces = cell_sums_of(
        stress_trial, mean_stress, consolidation, point_velocity, point_weight, point_cell,
        yield_flag, point_count, levels, extent, breadth,
    )
    sides = (("gx", 2), ("gy", 3), ("gz", 1))
    stress_sums = cell_sums[:6]
    sf, (all_porosity, all_permeability) = exchange(
        stress_sums, sides, 0, (porosity, permeability), given=stress_faces
    )
    height = all_porosity.shape[0]
    def part(dim, parts, c):
        s = parts.index(c)
        return {dim: (sf[dim][0][s:s + 1], sf[dim][1][s:s + 1])}

    d_x = lambda c: along(stress_sums[c:c + 1], part(2, X_PARTS, c), 2)[0]
    d_y = lambda c: along(stress_sums[c:c + 1], part(3, Y_PARTS, c), 3)[0]
    d_z = lambda c: along(stress_sums[c:c + 1], part(1, Z_PARTS, c), 1)[0]
    floored = jnp.maximum(cell_sums[9], mass_floor)
    force_x = d_x(0) + d_y(3) + d_z(5)
    force_y = d_x(3) + d_y(1) + d_z(4)
    force_z = d_x(5) + d_y(4) + d_z(2)
    velocity = jnp.stack(
        [
            (cell_sums[6] + time_step * force_x) / floored,
            (cell_sums[7] + time_step * force_y) / floored,
            (cell_sums[8] + time_step * force_z) / floored,
        ]
    )
    vf, _ = exchange(velocity, sides, 1, given=faces_by_kernel(velocity, ((0,), (1,), (2,))))
    dilation = (
        along(velocity[0:1], {2: vf[2]}, 2)[0]
        + along(velocity[1:2], {3: vf[3]}, 3)[0]
        + along(velocity[2:3], {1: vf[1]}, 1)[0]
    )
    right_side = -source_rate * (1.0 - porosity) * dilation
    _, (all_right,) = exchange(right_side, (), 3, (right_side,))
    zero_level = jnp.zeros((1, extent, breadth), jnp.float32)
    solved = column_solve(all_porosity, all_permeability, all_right)
    first = lax.axis_index("gz") * levels
    around = lax.dynamic_slice_in_dim(
        jnp.concatenate([zero_level, solved, zero_level], axis=0), first, levels + 2, axis=0
    )
    pressure = around[1:-1]
    pressure_faces = [f[0] for f in faces_by_kernel(pressure[None], ((0,), (0,)))]
    pf, _ = exchange(pressure, (("gx", 1), ("gy", 2)), 2, given=pressure_faces)
    gradient = jnp.stack(
        [
            along(pressure, pf, 1),
            along(pressure, pf, 2),
            (around[2:] - around[:-2]) * 0.5,
        ]
    )
    return (velocity - time_step * gradient, pressure)


def solution(mesh):
    placed = (
        P(None, ("gx", "gy", "gz")),
        P(("gx", "gy", "gz")),
        P(("gx", "gy", "gz")),
        P(None, ("gx", "gy", "gz")),
        P(("gx", "gy", "gz")),
        P(("gx", "gy", "gz")),
        P(("gx", "gy", "gz")),
        P("gx", "gy", "gz"),
        P("gz", "gx", "gy"),
        P("gz", "gx", "gy"),
    )
    return jax.shard_map(
        shards,
        mesh=mesh,
        in_specs=placed,
        out_specs=(P(None, "gz", "gx", "gy"), P("gz", "gx", "gy")),
        check_vma=False,
    )
```

```python
import functools

import jax
import jax.numpy as jnp
from jax import lax
from jax.sharding import PartitionSpec as P

time_step = 0.25
storage_rate = 0.002
source_rate = 0.003
critical_slope = 1.2
mass_floor = 0.5
shear_floor = 1.0

from jax.experimental import pallas as pl
from jax.experimental.pallas import tpu as pltpu

CHUNK = 1024
M_ROWS = 32
N_COLS = 512


SPLITS = 2
X_PARTS = (0, 3, 5)
Y_PARTS = (3, 1, 4)
Z_PARTS = (5, 4, 2)


def _split(v):
    hi = v.astype(jnp.bfloat16)
    lo = (v - hi.astype(jnp.float32)).astype(jnp.bfloat16)
    return [hi, lo]


def sums_kernel(count_ref, st_ref, ms_ref, cons_ref, vel_ref, w_ref, cell_ref, yf_ref, out_ref, xlo_ref, xhi_ref, ylo_ref, yhi_ref, zlo_ref, zhi_ref, acc_ref):
    count = count_ref[0, 0]
    acc_ref[...] = jnp.zeros_like(acc_ref)
    chunks = st_ref.shape[1] // CHUNK

    def body(k, carry):
        start = pl.multiple_of(k * CHUNK, CHUNK)
        span = pl.ds(start, CHUNK)
        st = [st_ref[pl.ds(i, 1), span] for i in range(6)]
        ms = ms_ref[:, span]
        cons = cons_ref[:, span]
        yf = yf_ref[:, span]
        slot = start + lax.broadcasted_iota(jnp.int32, (1, CHUNK), 1)
        weight = jnp.where(slot < count, w_ref[:, span], 0.0)
        sq_normal = st[0] * st[0] + st[1] * st[1] + st[2] * st[2]
        sq_shear = st[3] * st[3] + st[4] * st[4] + st[5] * st[5]
        shear_size = jnp.sqrt(1.5 * (sq_normal + 2.0 * sq_shear))
        yield_size = critical_slope * jnp.sqrt(ms * (cons - ms))
        factor = jnp.where(yf == 1, yield_size / jnp.maximum(shear_size, shear_floor), 1.0)
        stress = [st[i] * factor - ms if i < 3 else st[i] * factor for i in range(6)]
        values = [s * weight for s in stress]
        values += [vel_ref[pl.ds(i, 1), span] * weight for i in range(3)]
        values.append(weight)
        cell = cell_ref[:, span]
        m_key = (cell >> 12) * 8 + ((cell >> 7) & 7)
        n_key = ((cell >> 10) & 3) * 128 + (cell & 127)
        m_mask = lax.broadcasted_iota(jnp.int32, (M_ROWS, CHUNK), 0) == m_key
        zero = jnp.zeros((M_ROWS, CHUNK), jnp.bfloat16)
        pieces = []
        for v in values:
            for part in _split(v):
                pieces.append(jnp.where(m_mask, jnp.broadcast_to(part, (M_ROWS, CHUNK)), zero))
        lhs = jnp.concatenate(pieces, axis=0)
        one_hot = jnp.where(
            lax.broadcasted_iota(jnp.int32, (N_COLS, CHUNK), 0) == n_key, 1.0, 0.0
        ).astype(jnp.bfloat16)
        acc_ref[...] += lax.dot_general(
            lhs, one_hot, (((1,), (1,)), ((), ())), preferred_element_type=jnp.float32
        )
        return carry

    lax.fori_loop(0, chunks, body, 0)
    for comp in range(10):
        for level in range(16):
            rows = pl.ds((comp * SPLITS) * M_ROWS + (level >> 2) * 8, 8)
            lanes = pl.ds((level & 3) * 128, 128)
            total = acc_ref[rows, lanes]
            for s in range(1, SPLITS):
                total = total + acc_ref[pl.ds((comp * SPLITS + s) * M_ROWS + (level >> 2) * 8, 8), lanes]
            out_ref[comp, level] = total
            if comp in X_PARTS:
                slot = X_PARTS.index(comp)
                xlo_ref[slot, pl.ds(level, 1), :] = total[0:1, :]
                xhi_ref[slot, pl.ds(level, 1), :] = total[7:8, :]
            if comp in Y_PARTS:
                slot = Y_PARTS.index(comp)
                turned = total.T
                ylo_ref[slot, pl.ds(level, 1), :] = turned[0:1, :]
                yhi_ref[slot, pl.ds(level, 1), :] = turned[127:128, :]
            if comp in Z_PARTS:
                slot = Z_PARTS.index(comp)
                if level == 0:
                    zlo_ref[slot] = total
                if level == 15:
                    zhi_ref[slot] = total


def cell_sums_of(stress_trial, mean_stress, consolidation, point_velocity, point_weight, point_cell, yield_flag, point_count, levels, extent, breadth):
    n = mean_stress.shape[0]
    row = lambda a: a.reshape(1, n)
    vmem = pl.BlockSpec(memory_space=pltpu.VMEM)
    return pl.pallas_call(
        sums_kernel,
        out_shape=[
            jax.ShapeDtypeStruct(s, jnp.float32)
            for s in [(10, levels, extent, breadth)] + [(3, levels, breadth)] * 2 + [(3, levels, extent)] * 2
            + [(3, extent, breadth)] * 2
        ],
        in_specs=[pl.BlockSpec(memory_space=pltpu.SMEM)] + [vmem] * 7,
        out_specs=[vmem] * 7,
        scratch_shapes=[pltpu.VMEM((10 * SPLITS * M_ROWS, N_COLS), jnp.float32)],
        cost_estimate=pl.CostEstimate(
            flops=2 * 10 * SPLITS * M_ROWS * N_COLS * n, bytes_accessed=13 * 4 * n + 10 * 4 * levels * extent * breadth,
            transcendentals=3 * n,
        ),
    )(
        point_count.reshape(1, 1), stress_trial, row(mean_stress), row(consolidation), point_velocity,
        row(point_weight), row(point_cell), row(yield_flag),
    )


def padded_2(cells, sides, width):
    for axis, dim in sides:
        count = lax.axis_size(axis)
        ends = count - 1
        head = lax.slice_in_dim(cells, 0, width, axis=dim)
        tail = lax.slice_in_dim(cells, cells.shape[dim] - width, cells.shape[dim], axis=dim)
        cells = jnp.concatenate(
            [
                lax.ppermute(tail, axis, [(i, (i + 1) % count) for i in range(ends)]),
                cells,
                lax.ppermute(head, axis, [((i + 1) % count, i) for i in range(ends)]),
            ],
            axis=dim,
        )
    return cells


def along_x(padded):
    return (padded[..., 1:-1, 2:, 1:-1] - padded[..., 1:-1, :-2, 1:-1]) * 0.5


def along_y(padded):
    return (padded[..., 1:-1, 1:-1, 2:] - padded[..., 1:-1, 1:-1, :-2]) * 0.5


def along_z(padded):
    return (padded[..., 2:, 1:-1, 1:-1] - padded[..., :-2, 1:-1, 1:-1]) * 0.5


def harmonic(former, latter):
    return 2.0 * former * latter / (former + latter)


def returned_stress(stress_trial, mean_stress, consolidation, yield_flag):
    sq_normal = (
        stress_trial[0] * stress_trial[0]
        + stress_trial[1] * stress_trial[1]
        + stress_trial[2] * stress_trial[2]
    )
    sq_shear = (
        stress_trial[3] * stress_trial[3]
        + stress_trial[4] * stress_trial[4]
        + stress_trial[5] * stress_trial[5]
    )
    shear_size = jnp.sqrt(1.5 * (sq_normal + 2.0 * sq_shear))
    yield_size = critical_slope * jnp.sqrt(mean_stress * (consolidation - mean_stress))
    factor = jnp.where(yield_flag == 1, yield_size / jnp.maximum(shear_size, shear_floor), 1.0)
    isotropic = jnp.array([1.0, 1.0, 1.0, 0.0, 0.0, 0.0], dtype=jnp.float32)[:, None]
    return stress_trial * factor - isotropic * mean_stress


def point_sums(stress, point_velocity, weight, cell_index, segments):
    stacked = jnp.concatenate([stress * weight, point_velocity * weight, weight[None]], axis=0)
    return jax.vmap(
        lambda component: jax.ops.segment_sum(component, cell_index, num_segments=segments)
    )(stacked)


def brick_velocity(cell_sums, padded):
    floored = jnp.maximum(cell_sums[9], mass_floor)
    force_x = along_x(padded[0]) + along_y(padded[3]) + along_z(padded[5])
    force_y = along_x(padded[3]) + along_y(padded[1]) + along_z(padded[4])
    force_z = along_x(padded[5]) + along_y(padded[4]) + along_z(padded[2])
    return jnp.stack(
        [
            (cell_sums[6] + time_step * force_x) / floored,
            (cell_sums[7] + time_step * force_y) / floored,
            (cell_sums[8] + time_step * force_z) / floored,
        ]
    )


def divergence(padded_velocity):
    return along_x(padded_velocity[0]) + along_y(padded_velocity[1]) + along_z(padded_velocity[2])


def band_terms(porosity, permeability, level_below, level_above, at_top, dilation):
    up_face = harmonic(permeability, level_above)
    down_face = harmonic(level_below, permeability)
    top_face = jnp.where(at_top, permeability, up_face)
    lower_band = -time_step * down_face
    upper_band = -time_step * up_face
    main_band = storage_rate * porosity + time_step * (down_face + top_face)
    right_side = -source_rate * (1.0 - porosity) * dilation
    return (lower_band, main_band, upper_band, right_side)


def earlier(values, stride, filler):
    head = jnp.full((stride,) + values.shape[1:], filler, values.dtype)
    return jnp.concatenate([head, values[:-stride]], axis=0)


def later(values, stride, filler):
    tail = jnp.full((stride,) + values.shape[1:], filler, values.dtype)
    return jnp.concatenate([values[stride:], tail], axis=0)


def cyclic_solve(lower_band, main_band, upper_band, right_side):
    length = main_band.shape[0]
    for bit in range((length - 1).bit_length()):
        stride = 1 << bit
        back_weight = -lower_band / earlier(main_band, stride, 1.0)
        ahead_weight = -upper_band / later(main_band, stride, 1.0)
        new_lower = back_weight * earlier(lower_band, stride, 0.0)
        new_upper = ahead_weight * later(upper_band, stride, 0.0)
        new_main = (
            main_band
            + back_weight * earlier(upper_band, stride, 0.0)
            + ahead_weight * later(lower_band, stride, 0.0)
        )
        new_right = (
            right_side
            + back_weight * earlier(right_side, stride, 0.0)
            + ahead_weight * later(right_side, stride, 0.0)
        )
        lower_band, main_band, upper_band, right_side = (new_lower, new_main, new_upper, new_right)
    return right_side / main_band


MESH_AXES = ("gx", "gy", "gz")


def halo_kernel(sides, sizes, gathered, group, *refs):
    count = len(sides)
    sends = refs[:2 * count]
    gins = refs[2 * count:2 * count + gathered]
    recvs = refs[2 * count + gathered:4 * count + gathered]
    gouts = refs[4 * count + gathered:4 * count + 2 * gathered]
    send_sem, recv_sem, gsend_sem, grecv_sem = refs[4 * count + 2 * gathered:]
    me = {a: lax.axis_index(a) for a in MESH_AXES}

    def peer(axis, delta):
        return tuple(me[a] + delta if a == axis else me[a] for a in MESH_AXES)

    def across(level):
        return tuple(level if a == "gz" else me[a] for a in MESH_AXES)

    links = []
    for i, axis in enumerate(sides):
        links.append((axis, -1, me[axis] > 0, 2 * i, 2 * i + 1))
        links.append((axis, 1, me[axis] < sizes[i] - 1, 2 * i + 1, 2 * i))
    barrier = pltpu.get_barrier_semaphore()
    peers = 0
    for axis, delta, present, _, _ in links:
        if gathered and axis == "gz":
            continue
        peers = peers + present.astype(jnp.int32)

        @pl.when(present)
        def _():
            pl.semaphore_signal(barrier, 1, device_id=peer(axis, delta), device_id_type=pl.DeviceIdType.MESH)
    if gathered:
        for d in range(1, group):
            pl.semaphore_signal(
                barrier, 1, device_id=across(lax.rem(me["gz"] + d, group)), device_id_type=pl.DeviceIdType.MESH
            )
        peers = peers + (group - 1)
    pl.semaphore_wait(barrier, peers)
    copies = []
    for axis, delta, present, src, dst in links:
        copy = pltpu.make_async_remote_copy(
            src_ref=sends[src], dst_ref=recvs[dst], send_sem=send_sem.at[src], recv_sem=recv_sem.at[dst],
            device_id=peer(axis, delta), device_id_type=pl.DeviceIdType.MESH,
        )
        copies.append((present, copy))

        @pl.when(present)
        def _():
            copy.start()
    gcopies = []
    for j in range(gathered):
        for d in range(1, group):
            slot = j * (group - 1) + d - 1
            copy = pltpu.make_async_remote_copy(
                src_ref=gins[j], dst_ref=gouts[j].at[me["gz"]], send_sem=gsend_sem.at[slot],
                recv_sem=grecv_sem.at[slot], device_id=across(lax.rem(me["gz"] + d, group)),
                device_id_type=pl.DeviceIdType.MESH,
            )
            copy.start()
            gcopies.append(copy)
    for j in range(gathered):
        gouts[j][me["gz"]] = gins[j][...]
    for axis, delta, present, src, dst in links:
        incoming = pltpu.make_async_remote_copy(
            src_ref=sends[dst], dst_ref=recvs[src], send_sem=send_sem.at[dst], recv_sem=recv_sem.at[src],
            device_id=peer(axis, delta), device_id_type=pl.DeviceIdType.MESH,
        )

        @pl.when(present)
        def _():
            incoming.wait_recv()

        @pl.when(jnp.logical_not(present))
        def _():
            recvs[src][...] = jnp.zeros(recvs[src].shape, recvs[src].dtype)
    for j in range(gathered):
        for d in range(1, group):
            slot = j * (group - 1) + d - 1
            origin = lax.rem(me["gz"] + group - d, group)
            incoming = pltpu.make_async_remote_copy(
                src_ref=gins[j], dst_ref=gouts[j].at[origin], send_sem=gsend_sem.at[slot],
                recv_sem=grecv_sem.at[slot], device_id=across(origin), device_id_type=pl.DeviceIdType.MESH,
            )
            incoming.wait_recv()
    for present, copy in copies:
        @pl.when(present)
        def _():
            copy.wait_send()
    for copy in gcopies:
        copy.wait_send()


def exchange(cells, sides, collective, gathers=(), given=None):
    sends = []
    for axis, dim in sides:
        size = cells.shape[dim]
        sends.append(lax.index_in_dim(cells, 0, axis=dim, keepdims=False))
        sends.append(lax.index_in_dim(cells, size - 1, axis=dim, keepdims=False))
    if given is not None:
        sends = list(given)
    axes = tuple(axis for axis, _ in sides)
    sizes = tuple(lax.axis_size(axis) for axis in axes)
    group = lax.axis_size("gz")
    vmem = pl.BlockSpec(memory_space=pltpu.VMEM)
    slots = max(1, len(gathers) * (group - 1))
    outs = pl.pallas_call(
        functools.partial(halo_kernel, axes, sizes, len(gathers), group),
        out_shape=[jax.ShapeDtypeStruct(s.shape, s.dtype) for s in sends]
        + [jax.ShapeDtypeStruct((group,) + g.shape, g.dtype) for g in gathers],
        in_specs=[vmem] * (len(sends) + len(gathers)),
        out_specs=[vmem] * (len(sends) + len(gathers)),
        scratch_shapes=[
            pltpu.SemaphoreType.DMA((max(1, len(sends)),)), pltpu.SemaphoreType.DMA((max(1, len(sends)),)),
            pltpu.SemaphoreType.DMA((slots,)), pltpu.SemaphoreType.DMA((slots,)),
        ],
        compiler_params=pltpu.CompilerParams(collective_id=collective, has_side_effects=True),
    )(*sends, *gathers)
    recvs = outs[:len(sends)]
    faces = {
        dim: (jnp.expand_dims(recvs[2 * i], dim), jnp.expand_dims(recvs[2 * i + 1], dim))
        for i, (axis, dim) in enumerate(sides)
    }
    stacked = [g.reshape((group * g.shape[1],) + g.shape[2:]) for g in outs[len(sends):]]
    return faces, stacked


def faces_kernel(parts, cells_ref, *out_refs):
    chans, levels, extent, breadth = cells_ref.shape
    xlo, xhi, ylo, yhi = out_refs[:4]
    for slot, c in enumerate(parts[0]):
        for level in range(levels):
            tile = cells_ref[c, level]
            xlo[slot, pl.ds(level, 1), :] = tile[0:1, :]
            xhi[slot, pl.ds(level, 1), :] = tile[extent - 1:extent, :]
    for slot, c in enumerate(parts[1]):
        for level in range(levels):
            turned = cells_ref[c, level].T
            ylo[slot, pl.ds(level, 1), :] = turned[0:1, :]
            yhi[slot, pl.ds(level, 1), :] = turned[breadth - 1:breadth, :]
    if len(parts) > 2:
        for slot, c in enumerate(parts[2]):
            out_refs[4][slot] = cells_ref[c, 0]
            out_refs[5][slot] = cells_ref[c, levels - 1]


def faces_by_kernel(cells, parts):
    chans, levels, extent, breadth = cells.shape
    shapes = [(len(parts[0]), levels, breadth)] * 2 + [(len(parts[1]), levels, extent)] * 2
    if len(parts) > 2:
        shapes += [(len(parts[2]), extent, breadth)] * 2
    vmem = pl.BlockSpec(memory_space=pltpu.VMEM)
    return pl.pallas_call(
        functools.partial(faces_kernel, parts),
        out_shape=[jax.ShapeDtypeStruct(s, cells.dtype) for s in shapes],
        in_specs=[vmem],
        out_specs=[vmem] * len(shapes),
    )(cells)


def solve_kernel(levels, poro_ref, perm_ref, right_ref, out_ref, grad_ref, xlo, xhi, ylo, yhi, padded_ref):
    perm = perm_ref[...]
    lid = jnp.zeros((1,) + perm.shape[1:], jnp.float32)
    level_above = jnp.concatenate([perm[1:], lid], axis=0)
    level_below = jnp.concatenate([lid, perm[:-1]], axis=0)
    up_face = harmonic(perm, level_above)
    down_face = harmonic(level_below, perm)
    top_face = jnp.concatenate([up_face[:-1], perm[-1:]], axis=0)
    lower_band = -time_step * down_face
    upper_band = -time_step * up_face
    main_band = storage_rate * poro_ref[...] + time_step * (down_face + top_face)
    solved = cyclic_solve(lower_band, main_band, upper_band, right_ref[...])
    height, extent, breadth = solved.shape
    padded_ref[pl.ds(0, 1)] = lid
    padded_ref[pl.ds(height + 1, 1)] = lid
    padded_ref[pl.ds(1, height)] = solved
    first = lax.axis_index("gz") * levels
    out_ref[...] = padded_ref[pl.ds(first + 1, levels)]
    grad_ref[...] = (padded_ref[pl.ds(first + 2, levels)] - padded_ref[pl.ds(first, levels)]) * 0.5
    for level in range(levels):
        tile = out_ref[level]
        xlo[pl.ds(level, 1), :] = tile[0:1, :]
        xhi[pl.ds(level, 1), :] = tile[extent - 1:extent, :]
        turned = tile.T
        ylo[pl.ds(level, 1), :] = turned[0:1, :]
        yhi[pl.ds(level, 1), :] = turned[breadth - 1:breadth, :]


def column_solve(porosity, permeability, right_side, levels):
    height, extent, breadth = right_side.shape
    vmem = pl.BlockSpec(memory_space=pltpu.VMEM)
    shapes = [(levels, extent, breadth)] * 2 + [(levels, breadth)] * 2 + [(levels, extent)] * 2
    return pl.pallas_call(
        functools.partial(solve_kernel, levels),
        out_shape=[jax.ShapeDtypeStruct(s, jnp.float32) for s in shapes],
        in_specs=[vmem] * 3,
        out_specs=[vmem] * len(shapes),
        scratch_shapes=[pltpu.VMEM((height + 2, extent, breadth), jnp.float32)],
    )(porosity, permeability, right_side)


def face_from(part, axis, from_lower):
    count = lax.axis_size(axis)
    if from_lower:
        pairs = [(i, i + 1) for i in range(count - 1)]
    else:
        pairs = [(i + 1, i) for i in range(count - 1)]
    return lax.ppermute(part, axis, pairs)


def faces_of(cells, sides):
    got = {}
    for axis, dim in sides:
        size = cells.shape[dim]
        got[dim] = (
            face_from(lax.slice_in_dim(cells, size - 1, size, axis=dim), axis, True),
            face_from(lax.slice_in_dim(cells, 0, 1, axis=dim), axis, False),
        )
    return got


def along(cells, faces, dim):
    size = cells.shape[dim]
    lower, upper = faces[dim]
    ahead = jnp.concatenate([lax.slice_in_dim(cells, 1, size, axis=dim), upper], axis=dim)
    behind = jnp.concatenate([lower, lax.slice_in_dim(cells, 0, size - 1, axis=dim)], axis=dim)
    return (ahead - behind) * 0.5


def shards(
    stress_trial,
    mean_stress,
    consolidation,
    point_velocity,
    point_weight,
    point_cell,
    yield_flag,
    point_count,
    porosity,
    permeability,
):
    levels, extent, breadth = porosity.shape
    cell_sums, *stress_faces = cell_sums_of(
        stress_trial, mean_stress, consolidation, point_velocity, point_weight, point_cell,
        yield_flag, point_count, levels, extent, breadth,
    )
    sides = (("gx", 2), ("gy", 3), ("gz", 1))
    stress_sums = cell_sums[:6]
    sf, (all_porosity, all_permeability) = exchange(
        stress_sums, sides, 0, (porosity, permeability), given=stress_faces
    )
    height = all_porosity.shape[0]
    def part(dim, parts, c):
        s = parts.index(c)
        return {dim: (sf[dim][0][s:s + 1], sf[dim][1][s:s + 1])}

    d_x = lambda c: along(stress_sums[c:c + 1], part(2, X_PARTS, c), 2)[0]
    d_y = lambda c: along(stress_sums[c:c + 1], part(3, Y_PARTS, c), 3)[0]
    d_z = lambda c: along(stress_sums[c:c + 1], part(1, Z_PARTS, c), 1)[0]
    floored = jnp.maximum(cell_sums[9], mass_floor)
    force_x = d_x(0) + d_y(3) + d_z(5)
    force_y = d_x(3) + d_y(1) + d_z(4)
    force_z = d_x(5) + d_y(4) + d_z(2)
    velocity = jnp.stack(
        [
            (cell_sums[6] + time_step * force_x) / floored,
            (cell_sums[7] + time_step * force_y) / floored,
            (cell_sums[8] + time_step * force_z) / floored,
        ]
    )
    vf, _ = exchange(velocity, sides, 1, given=faces_by_kernel(velocity, ((0,), (1,), (2,))))
    dilation = (
        along(velocity[0:1], {2: vf[2]}, 2)[0]
        + along(velocity[1:2], {3: vf[3]}, 3)[0]
        + along(velocity[2:3], {1: vf[1]}, 1)[0]
    )
    right_side = -source_rate * (1.0 - porosity) * dilation
    _, (all_right,) = exchange(right_side, (), 3, (right_side,))
    zero_level = jnp.zeros((1, extent, breadth), jnp.float32)
    pressure, rise, *pressure_faces = column_solve(all_porosity, all_permeability, all_right, levels)
    pf, _ = exchange(pressure, (("gx", 1), ("gy", 2)), 2, given=pressure_faces)
    gradient = jnp.stack([along(pressure, pf, 1), along(pressure, pf, 2), rise])
    return (velocity - time_step * gradient, pressure)


def solution(mesh):
    placed = (
        P(None, ("gx", "gy", "gz")),
        P(("gx", "gy", "gz")),
        P(("gx", "gy", "gz")),
        P(None, ("gx", "gy", "gz")),
        P(("gx", "gy", "gz")),
        P(("gx", "gy", "gz")),
        P(("gx", "gy", "gz")),
        P("gx", "gy", "gz"),
        P("gz", "gx", "gy"),
        P("gz", "gx", "gy"),
    )
    return jax.shard_map(
        shards,
        mesh=mesh,
        in_specs=placed,
        out_specs=(P(None, "gz", "gx", "gy"), P("gz", "gx", "gy")),
        check_vma=False,
    )
```

```python
import functools

import jax
import jax.numpy as jnp
from jax import lax
from jax.sharding import PartitionSpec as P

time_step = 0.25
storage_rate = 0.002
source_rate = 0.003
critical_slope = 1.2
mass_floor = 0.5
shear_floor = 1.0

from jax.experimental import pallas as pl
from jax.experimental.pallas import tpu as pltpu

CHUNK = 2048
M_ROWS = 32
N_COLS = 512


SPLITS = 2
X_PARTS = (0, 3, 5)
Y_PARTS = (3, 1, 4)
Z_PARTS = (5, 4, 2)


def _split(v):
    hi = v.astype(jnp.bfloat16)
    lo = (v - hi.astype(jnp.float32)).astype(jnp.bfloat16)
    return [hi, lo]


def sums_kernel(count_ref, st_ref, ms_ref, cons_ref, vel_ref, w_ref, cell_ref, yf_ref, out_ref, xlo_ref, xhi_ref, ylo_ref, yhi_ref, zlo_ref, zhi_ref, acc_ref):
    count = count_ref[0, 0]
    acc_ref[...] = jnp.zeros_like(acc_ref)
    chunks = st_ref.shape[1] // CHUNK

    def body(k, carry):
        start = pl.multiple_of(k * CHUNK, CHUNK)
        span = pl.ds(start, CHUNK)
        st = [st_ref[pl.ds(i, 1), span] for i in range(6)]
        ms = ms_ref[:, span]
        cons = cons_ref[:, span]
        yf = yf_ref[:, span]
        slot = start + lax.broadcasted_iota(jnp.int32, (1, CHUNK), 1)
        weight = jnp.where(slot < count, w_ref[:, span], 0.0)
        sq_normal = st[0] * st[0] + st[1] * st[1] + st[2] * st[2]
        sq_shear = st[3] * st[3] + st[4] * st[4] + st[5] * st[5]
        shear_size = jnp.sqrt(1.5 * (sq_normal + 2.0 * sq_shear))
        yield_size = critical_slope * jnp.sqrt(ms * (cons - ms))
        factor = jnp.where(yf == 1, yield_size / jnp.maximum(shear_size, shear_floor), 1.0)
        stress = [st[i] * factor - ms if i < 3 else st[i] * factor for i in range(6)]
        values = [s * weight for s in stress]
        values += [vel_ref[pl.ds(i, 1), span] * weight for i in range(3)]
        values.append(weight)
        cell = cell_ref[:, span]
        m_key = (cell >> 12) * 8 + ((cell >> 7) & 7)
        n_key = ((cell >> 10) & 3) * 128 + (cell & 127)
        m_mask = lax.broadcasted_iota(jnp.int32, (M_ROWS, CHUNK), 0) == m_key
        zero = jnp.zeros((M_ROWS, CHUNK), jnp.bfloat16)
        pieces = []
        for v in values:
            for part in _split(v):
                pieces.append(jnp.where(m_mask, jnp.broadcast_to(part, (M_ROWS, CHUNK)), zero))
        lhs = jnp.concatenate(pieces, axis=0)
        one_hot = jnp.where(
            lax.broadcasted_iota(jnp.int32, (N_COLS, CHUNK), 0) == n_key, 1.0, 0.0
        ).astype(jnp.bfloat16)
        acc_ref[...] += lax.dot_general(
            lhs, one_hot, (((1,), (1,)), ((), ())), preferred_element_type=jnp.float32
        )
        return carry

    lax.fori_loop(0, chunks, body, 0)
    for comp in range(10):
        for level in range(16):
            rows = pl.ds((comp * SPLITS) * M_ROWS + (level >> 2) * 8, 8)
            lanes = pl.ds((level & 3) * 128, 128)
            total = acc_ref[rows, lanes]
            for s in range(1, SPLITS):
                total = total + acc_ref[pl.ds((comp * SPLITS + s) * M_ROWS + (level >> 2) * 8, 8), lanes]
            out_ref[comp, level] = total
            if comp in X_PARTS:
                slot = X_PARTS.index(comp)
                xlo_ref[slot, pl.ds(level, 1), :] = total[0:1, :]
                xhi_ref[slot, pl.ds(level, 1), :] = total[7:8, :]
            if comp in Y_PARTS:
                slot = Y_PARTS.index(comp)
                turned = total.T
                ylo_ref[slot, pl.ds(level, 1), :] = turned[0:1, :]
                yhi_ref[slot, pl.ds(level, 1), :] = turned[127:128, :]
            if comp in Z_PARTS:
                slot = Z_PARTS.index(comp)
                if level == 0:
                    zlo_ref[slot] = total
                if level == 15:
                    zhi_ref[slot] = total


def cell_sums_of(stress_trial, mean_stress, consolidation, point_velocity, point_weight, point_cell, yield_flag, point_count, levels, extent, breadth):
    n = mean_stress.shape[0]
    row = lambda a: a.reshape(1, n)
    vmem = pl.BlockSpec(memory_space=pltpu.VMEM)
    return pl.pallas_call(
        sums_kernel,
        out_shape=[
            jax.ShapeDtypeStruct(s, jnp.float32)
            for s in [(10, levels, extent, breadth)] + [(3, levels, breadth)] * 2 + [(3, levels, extent)] * 2
            + [(3, extent, breadth)] * 2
        ],
        in_specs=[pl.BlockSpec(memory_space=pltpu.SMEM)] + [vmem] * 7,
        out_specs=[vmem] * 7,
        scratch_shapes=[pltpu.VMEM((10 * SPLITS * M_ROWS, N_COLS), jnp.float32)],
        cost_estimate=pl.CostEstimate(
            flops=2 * 10 * SPLITS * M_ROWS * N_COLS * n, bytes_accessed=13 * 4 * n + 10 * 4 * levels * extent * breadth,
            transcendentals=3 * n,
        ),
    )(
        point_count.reshape(1, 1), stress_trial, row(mean_stress), row(consolidation), point_velocity,
        row(point_weight), row(point_cell), row(yield_flag),
    )


def padded_2(cells, sides, width):
    for axis, dim in sides:
        count = lax.axis_size(axis)
        ends = count - 1
        head = lax.slice_in_dim(cells, 0, width, axis=dim)
        tail = lax.slice_in_dim(cells, cells.shape[dim] - width, cells.shape[dim], axis=dim)
        cells = jnp.concatenate(
            [
                lax.ppermute(tail, axis, [(i, (i + 1) % count) for i in range(ends)]),
                cells,
                lax.ppermute(head, axis, [((i + 1) % count, i) for i in range(ends)]),
            ],
            axis=dim,
        )
    return cells


def along_x(padded):
    return (padded[..., 1:-1, 2:, 1:-1] - padded[..., 1:-1, :-2, 1:-1]) * 0.5


def along_y(padded):
    return (padded[..., 1:-1, 1:-1, 2:] - padded[..., 1:-1, 1:-1, :-2]) * 0.5


def along_z(padded):
    return (padded[..., 2:, 1:-1, 1:-1] - padded[..., :-2, 1:-1, 1:-1]) * 0.5


def harmonic(former, latter):
    return 2.0 * former * latter / (former + latter)


def returned_stress(stress_trial, mean_stress, consolidation, yield_flag):
    sq_normal = (
        stress_trial[0] * stress_trial[0]
        + stress_trial[1] * stress_trial[1]
        + stress_trial[2] * stress_trial[2]
    )
    sq_shear = (
        stress_trial[3] * stress_trial[3]
        + stress_trial[4] * stress_trial[4]
        + stress_trial[5] * stress_trial[5]
    )
    shear_size = jnp.sqrt(1.5 * (sq_normal + 2.0 * sq_shear))
    yield_size = critical_slope * jnp.sqrt(mean_stress * (consolidation - mean_stress))
    factor = jnp.where(yield_flag == 1, yield_size / jnp.maximum(shear_size, shear_floor), 1.0)
    isotropic = jnp.array([1.0, 1.0, 1.0, 0.0, 0.0, 0.0], dtype=jnp.float32)[:, None]
    return stress_trial * factor - isotropic * mean_stress


def point_sums(stress, point_velocity, weight, cell_index, segments):
    stacked = jnp.concatenate([stress * weight, point_velocity * weight, weight[None]], axis=0)
    return jax.vmap(
        lambda component: jax.ops.segment_sum(component, cell_index, num_segments=segments)
    )(stacked)


def brick_velocity(cell_sums, padded):
    floored = jnp.maximum(cell_sums[9], mass_floor)
    force_x = along_x(padded[0]) + along_y(padded[3]) + along_z(padded[5])
    force_y = along_x(padded[3]) + along_y(padded[1]) + along_z(padded[4])
    force_z = along_x(padded[5]) + along_y(padded[4]) + along_z(padded[2])
    return jnp.stack(
        [
            (cell_sums[6] + time_step * force_x) / floored,
            (cell_sums[7] + time_step * force_y) / floored,
            (cell_sums[8] + time_step * force_z) / floored,
        ]
    )


def divergence(padded_velocity):
    return along_x(padded_velocity[0]) + along_y(padded_velocity[1]) + along_z(padded_velocity[2])


def band_terms(porosity, permeability, level_below, level_above, at_top, dilation):
    up_face = harmonic(permeability, level_above)
    down_face = harmonic(level_below, permeability)
    top_face = jnp.where(at_top, permeability, up_face)
    lower_band = -time_step * down_face
    upper_band = -time_step * up_face
    main_band = storage_rate * porosity + time_step * (down_face + top_face)
    right_side = -source_rate * (1.0 - porosity) * dilation
    return (lower_band, main_band, upper_band, right_side)


def earlier(values, stride, filler):
    head = jnp.full((stride,) + values.shape[1:], filler, values.dtype)
    return jnp.concatenate([head, values[:-stride]], axis=0)


def later(values, stride, filler):
    tail = jnp.full((stride,) + values.shape[1:], filler, values.dtype)
    return jnp.concatenate([values[stride:], tail], axis=0)


def cyclic_solve(lower_band, main_band, upper_band, right_side):
    length = main_band.shape[0]
    for bit in range((length - 1).bit_length()):
        stride = 1 << bit
        back_weight = -lower_band / earlier(main_band, stride, 1.0)
        ahead_weight = -upper_band / later(main_band, stride, 1.0)
        new_lower = back_weight * earlier(lower_band, stride, 0.0)
        new_upper = ahead_weight * later(upper_band, stride, 0.0)
        new_main = (
            main_band
            + back_weight * earlier(upper_band, stride, 0.0)
            + ahead_weight * later(lower_band, stride, 0.0)
        )
        new_right = (
            right_side
            + back_weight * earlier(right_side, stride, 0.0)
            + ahead_weight * later(right_side, stride, 0.0)
        )
        lower_band, main_band, upper_band, right_side = (new_lower, new_main, new_upper, new_right)
    return right_side / main_band


MESH_AXES = ("gx", "gy", "gz")


def halo_kernel(sides, sizes, gathered, group, *refs):
    count = len(sides)
    sends = refs[:2 * count]
    gins = refs[2 * count:2 * count + gathered]
    recvs = refs[2 * count + gathered:4 * count + gathered]
    gouts = refs[4 * count + gathered:4 * count + 2 * gathered]
    send_sem, recv_sem, gsend_sem, grecv_sem = refs[4 * count + 2 * gathered:]
    me = {a: lax.axis_index(a) for a in MESH_AXES}

    def peer(axis, delta):
        return tuple(me[a] + delta if a == axis else me[a] for a in MESH_AXES)

    def across(level):
        return tuple(level if a == "gz" else me[a] for a in MESH_AXES)

    links = []
    for i, axis in enumerate(sides):
        links.append((axis, -1, me[axis] > 0, 2 * i, 2 * i + 1))
        links.append((axis, 1, me[axis] < sizes[i] - 1, 2 * i + 1, 2 * i))
    barrier = pltpu.get_barrier_semaphore()
    peers = 0
    for axis, delta, present, _, _ in links:
        if gathered and axis == "gz":
            continue
        peers = peers + present.astype(jnp.int32)

        @pl.when(present)
        def _():
            pl.semaphore_signal(barrier, 1, device_id=peer(axis, delta), device_id_type=pl.DeviceIdType.MESH)
    if gathered:
        for d in range(1, group):
            pl.semaphore_signal(
                barrier, 1, device_id=across(lax.rem(me["gz"] + d, group)), device_id_type=pl.DeviceIdType.MESH
            )
        peers = peers + (group - 1)
    pl.semaphore_wait(barrier, peers)
    copies = []
    for axis, delta, present, src, dst in links:
        copy = pltpu.make_async_remote_copy(
            src_ref=sends[src], dst_ref=recvs[dst], send_sem=send_sem.at[src], recv_sem=recv_sem.at[dst],
            device_id=peer(axis, delta), device_id_type=pl.DeviceIdType.MESH,
        )
        copies.append((present, copy))

        @pl.when(present)
        def _():
            copy.start()
    gcopies = []
    for j in range(gathered):
        for d in range(1, group):
            slot = j * (group - 1) + d - 1
            copy = pltpu.make_async_remote_copy(
                src_ref=gins[j], dst_ref=gouts[j].at[me["gz"]], send_sem=gsend_sem.at[slot],
                recv_sem=grecv_sem.at[slot], device_id=across(lax.rem(me["gz"] + d, group)),
                device_id_type=pl.DeviceIdType.MESH,
            )
            copy.start()
            gcopies.append(copy)
    for j in range(gathered):
        gouts[j][me["gz"]] = gins[j][...]
    for axis, delta, present, src, dst in links:
        incoming = pltpu.make_async_remote_copy(
            src_ref=sends[dst], dst_ref=recvs[src], send_sem=send_sem.at[dst], recv_sem=recv_sem.at[src],
            device_id=peer(axis, delta), device_id_type=pl.DeviceIdType.MESH,
        )

        @pl.when(present)
        def _():
            incoming.wait_recv()

        @pl.when(jnp.logical_not(present))
        def _():
            recvs[src][...] = jnp.zeros(recvs[src].shape, recvs[src].dtype)
    for j in range(gathered):
        for d in range(1, group):
            slot = j * (group - 1) + d - 1
            origin = lax.rem(me["gz"] + group - d, group)
            incoming = pltpu.make_async_remote_copy(
                src_ref=gins[j], dst_ref=gouts[j].at[origin], send_sem=gsend_sem.at[slot],
                recv_sem=grecv_sem.at[slot], device_id=across(origin), device_id_type=pl.DeviceIdType.MESH,
            )
            incoming.wait_recv()
    for present, copy in copies:
        @pl.when(present)
        def _():
            copy.wait_send()
    for copy in gcopies:
        copy.wait_send()


def exchange(cells, sides, collective, gathers=(), given=None):
    sends = []
    for axis, dim in sides:
        size = cells.shape[dim]
        sends.append(lax.index_in_dim(cells, 0, axis=dim, keepdims=False))
        sends.append(lax.index_in_dim(cells, size - 1, axis=dim, keepdims=False))
    if given is not None:
        sends = list(given)
    axes = tuple(axis for axis, _ in sides)
    sizes = tuple(lax.axis_size(axis) for axis in axes)
    group = lax.axis_size("gz")
    vmem = pl.BlockSpec(memory_space=pltpu.VMEM)
    slots = max(1, len(gathers) * (group - 1))
    outs = pl.pallas_call(
        functools.partial(halo_kernel, axes, sizes, len(gathers), group),
        out_shape=[jax.ShapeDtypeStruct(s.shape, s.dtype) for s in sends]
        + [jax.ShapeDtypeStruct((group,) + g.shape, g.dtype) for g in gathers],
        in_specs=[vmem] * (len(sends) + len(gathers)),
        out_specs=[vmem] * (len(sends) + len(gathers)),
        scratch_shapes=[
            pltpu.SemaphoreType.DMA((max(1, len(sends)),)), pltpu.SemaphoreType.DMA((max(1, len(sends)),)),
            pltpu.SemaphoreType.DMA((slots,)), pltpu.SemaphoreType.DMA((slots,)),
        ],
        compiler_params=pltpu.CompilerParams(collective_id=collective, has_side_effects=True),
    )(*sends, *gathers)
    recvs = outs[:len(sends)]
    faces = {
        dim: (jnp.expand_dims(recvs[2 * i], dim), jnp.expand_dims(recvs[2 * i + 1], dim))
        for i, (axis, dim) in enumerate(sides)
    }
    stacked = [g.reshape((group * g.shape[1],) + g.shape[2:]) for g in outs[len(sends):]]
    return faces, stacked


def faces_kernel(parts, cells_ref, *out_refs):
    chans, levels, extent, breadth = cells_ref.shape
    xlo, xhi, ylo, yhi = out_refs[:4]
    for slot, c in enumerate(parts[0]):
        for level in range(levels):
            tile = cells_ref[c, level]
            xlo[slot, pl.ds(level, 1), :] = tile[0:1, :]
            xhi[slot, pl.ds(level, 1), :] = tile[extent - 1:extent, :]
    for slot, c in enumerate(parts[1]):
        for level in range(levels):
            turned = cells_ref[c, level].T
            ylo[slot, pl.ds(level, 1), :] = turned[0:1, :]
            yhi[slot, pl.ds(level, 1), :] = turned[breadth - 1:breadth, :]
    if len(parts) > 2:
        for slot, c in enumerate(parts[2]):
            out_refs[4][slot] = cells_ref[c, 0]
            out_refs[5][slot] = cells_ref[c, levels - 1]


def faces_by_kernel(cells, parts):
    chans, levels, extent, breadth = cells.shape
    shapes = [(len(parts[0]), levels, breadth)] * 2 + [(len(parts[1]), levels, extent)] * 2
    if len(parts) > 2:
        shapes += [(len(parts[2]), extent, breadth)] * 2
    vmem = pl.BlockSpec(memory_space=pltpu.VMEM)
    return pl.pallas_call(
        functools.partial(faces_kernel, parts),
        out_shape=[jax.ShapeDtypeStruct(s, cells.dtype) for s in shapes],
        in_specs=[vmem],
        out_specs=[vmem] * len(shapes),
    )(cells)


def solve_kernel(levels, poro_ref, perm_ref, right_ref, out_ref, grad_ref, xlo, xhi, ylo, yhi, padded_ref):
    perm = perm_ref[...]
    lid = jnp.zeros((1,) + perm.shape[1:], jnp.float32)
    level_above = jnp.concatenate([perm[1:], lid], axis=0)
    level_below = jnp.concatenate([lid, perm[:-1]], axis=0)
    up_face = harmonic(perm, level_above)
    down_face = harmonic(level_below, perm)
    top_face = jnp.concatenate([up_face[:-1], perm[-1:]], axis=0)
    lower_band = -time_step * down_face
    upper_band = -time_step * up_face
    main_band = storage_rate * poro_ref[...] + time_step * (down_face + top_face)
    solved = cyclic_solve(lower_band, main_band, upper_band, right_ref[...])
    height, extent, breadth = solved.shape
    padded_ref[pl.ds(0, 1)] = lid
    padded_ref[pl.ds(height + 1, 1)] = lid
    padded_ref[pl.ds(1, height)] = solved
    first = lax.axis_index("gz") * levels
    out_ref[...] = padded_ref[pl.ds(first + 1, levels)]
    grad_ref[...] = (padded_ref[pl.ds(first + 2, levels)] - padded_ref[pl.ds(first, levels)]) * 0.5
    for level in range(levels):
        tile = out_ref[level]
        xlo[pl.ds(level, 1), :] = tile[0:1, :]
        xhi[pl.ds(level, 1), :] = tile[extent - 1:extent, :]
        turned = tile.T
        ylo[pl.ds(level, 1), :] = turned[0:1, :]
        yhi[pl.ds(level, 1), :] = turned[breadth - 1:breadth, :]


def column_solve(porosity, permeability, right_side, levels):
    height, extent, breadth = right_side.shape
    vmem = pl.BlockSpec(memory_space=pltpu.VMEM)
    shapes = [(levels, extent, breadth)] * 2 + [(levels, breadth)] * 2 + [(levels, extent)] * 2
    return pl.pallas_call(
        functools.partial(solve_kernel, levels),
        out_shape=[jax.ShapeDtypeStruct(s, jnp.float32) for s in shapes],
        in_specs=[vmem] * 3,
        out_specs=[vmem] * len(shapes),
        scratch_shapes=[pltpu.VMEM((height + 2, extent, breadth), jnp.float32)],
    )(porosity, permeability, right_side)


def face_from(part, axis, from_lower):
    count = lax.axis_size(axis)
    if from_lower:
        pairs = [(i, i + 1) for i in range(count - 1)]
    else:
        pairs = [(i + 1, i) for i in range(count - 1)]
    return lax.ppermute(part, axis, pairs)


def faces_of(cells, sides):
    got = {}
    for axis, dim in sides:
        size = cells.shape[dim]
        got[dim] = (
            face_from(lax.slice_in_dim(cells, size - 1, size, axis=dim), axis, True),
            face_from(lax.slice_in_dim(cells, 0, 1, axis=dim), axis, False),
        )
    return got


def along(cells, faces, dim):
    size = cells.shape[dim]
    lower, upper = faces[dim]
    ahead = jnp.concatenate([lax.slice_in_dim(cells, 1, size, axis=dim), upper], axis=dim)
    behind = jnp.concatenate([lower, lax.slice_in_dim(cells, 0, size - 1, axis=dim)], axis=dim)
    return (ahead - behind) * 0.5


def shards(
    stress_trial,
    mean_stress,
    consolidation,
    point_velocity,
    point_weight,
    point_cell,
    yield_flag,
    point_count,
    porosity,
    permeability,
):
    levels, extent, breadth = porosity.shape
    cell_sums, *stress_faces = cell_sums_of(
        stress_trial, mean_stress, consolidation, point_velocity, point_weight, point_cell,
        yield_flag, point_count, levels, extent, breadth,
    )
    sides = (("gx", 2), ("gy", 3), ("gz", 1))
    stress_sums = cell_sums[:6]
    sf, (all_porosity, all_permeability) = exchange(
        stress_sums, sides, 0, (porosity, permeability), given=stress_faces
    )
    height = all_porosity.shape[0]
    def part(dim, parts, c):
        s = parts.index(c)
        return {dim: (sf[dim][0][s:s + 1], sf[dim][1][s:s + 1])}

    d_x = lambda c: along(stress_sums[c:c + 1], part(2, X_PARTS, c), 2)[0]
    d_y = lambda c: along(stress_sums[c:c + 1], part(3, Y_PARTS, c), 3)[0]
    d_z = lambda c: along(stress_sums[c:c + 1], part(1, Z_PARTS, c), 1)[0]
    floored = jnp.maximum(cell_sums[9], mass_floor)
    force_x = d_x(0) + d_y(3) + d_z(5)
    force_y = d_x(3) + d_y(1) + d_z(4)
    force_z = d_x(5) + d_y(4) + d_z(2)
    velocity = jnp.stack(
        [
            (cell_sums[6] + time_step * force_x) / floored,
            (cell_sums[7] + time_step * force_y) / floored,
            (cell_sums[8] + time_step * force_z) / floored,
        ]
    )
    vf, _ = exchange(velocity, sides, 1, given=faces_by_kernel(velocity, ((0,), (1,), (2,))))
    dilation = (
        along(velocity[0:1], {2: vf[2]}, 2)[0]
        + along(velocity[1:2], {3: vf[3]}, 3)[0]
        + along(velocity[2:3], {1: vf[1]}, 1)[0]
    )
    right_side = -source_rate * (1.0 - porosity) * dilation
    _, (all_right,) = exchange(right_side, (), 3, (right_side,))
    zero_level = jnp.zeros((1, extent, breadth), jnp.float32)
    pressure, rise, *pressure_faces = column_solve(all_porosity, all_permeability, all_right, levels)
    pf, _ = exchange(pressure, (("gx", 1), ("gy", 2)), 2, given=pressure_faces)
    gradient = jnp.stack([along(pressure, pf, 1), along(pressure, pf, 2), rise])
    return (velocity - time_step * gradient, pressure)


def solution(mesh):
    placed = (
        P(None, ("gx", "gy", "gz")),
        P(("gx", "gy", "gz")),
        P(("gx", "gy", "gz")),
        P(None, ("gx", "gy", "gz")),
        P(("gx", "gy", "gz")),
        P(("gx", "gy", "gz")),
        P(("gx", "gy", "gz")),
        P("gx", "gy", "gz"),
        P("gz", "gx", "gy"),
        P("gz", "gx", "gy"),
    )
    return jax.shard_map(
        shards,
        mesh=mesh,
        in_specs=placed,
        out_specs=(P(None, "gz", "gx", "gy"), P("gz", "gx", "gy")),
        check_vma=False,
    )
```

```python
import functools

import jax
import jax.numpy as jnp
from jax import lax
from jax.sharding import PartitionSpec as P

time_step = 0.25
storage_rate = 0.002
source_rate = 0.003
critical_slope = 1.2
mass_floor = 0.5
shear_floor = 1.0

from jax.experimental import pallas as pl
from jax.experimental.pallas import tpu as pltpu

CHUNK = 4096
M_ROWS = 32
N_COLS = 512


SPLITS = 2
X_PARTS = (0, 3, 5)
Y_PARTS = (3, 1, 4)
Z_PARTS = (5, 4, 2)


def _split(v):
    hi = v.astype(jnp.bfloat16)
    lo = (v - hi.astype(jnp.float32)).astype(jnp.bfloat16)
    return [hi, lo]


def sums_kernel(count_ref, st_ref, ms_ref, cons_ref, vel_ref, w_ref, cell_ref, yf_ref, out_ref, xlo_ref, xhi_ref, ylo_ref, yhi_ref, zlo_ref, zhi_ref, acc_ref):
    count = count_ref[0, 0]
    acc_ref[...] = jnp.zeros_like(acc_ref)
    chunks = st_ref.shape[1] // CHUNK

    def body(k, carry):
        start = pl.multiple_of(k * CHUNK, CHUNK)
        span = pl.ds(start, CHUNK)
        st = [st_ref[pl.ds(i, 1), span] for i in range(6)]
        ms = ms_ref[:, span]
        cons = cons_ref[:, span]
        yf = yf_ref[:, span]
        slot = start + lax.broadcasted_iota(jnp.int32, (1, CHUNK), 1)
        weight = jnp.where(slot < count, w_ref[:, span], 0.0)
        sq_normal = st[0] * st[0] + st[1] * st[1] + st[2] * st[2]
        sq_shear = st[3] * st[3] + st[4] * st[4] + st[5] * st[5]
        shear_size = jnp.sqrt(1.5 * (sq_normal + 2.0 * sq_shear))
        yield_size = critical_slope * jnp.sqrt(ms * (cons - ms))
        factor = jnp.where(yf == 1, yield_size / jnp.maximum(shear_size, shear_floor), 1.0)
        stress = [st[i] * factor - ms if i < 3 else st[i] * factor for i in range(6)]
        values = [s * weight for s in stress]
        values += [vel_ref[pl.ds(i, 1), span] * weight for i in range(3)]
        values.append(weight)
        cell = cell_ref[:, span]
        m_key = (cell >> 12) * 8 + ((cell >> 7) & 7)
        n_key = ((cell >> 10) & 3) * 128 + (cell & 127)
        m_mask = lax.broadcasted_iota(jnp.int32, (M_ROWS, CHUNK), 0) == m_key
        zero = jnp.zeros((M_ROWS, CHUNK), jnp.bfloat16)
        pieces = []
        for v in values:
            for part in _split(v):
                pieces.append(jnp.where(m_mask, jnp.broadcast_to(part, (M_ROWS, CHUNK)), zero))
        lhs = jnp.concatenate(pieces, axis=0)
        one_hot = jnp.where(
            lax.broadcasted_iota(jnp.int32, (N_COLS, CHUNK), 0) == n_key, 1.0, 0.0
        ).astype(jnp.bfloat16)
        acc_ref[...] += lax.dot_general(
            lhs, one_hot, (((1,), (1,)), ((), ())), preferred_element_type=jnp.float32
        )
        return carry

    lax.fori_loop(0, chunks, body, 0)
    for comp in range(10):
        for level in range(16):
            rows = pl.ds((comp * SPLITS) * M_ROWS + (level >> 2) * 8, 8)
            lanes = pl.ds((level & 3) * 128, 128)
            total = acc_ref[rows, lanes]
            for s in range(1, SPLITS):
                total = total + acc_ref[pl.ds((comp * SPLITS + s) * M_ROWS + (level >> 2) * 8, 8), lanes]
            out_ref[comp, level] = total
            if comp in X_PARTS:
                slot = X_PARTS.index(comp)
                xlo_ref[slot, pl.ds(level, 1), :] = total[0:1, :]
                xhi_ref[slot, pl.ds(level, 1), :] = total[7:8, :]
            if comp in Y_PARTS:
                slot = Y_PARTS.index(comp)
                turned = total.T
                ylo_ref[slot, pl.ds(level, 1), :] = turned[0:1, :]
                yhi_ref[slot, pl.ds(level, 1), :] = turned[127:128, :]
            if comp in Z_PARTS:
                slot = Z_PARTS.index(comp)
                if level == 0:
                    zlo_ref[slot] = total
                if level == 15:
                    zhi_ref[slot] = total


def cell_sums_of(stress_trial, mean_stress, consolidation, point_velocity, point_weight, point_cell, yield_flag, point_count, levels, extent, breadth):
    n = mean_stress.shape[0]
    row = lambda a: a.reshape(1, n)
    vmem = pl.BlockSpec(memory_space=pltpu.VMEM)
    return pl.pallas_call(
        sums_kernel,
        out_shape=[
            jax.ShapeDtypeStruct(s, jnp.float32)
            for s in [(10, levels, extent, breadth)] + [(3, levels, breadth)] * 2 + [(3, levels, extent)] * 2
            + [(3, extent, breadth)] * 2
        ],
        in_specs=[pl.BlockSpec(memory_space=pltpu.SMEM)] + [vmem] * 7,
        out_specs=[vmem] * 7,
        scratch_shapes=[pltpu.VMEM((10 * SPLITS * M_ROWS, N_COLS), jnp.float32)],
        cost_estimate=pl.CostEstimate(
            flops=2 * 10 * SPLITS * M_ROWS * N_COLS * n, bytes_accessed=13 * 4 * n + 10 * 4 * levels * extent * breadth,
            transcendentals=3 * n,
        ),
    )(
        point_count.reshape(1, 1), stress_trial, row(mean_stress), row(consolidation), point_velocity,
        row(point_weight), row(point_cell), row(yield_flag),
    )


def padded_2(cells, sides, width):
    for axis, dim in sides:
        count = lax.axis_size(axis)
        ends = count - 1
        head = lax.slice_in_dim(cells, 0, width, axis=dim)
        tail = lax.slice_in_dim(cells, cells.shape[dim] - width, cells.shape[dim], axis=dim)
        cells = jnp.concatenate(
            [
                lax.ppermute(tail, axis, [(i, (i + 1) % count) for i in range(ends)]),
                cells,
                lax.ppermute(head, axis, [((i + 1) % count, i) for i in range(ends)]),
            ],
            axis=dim,
        )
    return cells


def along_x(padded):
    return (padded[..., 1:-1, 2:, 1:-1] - padded[..., 1:-1, :-2, 1:-1]) * 0.5


def along_y(padded):
    return (padded[..., 1:-1, 1:-1, 2:] - padded[..., 1:-1, 1:-1, :-2]) * 0.5


def along_z(padded):
    return (padded[..., 2:, 1:-1, 1:-1] - padded[..., :-2, 1:-1, 1:-1]) * 0.5


def harmonic(former, latter):
    return 2.0 * former * latter / (former + latter)


def returned_stress(stress_trial, mean_stress, consolidation, yield_flag):
    sq_normal = (
        stress_trial[0] * stress_trial[0]
        + stress_trial[1] * stress_trial[1]
        + stress_trial[2] * stress_trial[2]
    )
    sq_shear = (
        stress_trial[3] * stress_trial[3]
        + stress_trial[4] * stress_trial[4]
        + stress_trial[5] * stress_trial[5]
    )
    shear_size = jnp.sqrt(1.5 * (sq_normal + 2.0 * sq_shear))
    yield_size = critical_slope * jnp.sqrt(mean_stress * (consolidation - mean_stress))
    factor = jnp.where(yield_flag == 1, yield_size / jnp.maximum(shear_size, shear_floor), 1.0)
    isotropic = jnp.array([1.0, 1.0, 1.0, 0.0, 0.0, 0.0], dtype=jnp.float32)[:, None]
    return stress_trial * factor - isotropic * mean_stress


def point_sums(stress, point_velocity, weight, cell_index, segments):
    stacked = jnp.concatenate([stress * weight, point_velocity * weight, weight[None]], axis=0)
    return jax.vmap(
        lambda component: jax.ops.segment_sum(component, cell_index, num_segments=segments)
    )(stacked)


def brick_velocity(cell_sums, padded):
    floored = jnp.maximum(cell_sums[9], mass_floor)
    force_x = along_x(padded[0]) + along_y(padded[3]) + along_z(padded[5])
    force_y = along_x(padded[3]) + along_y(padded[1]) + along_z(padded[4])
    force_z = along_x(padded[5]) + along_y(padded[4]) + along_z(padded[2])
    return jnp.stack(
        [
            (cell_sums[6] + time_step * force_x) / floored,
            (cell_sums[7] + time_step * force_y) / floored,
            (cell_sums[8] + time_step * force_z) / floored,
        ]
    )


def divergence(padded_velocity):
    return along_x(padded_velocity[0]) + along_y(padded_velocity[1]) + along_z(padded_velocity[2])


def band_terms(porosity, permeability, level_below, level_above, at_top, dilation):
    up_face = harmonic(permeability, level_above)
    down_face = harmonic(level_below, permeability)
    top_face = jnp.where(at_top, permeability, up_face)
    lower_band = -time_step * down_face
    upper_band = -time_step * up_face
    main_band = storage_rate * porosity + time_step * (down_face + top_face)
    right_side = -source_rate * (1.0 - porosity) * dilation
    return (lower_band, main_band, upper_band, right_side)


def earlier(values, stride, filler):
    head = jnp.full((stride,) + values.shape[1:], filler, values.dtype)
    return jnp.concatenate([head, values[:-stride]], axis=0)


def later(values, stride, filler):
    tail = jnp.full((stride,) + values.shape[1:], filler, values.dtype)
    return jnp.concatenate([values[stride:], tail], axis=0)


def cyclic_solve(lower_band, main_band, upper_band, right_side):
    length = main_band.shape[0]
    for bit in range((length - 1).bit_length()):
        stride = 1 << bit
        back_weight = -lower_band / earlier(main_band, stride, 1.0)
        ahead_weight = -upper_band / later(main_band, stride, 1.0)
        new_lower = back_weight * earlier(lower_band, stride, 0.0)
        new_upper = ahead_weight * later(upper_band, stride, 0.0)
        new_main = (
            main_band
            + back_weight * earlier(upper_band, stride, 0.0)
            + ahead_weight * later(lower_band, stride, 0.0)
        )
        new_right = (
            right_side
            + back_weight * earlier(right_side, stride, 0.0)
            + ahead_weight * later(right_side, stride, 0.0)
        )
        lower_band, main_band, upper_band, right_side = (new_lower, new_main, new_upper, new_right)
    return right_side / main_band


MESH_AXES = ("gx", "gy", "gz")


def halo_kernel(sides, sizes, gathered, group, *refs):
    count = len(sides)
    sends = refs[:2 * count]
    gins = refs[2 * count:2 * count + gathered]
    recvs = refs[2 * count + gathered:4 * count + gathered]
    gouts = refs[4 * count + gathered:4 * count + 2 * gathered]
    send_sem, recv_sem, gsend_sem, grecv_sem = refs[4 * count + 2 * gathered:]
    me = {a: lax.axis_index(a) for a in MESH_AXES}

    def peer(axis, delta):
        return tuple(me[a] + delta if a == axis else me[a] for a in MESH_AXES)

    def across(level):
        return tuple(level if a == "gz" else me[a] for a in MESH_AXES)

    links = []
    for i, axis in enumerate(sides):
        links.append((axis, -1, me[axis] > 0, 2 * i, 2 * i + 1))
        links.append((axis, 1, me[axis] < sizes[i] - 1, 2 * i + 1, 2 * i))
    barrier = pltpu.get_barrier_semaphore()
    peers = 0
    for axis, delta, present, _, _ in links:
        if gathered and axis == "gz":
            continue
        peers = peers + present.astype(jnp.int32)

        @pl.when(present)
        def _():
            pl.semaphore_signal(barrier, 1, device_id=peer(axis, delta), device_id_type=pl.DeviceIdType.MESH)
    if gathered:
        for d in range(1, group):
            pl.semaphore_signal(
                barrier, 1, device_id=across(lax.rem(me["gz"] + d, group)), device_id_type=pl.DeviceIdType.MESH
            )
        peers = peers + (group - 1)
    pl.semaphore_wait(barrier, peers)
    copies = []
    for axis, delta, present, src, dst in links:
        copy = pltpu.make_async_remote_copy(
            src_ref=sends[src], dst_ref=recvs[dst], send_sem=send_sem.at[src], recv_sem=recv_sem.at[dst],
            device_id=peer(axis, delta), device_id_type=pl.DeviceIdType.MESH,
        )
        copies.append((present, copy))

        @pl.when(present)
        def _():
            copy.start()
    gcopies = []
    for j in range(gathered):
        for d in range(1, group):
            slot = j * (group - 1) + d - 1
            copy = pltpu.make_async_remote_copy(
                src_ref=gins[j], dst_ref=gouts[j].at[me["gz"]], send_sem=gsend_sem.at[slot],
                recv_sem=grecv_sem.at[slot], device_id=across(lax.rem(me["gz"] + d, group)),
                device_id_type=pl.DeviceIdType.MESH,
            )
            copy.start()
            gcopies.append(copy)
    for j in range(gathered):
        gouts[j][me["gz"]] = gins[j][...]
    for axis, delta, present, src, dst in links:
        incoming = pltpu.make_async_remote_copy(
            src_ref=sends[dst], dst_ref=recvs[src], send_sem=send_sem.at[dst], recv_sem=recv_sem.at[src],
            device_id=peer(axis, delta), device_id_type=pl.DeviceIdType.MESH,
        )

        @pl.when(present)
        def _():
            incoming.wait_recv()

        @pl.when(jnp.logical_not(present))
        def _():
            recvs[src][...] = jnp.zeros(recvs[src].shape, recvs[src].dtype)
    for j in range(gathered):
        for d in range(1, group):
            slot = j * (group - 1) + d - 1
            origin = lax.rem(me["gz"] + group - d, group)
            incoming = pltpu.make_async_remote_copy(
                src_ref=gins[j], dst_ref=gouts[j].at[origin], send_sem=gsend_sem.at[slot],
                recv_sem=grecv_sem.at[slot], device_id=across(origin), device_id_type=pl.DeviceIdType.MESH,
            )
            incoming.wait_recv()
    for present, copy in copies:
        @pl.when(present)
        def _():
            copy.wait_send()
    for copy in gcopies:
        copy.wait_send()


def exchange(cells, sides, collective, gathers=(), given=None):
    sends = []
    for axis, dim in sides:
        size = cells.shape[dim]
        sends.append(lax.index_in_dim(cells, 0, axis=dim, keepdims=False))
        sends.append(lax.index_in_dim(cells, size - 1, axis=dim, keepdims=False))
    if given is not None:
        sends = list(given)
    axes = tuple(axis for axis, _ in sides)
    sizes = tuple(lax.axis_size(axis) for axis in axes)
    group = lax.axis_size("gz")
    vmem = pl.BlockSpec(memory_space=pltpu.VMEM)
    slots = max(1, len(gathers) * (group - 1))
    outs = pl.pallas_call(
        functools.partial(halo_kernel, axes, sizes, len(gathers), group),
        out_shape=[jax.ShapeDtypeStruct(s.shape, s.dtype) for s in sends]
        + [jax.ShapeDtypeStruct((group,) + g.shape, g.dtype) for g in gathers],
        in_specs=[vmem] * (len(sends) + len(gathers)),
        out_specs=[vmem] * (len(sends) + len(gathers)),
        scratch_shapes=[
            pltpu.SemaphoreType.DMA((max(1, len(sends)),)), pltpu.SemaphoreType.DMA((max(1, len(sends)),)),
            pltpu.SemaphoreType.DMA((slots,)), pltpu.SemaphoreType.DMA((slots,)),
        ],
        compiler_params=pltpu.CompilerParams(collective_id=collective, has_side_effects=True),
    )(*sends, *gathers)
    recvs = outs[:len(sends)]
    faces = {
        dim: (jnp.expand_dims(recvs[2 * i], dim), jnp.expand_dims(recvs[2 * i + 1], dim))
        for i, (axis, dim) in enumerate(sides)
    }
    stacked = [g.reshape((group * g.shape[1],) + g.shape[2:]) for g in outs[len(sends):]]
    return faces, stacked


def faces_kernel(parts, cells_ref, *out_refs):
    chans, levels, extent, breadth = cells_ref.shape
    xlo, xhi, ylo, yhi = out_refs[:4]
    for slot, c in enumerate(parts[0]):
        for level in range(levels):
            tile = cells_ref[c, level]
            xlo[slot, pl.ds(level, 1), :] = tile[0:1, :]
            xhi[slot, pl.ds(level, 1), :] = tile[extent - 1:extent, :]
    for slot, c in enumerate(parts[1]):
        for level in range(levels):
            turned = cells_ref[c, level].T
            ylo[slot, pl.ds(level, 1), :] = turned[0:1, :]
            yhi[slot, pl.ds(level, 1), :] = turned[breadth - 1:breadth, :]
    if len(parts) > 2:
        for slot, c in enumerate(parts[2]):
            out_refs[4][slot] = cells_ref[c, 0]
            out_refs[5][slot] = cells_ref[c, levels - 1]


def faces_by_kernel(cells, parts):
    chans, levels, extent, breadth = cells.shape
    shapes = [(len(parts[0]), levels, breadth)] * 2 + [(len(parts[1]), levels, extent)] * 2
    if len(parts) > 2:
        shapes += [(len(parts[2]), extent, breadth)] * 2
    vmem = pl.BlockSpec(memory_space=pltpu.VMEM)
    return pl.pallas_call(
        functools.partial(faces_kernel, parts),
        out_shape=[jax.ShapeDtypeStruct(s, cells.dtype) for s in shapes],
        in_specs=[vmem],
        out_specs=[vmem] * len(shapes),
    )(cells)


def solve_kernel(levels, poro_ref, perm_ref, right_ref, out_ref, grad_ref, xlo, xhi, ylo, yhi, padded_ref):
    perm = perm_ref[...]
    lid = jnp.zeros((1,) + perm.shape[1:], jnp.float32)
    level_above = jnp.concatenate([perm[1:], lid], axis=0)
    level_below = jnp.concatenate([lid, perm[:-1]], axis=0)
    up_face = harmonic(perm, level_above)
    down_face = harmonic(level_below, perm)
    top_face = jnp.concatenate([up_face[:-1], perm[-1:]], axis=0)
    lower_band = -time_step * down_face
    upper_band = -time_step * up_face
    main_band = storage_rate * poro_ref[...] + time_step * (down_face + top_face)
    solved = cyclic_solve(lower_band, main_band, upper_band, right_ref[...])
    height, extent, breadth = solved.shape
    padded_ref[pl.ds(0, 1)] = lid
    padded_ref[pl.ds(height + 1, 1)] = lid
    padded_ref[pl.ds(1, height)] = solved
    first = lax.axis_index("gz") * levels
    out_ref[...] = padded_ref[pl.ds(first + 1, levels)]
    grad_ref[...] = (padded_ref[pl.ds(first + 2, levels)] - padded_ref[pl.ds(first, levels)]) * 0.5
    for level in range(levels):
        tile = out_ref[level]
        xlo[pl.ds(level, 1), :] = tile[0:1, :]
        xhi[pl.ds(level, 1), :] = tile[extent - 1:extent, :]
        turned = tile.T
        ylo[pl.ds(level, 1), :] = turned[0:1, :]
        yhi[pl.ds(level, 1), :] = turned[breadth - 1:breadth, :]


def column_solve(porosity, permeability, right_side, levels):
    height, extent, breadth = right_side.shape
    vmem = pl.BlockSpec(memory_space=pltpu.VMEM)
    shapes = [(levels, extent, breadth)] * 2 + [(levels, breadth)] * 2 + [(levels, extent)] * 2
    return pl.pallas_call(
        functools.partial(solve_kernel, levels),
        out_shape=[jax.ShapeDtypeStruct(s, jnp.float32) for s in shapes],
        in_specs=[vmem] * 3,
        out_specs=[vmem] * len(shapes),
        scratch_shapes=[pltpu.VMEM((height + 2, extent, breadth), jnp.float32)],
    )(porosity, permeability, right_side)


def face_from(part, axis, from_lower):
    count = lax.axis_size(axis)
    if from_lower:
        pairs = [(i, i + 1) for i in range(count - 1)]
    else:
        pairs = [(i + 1, i) for i in range(count - 1)]
    return lax.ppermute(part, axis, pairs)


def faces_of(cells, sides):
    got = {}
    for axis, dim in sides:
        size = cells.shape[dim]
        got[dim] = (
            face_from(lax.slice_in_dim(cells, size - 1, size, axis=dim), axis, True),
            face_from(lax.slice_in_dim(cells, 0, 1, axis=dim), axis, False),
        )
    return got


def along(cells, faces, dim):
    size = cells.shape[dim]
    lower, upper = faces[dim]
    ahead = jnp.concatenate([lax.slice_in_dim(cells, 1, size, axis=dim), upper], axis=dim)
    behind = jnp.concatenate([lower, lax.slice_in_dim(cells, 0, size - 1, axis=dim)], axis=dim)
    return (ahead - behind) * 0.5


def shards(
    stress_trial,
    mean_stress,
    consolidation,
    point_velocity,
    point_weight,
    point_cell,
    yield_flag,
    point_count,
    porosity,
    permeability,
):
    levels, extent, breadth = porosity.shape
    cell_sums, *stress_faces = cell_sums_of(
        stress_trial, mean_stress, consolidation, point_velocity, point_weight, point_cell,
        yield_flag, point_count, levels, extent, breadth,
    )
    sides = (("gx", 2), ("gy", 3), ("gz", 1))
    stress_sums = cell_sums[:6]
    sf, (all_porosity, all_permeability) = exchange(
        stress_sums, sides, 0, (porosity, permeability), given=stress_faces
    )
    height = all_porosity.shape[0]
    def part(dim, parts, c):
        s = parts.index(c)
        return {dim: (sf[dim][0][s:s + 1], sf[dim][1][s:s + 1])}

    d_x = lambda c: along(stress_sums[c:c + 1], part(2, X_PARTS, c), 2)[0]
    d_y = lambda c: along(stress_sums[c:c + 1], part(3, Y_PARTS, c), 3)[0]
    d_z = lambda c: along(stress_sums[c:c + 1], part(1, Z_PARTS, c), 1)[0]
    floored = jnp.maximum(cell_sums[9], mass_floor)
    force_x = d_x(0) + d_y(3) + d_z(5)
    force_y = d_x(3) + d_y(1) + d_z(4)
    force_z = d_x(5) + d_y(4) + d_z(2)
    velocity = jnp.stack(
        [
            (cell_sums[6] + time_step * force_x) / floored,
            (cell_sums[7] + time_step * force_y) / floored,
            (cell_sums[8] + time_step * force_z) / floored,
        ]
    )
    vf, _ = exchange(velocity, sides, 1, given=faces_by_kernel(velocity, ((0,), (1,), (2,))))
    dilation = (
        along(velocity[0:1], {2: vf[2]}, 2)[0]
        + along(velocity[1:2], {3: vf[3]}, 3)[0]
        + along(velocity[2:3], {1: vf[1]}, 1)[0]
    )
    right_side = -source_rate * (1.0 - porosity) * dilation
    _, (all_right,) = exchange(right_side, (), 3, (right_side,))
    zero_level = jnp.zeros((1, extent, breadth), jnp.float32)
    pressure, rise, *pressure_faces = column_solve(all_porosity, all_permeability, all_right, levels)
    pf, _ = exchange(pressure, (("gx", 1), ("gy", 2)), 2, given=pressure_faces)
    gradient = jnp.stack([along(pressure, pf, 1), along(pressure, pf, 2), rise])
    return (velocity - time_step * gradient, pressure)


def solution(mesh):
    placed = (
        P(None, ("gx", "gy", "gz")),
        P(("gx", "gy", "gz")),
        P(("gx", "gy", "gz")),
        P(None, ("gx", "gy", "gz")),
        P(("gx", "gy", "gz")),
        P(("gx", "gy", "gz")),
        P(("gx", "gy", "gz")),
        P("gx", "gy", "gz"),
        P("gz", "gx", "gy"),
        P("gz", "gx", "gy"),
    )
    return jax.shard_map(
        shards,
        mesh=mesh,
        in_specs=placed,
        out_specs=(P(None, "gz", "gx", "gy"), P("gz", "gx", "gy")),
        check_vma=False,
    )
```

```python
import functools

import jax
import jax.numpy as jnp
from jax import lax
from jax.sharding import PartitionSpec as P

time_step = 0.25
storage_rate = 0.002
source_rate = 0.003
critical_slope = 1.2
mass_floor = 0.5
shear_floor = 1.0

from jax.experimental import pallas as pl
from jax.experimental.pallas import tpu as pltpu

CHUNK = 8192
M_ROWS = 32
N_COLS = 512


SPLITS = 2
X_PARTS = (0, 3, 5)
Y_PARTS = (3, 1, 4)
Z_PARTS = (5, 4, 2)


def _split(v):
    hi = v.astype(jnp.bfloat16)
    lo = (v - hi.astype(jnp.float32)).astype(jnp.bfloat16)
    return [hi, lo]


def sums_kernel(count_ref, st_ref, ms_ref, cons_ref, vel_ref, w_ref, cell_ref, yf_ref, out_ref, xlo_ref, xhi_ref, ylo_ref, yhi_ref, zlo_ref, zhi_ref, acc_ref):
    count = count_ref[0, 0]
    acc_ref[...] = jnp.zeros_like(acc_ref)
    chunks = st_ref.shape[1] // CHUNK

    def body(k, carry):
        start = pl.multiple_of(k * CHUNK, CHUNK)
        span = pl.ds(start, CHUNK)
        st = [st_ref[pl.ds(i, 1), span] for i in range(6)]
        ms = ms_ref[:, span]
        cons = cons_ref[:, span]
        yf = yf_ref[:, span]
        slot = start + lax.broadcasted_iota(jnp.int32, (1, CHUNK), 1)
        weight = jnp.where(slot < count, w_ref[:, span], 0.0)
        sq_normal = st[0] * st[0] + st[1] * st[1] + st[2] * st[2]
        sq_shear = st[3] * st[3] + st[4] * st[4] + st[5] * st[5]
        shear_size = jnp.sqrt(1.5 * (sq_normal + 2.0 * sq_shear))
        yield_size = critical_slope * jnp.sqrt(ms * (cons - ms))
        factor = jnp.where(yf == 1, yield_size / jnp.maximum(shear_size, shear_floor), 1.0)
        stress = [st[i] * factor - ms if i < 3 else st[i] * factor for i in range(6)]
        values = [s * weight for s in stress]
        values += [vel_ref[pl.ds(i, 1), span] * weight for i in range(3)]
        values.append(weight)
        cell = cell_ref[:, span]
        m_key = (cell >> 12) * 8 + ((cell >> 7) & 7)
        n_key = ((cell >> 10) & 3) * 128 + (cell & 127)
        m_mask = lax.broadcasted_iota(jnp.int32, (M_ROWS, CHUNK), 0) == m_key
        zero = jnp.zeros((M_ROWS, CHUNK), jnp.bfloat16)
        pieces = []
        for v in values:
            for part in _split(v):
                pieces.append(jnp.where(m_mask, jnp.broadcast_to(part, (M_ROWS, CHUNK)), zero))
        lhs = jnp.concatenate(pieces, axis=0)
        one_hot = jnp.where(
            lax.broadcasted_iota(jnp.int32, (N_COLS, CHUNK), 0) == n_key, 1.0, 0.0
        ).astype(jnp.bfloat16)
        acc_ref[...] += lax.dot_general(
            lhs, one_hot, (((1,), (1,)), ((), ())), preferred_element_type=jnp.float32
        )
        return carry

    lax.fori_loop(0, chunks, body, 0)
    for comp in range(10):
        for level in range(16):
            rows = pl.ds((comp * SPLITS) * M_ROWS + (level >> 2) * 8, 8)
            lanes = pl.ds((level & 3) * 128, 128)
            total = acc_ref[rows, lanes]
            for s in range(1, SPLITS):
                total = total + acc_ref[pl.ds((comp * SPLITS + s) * M_ROWS + (level >> 2) * 8, 8), lanes]
            out_ref[comp, level] = total
            if comp in X_PARTS:
                slot = X_PARTS.index(comp)
                xlo_ref[slot, pl.ds(level, 1), :] = total[0:1, :]
                xhi_ref[slot, pl.ds(level, 1), :] = total[7:8, :]
            if comp in Y_PARTS:
                slot = Y_PARTS.index(comp)
                turned = total.T
                ylo_ref[slot, pl.ds(level, 1), :] = turned[0:1, :]
                yhi_ref[slot, pl.ds(level, 1), :] = turned[127:128, :]
            if comp in Z_PARTS:
                slot = Z_PARTS.index(comp)
                if level == 0:
                    zlo_ref[slot] = total
                if level == 15:
                    zhi_ref[slot] = total


def cell_sums_of(stress_trial, mean_stress, consolidation, point_velocity, point_weight, point_cell, yield_flag, point_count, levels, extent, breadth):
    n = mean_stress.shape[0]
    row = lambda a: a.reshape(1, n)
    vmem = pl.BlockSpec(memory_space=pltpu.VMEM)
    return pl.pallas_call(
        sums_kernel,
        out_shape=[
            jax.ShapeDtypeStruct(s, jnp.float32)
            for s in [(10, levels, extent, breadth)] + [(3, levels, breadth)] * 2 + [(3, levels, extent)] * 2
            + [(3, extent, breadth)] * 2
        ],
        in_specs=[pl.BlockSpec(memory_space=pltpu.SMEM)] + [vmem] * 7,
        out_specs=[vmem] * 7,
        scratch_shapes=[pltpu.VMEM((10 * SPLITS * M_ROWS, N_COLS), jnp.float32)],
        cost_estimate=pl.CostEstimate(
            flops=2 * 10 * SPLITS * M_ROWS * N_COLS * n, bytes_accessed=13 * 4 * n + 10 * 4 * levels * extent * breadth,
            transcendentals=3 * n,
        ),
    )(
        point_count.reshape(1, 1), stress_trial, row(mean_stress), row(consolidation), point_velocity,
        row(point_weight), row(point_cell), row(yield_flag),
    )


def padded_2(cells, sides, width):
    for axis, dim in sides:
        count = lax.axis_size(axis)
        ends = count - 1
        head = lax.slice_in_dim(cells, 0, width, axis=dim)
        tail = lax.slice_in_dim(cells, cells.shape[dim] - width, cells.shape[dim], axis=dim)
        cells = jnp.concatenate(
            [
                lax.ppermute(tail, axis, [(i, (i + 1) % count) for i in range(ends)]),
                cells,
                lax.ppermute(head, axis, [((i + 1) % count, i) for i in range(ends)]),
            ],
            axis=dim,
        )
    return cells


def along_x(padded):
    return (padded[..., 1:-1, 2:, 1:-1] - padded[..., 1:-1, :-2, 1:-1]) * 0.5


def along_y(padded):
    return (padded[..., 1:-1, 1:-1, 2:] - padded[..., 1:-1, 1:-1, :-2]) * 0.5


def along_z(padded):
    return (padded[..., 2:, 1:-1, 1:-1] - padded[..., :-2, 1:-1, 1:-1]) * 0.5


def harmonic(former, latter):
    return 2.0 * former * latter / (former + latter)


def returned_stress(stress_trial, mean_stress, consolidation, yield_flag):
    sq_normal = (
        stress_trial[0] * stress_trial[0]
        + stress_trial[1] * stress_trial[1]
        + stress_trial[2] * stress_trial[2]
    )
    sq_shear = (
        stress_trial[3] * stress_trial[3]
        + stress_trial[4] * stress_trial[4]
        + stress_trial[5] * stress_trial[5]
    )
    shear_size = jnp.sqrt(1.5 * (sq_normal + 2.0 * sq_shear))
    yield_size = critical_slope * jnp.sqrt(mean_stress * (consolidation - mean_stress))
    factor = jnp.where(yield_flag == 1, yield_size / jnp.maximum(shear_size, shear_floor), 1.0)
    isotropic = jnp.array([1.0, 1.0, 1.0, 0.0, 0.0, 0.0], dtype=jnp.float32)[:, None]
    return stress_trial * factor - isotropic * mean_stress


def point_sums(stress, point_velocity, weight, cell_index, segments):
    stacked = jnp.concatenate([stress * weight, point_velocity * weight, weight[None]], axis=0)
    return jax.vmap(
        lambda component: jax.ops.segment_sum(component, cell_index, num_segments=segments)
    )(stacked)


def brick_velocity(cell_sums, padded):
    floored = jnp.maximum(cell_sums[9], mass_floor)
    force_x = along_x(padded[0]) + along_y(padded[3]) + along_z(padded[5])
    force_y = along_x(padded[3]) + along_y(padded[1]) + along_z(padded[4])
    force_z = along_x(padded[5]) + along_y(padded[4]) + along_z(padded[2])
    return jnp.stack(
        [
            (cell_sums[6] + time_step * force_x) / floored,
            (cell_sums[7] + time_step * force_y) / floored,
            (cell_sums[8] + time_step * force_z) / floored,
        ]
    )


def divergence(padded_velocity):
    return along_x(padded_velocity[0]) + along_y(padded_velocity[1]) + along_z(padded_velocity[2])


def band_terms(porosity, permeability, level_below, level_above, at_top, dilation):
    up_face = harmonic(permeability, level_above)
    down_face = harmonic(level_below, permeability)
    top_face = jnp.where(at_top, permeability, up_face)
    lower_band = -time_step * down_face
    upper_band = -time_step * up_face
    main_band = storage_rate * porosity + time_step * (down_face + top_face)
    right_side = -source_rate * (1.0 - porosity) * dilation
    return (lower_band, main_band, upper_band, right_side)


def earlier(values, stride, filler):
    head = jnp.full((stride,) + values.shape[1:], filler, values.dtype)
    return jnp.concatenate([head, values[:-stride]], axis=0)


def later(values, stride, filler):
    tail = jnp.full((stride,) + values.shape[1:], filler, values.dtype)
    return jnp.concatenate([values[stride:], tail], axis=0)


def cyclic_solve(lower_band, main_band, upper_band, right_side):
    length = main_band.shape[0]
    for bit in range((length - 1).bit_length()):
        stride = 1 << bit
        back_weight = -lower_band / earlier(main_band, stride, 1.0)
        ahead_weight = -upper_band / later(main_band, stride, 1.0)
        new_lower = back_weight * earlier(lower_band, stride, 0.0)
        new_upper = ahead_weight * later(upper_band, stride, 0.0)
        new_main = (
            main_band
            + back_weight * earlier(upper_band, stride, 0.0)
            + ahead_weight * later(lower_band, stride, 0.0)
        )
        new_right = (
            right_side
            + back_weight * earlier(right_side, stride, 0.0)
            + ahead_weight * later(right_side, stride, 0.0)
        )
        lower_band, main_band, upper_band, right_side = (new_lower, new_main, new_upper, new_right)
    return right_side / main_band


MESH_AXES = ("gx", "gy", "gz")


def halo_kernel(sides, sizes, gathered, group, *refs):
    count = len(sides)
    sends = refs[:2 * count]
    gins = refs[2 * count:2 * count + gathered]
    recvs = refs[2 * count + gathered:4 * count + gathered]
    gouts = refs[4 * count + gathered:4 * count + 2 * gathered]
    send_sem, recv_sem, gsend_sem, grecv_sem = refs[4 * count + 2 * gathered:]
    me = {a: lax.axis_index(a) for a in MESH_AXES}

    def peer(axis, delta):
        return tuple(me[a] + delta if a == axis else me[a] for a in MESH_AXES)

    def across(level):
        return tuple(level if a == "gz" else me[a] for a in MESH_AXES)

    links = []
    for i, axis in enumerate(sides):
        links.append((axis, -1, me[axis] > 0, 2 * i, 2 * i + 1))
        links.append((axis, 1, me[axis] < sizes[i] - 1, 2 * i + 1, 2 * i))
    barrier = pltpu.get_barrier_semaphore()
    peers = 0
    for axis, delta, present, _, _ in links:
        if gathered and axis == "gz":
            continue
        peers = peers + present.astype(jnp.int32)

        @pl.when(present)
        def _():
            pl.semaphore_signal(barrier, 1, device_id=peer(axis, delta), device_id_type=pl.DeviceIdType.MESH)
    if gathered:
        for d in range(1, group):
            pl.semaphore_signal(
                barrier, 1, device_id=across(lax.rem(me["gz"] + d, group)), device_id_type=pl.DeviceIdType.MESH
            )
        peers = peers + (group - 1)
    pl.semaphore_wait(barrier, peers)
    copies = []
    for axis, delta, present, src, dst in links:
        copy = pltpu.make_async_remote_copy(
            src_ref=sends[src], dst_ref=recvs[dst], send_sem=send_sem.at[src], recv_sem=recv_sem.at[dst],
            device_id=peer(axis, delta), device_id_type=pl.DeviceIdType.MESH,
        )
        copies.append((present, copy))

        @pl.when(present)
        def _():
            copy.start()
    gcopies = []
    for j in range(gathered):
        for d in range(1, group):
            slot = j * (group - 1) + d - 1
            copy = pltpu.make_async_remote_copy(
                src_ref=gins[j], dst_ref=gouts[j].at[me["gz"]], send_sem=gsend_sem.at[slot],
                recv_sem=grecv_sem.at[slot], device_id=across(lax.rem(me["gz"] + d, group)),
                device_id_type=pl.DeviceIdType.MESH,
            )
            copy.start()
            gcopies.append(copy)
    for j in range(gathered):
        gouts[j][me["gz"]] = gins[j][...]
    for axis, delta, present, src, dst in links:
        incoming = pltpu.make_async_remote_copy(
            src_ref=sends[dst], dst_ref=recvs[src], send_sem=send_sem.at[dst], recv_sem=recv_sem.at[src],
            device_id=peer(axis, delta), device_id_type=pl.DeviceIdType.MESH,
        )

        @pl.when(present)
        def _():
            incoming.wait_recv()

        @pl.when(jnp.logical_not(present))
        def _():
            recvs[src][...] = jnp.zeros(recvs[src].shape, recvs[src].dtype)
    for j in range(gathered):
        for d in range(1, group):
            slot = j * (group - 1) + d - 1
            origin = lax.rem(me["gz"] + group - d, group)
            incoming = pltpu.make_async_remote_copy(
                src_ref=gins[j], dst_ref=gouts[j].at[origin], send_sem=gsend_sem.at[slot],
                recv_sem=grecv_sem.at[slot], device_id=across(origin), device_id_type=pl.DeviceIdType.MESH,
            )
            incoming.wait_recv()
    for present, copy in copies:
        @pl.when(present)
        def _():
            copy.wait_send()
    for copy in gcopies:
        copy.wait_send()


def exchange(cells, sides, collective, gathers=(), given=None):
    sends = []
    for axis, dim in sides:
        size = cells.shape[dim]
        sends.append(lax.index_in_dim(cells, 0, axis=dim, keepdims=False))
        sends.append(lax.index_in_dim(cells, size - 1, axis=dim, keepdims=False))
    if given is not None:
        sends = list(given)
    axes = tuple(axis for axis, _ in sides)
    sizes = tuple(lax.axis_size(axis) for axis in axes)
    group = lax.axis_size("gz")
    vmem = pl.BlockSpec(memory_space=pltpu.VMEM)
    slots = max(1, len(gathers) * (group - 1))
    outs = pl.pallas_call(
        functools.partial(halo_kernel, axes, sizes, len(gathers), group),
        out_shape=[jax.ShapeDtypeStruct(s.shape, s.dtype) for s in sends]
        + [jax.ShapeDtypeStruct((group,) + g.shape, g.dtype) for g in gathers],
        in_specs=[vmem] * (len(sends) + len(gathers)),
        out_specs=[vmem] * (len(sends) + len(gathers)),
        scratch_shapes=[
            pltpu.SemaphoreType.DMA((max(1, len(sends)),)), pltpu.SemaphoreType.DMA((max(1, len(sends)),)),
            pltpu.SemaphoreType.DMA((slots,)), pltpu.SemaphoreType.DMA((slots,)),
        ],
        compiler_params=pltpu.CompilerParams(collective_id=collective, has_side_effects=True),
    )(*sends, *gathers)
    recvs = outs[:len(sends)]
    faces = {
        dim: (jnp.expand_dims(recvs[2 * i], dim), jnp.expand_dims(recvs[2 * i + 1], dim))
        for i, (axis, dim) in enumerate(sides)
    }
    stacked = [g.reshape((group * g.shape[1],) + g.shape[2:]) for g in outs[len(sends):]]
    return faces, stacked


def faces_kernel(parts, cells_ref, *out_refs):
    chans, levels, extent, breadth = cells_ref.shape
    xlo, xhi, ylo, yhi = out_refs[:4]
    for slot, c in enumerate(parts[0]):
        for level in range(levels):
            tile = cells_ref[c, level]
            xlo[slot, pl.ds(level, 1), :] = tile[0:1, :]
            xhi[slot, pl.ds(level, 1), :] = tile[extent - 1:extent, :]
    for slot, c in enumerate(parts[1]):
        for level in range(levels):
            turned = cells_ref[c, level].T
            ylo[slot, pl.ds(level, 1), :] = turned[0:1, :]
            yhi[slot, pl.ds(level, 1), :] = turned[breadth - 1:breadth, :]
    if len(parts) > 2:
        for slot, c in enumerate(parts[2]):
            out_refs[4][slot] = cells_ref[c, 0]
            out_refs[5][slot] = cells_ref[c, levels - 1]


def faces_by_kernel(cells, parts):
    chans, levels, extent, breadth = cells.shape
    shapes = [(len(parts[0]), levels, breadth)] * 2 + [(len(parts[1]), levels, extent)] * 2
    if len(parts) > 2:
        shapes += [(len(parts[2]), extent, breadth)] * 2
    vmem = pl.BlockSpec(memory_space=pltpu.VMEM)
    return pl.pallas_call(
        functools.partial(faces_kernel, parts),
        out_shape=[jax.ShapeDtypeStruct(s, cells.dtype) for s in shapes],
        in_specs=[vmem],
        out_specs=[vmem] * len(shapes),
    )(cells)


def solve_kernel(levels, poro_ref, perm_ref, right_ref, out_ref, grad_ref, xlo, xhi, ylo, yhi, padded_ref):
    perm = perm_ref[...]
    lid = jnp.zeros((1,) + perm.shape[1:], jnp.float32)
    level_above = jnp.concatenate([perm[1:], lid], axis=0)
    level_below = jnp.concatenate([lid, perm[:-1]], axis=0)
    up_face = harmonic(perm, level_above)
    down_face = harmonic(level_below, perm)
    top_face = jnp.concatenate([up_face[:-1], perm[-1:]], axis=0)
    lower_band = -time_step * down_face
    upper_band = -time_step * up_face
    main_band = storage_rate * poro_ref[...] + time_step * (down_face + top_face)
    solved = cyclic_solve(lower_band, main_band, upper_band, right_ref[...])
    height, extent, breadth = solved.shape
    padded_ref[pl.ds(0, 1)] = lid
    padded_ref[pl.ds(height + 1, 1)] = lid
    padded_ref[pl.ds(1, height)] = solved
    first = lax.axis_index("gz") * levels
    out_ref[...] = padded_ref[pl.ds(first + 1, levels)]
    grad_ref[...] = (padded_ref[pl.ds(first + 2, levels)] - padded_ref[pl.ds(first, levels)]) * 0.5
    for level in range(levels):
        tile = out_ref[level]
        xlo[pl.ds(level, 1), :] = tile[0:1, :]
        xhi[pl.ds(level, 1), :] = tile[extent - 1:extent, :]
        turned = tile.T
        ylo[pl.ds(level, 1), :] = turned[0:1, :]
        yhi[pl.ds(level, 1), :] = turned[breadth - 1:breadth, :]


def column_solve(porosity, permeability, right_side, levels):
    height, extent, breadth = right_side.shape
    vmem = pl.BlockSpec(memory_space=pltpu.VMEM)
    shapes = [(levels, extent, breadth)] * 2 + [(levels, breadth)] * 2 + [(levels, extent)] * 2
    return pl.pallas_call(
        functools.partial(solve_kernel, levels),
        out_shape=[jax.ShapeDtypeStruct(s, jnp.float32) for s in shapes],
        in_specs=[vmem] * 3,
        out_specs=[vmem] * len(shapes),
        scratch_shapes=[pltpu.VMEM((height + 2, extent, breadth), jnp.float32)],
    )(porosity, permeability, right_side)


def face_from(part, axis, from_lower):
    count = lax.axis_size(axis)
    if from_lower:
        pairs = [(i, i + 1) for i in range(count - 1)]
    else:
        pairs = [(i + 1, i) for i in range(count - 1)]
    return lax.ppermute(part, axis, pairs)


def faces_of(cells, sides):
    got = {}
    for axis, dim in sides:
        size = cells.shape[dim]
        got[dim] = (
            face_from(lax.slice_in_dim(cells, size - 1, size, axis=dim), axis, True),
            face_from(lax.slice_in_dim(cells, 0, 1, axis=dim), axis, False),
        )
    return got


def along(cells, faces, dim):
    size = cells.shape[dim]
    lower, upper = faces[dim]
    ahead = jnp.concatenate([lax.slice_in_dim(cells, 1, size, axis=dim), upper], axis=dim)
    behind = jnp.concatenate([lower, lax.slice_in_dim(cells, 0, size - 1, axis=dim)], axis=dim)
    return (ahead - behind) * 0.5


def shards(
    stress_trial,
    mean_stress,
    consolidation,
    point_velocity,
    point_weight,
    point_cell,
    yield_flag,
    point_count,
    porosity,
    permeability,
):
    levels, extent, breadth = porosity.shape
    cell_sums, *stress_faces = cell_sums_of(
        stress_trial, mean_stress, consolidation, point_velocity, point_weight, point_cell,
        yield_flag, point_count, levels, extent, breadth,
    )
    sides = (("gx", 2), ("gy", 3), ("gz", 1))
    stress_sums = cell_sums[:6]
    sf, (all_porosity, all_permeability) = exchange(
        stress_sums, sides, 0, (porosity, permeability), given=stress_faces
    )
    height = all_porosity.shape[0]
    def part(dim, parts, c):
        s = parts.index(c)
        return {dim: (sf[dim][0][s:s + 1], sf[dim][1][s:s + 1])}

    d_x = lambda c: along(stress_sums[c:c + 1], part(2, X_PARTS, c), 2)[0]
    d_y = lambda c: along(stress_sums[c:c + 1], part(3, Y_PARTS, c), 3)[0]
    d_z = lambda c: along(stress_sums[c:c + 1], part(1, Z_PARTS, c), 1)[0]
    floored = jnp.maximum(cell_sums[9], mass_floor)
    force_x = d_x(0) + d_y(3) + d_z(5)
    force_y = d_x(3) + d_y(1) + d_z(4)
    force_z = d_x(5) + d_y(4) + d_z(2)
    velocity = jnp.stack(
        [
            (cell_sums[6] + time_step * force_x) / floored,
            (cell_sums[7] + time_step * force_y) / floored,
            (cell_sums[8] + time_step * force_z) / floored,
        ]
    )
    vf, _ = exchange(velocity, sides, 1, given=faces_by_kernel(velocity, ((0,), (1,), (2,))))
    dilation = (
        along(velocity[0:1], {2: vf[2]}, 2)[0]
        + along(velocity[1:2], {3: vf[3]}, 3)[0]
        + along(velocity[2:3], {1: vf[1]}, 1)[0]
    )
    right_side = -source_rate * (1.0 - porosity) * dilation
    _, (all_right,) = exchange(right_side, (), 3, (right_side,))
    zero_level = jnp.zeros((1, extent, breadth), jnp.float32)
    pressure, rise, *pressure_faces = column_solve(all_porosity, all_permeability, all_right, levels)
    pf, _ = exchange(pressure, (("gx", 1), ("gy", 2)), 2, given=pressure_faces)
    gradient = jnp.stack([along(pressure, pf, 1), along(pressure, pf, 2), rise])
    return (velocity - time_step * gradient, pressure)


def solution(mesh):
    placed = (
        P(None, ("gx", "gy", "gz")),
        P(("gx", "gy", "gz")),
        P(("gx", "gy", "gz")),
        P(None, ("gx", "gy", "gz")),
        P(("gx", "gy", "gz")),
        P(("gx", "gy", "gz")),
        P(("gx", "gy", "gz")),
        P("gx", "gy", "gz"),
        P("gz", "gx", "gy"),
        P("gz", "gx", "gy"),
    )
    return jax.shard_map(
        shards,
        mesh=mesh,
        in_specs=placed,
        out_specs=(P(None, "gz", "gx", "gy"), P("gz", "gx", "gy")),
        check_vma=False,
    )
```

```python
import functools

import jax
import jax.numpy as jnp
from jax import lax
from jax.sharding import PartitionSpec as P

time_step = 0.25
storage_rate = 0.002
source_rate = 0.003
critical_slope = 1.2
mass_floor = 0.5
shear_floor = 1.0

from jax.experimental import pallas as pl
from jax.experimental.pallas import tpu as pltpu

CHUNK = 12288
M_ROWS = 32
N_COLS = 512


SPLITS = 2
X_PARTS = (0, 3, 5)
Y_PARTS = (3, 1, 4)
Z_PARTS = (5, 4, 2)


def _split(v):
    hi = v.astype(jnp.bfloat16)
    lo = (v - hi.astype(jnp.float32)).astype(jnp.bfloat16)
    return [hi, lo]


def sums_kernel(count_ref, st_ref, ms_ref, cons_ref, vel_ref, w_ref, cell_ref, yf_ref, out_ref, xlo_ref, xhi_ref, ylo_ref, yhi_ref, zlo_ref, zhi_ref, acc_ref):
    count = count_ref[0, 0]
    acc_ref[...] = jnp.zeros_like(acc_ref)
    chunks = st_ref.shape[1] // CHUNK

    def body(k, carry):
        start = pl.multiple_of(k * CHUNK, CHUNK)
        span = pl.ds(start, CHUNK)
        st = [st_ref[pl.ds(i, 1), span] for i in range(6)]
        ms = ms_ref[:, span]
        cons = cons_ref[:, span]
        yf = yf_ref[:, span]
        slot = start + lax.broadcasted_iota(jnp.int32, (1, CHUNK), 1)
        weight = jnp.where(slot < count, w_ref[:, span], 0.0)
        sq_normal = st[0] * st[0] + st[1] * st[1] + st[2] * st[2]
        sq_shear = st[3] * st[3] + st[4] * st[4] + st[5] * st[5]
        shear_size = jnp.sqrt(1.5 * (sq_normal + 2.0 * sq_shear))
        yield_size = critical_slope * jnp.sqrt(ms * (cons - ms))
        factor = jnp.where(yf == 1, yield_size / jnp.maximum(shear_size, shear_floor), 1.0)
        stress = [st[i] * factor - ms if i < 3 else st[i] * factor for i in range(6)]
        values = [s * weight for s in stress]
        values += [vel_ref[pl.ds(i, 1), span] * weight for i in range(3)]
        values.append(weight)
        cell = cell_ref[:, span]
        m_key = (cell >> 12) * 8 + ((cell >> 7) & 7)
        n_key = ((cell >> 10) & 3) * 128 + (cell & 127)
        m_mask = lax.broadcasted_iota(jnp.int32, (M_ROWS, CHUNK), 0) == m_key
        zero = jnp.zeros((M_ROWS, CHUNK), jnp.bfloat16)
        pieces = []
        for v in values:
            for part in _split(v):
                pieces.append(jnp.where(m_mask, jnp.broadcast_to(part, (M_ROWS, CHUNK)), zero))
        lhs = jnp.concatenate(pieces, axis=0)
        one_hot = jnp.where(
            lax.broadcasted_iota(jnp.int32, (N_COLS, CHUNK), 0) == n_key, 1.0, 0.0
        ).astype(jnp.bfloat16)
        acc_ref[...] += lax.dot_general(
            lhs, one_hot, (((1,), (1,)), ((), ())), preferred_element_type=jnp.float32
        )
        return carry

    lax.fori_loop(0, chunks, body, 0)
    for comp in range(10):
        for level in range(16):
            rows = pl.ds((comp * SPLITS) * M_ROWS + (level >> 2) * 8, 8)
            lanes = pl.ds((level & 3) * 128, 128)
            total = acc_ref[rows, lanes]
            for s in range(1, SPLITS):
                total = total + acc_ref[pl.ds((comp * SPLITS + s) * M_ROWS + (level >> 2) * 8, 8), lanes]
            out_ref[comp, level] = total
            if comp in X_PARTS:
                slot = X_PARTS.index(comp)
                xlo_ref[slot, pl.ds(level, 1), :] = total[0:1, :]
                xhi_ref[slot, pl.ds(level, 1), :] = total[7:8, :]
            if comp in Y_PARTS:
                slot = Y_PARTS.index(comp)
                turned = total.T
                ylo_ref[slot, pl.ds(level, 1), :] = turned[0:1, :]
                yhi_ref[slot, pl.ds(level, 1), :] = turned[127:128, :]
            if comp in Z_PARTS:
                slot = Z_PARTS.index(comp)
                if level == 0:
                    zlo_ref[slot] = total
                if level == 15:
                    zhi_ref[slot] = total


def cell_sums_of(stress_trial, mean_stress, consolidation, point_velocity, point_weight, point_cell, yield_flag, point_count, levels, extent, breadth):
    n = mean_stress.shape[0]
    row = lambda a: a.reshape(1, n)
    vmem = pl.BlockSpec(memory_space=pltpu.VMEM)
    return pl.pallas_call(
        sums_kernel,
        out_shape=[
            jax.ShapeDtypeStruct(s, jnp.float32)
            for s in [(10, levels, extent, breadth)] + [(3, levels, breadth)] * 2 + [(3, levels, extent)] * 2
            + [(3, extent, breadth)] * 2
        ],
        in_specs=[pl.BlockSpec(memory_space=pltpu.SMEM)] + [vmem] * 7,
        out_specs=[vmem] * 7,
        scratch_shapes=[pltpu.VMEM((10 * SPLITS * M_ROWS, N_COLS), jnp.float32)],
        cost_estimate=pl.CostEstimate(
            flops=2 * 10 * SPLITS * M_ROWS * N_COLS * n, bytes_accessed=13 * 4 * n + 10 * 4 * levels * extent * breadth,
            transcendentals=3 * n,
        ),
    )(
        point_count.reshape(1, 1), stress_trial, row(mean_stress), row(consolidation), point_velocity,
        row(point_weight), row(point_cell), row(yield_flag),
    )


def padded_2(cells, sides, width):
    for axis, dim in sides:
        count = lax.axis_size(axis)
        ends = count - 1
        head = lax.slice_in_dim(cells, 0, width, axis=dim)
        tail = lax.slice_in_dim(cells, cells.shape[dim] - width, cells.shape[dim], axis=dim)
        cells = jnp.concatenate(
            [
                lax.ppermute(tail, axis, [(i, (i + 1) % count) for i in range(ends)]),
                cells,
                lax.ppermute(head, axis, [((i + 1) % count, i) for i in range(ends)]),
            ],
            axis=dim,
        )
    return cells


def along_x(padded):
    return (padded[..., 1:-1, 2:, 1:-1] - padded[..., 1:-1, :-2, 1:-1]) * 0.5


def along_y(padded):
    return (padded[..., 1:-1, 1:-1, 2:] - padded[..., 1:-1, 1:-1, :-2]) * 0.5


def along_z(padded):
    return (padded[..., 2:, 1:-1, 1:-1] - padded[..., :-2, 1:-1, 1:-1]) * 0.5


def harmonic(former, latter):
    return 2.0 * former * latter / (former + latter)


def returned_stress(stress_trial, mean_stress, consolidation, yield_flag):
    sq_normal = (
        stress_trial[0] * stress_trial[0]
        + stress_trial[1] * stress_trial[1]
        + stress_trial[2] * stress_trial[2]
    )
    sq_shear = (
        stress_trial[3] * stress_trial[3]
        + stress_trial[4] * stress_trial[4]
        + stress_trial[5] * stress_trial[5]
    )
    shear_size = jnp.sqrt(1.5 * (sq_normal + 2.0 * sq_shear))
    yield_size = critical_slope * jnp.sqrt(mean_stress * (consolidation - mean_stress))
    factor = jnp.where(yield_flag == 1, yield_size / jnp.maximum(shear_size, shear_floor), 1.0)
    isotropic = jnp.array([1.0, 1.0, 1.0, 0.0, 0.0, 0.0], dtype=jnp.float32)[:, None]
    return stress_trial * factor - isotropic * mean_stress


def point_sums(stress, point_velocity, weight, cell_index, segments):
    stacked = jnp.concatenate([stress * weight, point_velocity * weight, weight[None]], axis=0)
    return jax.vmap(
        lambda component: jax.ops.segment_sum(component, cell_index, num_segments=segments)
    )(stacked)


def brick_velocity(cell_sums, padded):
    floored = jnp.maximum(cell_sums[9], mass_floor)
    force_x = along_x(padded[0]) + along_y(padded[3]) + along_z(padded[5])
    force_y = along_x(padded[3]) + along_y(padded[1]) + along_z(padded[4])
    force_z = along_x(padded[5]) + along_y(padded[4]) + along_z(padded[2])
    return jnp.stack(
        [
            (cell_sums[6] + time_step * force_x) / floored,
            (cell_sums[7] + time_step * force_y) / floored,
            (cell_sums[8] + time_step * force_z) / floored,
        ]
    )


def divergence(padded_velocity):
    return along_x(padded_velocity[0]) + along_y(padded_velocity[1]) + along_z(padded_velocity[2])


def band_terms(porosity, permeability, level_below, level_above, at_top, dilation):
    up_face = harmonic(permeability, level_above)
    down_face = harmonic(level_below, permeability)
    top_face = jnp.where(at_top, permeability, up_face)
    lower_band = -time_step * down_face
    upper_band = -time_step * up_face
    main_band = storage_rate * porosity + time_step * (down_face + top_face)
    right_side = -source_rate * (1.0 - porosity) * dilation
    return (lower_band, main_band, upper_band, right_side)


def earlier(values, stride, filler):
    head = jnp.full((stride,) + values.shape[1:], filler, values.dtype)
    return jnp.concatenate([head, values[:-stride]], axis=0)


def later(values, stride, filler):
    tail = jnp.full((stride,) + values.shape[1:], filler, values.dtype)
    return jnp.concatenate([values[stride:], tail], axis=0)


def cyclic_solve(lower_band, main_band, upper_band, right_side):
    length = main_band.shape[0]
    for bit in range((length - 1).bit_length()):
        stride = 1 << bit
        back_weight = -lower_band / earlier(main_band, stride, 1.0)
        ahead_weight = -upper_band / later(main_band, stride, 1.0)
        new_lower = back_weight * earlier(lower_band, stride, 0.0)
        new_upper = ahead_weight * later(upper_band, stride, 0.0)
        new_main = (
            main_band
            + back_weight * earlier(upper_band, stride, 0.0)
            + ahead_weight * later(lower_band, stride, 0.0)
        )
        new_right = (
            right_side
            + back_weight * earlier(right_side, stride, 0.0)
            + ahead_weight * later(right_side, stride, 0.0)
        )
        lower_band, main_band, upper_band, right_side = (new_lower, new_main, new_upper, new_right)
    return right_side / main_band


MESH_AXES = ("gx", "gy", "gz")


def halo_kernel(sides, sizes, gathered, group, *refs):
    count = len(sides)
    sends = refs[:2 * count]
    gins = refs[2 * count:2 * count + gathered]
    recvs = refs[2 * count + gathered:4 * count + gathered]
    gouts = refs[4 * count + gathered:4 * count + 2 * gathered]
    send_sem, recv_sem, gsend_sem, grecv_sem = refs[4 * count + 2 * gathered:]
    me = {a: lax.axis_index(a) for a in MESH_AXES}

    def peer(axis, delta):
        return tuple(me[a] + delta if a == axis else me[a] for a in MESH_AXES)

    def across(level):
        return tuple(level if a == "gz" else me[a] for a in MESH_AXES)

    links = []
    for i, axis in enumerate(sides):
        links.append((axis, -1, me[axis] > 0, 2 * i, 2 * i + 1))
        links.append((axis, 1, me[axis] < sizes[i] - 1, 2 * i + 1, 2 * i))
    barrier = pltpu.get_barrier_semaphore()
    peers = 0
    for axis, delta, present, _, _ in links:
        if gathered and axis == "gz":
            continue
        peers = peers + present.astype(jnp.int32)

        @pl.when(present)
        def _():
            pl.semaphore_signal(barrier, 1, device_id=peer(axis, delta), device_id_type=pl.DeviceIdType.MESH)
    if gathered:
        for d in range(1, group):
            pl.semaphore_signal(
                barrier, 1, device_id=across(lax.rem(me["gz"] + d, group)), device_id_type=pl.DeviceIdType.MESH
            )
        peers = peers + (group - 1)
    pl.semaphore_wait(barrier, peers)
    copies = []
    for axis, delta, present, src, dst in links:
        copy = pltpu.make_async_remote_copy(
            src_ref=sends[src], dst_ref=recvs[dst], send_sem=send_sem.at[src], recv_sem=recv_sem.at[dst],
            device_id=peer(axis, delta), device_id_type=pl.DeviceIdType.MESH,
        )
        copies.append((present, copy))

        @pl.when(present)
        def _():
            copy.start()
    gcopies = []
    for j in range(gathered):
        for d in range(1, group):
            slot = j * (group - 1) + d - 1
            copy = pltpu.make_async_remote_copy(
                src_ref=gins[j], dst_ref=gouts[j].at[me["gz"]], send_sem=gsend_sem.at[slot],
                recv_sem=grecv_sem.at[slot], device_id=across(lax.rem(me["gz"] + d, group)),
                device_id_type=pl.DeviceIdType.MESH,
            )
            copy.start()
            gcopies.append(copy)
    for j in range(gathered):
        gouts[j][me["gz"]] = gins[j][...]
    for axis, delta, present, src, dst in links:
        incoming = pltpu.make_async_remote_copy(
            src_ref=sends[dst], dst_ref=recvs[src], send_sem=send_sem.at[dst], recv_sem=recv_sem.at[src],
            device_id=peer(axis, delta), device_id_type=pl.DeviceIdType.MESH,
        )

        @pl.when(present)
        def _():
            incoming.wait_recv()

        @pl.when(jnp.logical_not(present))
        def _():
            recvs[src][...] = jnp.zeros(recvs[src].shape, recvs[src].dtype)
    for j in range(gathered):
        for d in range(1, group):
            slot = j * (group - 1) + d - 1
            origin = lax.rem(me["gz"] + group - d, group)
            incoming = pltpu.make_async_remote_copy(
                src_ref=gins[j], dst_ref=gouts[j].at[origin], send_sem=gsend_sem.at[slot],
                recv_sem=grecv_sem.at[slot], device_id=across(origin), device_id_type=pl.DeviceIdType.MESH,
            )
            incoming.wait_recv()
    for present, copy in copies:
        @pl.when(present)
        def _():
            copy.wait_send()
    for copy in gcopies:
        copy.wait_send()


def exchange(cells, sides, collective, gathers=(), given=None):
    sends = []
    for axis, dim in sides:
        size = cells.shape[dim]
        sends.append(lax.index_in_dim(cells, 0, axis=dim, keepdims=False))
        sends.append(lax.index_in_dim(cells, size - 1, axis=dim, keepdims=False))
    if given is not None:
        sends = list(given)
    axes = tuple(axis for axis, _ in sides)
    sizes = tuple(lax.axis_size(axis) for axis in axes)
    group = lax.axis_size("gz")
    vmem = pl.BlockSpec(memory_space=pltpu.VMEM)
    slots = max(1, len(gathers) * (group - 1))
    outs = pl.pallas_call(
        functools.partial(halo_kernel, axes, sizes, len(gathers), group),
        out_shape=[jax.ShapeDtypeStruct(s.shape, s.dtype) for s in sends]
        + [jax.ShapeDtypeStruct((group,) + g.shape, g.dtype) for g in gathers],
        in_specs=[vmem] * (len(sends) + len(gathers)),
        out_specs=[vmem] * (len(sends) + len(gathers)),
        scratch_shapes=[
            pltpu.SemaphoreType.DMA((max(1, len(sends)),)), pltpu.SemaphoreType.DMA((max(1, len(sends)),)),
            pltpu.SemaphoreType.DMA((slots,)), pltpu.SemaphoreType.DMA((slots,)),
        ],
        compiler_params=pltpu.CompilerParams(collective_id=collective, has_side_effects=True),
    )(*sends, *gathers)
    recvs = outs[:len(sends)]
    faces = {
        dim: (jnp.expand_dims(recvs[2 * i], dim), jnp.expand_dims(recvs[2 * i + 1], dim))
        for i, (axis, dim) in enumerate(sides)
    }
    stacked = [g.reshape((group * g.shape[1],) + g.shape[2:]) for g in outs[len(sends):]]
    return faces, stacked


def faces_kernel(parts, cells_ref, *out_refs):
    chans, levels, extent, breadth = cells_ref.shape
    xlo, xhi, ylo, yhi = out_refs[:4]
    for slot, c in enumerate(parts[0]):
        for level in range(levels):
            tile = cells_ref[c, level]
            xlo[slot, pl.ds(level, 1), :] = tile[0:1, :]
            xhi[slot, pl.ds(level, 1), :] = tile[extent - 1:extent, :]
    for slot, c in enumerate(parts[1]):
        for level in range(levels):
            turned = cells_ref[c, level].T
            ylo[slot, pl.ds(level, 1), :] = turned[0:1, :]
            yhi[slot, pl.ds(level, 1), :] = turned[breadth - 1:breadth, :]
    if len(parts) > 2:
        for slot, c in enumerate(parts[2]):
            out_refs[4][slot] = cells_ref[c, 0]
            out_refs[5][slot] = cells_ref[c, levels - 1]


def faces_by_kernel(cells, parts):
    chans, levels, extent, breadth = cells.shape
    shapes = [(len(parts[0]), levels, breadth)] * 2 + [(len(parts[1]), levels, extent)] * 2
    if len(parts) > 2:
        shapes += [(len(parts[2]), extent, breadth)] * 2
    vmem = pl.BlockSpec(memory_space=pltpu.VMEM)
    return pl.pallas_call(
        functools.partial(faces_kernel, parts),
        out_shape=[jax.ShapeDtypeStruct(s, cells.dtype) for s in shapes],
        in_specs=[vmem],
        out_specs=[vmem] * len(shapes),
    )(cells)


def solve_kernel(levels, poro_ref, perm_ref, right_ref, out_ref, grad_ref, xlo, xhi, ylo, yhi, padded_ref):
    perm = perm_ref[...]
    lid = jnp.zeros((1,) + perm.shape[1:], jnp.float32)
    level_above = jnp.concatenate([perm[1:], lid], axis=0)
    level_below = jnp.concatenate([lid, perm[:-1]], axis=0)
    up_face = harmonic(perm, level_above)
    down_face = harmonic(level_below, perm)
    top_face = jnp.concatenate([up_face[:-1], perm[-1:]], axis=0)
    lower_band = -time_step * down_face
    upper_band = -time_step * up_face
    main_band = storage_rate * poro_ref[...] + time_step * (down_face + top_face)
    solved = cyclic_solve(lower_band, main_band, upper_band, right_ref[...])
    height, extent, breadth = solved.shape
    padded_ref[pl.ds(0, 1)] = lid
    padded_ref[pl.ds(height + 1, 1)] = lid
    padded_ref[pl.ds(1, height)] = solved
    first = lax.axis_index("gz") * levels
    out_ref[...] = padded_ref[pl.ds(first + 1, levels)]
    grad_ref[...] = (padded_ref[pl.ds(first + 2, levels)] - padded_ref[pl.ds(first, levels)]) * 0.5
    for level in range(levels):
        tile = out_ref[level]
        xlo[pl.ds(level, 1), :] = tile[0:1, :]
        xhi[pl.ds(level, 1), :] = tile[extent - 1:extent, :]
        turned = tile.T
        ylo[pl.ds(level, 1), :] = turned[0:1, :]
        yhi[pl.ds(level, 1), :] = turned[breadth - 1:breadth, :]


def column_solve(porosity, permeability, right_side, levels):
    height, extent, breadth = right_side.shape
    vmem = pl.BlockSpec(memory_space=pltpu.VMEM)
    shapes = [(levels, extent, breadth)] * 2 + [(levels, breadth)] * 2 + [(levels, extent)] * 2
    return pl.pallas_call(
        functools.partial(solve_kernel, levels),
        out_shape=[jax.ShapeDtypeStruct(s, jnp.float32) for s in shapes],
        in_specs=[vmem] * 3,
        out_specs=[vmem] * len(shapes),
        scratch_shapes=[pltpu.VMEM((height + 2, extent, breadth), jnp.float32)],
    )(porosity, permeability, right_side)


def face_from(part, axis, from_lower):
    count = lax.axis_size(axis)
    if from_lower:
        pairs = [(i, i + 1) for i in range(count - 1)]
    else:
        pairs = [(i + 1, i) for i in range(count - 1)]
    return lax.ppermute(part, axis, pairs)


def faces_of(cells, sides):
    got = {}
    for axis, dim in sides:
        size = cells.shape[dim]
        got[dim] = (
            face_from(lax.slice_in_dim(cells, size - 1, size, axis=dim), axis, True),
            face_from(lax.slice_in_dim(cells, 0, 1, axis=dim), axis, False),
        )
    return got


def along(cells, faces, dim):
    size = cells.shape[dim]
    lower, upper = faces[dim]
    ahead = jnp.concatenate([lax.slice_in_dim(cells, 1, size, axis=dim), upper], axis=dim)
    behind = jnp.concatenate([lower, lax.slice_in_dim(cells, 0, size - 1, axis=dim)], axis=dim)
    return (ahead - behind) * 0.5


def shards(
    stress_trial,
    mean_stress,
    consolidation,
    point_velocity,
    point_weight,
    point_cell,
    yield_flag,
    point_count,
    porosity,
    permeability,
):
    levels, extent, breadth = porosity.shape
    cell_sums, *stress_faces = cell_sums_of(
        stress_trial, mean_stress, consolidation, point_velocity, point_weight, point_cell,
        yield_flag, point_count, levels, extent, breadth,
    )
    sides = (("gx", 2), ("gy", 3), ("gz", 1))
    stress_sums = cell_sums[:6]
    sf, (all_porosity, all_permeability) = exchange(
        stress_sums, sides, 0, (porosity, permeability), given=stress_faces
    )
    height = all_porosity.shape[0]
    def part(dim, parts, c):
        s = parts.index(c)
        return {dim: (sf[dim][0][s:s + 1], sf[dim][1][s:s + 1])}

    d_x = lambda c: along(stress_sums[c:c + 1], part(2, X_PARTS, c), 2)[0]
    d_y = lambda c: along(stress_sums[c:c + 1], part(3, Y_PARTS, c), 3)[0]
    d_z = lambda c: along(stress_sums[c:c + 1], part(1, Z_PARTS, c), 1)[0]
    floored = jnp.maximum(cell_sums[9], mass_floor)
    force_x = d_x(0) + d_y(3) + d_z(5)
    force_y = d_x(3) + d_y(1) + d_z(4)
    force_z = d_x(5) + d_y(4) + d_z(2)
    velocity = jnp.stack(
        [
            (cell_sums[6] + time_step * force_x) / floored,
            (cell_sums[7] + time_step * force_y) / floored,
            (cell_sums[8] + time_step * force_z) / floored,
        ]
    )
    vf, _ = exchange(velocity, sides, 1, given=faces_by_kernel(velocity, ((0,), (1,), (2,))))
    dilation = (
        along(velocity[0:1], {2: vf[2]}, 2)[0]
        + along(velocity[1:2], {3: vf[3]}, 3)[0]
        + along(velocity[2:3], {1: vf[1]}, 1)[0]
    )
    right_side = -source_rate * (1.0 - porosity) * dilation
    _, (all_right,) = exchange(right_side, (), 3, (right_side,))
    zero_level = jnp.zeros((1, extent, breadth), jnp.float32)
    pressure, rise, *pressure_faces = column_solve(all_porosity, all_permeability, all_right, levels)
    pf, _ = exchange(pressure, (("gx", 1), ("gy", 2)), 2, given=pressure_faces)
    gradient = jnp.stack([along(pressure, pf, 1), along(pressure, pf, 2), rise])
    return (velocity - time_step * gradient, pressure)


def solution(mesh):
    placed = (
        P(None, ("gx", "gy", "gz")),
        P(("gx", "gy", "gz")),
        P(("gx", "gy", "gz")),
        P(None, ("gx", "gy", "gz")),
        P(("gx", "gy", "gz")),
        P(("gx", "gy", "gz")),
        P(("gx", "gy", "gz")),
        P("gx", "gy", "gz"),
        P("gz", "gx", "gy"),
        P("gz", "gx", "gy"),
    )
    return jax.shard_map(
        shards,
        mesh=mesh,
        in_specs=placed,
        out_specs=(P(None, "gz", "gx", "gy"), P("gz", "gx", "gy")),
        check_vma=False,
    )
```

```python
import functools

import jax
import jax.numpy as jnp
from jax import lax
from jax.sharding import PartitionSpec as P

time_step = 0.25
storage_rate = 0.002
source_rate = 0.003
critical_slope = 1.2
mass_floor = 0.5
shear_floor = 1.0

from jax.experimental import pallas as pl
from jax.experimental.pallas import tpu as pltpu

CHUNK = 12288
M_ROWS = 32
N_COLS = 512


SPLITS = 2
X_PARTS = (0, 3, 5)
Y_PARTS = (3, 1, 4)
Z_PARTS = (5, 4, 2)


def _split(v):
    hi = v.astype(jnp.bfloat16)
    lo = (v - hi.astype(jnp.float32)).astype(jnp.bfloat16)
    return [hi, lo]


def sums_kernel(count_ref, st_ref, ms_ref, cons_ref, vel_ref, w_ref, cell_ref, yf_ref, out_ref, xlo_ref, xhi_ref, ylo_ref, yhi_ref, zlo_ref, zhi_ref, acc_ref):
    count = count_ref[0, 0]
    acc_ref[...] = jnp.zeros_like(acc_ref)
    chunks = st_ref.shape[1] // CHUNK

    def body(k, carry):
        start = pl.multiple_of(k * CHUNK, CHUNK)
        span = pl.ds(start, CHUNK)
        st = [st_ref[pl.ds(i, 1), span] for i in range(6)]
        ms = ms_ref[:, span]
        cons = cons_ref[:, span]
        yf = yf_ref[:, span]
        slot = start + lax.broadcasted_iota(jnp.int32, (1, CHUNK), 1)
        weight = jnp.where(slot < count, w_ref[:, span], 0.0)
        sq_normal = st[0] * st[0] + st[1] * st[1] + st[2] * st[2]
        sq_shear = st[3] * st[3] + st[4] * st[4] + st[5] * st[5]
        shear_size = jnp.sqrt(1.5 * (sq_normal + 2.0 * sq_shear))
        yield_size = critical_slope * jnp.sqrt(ms * (cons - ms))
        factor = jnp.where(yf == 1, yield_size / jnp.maximum(shear_size, shear_floor), 1.0)
        stress = [st[i] * factor - ms if i < 3 else st[i] * factor for i in range(6)]
        values = [s * weight for s in stress]
        values += [vel_ref[pl.ds(i, 1), span] * weight for i in range(3)]
        values.append(weight)
        cell = cell_ref[:, span]
        m_key = (cell >> 12) * 8 + ((cell >> 7) & 7)
        n_key = ((cell >> 10) & 3) * 128 + (cell & 127)
        m_mask = lax.broadcasted_iota(jnp.int32, (M_ROWS, CHUNK), 0) == m_key
        zero = jnp.zeros((M_ROWS, CHUNK), jnp.bfloat16)
        pieces = []
        for v in values:
            for part in _split(v):
                pieces.append(jnp.where(m_mask, jnp.broadcast_to(part, (M_ROWS, CHUNK)), zero))
        lhs = jnp.concatenate(pieces, axis=0)
        one_hot = jnp.where(
            lax.broadcasted_iota(jnp.int32, (N_COLS, CHUNK), 0) == n_key, 1.0, 0.0
        ).astype(jnp.bfloat16)
        acc_ref[...] += lax.dot_general(
            lhs, one_hot, (((1,), (1,)), ((), ())), preferred_element_type=jnp.float32
        )
        return carry

    lax.fori_loop(0, chunks, body, 0)
    for comp in range(10):
        for level in range(16):
            rows = pl.ds((comp * SPLITS) * M_ROWS + (level >> 2) * 8, 8)
            lanes = pl.ds((level & 3) * 128, 128)
            total = acc_ref[rows, lanes]
            for s in range(1, SPLITS):
                total = total + acc_ref[pl.ds((comp * SPLITS + s) * M_ROWS + (level >> 2) * 8, 8), lanes]
            out_ref[comp, level] = total
            if comp in X_PARTS:
                slot = X_PARTS.index(comp)
                xlo_ref[slot, pl.ds(level, 1), :] = total[0:1, :]
                xhi_ref[slot, pl.ds(level, 1), :] = total[7:8, :]
            if comp in Y_PARTS:
                slot = Y_PARTS.index(comp)
                turned = total.T
                ylo_ref[slot, pl.ds(level, 1), :] = turned[0:1, :]
                yhi_ref[slot, pl.ds(level, 1), :] = turned[127:128, :]
            if comp in Z_PARTS:
                slot = Z_PARTS.index(comp)
                if level == 0:
                    zlo_ref[slot] = total
                if level == 15:
                    zhi_ref[slot] = total


def cell_sums_of(stress_trial, mean_stress, consolidation, point_velocity, point_weight, point_cell, yield_flag, point_count, levels, extent, breadth):
    n = mean_stress.shape[0]
    row = lambda a: a.reshape(1, n)
    vmem = pl.BlockSpec(memory_space=pltpu.VMEM)
    return pl.pallas_call(
        sums_kernel,
        out_shape=[
            jax.ShapeDtypeStruct(s, jnp.float32)
            for s in [(10, levels, extent, breadth)] + [(3, levels, breadth)] * 2 + [(3, levels, extent)] * 2
            + [(3, extent, breadth)] * 2
        ],
        in_specs=[pl.BlockSpec(memory_space=pltpu.SMEM)] + [vmem] * 7,
        out_specs=[vmem] * 7,
        scratch_shapes=[pltpu.VMEM((10 * SPLITS * M_ROWS, N_COLS), jnp.float32)],
        cost_estimate=pl.CostEstimate(
            flops=2 * 10 * SPLITS * M_ROWS * N_COLS * n, bytes_accessed=13 * 4 * n + 10 * 4 * levels * extent * breadth,
            transcendentals=3 * n,
        ),
    )(
        point_count.reshape(1, 1), stress_trial, row(mean_stress), row(consolidation), point_velocity,
        row(point_weight), row(point_cell), row(yield_flag),
    )


def padded_2(cells, sides, width):
    for axis, dim in sides:
        count = lax.axis_size(axis)
        ends = count - 1
        head = lax.slice_in_dim(cells, 0, width, axis=dim)
        tail = lax.slice_in_dim(cells, cells.shape[dim] - width, cells.shape[dim], axis=dim)
        cells = jnp.concatenate(
            [
                lax.ppermute(tail, axis, [(i, (i + 1) % count) for i in range(ends)]),
                cells,
                lax.ppermute(head, axis, [((i + 1) % count, i) for i in range(ends)]),
            ],
            axis=dim,
        )
    return cells


def along_x(padded):
    return (padded[..., 1:-1, 2:, 1:-1] - padded[..., 1:-1, :-2, 1:-1]) * 0.5


def along_y(padded):
    return (padded[..., 1:-1, 1:-1, 2:] - padded[..., 1:-1, 1:-1, :-2]) * 0.5


def along_z(padded):
    return (padded[..., 2:, 1:-1, 1:-1] - padded[..., :-2, 1:-1, 1:-1]) * 0.5


def harmonic(former, latter):
    return 2.0 * former * latter / (former + latter)


def returned_stress(stress_trial, mean_stress, consolidation, yield_flag):
    sq_normal = (
        stress_trial[0] * stress_trial[0]
        + stress_trial[1] * stress_trial[1]
        + stress_trial[2] * stress_trial[2]
    )
    sq_shear = (
        stress_trial[3] * stress_trial[3]
        + stress_trial[4] * stress_trial[4]
        + stress_trial[5] * stress_trial[5]
    )
    shear_size = jnp.sqrt(1.5 * (sq_normal + 2.0 * sq_shear))
    yield_size = critical_slope * jnp.sqrt(mean_stress * (consolidation - mean_stress))
    factor = jnp.where(yield_flag == 1, yield_size / jnp.maximum(shear_size, shear_floor), 1.0)
    isotropic = jnp.array([1.0, 1.0, 1.0, 0.0, 0.0, 0.0], dtype=jnp.float32)[:, None]
    return stress_trial * factor - isotropic * mean_stress


def point_sums(stress, point_velocity, weight, cell_index, segments):
    stacked = jnp.concatenate([stress * weight, point_velocity * weight, weight[None]], axis=0)
    return jax.vmap(
        lambda component: jax.ops.segment_sum(component, cell_index, num_segments=segments)
    )(stacked)


def brick_velocity(cell_sums, padded):
    floored = jnp.maximum(cell_sums[9], mass_floor)
    force_x = along_x(padded[0]) + along_y(padded[3]) + along_z(padded[5])
    force_y = along_x(padded[3]) + along_y(padded[1]) + along_z(padded[4])
    force_z = along_x(padded[5]) + along_y(padded[4]) + along_z(padded[2])
    return jnp.stack(
        [
            (cell_sums[6] + time_step * force_x) / floored,
            (cell_sums[7] + time_step * force_y) / floored,
            (cell_sums[8] + time_step * force_z) / floored,
        ]
    )


def divergence(padded_velocity):
    return along_x(padded_velocity[0]) + along_y(padded_velocity[1]) + along_z(padded_velocity[2])


def band_terms(porosity, permeability, level_below, level_above, at_top, dilation):
    up_face = harmonic(permeability, level_above)
    down_face = harmonic(level_below, permeability)
    top_face = jnp.where(at_top, permeability, up_face)
    lower_band = -time_step * down_face
    upper_band = -time_step * up_face
    main_band = storage_rate * porosity + time_step * (down_face + top_face)
    right_side = -source_rate * (1.0 - porosity) * dilation
    return (lower_band, main_band, upper_band, right_side)


def earlier(values, stride, filler):
    head = jnp.full((stride,) + values.shape[1:], filler, values.dtype)
    return jnp.concatenate([head, values[:-stride]], axis=0)


def later(values, stride, filler):
    tail = jnp.full((stride,) + values.shape[1:], filler, values.dtype)
    return jnp.concatenate([values[stride:], tail], axis=0)


def cyclic_solve(lower_band, main_band, upper_band, right_side):
    length = main_band.shape[0]
    for bit in range((length - 1).bit_length()):
        stride = 1 << bit
        back_weight = -lower_band / earlier(main_band, stride, 1.0)
        ahead_weight = -upper_band / later(main_band, stride, 1.0)
        new_lower = back_weight * earlier(lower_band, stride, 0.0)
        new_upper = ahead_weight * later(upper_band, stride, 0.0)
        new_main = (
            main_band
            + back_weight * earlier(upper_band, stride, 0.0)
            + ahead_weight * later(lower_band, stride, 0.0)
        )
        new_right = (
            right_side
            + back_weight * earlier(right_side, stride, 0.0)
            + ahead_weight * later(right_side, stride, 0.0)
        )
        lower_band, main_band, upper_band, right_side = (new_lower, new_main, new_upper, new_right)
    return right_side / main_band


MESH_AXES = ("gx", "gy", "gz")


def halo_kernel(sides, sizes, gathered, group, *refs):
    count = len(sides)
    sends = refs[:2 * count]
    gins = refs[2 * count:2 * count + gathered]
    recvs = refs[2 * count + gathered:4 * count + gathered]
    gouts = refs[4 * count + gathered:4 * count + 2 * gathered]
    send_sem, recv_sem, gsend_sem, grecv_sem = refs[4 * count + 2 * gathered:]
    me = {a: lax.axis_index(a) for a in MESH_AXES}

    def peer(axis, delta):
        return tuple(me[a] + delta if a == axis else me[a] for a in MESH_AXES)

    def across(level):
        return tuple(level if a == "gz" else me[a] for a in MESH_AXES)

    links = []
    for i, axis in enumerate(sides):
        links.append((axis, -1, me[axis] > 0, 2 * i, 2 * i + 1))
        links.append((axis, 1, me[axis] < sizes[i] - 1, 2 * i + 1, 2 * i))
    barrier = pltpu.get_barrier_semaphore()
    peers = 0
    k = me["gz"]
    partner = (k // 2) * 2 + (1 - k % 2)
    counterpart = (1 - k // 2) * 2 + k % 2
    diagonal = (1 - k // 2) * 2 + (1 - k % 2)
    for axis, delta, present, _, _ in links:
        if gathered and axis == "gz":
            present = jnp.logical_and(present, k + delta == diagonal)
        peers = peers + present.astype(jnp.int32)

        @pl.when(present)
        def _():
            pl.semaphore_signal(barrier, 1, device_id=peer(axis, delta), device_id_type=pl.DeviceIdType.MESH)
    if gathered:
        for target in (partner, counterpart):
            pl.semaphore_signal(barrier, 1, device_id=across(target), device_id_type=pl.DeviceIdType.MESH)
        peers = peers + 2
    pl.semaphore_wait(barrier, peers)
    copies = []
    for axis, delta, present, src, dst in links:
        copy = pltpu.make_async_remote_copy(
            src_ref=sends[src], dst_ref=recvs[dst], send_sem=send_sem.at[src], recv_sem=recv_sem.at[dst],
            device_id=peer(axis, delta), device_id_type=pl.DeviceIdType.MESH,
        )
        copies.append((present, copy))

        @pl.when(present)
        def _():
            copy.start()
    gcopies = []
    for j in range(gathered):
        for n, target in enumerate((partner, counterpart)):
            copy = pltpu.make_async_remote_copy(
                src_ref=gins[j], dst_ref=gouts[j].at[k], send_sem=gsend_sem.at[3 * j + n],
                recv_sem=grecv_sem.at[3 * j + n], device_id=across(target), device_id_type=pl.DeviceIdType.MESH,
            )
            copy.start()
            gcopies.append(copy)
    for j in range(gathered):
        gouts[j][k] = gins[j][...]
    for j in range(gathered):
        for n, origin in enumerate((partner, counterpart)):
            incoming = pltpu.make_async_remote_copy(
                src_ref=gins[j], dst_ref=gouts[j].at[origin], send_sem=gsend_sem.at[3 * j + n],
                recv_sem=grecv_sem.at[3 * j + n], device_id=across(origin), device_id_type=pl.DeviceIdType.MESH,
            )
            incoming.wait_recv()
        relay = pltpu.make_async_remote_copy(
            src_ref=gouts[j].at[counterpart], dst_ref=gouts[j].at[counterpart], send_sem=gsend_sem.at[3 * j + 2],
            recv_sem=grecv_sem.at[3 * j + 2], device_id=across(partner), device_id_type=pl.DeviceIdType.MESH,
        )
        relay.start()
        gcopies.append(relay)
    for j in range(gathered):
        relayed = pltpu.make_async_remote_copy(
            src_ref=gouts[j].at[diagonal], dst_ref=gouts[j].at[diagonal], send_sem=gsend_sem.at[3 * j + 2],
            recv_sem=grecv_sem.at[3 * j + 2], device_id=across(partner), device_id_type=pl.DeviceIdType.MESH,
        )
        relayed.wait_recv()
    for axis, delta, present, src, dst in links:
        incoming = pltpu.make_async_remote_copy(
            src_ref=sends[dst], dst_ref=recvs[src], send_sem=send_sem.at[dst], recv_sem=recv_sem.at[src],
            device_id=peer(axis, delta), device_id_type=pl.DeviceIdType.MESH,
        )

        @pl.when(present)
        def _():
            incoming.wait_recv()

        @pl.when(jnp.logical_not(present))
        def _():
            recvs[src][...] = jnp.zeros(recvs[src].shape, recvs[src].dtype)
    for present, copy in copies:
        @pl.when(present)
        def _():
            copy.wait_send()
    for copy in gcopies:
        copy.wait_send()


def exchange(cells, sides, collective, gathers=(), given=None):
    sends = []
    for axis, dim in sides:
        size = cells.shape[dim]
        sends.append(lax.index_in_dim(cells, 0, axis=dim, keepdims=False))
        sends.append(lax.index_in_dim(cells, size - 1, axis=dim, keepdims=False))
    if given is not None:
        sends = list(given)
    axes = tuple(axis for axis, _ in sides)
    sizes = tuple(lax.axis_size(axis) for axis in axes)
    group = lax.axis_size("gz")
    vmem = pl.BlockSpec(memory_space=pltpu.VMEM)
    assert group == 4 or not gathers
    slots = max(1, len(gathers) * (group - 1))
    outs = pl.pallas_call(
        functools.partial(halo_kernel, axes, sizes, len(gathers), group),
        out_shape=[jax.ShapeDtypeStruct(s.shape, s.dtype) for s in sends]
        + [jax.ShapeDtypeStruct((group,) + g.shape, g.dtype) for g in gathers],
        in_specs=[vmem] * (len(sends) + len(gathers)),
        out_specs=[vmem] * (len(sends) + len(gathers)),
        scratch_shapes=[
            pltpu.SemaphoreType.DMA((max(1, len(sends)),)), pltpu.SemaphoreType.DMA((max(1, len(sends)),)),
            pltpu.SemaphoreType.DMA((slots,)), pltpu.SemaphoreType.DMA((slots,)),
        ],
        compiler_params=pltpu.CompilerParams(collective_id=collective, has_side_effects=True),
    )(*sends, *gathers)
    recvs = outs[:len(sends)]
    faces = {
        dim: (jnp.expand_dims(recvs[2 * i], dim), jnp.expand_dims(recvs[2 * i + 1], dim))
        for i, (axis, dim) in enumerate(sides)
    }
    stacked = [g.reshape((group * g.shape[1],) + g.shape[2:]) for g in outs[len(sends):]]
    return faces, stacked


def faces_kernel(parts, cells_ref, *out_refs):
    chans, levels, extent, breadth = cells_ref.shape
    xlo, xhi, ylo, yhi = out_refs[:4]
    for slot, c in enumerate(parts[0]):
        for level in range(levels):
            tile = cells_ref[c, level]
            xlo[slot, pl.ds(level, 1), :] = tile[0:1, :]
            xhi[slot, pl.ds(level, 1), :] = tile[extent - 1:extent, :]
    for slot, c in enumerate(parts[1]):
        for level in range(levels):
            turned = cells_ref[c, level].T
            ylo[slot, pl.ds(level, 1), :] = turned[0:1, :]
            yhi[slot, pl.ds(level, 1), :] = turned[breadth - 1:breadth, :]
    if len(parts) > 2:
        for slot, c in enumerate(parts[2]):
            out_refs[4][slot] = cells_ref[c, 0]
            out_refs[5][slot] = cells_ref[c, levels - 1]


def faces_by_kernel(cells, parts):
    chans, levels, extent, breadth = cells.shape
    shapes = [(len(parts[0]), levels, breadth)] * 2 + [(len(parts[1]), levels, extent)] * 2
    if len(parts) > 2:
        shapes += [(len(parts[2]), extent, breadth)] * 2
    vmem = pl.BlockSpec(memory_space=pltpu.VMEM)
    return pl.pallas_call(
        functools.partial(faces_kernel, parts),
        out_shape=[jax.ShapeDtypeStruct(s, cells.dtype) for s in shapes],
        in_specs=[vmem],
        out_specs=[vmem] * len(shapes),
    )(cells)


def solve_kernel(levels, poro_ref, perm_ref, right_ref, out_ref, grad_ref, xlo, xhi, ylo, yhi, padded_ref):
    perm = perm_ref[...]
    lid = jnp.zeros((1,) + perm.shape[1:], jnp.float32)
    level_above = jnp.concatenate([perm[1:], lid], axis=0)
    level_below = jnp.concatenate([lid, perm[:-1]], axis=0)
    up_face = harmonic(perm, level_above)
    down_face = harmonic(level_below, perm)
    top_face = jnp.concatenate([up_face[:-1], perm[-1:]], axis=0)
    lower_band = -time_step * down_face
    upper_band = -time_step * up_face
    main_band = storage_rate * poro_ref[...] + time_step * (down_face + top_face)
    solved = cyclic_solve(lower_band, main_band, upper_band, right_ref[...])
    height, extent, breadth = solved.shape
    padded_ref[pl.ds(0, 1)] = lid
    padded_ref[pl.ds(height + 1, 1)] = lid
    padded_ref[pl.ds(1, height)] = solved
    first = lax.axis_index("gz") * levels
    out_ref[...] = padded_ref[pl.ds(first + 1, levels)]
    grad_ref[...] = (padded_ref[pl.ds(first + 2, levels)] - padded_ref[pl.ds(first, levels)]) * 0.5
    for level in range(levels):
        tile = out_ref[level]
        xlo[pl.ds(level, 1), :] = tile[0:1, :]
        xhi[pl.ds(level, 1), :] = tile[extent - 1:extent, :]
        turned = tile.T
        ylo[pl.ds(level, 1), :] = turned[0:1, :]
        yhi[pl.ds(level, 1), :] = turned[breadth - 1:breadth, :]


def column_solve(porosity, permeability, right_side, levels):
    height, extent, breadth = right_side.shape
    vmem = pl.BlockSpec(memory_space=pltpu.VMEM)
    shapes = [(levels, extent, breadth)] * 2 + [(levels, breadth)] * 2 + [(levels, extent)] * 2
    return pl.pallas_call(
        functools.partial(solve_kernel, levels),
        out_shape=[jax.ShapeDtypeStruct(s, jnp.float32) for s in shapes],
        in_specs=[vmem] * 3,
        out_specs=[vmem] * len(shapes),
        scratch_shapes=[pltpu.VMEM((height + 2, extent, breadth), jnp.float32)],
    )(porosity, permeability, right_side)


def face_from(part, axis, from_lower):
    count = lax.axis_size(axis)
    if from_lower:
        pairs = [(i, i + 1) for i in range(count - 1)]
    else:
        pairs = [(i + 1, i) for i in range(count - 1)]
    return lax.ppermute(part, axis, pairs)


def faces_of(cells, sides):
    got = {}
    for axis, dim in sides:
        size = cells.shape[dim]
        got[dim] = (
            face_from(lax.slice_in_dim(cells, size - 1, size, axis=dim), axis, True),
            face_from(lax.slice_in_dim(cells, 0, 1, axis=dim), axis, False),
        )
    return got


def along(cells, faces, dim):
    size = cells.shape[dim]
    lower, upper = faces[dim]
    ahead = jnp.concatenate([lax.slice_in_dim(cells, 1, size, axis=dim), upper], axis=dim)
    behind = jnp.concatenate([lower, lax.slice_in_dim(cells, 0, size - 1, axis=dim)], axis=dim)
    return (ahead - behind) * 0.5


def shards(
    stress_trial,
    mean_stress,
    consolidation,
    point_velocity,
    point_weight,
    point_cell,
    yield_flag,
    point_count,
    porosity,
    permeability,
):
    levels, extent, breadth = porosity.shape
    cell_sums, *stress_faces = cell_sums_of(
        stress_trial, mean_stress, consolidation, point_velocity, point_weight, point_cell,
        yield_flag, point_count, levels, extent, breadth,
    )
    sides = (("gx", 2), ("gy", 3), ("gz", 1))
    stress_sums = cell_sums[:6]
    sf, (all_porosity, all_permeability) = exchange(
        stress_sums, sides, 0, (porosity, permeability), given=stress_faces
    )
    height = all_porosity.shape[0]
    def part(dim, parts, c):
        s = parts.index(c)
        return {dim: (sf[dim][0][s:s + 1], sf[dim][1][s:s + 1])}

    d_x = lambda c: along(stress_sums[c:c + 1], part(2, X_PARTS, c), 2)[0]
    d_y = lambda c: along(stress_sums[c:c + 1], part(3, Y_PARTS, c), 3)[0]
    d_z = lambda c: along(stress_sums[c:c + 1], part(1, Z_PARTS, c), 1)[0]
    floored = jnp.maximum(cell_sums[9], mass_floor)
    force_x = d_x(0) + d_y(3) + d_z(5)
    force_y = d_x(3) + d_y(1) + d_z(4)
    force_z = d_x(5) + d_y(4) + d_z(2)
    velocity = jnp.stack(
        [
            (cell_sums[6] + time_step * force_x) / floored,
            (cell_sums[7] + time_step * force_y) / floored,
            (cell_sums[8] + time_step * force_z) / floored,
        ]
    )
    vf, _ = exchange(velocity, sides, 1, given=faces_by_kernel(velocity, ((0,), (1,), (2,))))
    dilation = (
        along(velocity[0:1], {2: vf[2]}, 2)[0]
        + along(velocity[1:2], {3: vf[3]}, 3)[0]
        + along(velocity[2:3], {1: vf[1]}, 1)[0]
    )
    right_side = -source_rate * (1.0 - porosity) * dilation
    _, (all_right,) = exchange(right_side, (), 3, (right_side,))
    zero_level = jnp.zeros((1, extent, breadth), jnp.float32)
    pressure, rise, *pressure_faces = column_solve(all_porosity, all_permeability, all_right, levels)
    pf, _ = exchange(pressure, (("gx", 1), ("gy", 2)), 2, given=pressure_faces)
    gradient = jnp.stack([along(pressure, pf, 1), along(pressure, pf, 2), rise])
    return (velocity - time_step * gradient, pressure)


def solution(mesh):
    placed = (
        P(None, ("gx", "gy", "gz")),
        P(("gx", "gy", "gz")),
        P(("gx", "gy", "gz")),
        P(None, ("gx", "gy", "gz")),
        P(("gx", "gy", "gz")),
        P(("gx", "gy", "gz")),
        P(("gx", "gy", "gz")),
        P("gx", "gy", "gz"),
        P("gz", "gx", "gy"),
        P("gz", "gx", "gy"),
    )
    return jax.shard_map(
        shards,
        mesh=mesh,
        in_specs=placed,
        out_specs=(P(None, "gz", "gx", "gy"), P("gz", "gx", "gy")),
        check_vma=False,
    )
```

```python
import functools

import jax
import jax.numpy as jnp
from jax import lax
from jax.sharding import PartitionSpec as P

time_step = 0.25
storage_rate = 0.002
source_rate = 0.003
critical_slope = 1.2
mass_floor = 0.5
shear_floor = 1.0

from jax.experimental import pallas as pl
from jax.experimental.pallas import tpu as pltpu

CHUNK = 24576
M_ROWS = 32
N_COLS = 512


SPLITS = 2
X_PARTS = (0, 3, 5)
Y_PARTS = (3, 1, 4)
Z_PARTS = (5, 4, 2)


def _split(v):
    hi = v.astype(jnp.bfloat16)
    lo = (v - hi.astype(jnp.float32)).astype(jnp.bfloat16)
    return [hi, lo]


def sums_kernel(count_ref, st_ref, ms_ref, cons_ref, vel_ref, w_ref, cell_ref, yf_ref, out_ref, xlo_ref, xhi_ref, ylo_ref, yhi_ref, zlo_ref, zhi_ref, acc_ref):
    count = count_ref[0, 0]
    acc_ref[...] = jnp.zeros_like(acc_ref)
    chunks = st_ref.shape[1] // CHUNK

    def body(k, carry):
        start = pl.multiple_of(k * CHUNK, CHUNK)
        span = pl.ds(start, CHUNK)
        st = [st_ref[pl.ds(i, 1), span] for i in range(6)]
        ms = ms_ref[:, span]
        cons = cons_ref[:, span]
        yf = yf_ref[:, span]
        slot = start + lax.broadcasted_iota(jnp.int32, (1, CHUNK), 1)
        weight = jnp.where(slot < count, w_ref[:, span], 0.0)
        sq_normal = st[0] * st[0] + st[1] * st[1] + st[2] * st[2]
        sq_shear = st[3] * st[3] + st[4] * st[4] + st[5] * st[5]
        shear_size = jnp.sqrt(1.5 * (sq_normal + 2.0 * sq_shear))
        yield_size = critical_slope * jnp.sqrt(ms * (cons - ms))
        factor = jnp.where(yf == 1, yield_size / jnp.maximum(shear_size, shear_floor), 1.0)
        stress = [st[i] * factor - ms if i < 3 else st[i] * factor for i in range(6)]
        values = [s * weight for s in stress]
        values += [vel_ref[pl.ds(i, 1), span] * weight for i in range(3)]
        values.append(weight)
        cell = cell_ref[:, span]
        m_key = (cell >> 12) * 8 + ((cell >> 7) & 7)
        n_key = ((cell >> 10) & 3) * 128 + (cell & 127)
        m_mask = lax.broadcasted_iota(jnp.int32, (M_ROWS, CHUNK), 0) == m_key
        zero = jnp.zeros((M_ROWS, CHUNK), jnp.bfloat16)
        pieces = []
        for v in values:
            for part in _split(v):
                pieces.append(jnp.where(m_mask, jnp.broadcast_to(part, (M_ROWS, CHUNK)), zero))
        lhs = jnp.concatenate(pieces, axis=0)
        one_hot = jnp.where(
            lax.broadcasted_iota(jnp.int32, (N_COLS, CHUNK), 0) == n_key, 1.0, 0.0
        ).astype(jnp.bfloat16)
        acc_ref[...] += lax.dot_general(
            lhs, one_hot, (((1,), (1,)), ((), ())), preferred_element_type=jnp.float32
        )
        return carry

    lax.fori_loop(0, chunks, body, 0)
    for comp in range(10):
        for level in range(16):
            rows = pl.ds((comp * SPLITS) * M_ROWS + (level >> 2) * 8, 8)
            lanes = pl.ds((level & 3) * 128, 128)
            total = acc_ref[rows, lanes]
            for s in range(1, SPLITS):
                total = total + acc_ref[pl.ds((comp * SPLITS + s) * M_ROWS + (level >> 2) * 8, 8), lanes]
            out_ref[comp, level] = total
            if comp in X_PARTS:
                slot = X_PARTS.index(comp)
                xlo_ref[slot, pl.ds(level, 1), :] = total[0:1, :]
                xhi_ref[slot, pl.ds(level, 1), :] = total[7:8, :]
            if comp in Y_PARTS:
                slot = Y_PARTS.index(comp)
                turned = total.T
                ylo_ref[slot, pl.ds(level, 1), :] = turned[0:1, :]
                yhi_ref[slot, pl.ds(level, 1), :] = turned[127:128, :]
            if comp in Z_PARTS:
                slot = Z_PARTS.index(comp)
                if level == 0:
                    zlo_ref[slot] = total
                if level == 15:
                    zhi_ref[slot] = total


def cell_sums_of(stress_trial, mean_stress, consolidation, point_velocity, point_weight, point_cell, yield_flag, point_count, levels, extent, breadth):
    n = mean_stress.shape[0]
    row = lambda a: a.reshape(1, n)
    vmem = pl.BlockSpec(memory_space=pltpu.VMEM)
    return pl.pallas_call(
        sums_kernel,
        out_shape=[
            jax.ShapeDtypeStruct(s, jnp.float32)
            for s in [(10, levels, extent, breadth)] + [(3, levels, breadth)] * 2 + [(3, levels, extent)] * 2
            + [(3, extent, breadth)] * 2
        ],
        in_specs=[pl.BlockSpec(memory_space=pltpu.SMEM)] + [vmem] * 7,
        out_specs=[vmem] * 7,
        scratch_shapes=[pltpu.VMEM((10 * SPLITS * M_ROWS, N_COLS), jnp.float32)],
        cost_estimate=pl.CostEstimate(
            flops=2 * 10 * SPLITS * M_ROWS * N_COLS * n, bytes_accessed=13 * 4 * n + 10 * 4 * levels * extent * breadth,
            transcendentals=3 * n,
        ),
    )(
        point_count.reshape(1, 1), stress_trial, row(mean_stress), row(consolidation), point_velocity,
        row(point_weight), row(point_cell), row(yield_flag),
    )


def padded_2(cells, sides, width):
    for axis, dim in sides:
        count = lax.axis_size(axis)
        ends = count - 1
        head = lax.slice_in_dim(cells, 0, width, axis=dim)
        tail = lax.slice_in_dim(cells, cells.shape[dim] - width, cells.shape[dim], axis=dim)
        cells = jnp.concatenate(
            [
                lax.ppermute(tail, axis, [(i, (i + 1) % count) for i in range(ends)]),
                cells,
                lax.ppermute(head, axis, [((i + 1) % count, i) for i in range(ends)]),
            ],
            axis=dim,
        )
    return cells


def along_x(padded):
    return (padded[..., 1:-1, 2:, 1:-1] - padded[..., 1:-1, :-2, 1:-1]) * 0.5


def along_y(padded):
    return (padded[..., 1:-1, 1:-1, 2:] - padded[..., 1:-1, 1:-1, :-2]) * 0.5


def along_z(padded):
    return (padded[..., 2:, 1:-1, 1:-1] - padded[..., :-2, 1:-1, 1:-1]) * 0.5


def harmonic(former, latter):
    return 2.0 * former * latter / (former + latter)


def returned_stress(stress_trial, mean_stress, consolidation, yield_flag):
    sq_normal = (
        stress_trial[0] * stress_trial[0]
        + stress_trial[1] * stress_trial[1]
        + stress_trial[2] * stress_trial[2]
    )
    sq_shear = (
        stress_trial[3] * stress_trial[3]
        + stress_trial[4] * stress_trial[4]
        + stress_trial[5] * stress_trial[5]
    )
    shear_size = jnp.sqrt(1.5 * (sq_normal + 2.0 * sq_shear))
    yield_size = critical_slope * jnp.sqrt(mean_stress * (consolidation - mean_stress))
    factor = jnp.where(yield_flag == 1, yield_size / jnp.maximum(shear_size, shear_floor), 1.0)
    isotropic = jnp.array([1.0, 1.0, 1.0, 0.0, 0.0, 0.0], dtype=jnp.float32)[:, None]
    return stress_trial * factor - isotropic * mean_stress


def point_sums(stress, point_velocity, weight, cell_index, segments):
    stacked = jnp.concatenate([stress * weight, point_velocity * weight, weight[None]], axis=0)
    return jax.vmap(
        lambda component: jax.ops.segment_sum(component, cell_index, num_segments=segments)
    )(stacked)


def brick_velocity(cell_sums, padded):
    floored = jnp.maximum(cell_sums[9], mass_floor)
    force_x = along_x(padded[0]) + along_y(padded[3]) + along_z(padded[5])
    force_y = along_x(padded[3]) + along_y(padded[1]) + along_z(padded[4])
    force_z = along_x(padded[5]) + along_y(padded[4]) + along_z(padded[2])
    return jnp.stack(
        [
            (cell_sums[6] + time_step * force_x) / floored,
            (cell_sums[7] + time_step * force_y) / floored,
            (cell_sums[8] + time_step * force_z) / floored,
        ]
    )


def divergence(padded_velocity):
    return along_x(padded_velocity[0]) + along_y(padded_velocity[1]) + along_z(padded_velocity[2])


def band_terms(porosity, permeability, level_below, level_above, at_top, dilation):
    up_face = harmonic(permeability, level_above)
    down_face = harmonic(level_below, permeability)
    top_face = jnp.where(at_top, permeability, up_face)
    lower_band = -time_step * down_face
    upper_band = -time_step * up_face
    main_band = storage_rate * porosity + time_step * (down_face + top_face)
    right_side = -source_rate * (1.0 - porosity) * dilation
    return (lower_band, main_band, upper_band, right_side)


def earlier(values, stride, filler):
    head = jnp.full((stride,) + values.shape[1:], filler, values.dtype)
    return jnp.concatenate([head, values[:-stride]], axis=0)


def later(values, stride, filler):
    tail = jnp.full((stride,) + values.shape[1:], filler, values.dtype)
    return jnp.concatenate([values[stride:], tail], axis=0)


def cyclic_solve(lower_band, main_band, upper_band, right_side):
    length = main_band.shape[0]
    for bit in range((length - 1).bit_length()):
        stride = 1 << bit
        back_weight = -lower_band / earlier(main_band, stride, 1.0)
        ahead_weight = -upper_band / later(main_band, stride, 1.0)
        new_lower = back_weight * earlier(lower_band, stride, 0.0)
        new_upper = ahead_weight * later(upper_band, stride, 0.0)
        new_main = (
            main_band
            + back_weight * earlier(upper_band, stride, 0.0)
            + ahead_weight * later(lower_band, stride, 0.0)
        )
        new_right = (
            right_side
            + back_weight * earlier(right_side, stride, 0.0)
            + ahead_weight * later(right_side, stride, 0.0)
        )
        lower_band, main_band, upper_band, right_side = (new_lower, new_main, new_upper, new_right)
    return right_side / main_band


MESH_AXES = ("gx", "gy", "gz")


def halo_kernel(sides, sizes, gathered, group, *refs):
    count = len(sides)
    sends = refs[:2 * count]
    gins = refs[2 * count:2 * count + gathered]
    recvs = refs[2 * count + gathered:4 * count + gathered]
    gouts = refs[4 * count + gathered:4 * count + 2 * gathered]
    send_sem, recv_sem, gsend_sem, grecv_sem = refs[4 * count + 2 * gathered:]
    me = {a: lax.axis_index(a) for a in MESH_AXES}

    def peer(axis, delta):
        return tuple(me[a] + delta if a == axis else me[a] for a in MESH_AXES)

    def across(level):
        return tuple(level if a == "gz" else me[a] for a in MESH_AXES)

    links = []
    for i, axis in enumerate(sides):
        links.append((axis, -1, me[axis] > 0, 2 * i, 2 * i + 1))
        links.append((axis, 1, me[axis] < sizes[i] - 1, 2 * i + 1, 2 * i))
    barrier = pltpu.get_barrier_semaphore()
    peers = 0
    k = me["gz"]
    partner = (k // 2) * 2 + (1 - k % 2)
    counterpart = (1 - k // 2) * 2 + k % 2
    diagonal = (1 - k // 2) * 2 + (1 - k % 2)
    for axis, delta, present, _, _ in links:
        if gathered and axis == "gz":
            present = jnp.logical_and(present, k + delta == diagonal)
        peers = peers + present.astype(jnp.int32)

        @pl.when(present)
        def _():
            pl.semaphore_signal(barrier, 1, device_id=peer(axis, delta), device_id_type=pl.DeviceIdType.MESH)
    if gathered:
        for target in (partner, counterpart):
            pl.semaphore_signal(barrier, 1, device_id=across(target), device_id_type=pl.DeviceIdType.MESH)
        peers = peers + 2
    pl.semaphore_wait(barrier, peers)
    copies = []
    for axis, delta, present, src, dst in links:
        copy = pltpu.make_async_remote_copy(
            src_ref=sends[src], dst_ref=recvs[dst], send_sem=send_sem.at[src], recv_sem=recv_sem.at[dst],
            device_id=peer(axis, delta), device_id_type=pl.DeviceIdType.MESH,
        )
        copies.append((present, copy))

        @pl.when(present)
        def _():
            copy.start()
    gcopies = []
    for j in range(gathered):
        for n, target in enumerate((partner, counterpart)):
            copy = pltpu.make_async_remote_copy(
                src_ref=gins[j], dst_ref=gouts[j].at[k], send_sem=gsend_sem.at[3 * j + n],
                recv_sem=grecv_sem.at[3 * j + n], device_id=across(target), device_id_type=pl.DeviceIdType.MESH,
            )
            copy.start()
            gcopies.append(copy)
    for j in range(gathered):
        gouts[j][k] = gins[j][...]
    for j in range(gathered):
        for n, origin in enumerate((partner, counterpart)):
            incoming = pltpu.make_async_remote_copy(
                src_ref=gins[j], dst_ref=gouts[j].at[origin], send_sem=gsend_sem.at[3 * j + n],
                recv_sem=grecv_sem.at[3 * j + n], device_id=across(origin), device_id_type=pl.DeviceIdType.MESH,
            )
            incoming.wait_recv()
        relay = pltpu.make_async_remote_copy(
            src_ref=gouts[j].at[counterpart], dst_ref=gouts[j].at[counterpart], send_sem=gsend_sem.at[3 * j + 2],
            recv_sem=grecv_sem.at[3 * j + 2], device_id=across(partner), device_id_type=pl.DeviceIdType.MESH,
        )
        relay.start()
        gcopies.append(relay)
    for j in range(gathered):
        relayed = pltpu.make_async_remote_copy(
            src_ref=gouts[j].at[diagonal], dst_ref=gouts[j].at[diagonal], send_sem=gsend_sem.at[3 * j + 2],
            recv_sem=grecv_sem.at[3 * j + 2], device_id=across(partner), device_id_type=pl.DeviceIdType.MESH,
        )
        relayed.wait_recv()
    for axis, delta, present, src, dst in links:
        incoming = pltpu.make_async_remote_copy(
            src_ref=sends[dst], dst_ref=recvs[src], send_sem=send_sem.at[dst], recv_sem=recv_sem.at[src],
            device_id=peer(axis, delta), device_id_type=pl.DeviceIdType.MESH,
        )

        @pl.when(present)
        def _():
            incoming.wait_recv()

        @pl.when(jnp.logical_not(present))
        def _():
            recvs[src][...] = jnp.zeros(recvs[src].shape, recvs[src].dtype)
    for present, copy in copies:
        @pl.when(present)
        def _():
            copy.wait_send()
    for copy in gcopies:
        copy.wait_send()


def exchange(cells, sides, collective, gathers=(), given=None):
    sends = []
    for axis, dim in sides:
        size = cells.shape[dim]
        sends.append(lax.index_in_dim(cells, 0, axis=dim, keepdims=False))
        sends.append(lax.index_in_dim(cells, size - 1, axis=dim, keepdims=False))
    if given is not None:
        sends = list(given)
    axes = tuple(axis for axis, _ in sides)
    sizes = tuple(lax.axis_size(axis) for axis in axes)
    group = lax.axis_size("gz")
    vmem = pl.BlockSpec(memory_space=pltpu.VMEM)
    assert group == 4 or not gathers
    slots = max(1, len(gathers) * (group - 1))
    outs = pl.pallas_call(
        functools.partial(halo_kernel, axes, sizes, len(gathers), group),
        out_shape=[jax.ShapeDtypeStruct(s.shape, s.dtype) for s in sends]
        + [jax.ShapeDtypeStruct((group,) + g.shape, g.dtype) for g in gathers],
        in_specs=[vmem] * (len(sends) + len(gathers)),
        out_specs=[vmem] * (len(sends) + len(gathers)),
        scratch_shapes=[
            pltpu.SemaphoreType.DMA((max(1, len(sends)),)), pltpu.SemaphoreType.DMA((max(1, len(sends)),)),
            pltpu.SemaphoreType.DMA((slots,)), pltpu.SemaphoreType.DMA((slots,)),
        ],
        compiler_params=pltpu.CompilerParams(collective_id=collective, has_side_effects=True),
    )(*sends, *gathers)
    recvs = outs[:len(sends)]
    faces = {
        dim: (jnp.expand_dims(recvs[2 * i], dim), jnp.expand_dims(recvs[2 * i + 1], dim))
        for i, (axis, dim) in enumerate(sides)
    }
    stacked = [g.reshape((group * g.shape[1],) + g.shape[2:]) for g in outs[len(sends):]]
    return faces, stacked


def faces_kernel(parts, cells_ref, *out_refs):
    chans, levels, extent, breadth = cells_ref.shape
    xlo, xhi, ylo, yhi = out_refs[:4]
    for slot, c in enumerate(parts[0]):
        for level in range(levels):
            tile = cells_ref[c, level]
            xlo[slot, pl.ds(level, 1), :] = tile[0:1, :]
            xhi[slot, pl.ds(level, 1), :] = tile[extent - 1:extent, :]
    for slot, c in enumerate(parts[1]):
        for level in range(levels):
            turned = cells_ref[c, level].T
            ylo[slot, pl.ds(level, 1), :] = turned[0:1, :]
            yhi[slot, pl.ds(level, 1), :] = turned[breadth - 1:breadth, :]
    if len(parts) > 2:
        for slot, c in enumerate(parts[2]):
            out_refs[4][slot] = cells_ref[c, 0]
            out_refs[5][slot] = cells_ref[c, levels - 1]


def faces_by_kernel(cells, parts):
    chans, levels, extent, breadth = cells.shape
    shapes = [(len(parts[0]), levels, breadth)] * 2 + [(len(parts[1]), levels, extent)] * 2
    if len(parts) > 2:
        shapes += [(len(parts[2]), extent, breadth)] * 2
    vmem = pl.BlockSpec(memory_space=pltpu.VMEM)
    return pl.pallas_call(
        functools.partial(faces_kernel, parts),
        out_shape=[jax.ShapeDtypeStruct(s, cells.dtype) for s in shapes],
        in_specs=[vmem],
        out_specs=[vmem] * len(shapes),
    )(cells)


def solve_kernel(levels, poro_ref, perm_ref, right_ref, out_ref, grad_ref, xlo, xhi, ylo, yhi, padded_ref):
    perm = perm_ref[...]
    lid = jnp.zeros((1,) + perm.shape[1:], jnp.float32)
    level_above = jnp.concatenate([perm[1:], lid], axis=0)
    level_below = jnp.concatenate([lid, perm[:-1]], axis=0)
    up_face = harmonic(perm, level_above)
    down_face = harmonic(level_below, perm)
    top_face = jnp.concatenate([up_face[:-1], perm[-1:]], axis=0)
    lower_band = -time_step * down_face
    upper_band = -time_step * up_face
    main_band = storage_rate * poro_ref[...] + time_step * (down_face + top_face)
    solved = cyclic_solve(lower_band, main_band, upper_band, right_ref[...])
    height, extent, breadth = solved.shape
    padded_ref[pl.ds(0, 1)] = lid
    padded_ref[pl.ds(height + 1, 1)] = lid
    padded_ref[pl.ds(1, height)] = solved
    first = lax.axis_index("gz") * levels
    out_ref[...] = padded_ref[pl.ds(first + 1, levels)]
    grad_ref[...] = (padded_ref[pl.ds(first + 2, levels)] - padded_ref[pl.ds(first, levels)]) * 0.5
    for level in range(levels):
        tile = out_ref[level]
        xlo[pl.ds(level, 1), :] = tile[0:1, :]
        xhi[pl.ds(level, 1), :] = tile[extent - 1:extent, :]
        turned = tile.T
        ylo[pl.ds(level, 1), :] = turned[0:1, :]
        yhi[pl.ds(level, 1), :] = turned[breadth - 1:breadth, :]


def column_solve(porosity, permeability, right_side, levels):
    height, extent, breadth = right_side.shape
    vmem = pl.BlockSpec(memory_space=pltpu.VMEM)
    shapes = [(levels, extent, breadth)] * 2 + [(levels, breadth)] * 2 + [(levels, extent)] * 2
    return pl.pallas_call(
        functools.partial(solve_kernel, levels),
        out_shape=[jax.ShapeDtypeStruct(s, jnp.float32) for s in shapes],
        in_specs=[vmem] * 3,
        out_specs=[vmem] * len(shapes),
        scratch_shapes=[pltpu.VMEM((height + 2, extent, breadth), jnp.float32)],
    )(porosity, permeability, right_side)


def face_from(part, axis, from_lower):
    count = lax.axis_size(axis)
    if from_lower:
        pairs = [(i, i + 1) for i in range(count - 1)]
    else:
        pairs = [(i + 1, i) for i in range(count - 1)]
    return lax.ppermute(part, axis, pairs)


def faces_of(cells, sides):
    got = {}
    for axis, dim in sides:
        size = cells.shape[dim]
        got[dim] = (
            face_from(lax.slice_in_dim(cells, size - 1, size, axis=dim), axis, True),
            face_from(lax.slice_in_dim(cells, 0, 1, axis=dim), axis, False),
        )
    return got


def along(cells, faces, dim):
    size = cells.shape[dim]
    lower, upper = faces[dim]
    ahead = jnp.concatenate([lax.slice_in_dim(cells, 1, size, axis=dim), upper], axis=dim)
    behind = jnp.concatenate([lower, lax.slice_in_dim(cells, 0, size - 1, axis=dim)], axis=dim)
    return (ahead - behind) * 0.5


def shards(
    stress_trial,
    mean_stress,
    consolidation,
    point_velocity,
    point_weight,
    point_cell,
    yield_flag,
    point_count,
    porosity,
    permeability,
):
    levels, extent, breadth = porosity.shape
    cell_sums, *stress_faces = cell_sums_of(
        stress_trial, mean_stress, consolidation, point_velocity, point_weight, point_cell,
        yield_flag, point_count, levels, extent, breadth,
    )
    sides = (("gx", 2), ("gy", 3), ("gz", 1))
    stress_sums = cell_sums[:6]
    sf, (all_porosity, all_permeability) = exchange(
        stress_sums, sides, 0, (porosity, permeability), given=stress_faces
    )
    height = all_porosity.shape[0]
    def part(dim, parts, c):
        s = parts.index(c)
        return {dim: (sf[dim][0][s:s + 1], sf[dim][1][s:s + 1])}

    d_x = lambda c: along(stress_sums[c:c + 1], part(2, X_PARTS, c), 2)[0]
    d_y = lambda c: along(stress_sums[c:c + 1], part(3, Y_PARTS, c), 3)[0]
    d_z = lambda c: along(stress_sums[c:c + 1], part(1, Z_PARTS, c), 1)[0]
    floored = jnp.maximum(cell_sums[9], mass_floor)
    force_x = d_x(0) + d_y(3) + d_z(5)
    force_y = d_x(3) + d_y(1) + d_z(4)
    force_z = d_x(5) + d_y(4) + d_z(2)
    velocity = jnp.stack(
        [
            (cell_sums[6] + time_step * force_x) / floored,
            (cell_sums[7] + time_step * force_y) / floored,
            (cell_sums[8] + time_step * force_z) / floored,
        ]
    )
    vf, _ = exchange(velocity, sides, 1, given=faces_by_kernel(velocity, ((0,), (1,), (2,))))
    dilation = (
        along(velocity[0:1], {2: vf[2]}, 2)[0]
        + along(velocity[1:2], {3: vf[3]}, 3)[0]
        + along(velocity[2:3], {1: vf[1]}, 1)[0]
    )
    right_side = -source_rate * (1.0 - porosity) * dilation
    _, (all_right,) = exchange(right_side, (), 3, (right_side,))
    zero_level = jnp.zeros((1, extent, breadth), jnp.float32)
    pressure, rise, *pressure_faces = column_solve(all_porosity, all_permeability, all_right, levels)
    pf, _ = exchange(pressure, (("gx", 1), ("gy", 2)), 2, given=pressure_faces)
    gradient = jnp.stack([along(pressure, pf, 1), along(pressure, pf, 2), rise])
    return (velocity - time_step * gradient, pressure)


def solution(mesh):
    placed = (
        P(None, ("gx", "gy", "gz")),
        P(("gx", "gy", "gz")),
        P(("gx", "gy", "gz")),
        P(None, ("gx", "gy", "gz")),
        P(("gx", "gy", "gz")),
        P(("gx", "gy", "gz")),
        P(("gx", "gy", "gz")),
        P("gx", "gy", "gz"),
        P("gz", "gx", "gy"),
        P("gz", "gx", "gy"),
    )
    return jax.shard_map(
        shards,
        mesh=mesh,
        in_specs=placed,
        out_specs=(P(None, "gz", "gx", "gy"), P("gz", "gx", "gy")),
        check_vma=False,
    )
```

```python
import functools

import jax
import jax.numpy as jnp
from jax import lax
from jax.sharding import PartitionSpec as P

time_step = 0.25
storage_rate = 0.002
source_rate = 0.003
critical_slope = 1.2
mass_floor = 0.5
shear_floor = 1.0

from jax.experimental import pallas as pl
from jax.experimental.pallas import tpu as pltpu

CHUNK = 12288
M_ROWS = 32
N_COLS = 512


SPLITS = 2
X_PARTS = (0, 3, 5)
Y_PARTS = (3, 1, 4)
Z_PARTS = (5, 4, 2)


def _split(v):
    hi = v.astype(jnp.bfloat16)
    lo = (v - hi.astype(jnp.float32)).astype(jnp.bfloat16)
    return [hi, lo]


def sums_kernel(count_ref, st_ref, ms_ref, cons_ref, vel_ref, w_ref, cell_ref, yf_ref, out_ref, xlo_ref, xhi_ref, ylo_ref, yhi_ref, zlo_ref, zhi_ref, acc_ref):
    count = count_ref[0, 0]
    acc_ref[...] = jnp.zeros_like(acc_ref)
    chunks = st_ref.shape[1] // CHUNK

    def body(k, carry):
        start = pl.multiple_of(k * CHUNK, CHUNK)
        span = pl.ds(start, CHUNK)
        st = [st_ref[pl.ds(i, 1), span] for i in range(6)]
        ms = ms_ref[:, span]
        cons = cons_ref[:, span]
        yf = yf_ref[:, span]
        slot = start + lax.broadcasted_iota(jnp.int32, (1, CHUNK), 1)
        weight = jnp.where(slot < count, w_ref[:, span], 0.0)
        sq_normal = st[0] * st[0] + st[1] * st[1] + st[2] * st[2]
        sq_shear = st[3] * st[3] + st[4] * st[4] + st[5] * st[5]
        shear_size = jnp.sqrt(1.5 * (sq_normal + 2.0 * sq_shear))
        yield_size = critical_slope * jnp.sqrt(ms * (cons - ms))
        factor = jnp.where(yf == 1, yield_size / jnp.maximum(shear_size, shear_floor), 1.0)
        stress = [st[i] * factor - ms if i < 3 else st[i] * factor for i in range(6)]
        values = [s * weight for s in stress]
        values += [vel_ref[pl.ds(i, 1), span] * weight for i in range(3)]
        values.append(weight)
        cell = cell_ref[:, span]
        m_key = (cell >> 12) * 8 + ((cell >> 7) & 7)
        n_key = ((cell >> 10) & 3) * 128 + (cell & 127)
        m_mask = lax.broadcasted_iota(jnp.int32, (M_ROWS, CHUNK), 0) == m_key
        zero = jnp.zeros((M_ROWS, CHUNK), jnp.bfloat16)
        pieces = []
        for v in values:
            for part in _split(v):
                pieces.append(jnp.where(m_mask, jnp.broadcast_to(part, (M_ROWS, CHUNK)), zero))
        lhs = jnp.concatenate(pieces, axis=0)
        one_hot = jnp.where(
            lax.broadcasted_iota(jnp.int32, (N_COLS, CHUNK), 0) == n_key, 1.0, 0.0
        ).astype(jnp.bfloat16)
        acc_ref[...] += lax.dot_general(
            lhs, one_hot, (((1,), (1,)), ((), ())), preferred_element_type=jnp.float32
        )
        return carry

    lax.fori_loop(0, chunks, body, 0)
    for comp in range(10):
        for level in range(16):
            rows = pl.ds((comp * SPLITS) * M_ROWS + (level >> 2) * 8, 8)
            lanes = pl.ds((level & 3) * 128, 128)
            total = acc_ref[rows, lanes]
            for s in range(1, SPLITS):
                total = total + acc_ref[pl.ds((comp * SPLITS + s) * M_ROWS + (level >> 2) * 8, 8), lanes]
            out_ref[comp, level] = total
            if comp in X_PARTS:
                slot = X_PARTS.index(comp)
                xlo_ref[slot, pl.ds(level, 1), :] = total[0:1, :]
                xhi_ref[slot, pl.ds(level, 1), :] = total[7:8, :]
            if comp in Y_PARTS:
                slot = Y_PARTS.index(comp)
                turned = total.T
                ylo_ref[slot, pl.ds(level, 1), :] = turned[0:1, :]
                yhi_ref[slot, pl.ds(level, 1), :] = turned[127:128, :]
            if comp in Z_PARTS:
                slot = Z_PARTS.index(comp)
                if level == 0:
                    zlo_ref[slot] = total
                if level == 15:
                    zhi_ref[slot] = total


def cell_sums_of(stress_trial, mean_stress, consolidation, point_velocity, point_weight, point_cell, yield_flag, point_count, levels, extent, breadth):
    n = mean_stress.shape[0]
    row = lambda a: a.reshape(1, n)
    vmem = pl.BlockSpec(memory_space=pltpu.VMEM)
    return pl.pallas_call(
        sums_kernel,
        out_shape=[
            jax.ShapeDtypeStruct(s, jnp.float32)
            for s in [(10, levels, extent, breadth)] + [(3, levels, breadth)] * 2 + [(3, levels, extent)] * 2
            + [(3, extent, breadth)] * 2
        ],
        in_specs=[pl.BlockSpec(memory_space=pltpu.SMEM)] + [vmem] * 7,
        out_specs=[vmem] * 7,
        scratch_shapes=[pltpu.VMEM((10 * SPLITS * M_ROWS, N_COLS), jnp.float32)],
        cost_estimate=pl.CostEstimate(
            flops=2 * 10 * SPLITS * M_ROWS * N_COLS * n, bytes_accessed=13 * 4 * n + 10 * 4 * levels * extent * breadth,
            transcendentals=3 * n,
        ),
    )(
        point_count.reshape(1, 1), stress_trial, row(mean_stress), row(consolidation), point_velocity,
        row(point_weight), row(point_cell), row(yield_flag),
    )


def padded_2(cells, sides, width):
    for axis, dim in sides:
        count = lax.axis_size(axis)
        ends = count - 1
        head = lax.slice_in_dim(cells, 0, width, axis=dim)
        tail = lax.slice_in_dim(cells, cells.shape[dim] - width, cells.shape[dim], axis=dim)
        cells = jnp.concatenate(
            [
                lax.ppermute(tail, axis, [(i, (i + 1) % count) for i in range(ends)]),
                cells,
                lax.ppermute(head, axis, [((i + 1) % count, i) for i in range(ends)]),
            ],
            axis=dim,
        )
    return cells


def along_x(padded):
    return (padded[..., 1:-1, 2:, 1:-1] - padded[..., 1:-1, :-2, 1:-1]) * 0.5


def along_y(padded):
    return (padded[..., 1:-1, 1:-1, 2:] - padded[..., 1:-1, 1:-1, :-2]) * 0.5


def along_z(padded):
    return (padded[..., 2:, 1:-1, 1:-1] - padded[..., :-2, 1:-1, 1:-1]) * 0.5


def harmonic(former, latter):
    return 2.0 * former * latter / (former + latter)


def returned_stress(stress_trial, mean_stress, consolidation, yield_flag):
    sq_normal = (
        stress_trial[0] * stress_trial[0]
        + stress_trial[1] * stress_trial[1]
        + stress_trial[2] * stress_trial[2]
    )
    sq_shear = (
        stress_trial[3] * stress_trial[3]
        + stress_trial[4] * stress_trial[4]
        + stress_trial[5] * stress_trial[5]
    )
    shear_size = jnp.sqrt(1.5 * (sq_normal + 2.0 * sq_shear))
    yield_size = critical_slope * jnp.sqrt(mean_stress * (consolidation - mean_stress))
    factor = jnp.where(yield_flag == 1, yield_size / jnp.maximum(shear_size, shear_floor), 1.0)
    isotropic = jnp.array([1.0, 1.0, 1.0, 0.0, 0.0, 0.0], dtype=jnp.float32)[:, None]
    return stress_trial * factor - isotropic * mean_stress


def point_sums(stress, point_velocity, weight, cell_index, segments):
    stacked = jnp.concatenate([stress * weight, point_velocity * weight, weight[None]], axis=0)
    return jax.vmap(
        lambda component: jax.ops.segment_sum(component, cell_index, num_segments=segments)
    )(stacked)


def brick_velocity(cell_sums, padded):
    floored = jnp.maximum(cell_sums[9], mass_floor)
    force_x = along_x(padded[0]) + along_y(padded[3]) + along_z(padded[5])
    force_y = along_x(padded[3]) + along_y(padded[1]) + along_z(padded[4])
    force_z = along_x(padded[5]) + along_y(padded[4]) + along_z(padded[2])
    return jnp.stack(
        [
            (cell_sums[6] + time_step * force_x) / floored,
            (cell_sums[7] + time_step * force_y) / floored,
            (cell_sums[8] + time_step * force_z) / floored,
        ]
    )


def divergence(padded_velocity):
    return along_x(padded_velocity[0]) + along_y(padded_velocity[1]) + along_z(padded_velocity[2])


def band_terms(porosity, permeability, level_below, level_above, at_top, dilation):
    up_face = harmonic(permeability, level_above)
    down_face = harmonic(level_below, permeability)
    top_face = jnp.where(at_top, permeability, up_face)
    lower_band = -time_step * down_face
    upper_band = -time_step * up_face
    main_band = storage_rate * porosity + time_step * (down_face + top_face)
    right_side = -source_rate * (1.0 - porosity) * dilation
    return (lower_band, main_band, upper_band, right_side)


def earlier(values, stride, filler):
    head = jnp.full((stride,) + values.shape[1:], filler, values.dtype)
    return jnp.concatenate([head, values[:-stride]], axis=0)


def later(values, stride, filler):
    tail = jnp.full((stride,) + values.shape[1:], filler, values.dtype)
    return jnp.concatenate([values[stride:], tail], axis=0)


def cyclic_solve(lower_band, main_band, upper_band, right_side):
    length = main_band.shape[0]
    for bit in range((length - 1).bit_length()):
        stride = 1 << bit
        back_weight = -lower_band / earlier(main_band, stride, 1.0)
        ahead_weight = -upper_band / later(main_band, stride, 1.0)
        new_lower = back_weight * earlier(lower_band, stride, 0.0)
        new_upper = ahead_weight * later(upper_band, stride, 0.0)
        new_main = (
            main_band
            + back_weight * earlier(upper_band, stride, 0.0)
            + ahead_weight * later(lower_band, stride, 0.0)
        )
        new_right = (
            right_side
            + back_weight * earlier(right_side, stride, 0.0)
            + ahead_weight * later(right_side, stride, 0.0)
        )
        lower_band, main_band, upper_band, right_side = (new_lower, new_main, new_upper, new_right)
    return right_side / main_band


MESH_AXES = ("gx", "gy", "gz")


def halo_kernel(sides, sizes, gathered, group, *refs):
    count = len(sides)
    sends = refs[:2 * count]
    gins = refs[2 * count:2 * count + gathered]
    recvs = refs[2 * count + gathered:4 * count + gathered]
    gouts = refs[4 * count + gathered:4 * count + 2 * gathered]
    send_sem, recv_sem, gsend_sem, grecv_sem = refs[4 * count + 2 * gathered:]
    me = {a: lax.axis_index(a) for a in MESH_AXES}

    def peer(axis, delta):
        return tuple(me[a] + delta if a == axis else me[a] for a in MESH_AXES)

    def across(level):
        return tuple(level if a == "gz" else me[a] for a in MESH_AXES)

    links = []
    for i, axis in enumerate(sides):
        links.append((axis, -1, me[axis] > 0, 2 * i, 2 * i + 1))
        links.append((axis, 1, me[axis] < sizes[i] - 1, 2 * i + 1, 2 * i))
    barrier = pltpu.get_barrier_semaphore()
    peers = 0
    k = me["gz"]
    partner = (k // 2) * 2 + (1 - k % 2)
    counterpart = (1 - k // 2) * 2 + k % 2
    diagonal = (1 - k // 2) * 2 + (1 - k % 2)
    for axis, delta, present, _, _ in links:
        if gathered and axis == "gz":
            present = jnp.logical_and(present, k + delta == diagonal)
        peers = peers + present.astype(jnp.int32)

        @pl.when(present)
        def _():
            pl.semaphore_signal(barrier, 1, device_id=peer(axis, delta), device_id_type=pl.DeviceIdType.MESH)
    if gathered:
        for target in (partner, counterpart):
            pl.semaphore_signal(barrier, 1, device_id=across(target), device_id_type=pl.DeviceIdType.MESH)
        peers = peers + 2
    pl.semaphore_wait(barrier, peers)
    copies = []
    for axis, delta, present, src, dst in links:
        copy = pltpu.make_async_remote_copy(
            src_ref=sends[src], dst_ref=recvs[dst], send_sem=send_sem.at[src], recv_sem=recv_sem.at[dst],
            device_id=peer(axis, delta), device_id_type=pl.DeviceIdType.MESH,
        )
        copies.append((present, copy))

        @pl.when(present)
        def _():
            copy.start()
    gcopies = []
    for j in range(gathered):
        for n, target in enumerate((partner, counterpart)):
            copy = pltpu.make_async_remote_copy(
                src_ref=gins[j], dst_ref=gouts[j].at[k], send_sem=gsend_sem.at[3 * j + n],
                recv_sem=grecv_sem.at[3 * j + n], device_id=across(target), device_id_type=pl.DeviceIdType.MESH,
            )
            copy.start()
            gcopies.append(copy)
    for j in range(gathered):
        gouts[j][k] = gins[j][...]
    for j in range(gathered):
        for n, origin in enumerate((partner, counterpart)):
            incoming = pltpu.make_async_remote_copy(
                src_ref=gins[j], dst_ref=gouts[j].at[origin], send_sem=gsend_sem.at[3 * j + n],
                recv_sem=grecv_sem.at[3 * j + n], device_id=across(origin), device_id_type=pl.DeviceIdType.MESH,
            )
            incoming.wait_recv()
        relay = pltpu.make_async_remote_copy(
            src_ref=gouts[j].at[counterpart], dst_ref=gouts[j].at[counterpart], send_sem=gsend_sem.at[3 * j + 2],
            recv_sem=grecv_sem.at[3 * j + 2], device_id=across(partner), device_id_type=pl.DeviceIdType.MESH,
        )
        relay.start()
        gcopies.append(relay)
    for j in range(gathered):
        relayed = pltpu.make_async_remote_copy(
            src_ref=gouts[j].at[diagonal], dst_ref=gouts[j].at[diagonal], send_sem=gsend_sem.at[3 * j + 2],
            recv_sem=grecv_sem.at[3 * j + 2], device_id=across(partner), device_id_type=pl.DeviceIdType.MESH,
        )
        relayed.wait_recv()
    for axis, delta, present, src, dst in links:
        incoming = pltpu.make_async_remote_copy(
            src_ref=sends[dst], dst_ref=recvs[src], send_sem=send_sem.at[dst], recv_sem=recv_sem.at[src],
            device_id=peer(axis, delta), device_id_type=pl.DeviceIdType.MESH,
        )

        @pl.when(present)
        def _():
            incoming.wait_recv()

        @pl.when(jnp.logical_not(present))
        def _():
            recvs[src][...] = jnp.zeros(recvs[src].shape, recvs[src].dtype)
    for present, copy in copies:
        @pl.when(present)
        def _():
            copy.wait_send()
    for copy in gcopies:
        copy.wait_send()


def exchange(cells, sides, collective, gathers=(), given=None):
    sends = []
    for axis, dim in sides:
        size = cells.shape[dim]
        sends.append(lax.index_in_dim(cells, 0, axis=dim, keepdims=False))
        sends.append(lax.index_in_dim(cells, size - 1, axis=dim, keepdims=False))
    if given is not None:
        sends = list(given)
    axes = tuple(axis for axis, _ in sides)
    sizes = tuple(lax.axis_size(axis) for axis in axes)
    group = lax.axis_size("gz")
    vmem = pl.BlockSpec(memory_space=pltpu.VMEM)
    assert group == 4 or not gathers
    slots = max(1, len(gathers) * (group - 1))
    outs = pl.pallas_call(
        functools.partial(halo_kernel, axes, sizes, len(gathers), group),
        out_shape=[jax.ShapeDtypeStruct(s.shape, s.dtype) for s in sends]
        + [jax.ShapeDtypeStruct((group,) + g.shape, g.dtype) for g in gathers],
        in_specs=[vmem] * (len(sends) + len(gathers)),
        out_specs=[vmem] * (len(sends) + len(gathers)),
        scratch_shapes=[
            pltpu.SemaphoreType.DMA((max(1, len(sends)),)), pltpu.SemaphoreType.DMA((max(1, len(sends)),)),
            pltpu.SemaphoreType.DMA((slots,)), pltpu.SemaphoreType.DMA((slots,)),
        ],
        compiler_params=pltpu.CompilerParams(collective_id=collective, has_side_effects=True),
    )(*sends, *gathers)
    recvs = outs[:len(sends)]
    faces = {
        dim: (jnp.expand_dims(recvs[2 * i], dim), jnp.expand_dims(recvs[2 * i + 1], dim))
        for i, (axis, dim) in enumerate(sides)
    }
    stacked = [g.reshape((group * g.shape[1],) + g.shape[2:]) for g in outs[len(sends):]]
    return faces, stacked


def faces_kernel(parts, cells_ref, *out_refs):
    chans, levels, extent, breadth = cells_ref.shape
    xlo, xhi, ylo, yhi = out_refs[:4]
    for slot, c in enumerate(parts[0]):
        for level in range(levels):
            tile = cells_ref[c, level]
            xlo[slot, pl.ds(level, 1), :] = tile[0:1, :]
            xhi[slot, pl.ds(level, 1), :] = tile[extent - 1:extent, :]
    for slot, c in enumerate(parts[1]):
        for level in range(levels):
            turned = cells_ref[c, level].T
            ylo[slot, pl.ds(level, 1), :] = turned[0:1, :]
            yhi[slot, pl.ds(level, 1), :] = turned[breadth - 1:breadth, :]
    if len(parts) > 2:
        for slot, c in enumerate(parts[2]):
            out_refs[4][slot] = cells_ref[c, 0]
            out_refs[5][slot] = cells_ref[c, levels - 1]


def faces_by_kernel(cells, parts):
    chans, levels, extent, breadth = cells.shape
    shapes = [(len(parts[0]), levels, breadth)] * 2 + [(len(parts[1]), levels, extent)] * 2
    if len(parts) > 2:
        shapes += [(len(parts[2]), extent, breadth)] * 2
    vmem = pl.BlockSpec(memory_space=pltpu.VMEM)
    return pl.pallas_call(
        functools.partial(faces_kernel, parts),
        out_shape=[jax.ShapeDtypeStruct(s, cells.dtype) for s in shapes],
        in_specs=[vmem],
        out_specs=[vmem] * len(shapes),
    )(cells)


def solve_kernel(levels, poro_ref, perm_ref, right_ref, out_ref, grad_ref, xlo, xhi, ylo, yhi, padded_ref):
    perm = perm_ref[...]
    lid = jnp.zeros((1,) + perm.shape[1:], jnp.float32)
    level_above = jnp.concatenate([perm[1:], lid], axis=0)
    level_below = jnp.concatenate([lid, perm[:-1]], axis=0)
    up_face = harmonic(perm, level_above)
    down_face = harmonic(level_below, perm)
    top_face = jnp.concatenate([up_face[:-1], perm[-1:]], axis=0)
    lower_band = -time_step * down_face
    upper_band = -time_step * up_face
    main_band = storage_rate * poro_ref[...] + time_step * (down_face + top_face)
    solved = cyclic_solve(lower_band, main_band, upper_band, right_ref[...])
    height, extent, breadth = solved.shape
    padded_ref[pl.ds(0, 1)] = lid
    padded_ref[pl.ds(height + 1, 1)] = lid
    padded_ref[pl.ds(1, height)] = solved
    first = lax.axis_index("gz") * levels
    out_ref[...] = padded_ref[pl.ds(first + 1, levels)]
    grad_ref[...] = (padded_ref[pl.ds(first + 2, levels)] - padded_ref[pl.ds(first, levels)]) * 0.5
    for level in range(levels):
        tile = out_ref[level]
        xlo[pl.ds(level, 1), :] = tile[0:1, :]
        xhi[pl.ds(level, 1), :] = tile[extent - 1:extent, :]
        turned = tile.T
        ylo[pl.ds(level, 1), :] = turned[0:1, :]
        yhi[pl.ds(level, 1), :] = turned[breadth - 1:breadth, :]


def column_solve(porosity, permeability, right_side, levels):
    height, extent, breadth = right_side.shape
    vmem = pl.BlockSpec(memory_space=pltpu.VMEM)
    shapes = [(levels, extent, breadth)] * 2 + [(levels, breadth)] * 2 + [(levels, extent)] * 2
    return pl.pallas_call(
        functools.partial(solve_kernel, levels),
        out_shape=[jax.ShapeDtypeStruct(s, jnp.float32) for s in shapes],
        in_specs=[vmem] * 3,
        out_specs=[vmem] * len(shapes),
        scratch_shapes=[pltpu.VMEM((height + 2, extent, breadth), jnp.float32)],
    )(porosity, permeability, right_side)


def face_from(part, axis, from_lower):
    count = lax.axis_size(axis)
    if from_lower:
        pairs = [(i, i + 1) for i in range(count - 1)]
    else:
        pairs = [(i + 1, i) for i in range(count - 1)]
    return lax.ppermute(part, axis, pairs)


def faces_of(cells, sides):
    got = {}
    for axis, dim in sides:
        size = cells.shape[dim]
        got[dim] = (
            face_from(lax.slice_in_dim(cells, size - 1, size, axis=dim), axis, True),
            face_from(lax.slice_in_dim(cells, 0, 1, axis=dim), axis, False),
        )
    return got


def along(cells, faces, dim):
    size = cells.shape[dim]
    lower, upper = faces[dim]
    ahead = jnp.concatenate([lax.slice_in_dim(cells, 1, size, axis=dim), upper], axis=dim)
    behind = jnp.concatenate([lower, lax.slice_in_dim(cells, 0, size - 1, axis=dim)], axis=dim)
    return (ahead - behind) * 0.5


def shards(
    stress_trial,
    mean_stress,
    consolidation,
    point_velocity,
    point_weight,
    point_cell,
    yield_flag,
    point_count,
    porosity,
    permeability,
):
    levels, extent, breadth = porosity.shape
    cell_sums, *stress_faces = cell_sums_of(
        stress_trial, mean_stress, consolidation, point_velocity, point_weight, point_cell,
        yield_flag, point_count, levels, extent, breadth,
    )
    sides = (("gx", 2), ("gy", 3), ("gz", 1))
    stress_sums = cell_sums[:6]
    sf, (all_porosity,) = exchange(stress_sums, sides, 0, (porosity,), given=stress_faces)
    height = all_porosity.shape[0]
    def part(dim, parts, c):
        s = parts.index(c)
        return {dim: (sf[dim][0][s:s + 1], sf[dim][1][s:s + 1])}

    d_x = lambda c: along(stress_sums[c:c + 1], part(2, X_PARTS, c), 2)[0]
    d_y = lambda c: along(stress_sums[c:c + 1], part(3, Y_PARTS, c), 3)[0]
    d_z = lambda c: along(stress_sums[c:c + 1], part(1, Z_PARTS, c), 1)[0]
    floored = jnp.maximum(cell_sums[9], mass_floor)
    force_x = d_x(0) + d_y(3) + d_z(5)
    force_y = d_x(3) + d_y(1) + d_z(4)
    force_z = d_x(5) + d_y(4) + d_z(2)
    velocity = jnp.stack(
        [
            (cell_sums[6] + time_step * force_x) / floored,
            (cell_sums[7] + time_step * force_y) / floored,
            (cell_sums[8] + time_step * force_z) / floored,
        ]
    )
    vf, (all_permeability,) = exchange(
        velocity, sides, 1, (permeability,), given=faces_by_kernel(velocity, ((0,), (1,), (2,)))
    )
    dilation = (
        along(velocity[0:1], {2: vf[2]}, 2)[0]
        + along(velocity[1:2], {3: vf[3]}, 3)[0]
        + along(velocity[2:3], {1: vf[1]}, 1)[0]
    )
    right_side = -source_rate * (1.0 - porosity) * dilation
    _, (all_right,) = exchange(right_side, (), 3, (right_side,))
    zero_level = jnp.zeros((1, extent, breadth), jnp.float32)
    pressure, rise, *pressure_faces = column_solve(all_porosity, all_permeability, all_right, levels)
    pf, _ = exchange(pressure, (("gx", 1), ("gy", 2)), 2, given=pressure_faces)
    gradient = jnp.stack([along(pressure, pf, 1), along(pressure, pf, 2), rise])
    return (velocity - time_step * gradient, pressure)


def solution(mesh):
    placed = (
        P(None, ("gx", "gy", "gz")),
        P(("gx", "gy", "gz")),
        P(("gx", "gy", "gz")),
        P(None, ("gx", "gy", "gz")),
        P(("gx", "gy", "gz")),
        P(("gx", "gy", "gz")),
        P(("gx", "gy", "gz")),
        P("gx", "gy", "gz"),
        P("gz", "gx", "gy"),
        P("gz", "gx", "gy"),
    )
    return jax.shard_map(
        shards,
        mesh=mesh,
        in_specs=placed,
        out_specs=(P(None, "gz", "gx", "gy"), P("gz", "gx", "gy")),
        check_vma=False,
    )
```

```python
import functools

import jax
import jax.numpy as jnp
from jax import lax
from jax.sharding import PartitionSpec as P

time_step = 0.25
storage_rate = 0.002
source_rate = 0.003
critical_slope = 1.2
mass_floor = 0.5
shear_floor = 1.0

from jax.experimental import pallas as pl
from jax.experimental.pallas import tpu as pltpu

CHUNK = 12288
M_ROWS = 32
N_COLS = 512


SPLITS = 2
X_PARTS = (0, 3, 5)
Y_PARTS = (3, 1, 4)
Z_PARTS = (5, 4, 2)


def _split(v):
    hi = v.astype(jnp.bfloat16)
    lo = (v - hi.astype(jnp.float32)).astype(jnp.bfloat16)
    return [hi, lo]


def sums_kernel(count_ref, st_ref, ms_ref, cons_ref, vel_ref, w_ref, cell_ref, yf_ref, out_ref, xlo_ref, xhi_ref, ylo_ref, yhi_ref, zlo_ref, zhi_ref, acc_ref):
    count = count_ref[0, 0]
    acc_ref[...] = jnp.zeros_like(acc_ref)
    chunks = st_ref.shape[1] // CHUNK

    def body(k, carry):
        start = pl.multiple_of(k * CHUNK, CHUNK)
        span = pl.ds(start, CHUNK)
        st = [st_ref[pl.ds(i, 1), span] for i in range(6)]
        ms = ms_ref[:, span]
        cons = cons_ref[:, span]
        yf = yf_ref[:, span]
        slot = start + lax.broadcasted_iota(jnp.int32, (1, CHUNK), 1)
        weight = jnp.where(slot < count, w_ref[:, span], 0.0)
        sq_normal = st[0] * st[0] + st[1] * st[1] + st[2] * st[2]
        sq_shear = st[3] * st[3] + st[4] * st[4] + st[5] * st[5]
        shear_size = jnp.sqrt(1.5 * (sq_normal + 2.0 * sq_shear))
        yield_size = critical_slope * jnp.sqrt(ms * (cons - ms))
        factor = jnp.where(yf == 1, yield_size / jnp.maximum(shear_size, shear_floor), 1.0)
        stress = [st[i] * factor - ms if i < 3 else st[i] * factor for i in range(6)]
        values = [s * weight for s in stress]
        values += [vel_ref[pl.ds(i, 1), span] * weight for i in range(3)]
        values.append(weight)
        cell = cell_ref[:, span]
        m_key = (cell >> 12) * 8 + ((cell >> 7) & 7)
        n_key = ((cell >> 10) & 3) * 128 + (cell & 127)
        m_mask = lax.broadcasted_iota(jnp.int32, (M_ROWS, CHUNK), 0) == m_key
        zero = jnp.zeros((M_ROWS, CHUNK), jnp.bfloat16)
        pieces = []
        for v in values:
            for part in _split(v):
                pieces.append(jnp.where(m_mask, jnp.broadcast_to(part, (M_ROWS, CHUNK)), zero))
        lhs = jnp.concatenate(pieces, axis=0)
        one_hot = jnp.where(
            lax.broadcasted_iota(jnp.int32, (N_COLS, CHUNK), 0) == n_key, 1.0, 0.0
        ).astype(jnp.bfloat16)
        acc_ref[...] += lax.dot_general(
            lhs, one_hot, (((1,), (1,)), ((), ())), preferred_element_type=jnp.float32
        )
        return carry

    lax.fori_loop(0, chunks, body, 0)
    for comp in range(10):
        for level in range(16):
            rows = pl.ds((comp * SPLITS) * M_ROWS + (level >> 2) * 8, 8)
            lanes = pl.ds((level & 3) * 128, 128)
            total = acc_ref[rows, lanes]
            for s in range(1, SPLITS):
                total = total + acc_ref[pl.ds((comp * SPLITS + s) * M_ROWS + (level >> 2) * 8, 8), lanes]
            out_ref[comp, level] = total
            if comp in X_PARTS:
                slot = X_PARTS.index(comp)
                xlo_ref[slot, pl.ds(level, 1), :] = total[0:1, :]
                xhi_ref[slot, pl.ds(level, 1), :] = total[7:8, :]
            if comp in Y_PARTS:
                slot = Y_PARTS.index(comp)
                turned = total.T
                ylo_ref[slot, pl.ds(level, 1), :] = turned[0:1, :]
                yhi_ref[slot, pl.ds(level, 1), :] = turned[127:128, :]
            if comp in Z_PARTS:
                slot = Z_PARTS.index(comp)
                if level == 0:
                    zlo_ref[slot] = total
                if level == 15:
                    zhi_ref[slot] = total


def cell_sums_of(stress_trial, mean_stress, consolidation, point_velocity, point_weight, point_cell, yield_flag, point_count, levels, extent, breadth):
    n = mean_stress.shape[0]
    row = lambda a: a.reshape(1, n)
    vmem = pl.BlockSpec(memory_space=pltpu.VMEM)
    return pl.pallas_call(
        sums_kernel,
        out_shape=[
            jax.ShapeDtypeStruct(s, jnp.float32)
            for s in [(10, levels, extent, breadth)] + [(3, levels, breadth)] * 2 + [(3, levels, extent)] * 2
            + [(3, extent, breadth)] * 2
        ],
        in_specs=[pl.BlockSpec(memory_space=pltpu.SMEM)] + [vmem] * 7,
        out_specs=[vmem] * 7,
        scratch_shapes=[pltpu.VMEM((10 * SPLITS * M_ROWS, N_COLS), jnp.float32)],
        cost_estimate=pl.CostEstimate(
            flops=2 * 10 * SPLITS * M_ROWS * N_COLS * n, bytes_accessed=13 * 4 * n + 10 * 4 * levels * extent * breadth,
            transcendentals=3 * n,
        ),
    )(
        point_count.reshape(1, 1), stress_trial, row(mean_stress), row(consolidation), point_velocity,
        row(point_weight), row(point_cell), row(yield_flag),
    )


def padded_2(cells, sides, width):
    for axis, dim in sides:
        count = lax.axis_size(axis)
        ends = count - 1
        head = lax.slice_in_dim(cells, 0, width, axis=dim)
        tail = lax.slice_in_dim(cells, cells.shape[dim] - width, cells.shape[dim], axis=dim)
        cells = jnp.concatenate(
            [
                lax.ppermute(tail, axis, [(i, (i + 1) % count) for i in range(ends)]),
                cells,
                lax.ppermute(head, axis, [((i + 1) % count, i) for i in range(ends)]),
            ],
            axis=dim,
        )
    return cells


def along_x(padded):
    return (padded[..., 1:-1, 2:, 1:-1] - padded[..., 1:-1, :-2, 1:-1]) * 0.5


def along_y(padded):
    return (padded[..., 1:-1, 1:-1, 2:] - padded[..., 1:-1, 1:-1, :-2]) * 0.5


def along_z(padded):
    return (padded[..., 2:, 1:-1, 1:-1] - padded[..., :-2, 1:-1, 1:-1]) * 0.5


def harmonic(former, latter):
    return 2.0 * former * latter / (former + latter)


def returned_stress(stress_trial, mean_stress, consolidation, yield_flag):
    sq_normal = (
        stress_trial[0] * stress_trial[0]
        + stress_trial[1] * stress_trial[1]
        + stress_trial[2] * stress_trial[2]
    )
    sq_shear = (
        stress_trial[3] * stress_trial[3]
        + stress_trial[4] * stress_trial[4]
        + stress_trial[5] * stress_trial[5]
    )
    shear_size = jnp.sqrt(1.5 * (sq_normal + 2.0 * sq_shear))
    yield_size = critical_slope * jnp.sqrt(mean_stress * (consolidation - mean_stress))
    factor = jnp.where(yield_flag == 1, yield_size / jnp.maximum(shear_size, shear_floor), 1.0)
    isotropic = jnp.array([1.0, 1.0, 1.0, 0.0, 0.0, 0.0], dtype=jnp.float32)[:, None]
    return stress_trial * factor - isotropic * mean_stress


def point_sums(stress, point_velocity, weight, cell_index, segments):
    stacked = jnp.concatenate([stress * weight, point_velocity * weight, weight[None]], axis=0)
    return jax.vmap(
        lambda component: jax.ops.segment_sum(component, cell_index, num_segments=segments)
    )(stacked)


def brick_velocity(cell_sums, padded):
    floored = jnp.maximum(cell_sums[9], mass_floor)
    force_x = along_x(padded[0]) + along_y(padded[3]) + along_z(padded[5])
    force_y = along_x(padded[3]) + along_y(padded[1]) + along_z(padded[4])
    force_z = along_x(padded[5]) + along_y(padded[4]) + along_z(padded[2])
    return jnp.stack(
        [
            (cell_sums[6] + time_step * force_x) / floored,
            (cell_sums[7] + time_step * force_y) / floored,
            (cell_sums[8] + time_step * force_z) / floored,
        ]
    )


def divergence(padded_velocity):
    return along_x(padded_velocity[0]) + along_y(padded_velocity[1]) + along_z(padded_velocity[2])


def band_terms(porosity, permeability, level_below, level_above, at_top, dilation):
    up_face = harmonic(permeability, level_above)
    down_face = harmonic(level_below, permeability)
    top_face = jnp.where(at_top, permeability, up_face)
    lower_band = -time_step * down_face
    upper_band = -time_step * up_face
    main_band = storage_rate * porosity + time_step * (down_face + top_face)
    right_side = -source_rate * (1.0 - porosity) * dilation
    return (lower_band, main_band, upper_band, right_side)


def earlier(values, stride, filler):
    head = jnp.full((stride,) + values.shape[1:], filler, values.dtype)
    return jnp.concatenate([head, values[:-stride]], axis=0)


def later(values, stride, filler):
    tail = jnp.full((stride,) + values.shape[1:], filler, values.dtype)
    return jnp.concatenate([values[stride:], tail], axis=0)


def cyclic_solve(lower_band, main_band, upper_band, right_side):
    length = main_band.shape[0]
    for bit in range((length - 1).bit_length()):
        stride = 1 << bit
        back_weight = -lower_band / earlier(main_band, stride, 1.0)
        ahead_weight = -upper_band / later(main_band, stride, 1.0)
        new_lower = back_weight * earlier(lower_band, stride, 0.0)
        new_upper = ahead_weight * later(upper_band, stride, 0.0)
        new_main = (
            main_band
            + back_weight * earlier(upper_band, stride, 0.0)
            + ahead_weight * later(lower_band, stride, 0.0)
        )
        new_right = (
            right_side
            + back_weight * earlier(right_side, stride, 0.0)
            + ahead_weight * later(right_side, stride, 0.0)
        )
        lower_band, main_band, upper_band, right_side = (new_lower, new_main, new_upper, new_right)
    return right_side / main_band


MESH_AXES = ("gx", "gy", "gz")


def halo_kernel(sides, sizes, gathered, group, *refs):
    count = len(sides)
    sends = refs[:2 * count]
    gins = refs[2 * count:2 * count + gathered]
    recvs = refs[2 * count + gathered:4 * count + gathered]
    gouts = refs[4 * count + gathered:4 * count + 2 * gathered]
    send_sem, recv_sem, gsend_sem, grecv_sem = refs[4 * count + 2 * gathered:]
    me = {a: lax.axis_index(a) for a in MESH_AXES}

    def peer(axis, delta):
        return tuple(me[a] + delta if a == axis else me[a] for a in MESH_AXES)

    def across(level):
        return tuple(level if a == "gz" else me[a] for a in MESH_AXES)

    links = []
    for i, axis in enumerate(sides):
        links.append((axis, -1, me[axis] > 0, 2 * i, 2 * i + 1))
        links.append((axis, 1, me[axis] < sizes[i] - 1, 2 * i + 1, 2 * i))
    barrier = pltpu.get_barrier_semaphore()
    peers = 0
    k = me["gz"]
    partner = (k // 2) * 2 + (1 - k % 2)
    counterpart = (1 - k // 2) * 2 + k % 2
    diagonal = (1 - k // 2) * 2 + (1 - k % 2)
    for axis, delta, present, _, _ in links:
        if gathered and axis == "gz":
            present = jnp.logical_and(present, k + delta == diagonal)
        peers = peers + present.astype(jnp.int32)

        @pl.when(present)
        def _():
            pl.semaphore_signal(barrier, 1, device_id=peer(axis, delta), device_id_type=pl.DeviceIdType.MESH)
    if gathered:
        for target in (partner, counterpart):
            pl.semaphore_signal(barrier, 1, device_id=across(target), device_id_type=pl.DeviceIdType.MESH)
        peers = peers + 2
    pl.semaphore_wait(barrier, peers)
    copies = []
    for axis, delta, present, src, dst in links:
        copy = pltpu.make_async_remote_copy(
            src_ref=sends[src], dst_ref=recvs[dst], send_sem=send_sem.at[src], recv_sem=recv_sem.at[dst],
            device_id=peer(axis, delta), device_id_type=pl.DeviceIdType.MESH,
        )
        copies.append((present, copy))

        @pl.when(present)
        def _():
            copy.start()
    gcopies = []
    for j in range(gathered):
        for n, target in enumerate((partner, counterpart)):
            copy = pltpu.make_async_remote_copy(
                src_ref=gins[j], dst_ref=gouts[j].at[k], send_sem=gsend_sem.at[3 * j + n],
                recv_sem=grecv_sem.at[3 * j + n], device_id=across(target), device_id_type=pl.DeviceIdType.MESH,
            )
            copy.start()
            gcopies.append(copy)
    for j in range(gathered):
        gouts[j][k] = gins[j][...]
    for j in range(gathered):
        for n, origin in enumerate((partner, counterpart)):
            incoming = pltpu.make_async_remote_copy(
                src_ref=gins[j], dst_ref=gouts[j].at[origin], send_sem=gsend_sem.at[3 * j + n],
                recv_sem=grecv_sem.at[3 * j + n], device_id=across(origin), device_id_type=pl.DeviceIdType.MESH,
            )
            incoming.wait_recv()
        relay = pltpu.make_async_remote_copy(
            src_ref=gouts[j].at[counterpart], dst_ref=gouts[j].at[counterpart], send_sem=gsend_sem.at[3 * j + 2],
            recv_sem=grecv_sem.at[3 * j + 2], device_id=across(partner), device_id_type=pl.DeviceIdType.MESH,
        )
        relay.start()
        gcopies.append(relay)
    for j in range(gathered):
        relayed = pltpu.make_async_remote_copy(
            src_ref=gouts[j].at[diagonal], dst_ref=gouts[j].at[diagonal], send_sem=gsend_sem.at[3 * j + 2],
            recv_sem=grecv_sem.at[3 * j + 2], device_id=across(partner), device_id_type=pl.DeviceIdType.MESH,
        )
        relayed.wait_recv()
    for axis, delta, present, src, dst in links:
        incoming = pltpu.make_async_remote_copy(
            src_ref=sends[dst], dst_ref=recvs[src], send_sem=send_sem.at[dst], recv_sem=recv_sem.at[src],
            device_id=peer(axis, delta), device_id_type=pl.DeviceIdType.MESH,
        )

        @pl.when(present)
        def _():
            incoming.wait_recv()

        @pl.when(jnp.logical_not(present))
        def _():
            recvs[src][...] = jnp.zeros(recvs[src].shape, recvs[src].dtype)
    for present, copy in copies:
        @pl.when(present)
        def _():
            copy.wait_send()
    for copy in gcopies:
        copy.wait_send()


def exchange(cells, sides, collective, gathers=(), given=None):
    sends = []
    for axis, dim in sides:
        size = cells.shape[dim]
        sends.append(lax.index_in_dim(cells, 0, axis=dim, keepdims=False))
        sends.append(lax.index_in_dim(cells, size - 1, axis=dim, keepdims=False))
    if given is not None:
        sends = list(given)
    axes = tuple(axis for axis, _ in sides)
    sizes = tuple(lax.axis_size(axis) for axis in axes)
    group = lax.axis_size("gz")
    vmem = pl.BlockSpec(memory_space=pltpu.VMEM)
    assert group == 4 or not gathers
    slots = max(1, len(gathers) * (group - 1))
    outs = pl.pallas_call(
        functools.partial(halo_kernel, axes, sizes, len(gathers), group),
        out_shape=[jax.ShapeDtypeStruct(s.shape, s.dtype) for s in sends]
        + [jax.ShapeDtypeStruct((group,) + g.shape, g.dtype) for g in gathers],
        in_specs=[vmem] * (len(sends) + len(gathers)),
        out_specs=[vmem] * (len(sends) + len(gathers)),
        scratch_shapes=[
            pltpu.SemaphoreType.DMA((max(1, len(sends)),)), pltpu.SemaphoreType.DMA((max(1, len(sends)),)),
            pltpu.SemaphoreType.DMA((slots,)), pltpu.SemaphoreType.DMA((slots,)),
        ],
        compiler_params=pltpu.CompilerParams(collective_id=collective, has_side_effects=True),
    )(*sends, *gathers)
    recvs = outs[:len(sends)]
    faces = {
        dim: (jnp.expand_dims(recvs[2 * i], dim), jnp.expand_dims(recvs[2 * i + 1], dim))
        for i, (axis, dim) in enumerate(sides)
    }
    stacked = [g.reshape((group * g.shape[1],) + g.shape[2:]) for g in outs[len(sends):]]
    return faces, stacked


def faces_kernel(parts, cells_ref, *out_refs):
    chans, levels, extent, breadth = cells_ref.shape
    xlo, xhi, ylo, yhi = out_refs[:4]
    for slot, c in enumerate(parts[0]):
        for level in range(levels):
            tile = cells_ref[c, level]
            xlo[slot, pl.ds(level, 1), :] = tile[0:1, :]
            xhi[slot, pl.ds(level, 1), :] = tile[extent - 1:extent, :]
    for slot, c in enumerate(parts[1]):
        for level in range(levels):
            turned = cells_ref[c, level].T
            ylo[slot, pl.ds(level, 1), :] = turned[0:1, :]
            yhi[slot, pl.ds(level, 1), :] = turned[breadth - 1:breadth, :]
    if len(parts) > 2:
        for slot, c in enumerate(parts[2]):
            out_refs[4][slot] = cells_ref[c, 0]
            out_refs[5][slot] = cells_ref[c, levels - 1]


def faces_by_kernel(cells, parts):
    chans, levels, extent, breadth = cells.shape
    shapes = [(len(parts[0]), levels, breadth)] * 2 + [(len(parts[1]), levels, extent)] * 2
    if len(parts) > 2:
        shapes += [(len(parts[2]), extent, breadth)] * 2
    vmem = pl.BlockSpec(memory_space=pltpu.VMEM)
    return pl.pallas_call(
        functools.partial(faces_kernel, parts),
        out_shape=[jax.ShapeDtypeStruct(s, cells.dtype) for s in shapes],
        in_specs=[vmem],
        out_specs=[vmem] * len(shapes),
    )(cells)


def solve_kernel(levels, poro_ref, perm_ref, right_ref, out_ref, grad_ref, xlo, xhi, ylo, yhi, padded_ref):
    perm = perm_ref[...]
    lid = jnp.zeros((1,) + perm.shape[1:], jnp.float32)
    level_above = jnp.concatenate([perm[1:], lid], axis=0)
    level_below = jnp.concatenate([lid, perm[:-1]], axis=0)
    up_face = harmonic(perm, level_above)
    down_face = harmonic(level_below, perm)
    top_face = jnp.concatenate([up_face[:-1], perm[-1:]], axis=0)
    lower_band = -time_step * down_face
    upper_band = -time_step * up_face
    main_band = storage_rate * poro_ref[...] + time_step * (down_face + top_face)
    solved = cyclic_solve(lower_band, main_band, upper_band, right_ref[...])
    height, extent, breadth = solved.shape
    padded_ref[pl.ds(0, 1)] = lid
    padded_ref[pl.ds(height + 1, 1)] = lid
    padded_ref[pl.ds(1, height)] = solved
    first = lax.axis_index("gz") * levels
    out_ref[...] = padded_ref[pl.ds(first + 1, levels)]
    grad_ref[...] = (padded_ref[pl.ds(first + 2, levels)] - padded_ref[pl.ds(first, levels)]) * 0.5
    for level in range(levels):
        tile = out_ref[level]
        xlo[pl.ds(level, 1), :] = tile[0:1, :]
        xhi[pl.ds(level, 1), :] = tile[extent - 1:extent, :]
        turned = tile.T
        ylo[pl.ds(level, 1), :] = turned[0:1, :]
        yhi[pl.ds(level, 1), :] = turned[breadth - 1:breadth, :]


def column_solve(porosity, permeability, right_side, levels):
    height, extent, breadth = right_side.shape
    vmem = pl.BlockSpec(memory_space=pltpu.VMEM)
    shapes = [(levels, extent, breadth)] * 2 + [(levels, breadth)] * 2 + [(levels, extent)] * 2
    return pl.pallas_call(
        functools.partial(solve_kernel, levels),
        out_shape=[jax.ShapeDtypeStruct(s, jnp.float32) for s in shapes],
        in_specs=[vmem] * 3,
        out_specs=[vmem] * len(shapes),
        scratch_shapes=[pltpu.VMEM((height + 2, extent, breadth), jnp.float32)],
    )(porosity, permeability, right_side)


def face_from(part, axis, from_lower):
    count = lax.axis_size(axis)
    if from_lower:
        pairs = [(i, i + 1) for i in range(count - 1)]
    else:
        pairs = [(i + 1, i) for i in range(count - 1)]
    return lax.ppermute(part, axis, pairs)


def faces_of(cells, sides):
    got = {}
    for axis, dim in sides:
        size = cells.shape[dim]
        got[dim] = (
            face_from(lax.slice_in_dim(cells, size - 1, size, axis=dim), axis, True),
            face_from(lax.slice_in_dim(cells, 0, 1, axis=dim), axis, False),
        )
    return got


def along(cells, faces, dim):
    size = cells.shape[dim]
    lower, upper = faces[dim]
    ahead = jnp.concatenate([lax.slice_in_dim(cells, 1, size, axis=dim), upper], axis=dim)
    behind = jnp.concatenate([lower, lax.slice_in_dim(cells, 0, size - 1, axis=dim)], axis=dim)
    return (ahead - behind) * 0.5


def shards(
    stress_trial,
    mean_stress,
    consolidation,
    point_velocity,
    point_weight,
    point_cell,
    yield_flag,
    point_count,
    porosity,
    permeability,
):
    levels, extent, breadth = porosity.shape
    cell_sums, *stress_faces = cell_sums_of(
        stress_trial, mean_stress, consolidation, point_velocity, point_weight, point_cell,
        yield_flag, point_count, levels, extent, breadth,
    )
    sides = (("gx", 2), ("gy", 3), ("gz", 1))
    stress_sums = cell_sums[:6]
    sf, _ = exchange(stress_sums, sides, 0, given=stress_faces)
    def part(dim, parts, c):
        s = parts.index(c)
        return {dim: (sf[dim][0][s:s + 1], sf[dim][1][s:s + 1])}

    d_x = lambda c: along(stress_sums[c:c + 1], part(2, X_PARTS, c), 2)[0]
    d_y = lambda c: along(stress_sums[c:c + 1], part(3, Y_PARTS, c), 3)[0]
    d_z = lambda c: along(stress_sums[c:c + 1], part(1, Z_PARTS, c), 1)[0]
    floored = jnp.maximum(cell_sums[9], mass_floor)
    force_x = d_x(0) + d_y(3) + d_z(5)
    force_y = d_x(3) + d_y(1) + d_z(4)
    force_z = d_x(5) + d_y(4) + d_z(2)
    velocity = jnp.stack(
        [
            (cell_sums[6] + time_step * force_x) / floored,
            (cell_sums[7] + time_step * force_y) / floored,
            (cell_sums[8] + time_step * force_z) / floored,
        ]
    )
    vf, (all_permeability,) = exchange(
        velocity, sides, 1, (permeability,), given=faces_by_kernel(velocity, ((0,), (1,), (2,)))
    )
    dilation = (
        along(velocity[0:1], {2: vf[2]}, 2)[0]
        + along(velocity[1:2], {3: vf[3]}, 3)[0]
        + along(velocity[2:3], {1: vf[1]}, 1)[0]
    )
    right_side = -source_rate * (1.0 - porosity) * dilation
    _, (all_right, all_porosity) = exchange(right_side, (), 3, (right_side, porosity))
    zero_level = jnp.zeros((1, extent, breadth), jnp.float32)
    pressure, rise, *pressure_faces = column_solve(all_porosity, all_permeability, all_right, levels)
    pf, _ = exchange(pressure, (("gx", 1), ("gy", 2)), 2, given=pressure_faces)
    gradient = jnp.stack([along(pressure, pf, 1), along(pressure, pf, 2), rise])
    return (velocity - time_step * gradient, pressure)


def solution(mesh):
    placed = (
        P(None, ("gx", "gy", "gz")),
        P(("gx", "gy", "gz")),
        P(("gx", "gy", "gz")),
        P(None, ("gx", "gy", "gz")),
        P(("gx", "gy", "gz")),
        P(("gx", "gy", "gz")),
        P(("gx", "gy", "gz")),
        P("gx", "gy", "gz"),
        P("gz", "gx", "gy"),
        P("gz", "gx", "gy"),
    )
    return jax.shard_map(
        shards,
        mesh=mesh,
        in_specs=placed,
        out_specs=(P(None, "gz", "gx", "gy"), P("gz", "gx", "gy")),
        check_vma=False,
    )
```
